32 devices in a mesh: dp: 8 (over z, y), tensor: 4 (over x, core).
Axes of the slice: x: 2, y: 2, z: 4, core: 2. Of those that a mesh axis runs over, the one named last changes fastest.
Arguments:
- tokens: bfloat16 [12288, 768], P('dp', 'tensor'), may hold values from -6 to 6
- cotangent: bfloat16 [12288, 768], P('dp', 'tensor'), may hold values from -6 to 6
- seq_start: int32 [12288], P('dp'), may hold values from 0 to 384, as said below
- row_place: int32 [8, 1536], P('dp'), may hold values from 0 to 1535, each once within a row
- qkv_weight: bfloat16 [3, 768, 768], P(None, None, 'tensor'), may hold values from -0.21875 to 0.21875
- qv_bias: bfloat16 [2, 768], P(None, 'tensor'), may hold values from -1.5 to 1.5
- out_weight: bfloat16 [768, 768], P('tensor'), may hold values from -0.875 to 0.875
- out_bias: bfloat16 [768], replicated, may hold values from -1.5 to 1.5
- first_gain: bfloat16 [768], replicated, may hold values from 0.5 to 1.5
- first_shift: bfloat16 [768], replicated, may hold values from -1.5 to 1.5
- up_weight: bfloat16 [2, 768, 3072], P(None, None, 'tensor'), may hold values from -0.21875 to 0.21875
- up_bias: bfloat16 [2, 3072], P(None, 'tensor'), may hold values from -1.5 to 1.5
- down_weight: bfloat16 [3072, 768], P('tensor'), may hold values from -0.15625 to 0.15625
- down_bias: bfloat16 [768], replicated, may hold values from -1.5 to 1.5
- second_gain: bfloat16 [768], replicated, may hold values from 0.5 to 1.5
- second_shift: bfloat16 [768], replicated, may hold values from -1.5 to 1.5
Outputs:
- layer_out: bfloat16 [12288, 768], P('dp', 'tensor')
- input_grad: bfloat16 [12288, 768], P('dp', 'tensor')
- qkv_grad: float32 [3, 768, 768], P(None, 'dp', 'tensor')
- qv_bias_grad: float32 [2, 768], P(None, 'tensor')
- out_grad: float32 [768, 768], P('tensor', 'dp')
- out_bias_grad: float32 [768], P('dp')
- first_gain_grad: float32 [768], P('dp')
- first_shift_grad: float32 [768], P('dp')
- up_grad: float32 [2, 768, 3072], P(None, 'dp', 'tensor')
- up_bias_grad: float32 [2, 3072], P(None, 'tensor')
- down_grad: float32 [3072, 768], P('tensor', 'dp')
- down_bias_grad: float32 [768], P('dp')
- second_gain_grad: float32 [768], P('dp')
- second_shift_grad: float32 [768], P('dp')
The draws below stay inside these ranges and needn't reach their ends.
Inputs may be any that keep to these rules, and one draw needn't show every extreme that they name: seq_start of a token is the offset, within its aligned block of 512 packed rows, of the first token of its sequence; sequences are 128, 256 or 512 tokens long, begin at multiples of 128 and never cross a block. Each row of row_place is a permutation of 0 to 1535.
All inputs are finite; a program needn't handle non-finite values.
Results may differ from the reference program's by a relative error of at most 0.02.
The reference program's roundings to bfloat16 on the way count: a program that leaves them out, or rounds other values in their place, can miss the bound.
Values may be sent and summed in bfloat16 or wider, within the bound.
A program may use at most 128 MiB of HBM per device.

```python
import jax
import jax.numpy as jnp
from jax import lax

D = 768
HEADS = 12
HEAD_DIM = 64
FF = 3072
UNIT = 128
BLOCK = 512
TOK_DEV = 1536
GROUPS = 8
TOKENS = 12288
N_DP = 8


def draw_seq_start(key, part):
    pattern_table = jnp.array([[0, 0, 0, 0], [0, 0, 2, 2], [0, 0, 2, 3], [0, 1, 2, 2], [0, 1, 1, 3], [0, 1, 2, 3]], jnp.int32)
    block_count = TOKENS // (4 * UNIT)
    picked = jax.random.randint(jax.random.fold_in(key, 11), (block_count,), 0, 6)
    picked = picked.at[0].set(5)
    unit_starts = pattern_table[picked] * UNIT
    return jnp.repeat(unit_starts, UNIT, axis=1).reshape(TOKENS).astype(jnp.int32)


def strengthened(result, key, source, target, parts, factor):
    owner, partner = [(jnp.arange(result.shape[dim]) // (result.shape[dim] // parts)).reshape([-1 if axis == dim else 1 for axis in range(result.ndim)]) for dim in (source, target)]
    chosen = jax.random.permutation(key, parts)[partner]
    strong = (owner == chosen) | (owner == (partner + parts // 2) % parts)
    return jnp.where(strong, factor * result, result)


def shard_levels(own_key, shape, pieces, smallest, high):
    def one(dim, blocks):
        steps = jax.random.uniform(jax.random.fold_in(jax.random.fold_in(own_key, 6), dim), (blocks,), jnp.float32, smallest / len(pieces), high / len(pieces))
        return jnp.repeat(jnp.exp(steps), shape[dim] // blocks).reshape((-1,) + (1,) * (len(shape) - dim - 1))

    factor_of = one(*pieces[0])
    for cut in pieces[1:]:
        factor_of = factor_of * one(*cut)
    return factor_of


def noise(rng, extent, scale, most, shards=(), kind=jnp.bfloat16):
    level = shard_levels(rng, extent, shards, -0.22, 0.18) if shards else 1.0
    values = jax.random.normal(rng, extent, jnp.float32) * scale * level
    return jnp.minimum(jnp.maximum(values, -most), most).astype(kind)


def noise_with(key, shape, scale, bound, shards, heavy, held_as=jnp.bfloat16):
    result = scale * jax.random.normal(key, shape, jnp.float32)
    if shards:
        result = result * shard_levels(key, shape, shards, -0.22, 0.18)
    return jnp.clip(strengthened(result, jax.random.fold_in(key, 3), *heavy), -bound, bound).astype(held_as)


def setup_inputs(seed: int = 0) -> dict:
    streams_of = jax.random.split(jax.random.key(seed), 17)
    tokens = noise_with(streams_of[0], (TOKENS, D), 1.0, 6.0, ((0, 8), (1, 4)), (0, 1, 8, 2.0))
    cotangent = noise_with(streams_of[1], (TOKENS, D), 1.0, 6.0, ((0, 8), (1, 4)), (0, 1, 8, 2.0))
    seq_start = draw_seq_start(jax.random.fold_in(streams_of[16], 71), 0)
    row_place = jax.vmap(lambda own: jax.random.permutation(own, TOK_DEV))(jax.random.split(streams_of[3], GROUPS)).reshape((GROUPS, TOK_DEV)).astype(jnp.int32)
    qkv_weight = noise(streams_of[4], (3, D, D), D ** -0.5, 0.21875, ((2, 4),))
    qv_bias = noise(streams_of[5], (2, D), 0.3, 1.5, ((1, 4),))
    out_weight = noise(streams_of[6], (D, D), (D // 16) ** -0.5, 0.875, ((0, 4),))
    out_bias = noise(streams_of[7], (D,), 0.3, 1.5)
    first_gain = jnp.clip(1.0 + 0.1 * jax.random.normal(streams_of[8], (D,), jnp.float32), 0.5, 1.5).astype(jnp.bfloat16)
    first_shift = noise(streams_of[9], (D,), 0.3, 1.5)
    up_weight = noise(streams_of[10], (2, D, FF), D ** -0.5, 0.21875, ((2, 4),))
    up_bias = noise(streams_of[11], (2, FF), 0.3, 1.5, ((1, 4),))
    down_weight = noise(streams_of[12], (FF, D), (FF // 2) ** -0.5, 0.15625, ((0, 4),))
    down_bias = noise(streams_of[13], (D,), 0.3, 1.5)
    second_gain = jnp.clip(1.0 + 0.1 * jax.random.normal(streams_of[14], (D,), jnp.float32), 0.5, 1.5).astype(jnp.bfloat16)
    second_shift = noise(streams_of[15], (D,), 0.3, 1.5)
    return {"tokens": tokens, "cotangent": cotangent, "seq_start": seq_start, "row_place": row_place, "qkv_weight": qkv_weight, "qv_bias": qv_bias, "out_weight": out_weight, "out_bias": out_bias, "first_gain": first_gain, "first_shift": first_shift, "up_weight": up_weight, "up_bias": up_bias, "down_weight": down_weight, "down_bias": down_bias, "second_gain": second_gain, "second_shift": second_shift}


@jax.custom_vjp
def low(v):
    return lax.optimization_barrier(v.astype(jnp.bfloat16)).astype(jnp.float32)

@jax.custom_vjp
def low_back(v):
    return v

def low_keep(v):
    return (low(v), None)

def low_pass(kept, grad):
    return (grad,)

def back_keep(v):
    return (v, None)

def back_low(kept, grad):
    return (low(grad),)
low.defvjp(low_keep, low_pass)
low_back.defvjp(back_keep, back_low)

def layer_norm(values, scale_row, shift_row):
    center = values - lax.optimization_barrier(jnp.mean(values, axis=-1, keepdims=True))
    spread = lax.optimization_barrier(jnp.mean(center * center, axis=-1, keepdims=True))
    return center * lax.rsqrt(spread + 1e-05) * scale_row + shift_row

def to_packed(arrival, row_place):
    piece_rows = TOK_DEV // N_DP
    columns = arrival.shape[1]
    received = arrival.reshape(N_DP, N_DP, piece_rows, columns).transpose(1, 0, 2, 3).reshape(N_DP, TOK_DEV, columns)

    def place_one(rows_in, slot_index):
        return jnp.zeros_like(rows_in).at[slot_index].set(rows_in)
    return jax.vmap(place_one)(received, row_place)

def from_packed(packed, row_place):
    piece_rows = TOK_DEV // N_DP
    columns = packed.shape[2]

    def take_one(rows_in, slot_index):
        return rows_in[slot_index]
    received = jax.vmap(take_one)(packed, row_place)
    return received.reshape(N_DP, N_DP, piece_rows, columns).transpose(1, 0, 2, 3).reshape(N_DP * TOK_DEV, columns)

def encoder_layer(params, packed, starts):
    qkv_weight, qv_bias, out_weight, out_bias, first_gain, first_shift, up_weight, up_bias, down_weight, down_bias, second_gain, second_shift = params
    highest = lax.Precision.HIGHEST
    row_count = packed.shape[0]
    blocks = row_count // BLOCK
    bias_rows = jnp.stack([qv_bias[0], jnp.zeros_like(qv_bias[0]), qv_bias[1]])
    projected = jnp.einsum('td,kde->kte', packed, qkv_weight, precision=highest) + bias_rows[:, None, :]
    qkv_rows = low_back(low(projected))
    split_heads = qkv_rows.reshape(3, blocks, BLOCK, HEADS, HEAD_DIM)
    queries = split_heads[0]
    key_rows = split_heads[1]
    value_rows = split_heads[2]
    heads_idx = jnp.arange(HEADS).astype(jnp.float32)
    slopes = 2.0 ** (-8.0 * (heads_idx + 1.0) / HEADS)
    position = jnp.arange(BLOCK).astype(jnp.float32)
    distance = jnp.abs(position[:, None] - position[None, :])
    alibi_bias = -slopes[:, None, None] * distance[None]
    raw_scores = jnp.einsum('bqhe,bkhe->bhqk', queries, key_rows, precision=highest)
    scored = raw_scores * HEAD_DIM ** (-0.5) + alibi_bias[None]
    block_starts = starts.reshape(blocks, BLOCK)
    same_seq = block_starts[:, :, None] == block_starts[:, None, :]
    scored = low_back(jnp.where(same_seq[:, None], scored, -1e+30))
    row_max = lax.optimization_barrier(jnp.max(scored, axis=-1, keepdims=True))
    exponent = jnp.exp(scored - row_max)
    attn_probs = exponent / lax.optimization_barrier(jnp.sum(exponent, axis=-1, keepdims=True))
    context = jnp.einsum('bhqk,bkhe->bqhe', low(attn_probs), value_rows, precision=highest)
    context = low_back(low(context.reshape(row_count, D)))
    attended = low_back(jnp.dot(context, out_weight, precision=highest)) + out_bias
    hidden = packed + attended
    normed = layer_norm(hidden, first_gain, first_shift)
    lifted = jnp.einsum('td,kdf->ktf', low(normed), up_weight, precision=highest) + up_bias[:, None, :]
    lifted = low_back(lifted)
    gated = low(jax.nn.gelu(lifted[0], approximate=False) * lifted[1])
    ffn_out = low_back(jnp.dot(gated, down_weight, precision=highest)) + down_bias
    mixed_rows = normed + ffn_out
    return layer_norm(mixed_rows, second_gain, second_shift)

def reference(tokens, cotangent, seq_start, row_place, qkv_weight, qv_bias, out_weight, out_bias, first_gain, first_shift, up_weight, up_bias, down_weight, down_bias, second_gain, second_shift):
    params = tuple((weight_arg.astype(jnp.float32) for weight_arg in (qkv_weight, qv_bias, out_weight, out_bias, first_gain, first_shift, up_weight, up_bias, down_weight, down_bias, second_gain, second_shift)))
    packed_in = to_packed(tokens, row_place)
    packed_cot = to_packed(cotangent, row_place)
    group_starts = seq_start.reshape(N_DP, TOK_DEV)

    def group_step(grad_total, inputs):
        group_rows, group_cot, starts = inputs

        def forward(param_set, rows_in):
            return encoder_layer(param_set, rows_in, starts)
        layer_rows, pullback = jax.vjp(forward, params, group_rows.astype(jnp.float32))
        param_grads, input_grads = pullback(group_cot.astype(jnp.float32))

        def add_up(former, latter):
            return former + latter
        grad_total = jax.tree.map(add_up, grad_total, param_grads)
        return (grad_total, (layer_rows.astype(jnp.bfloat16), input_grads.astype(jnp.bfloat16)))
    zero_grads = jax.tree.map(jnp.zeros_like, params)
    grad_total, (layer_rows, input_rows) = lax.scan(group_step, zero_grads, (packed_in, packed_cot, group_starts))
    layer_out = from_packed(layer_rows, row_place)
    input_grad = from_packed(input_rows, row_place)
    factor = TOKENS ** (-0.5)
    scaled = tuple((grad_part * factor for grad_part in grad_total))
    return (layer_out, input_grad, scaled[0], scaled[1], scaled[2], scaled[3], scaled[4], scaled[5], scaled[6], scaled[7], scaled[8], scaled[9], scaled[10], scaled[11])
```

```python
import jax
import jax.numpy as jnp
from jax import lax
from jax.sharding import PartitionSpec as P

HEADS = 12
HEAD_DIM = 64
BLOCK = 512
BF = jnp.bfloat16
F32 = jnp.float32


def dot(a, b, dims):
    return lax.dot_general(a, b, (dims, ((), ())), preferred_element_type=F32)


def alibi_terms(part_index, local_heads, block_rows):
    heads_idx = (part_index * local_heads + jnp.arange(local_heads)).astype(F32)
    slopes = 2.0 ** (-8.0 * (heads_idx + 1.0) / HEADS)
    position = jnp.arange(block_rows).astype(F32)
    distance = jnp.abs(position[:, None] - position[None, :])
    return -slopes[:, None, None] * distance[None]


def block_scores(queries, key_rows, alibi_bias, same_seq, score_scale):
    raw_scores = jnp.einsum("bqhe,bkhe->bhqk", queries, key_rows, preferred_element_type=F32)
    scored = raw_scores * score_scale + alibi_bias[None]
    return jnp.where(same_seq[:, None], scored, -1e30)


def softmax_rows(scored):
    row_max = jnp.max(scored, axis=-1, keepdims=True)
    exponent = jnp.exp(scored - row_max)
    denominator = jnp.sum(exponent, axis=-1, keepdims=True)
    return (exponent / denominator, row_max + jnp.log(denominator))


def gather_columns(rows):
    return lax.all_gather(rows, "tensor", axis=1, tiled=True)


def scatter_columns(rows):
    return lax.psum_scatter(rows, "tensor", scatter_dimension=1, tiled=True)


def merge_stats(values, weighted, columns):
    width = values.shape[1]
    own_mean = jnp.mean(values, axis=1)
    offset = values - own_mean[:, None]
    parts = jnp.stack(
        [own_mean, jnp.sum(offset * offset, axis=1), jnp.sum(weighted, axis=1), jnp.sum(weighted * offset, axis=1)]
    )
    shares = lax.all_gather(parts, "tensor", axis=0)
    mean = jnp.mean(shares[:, 0], axis=0)
    gap = shares[:, 0] - mean
    spread = jnp.sum(shares[:, 1] + width * gap * gap, axis=0) / columns
    rs = lax.rsqrt(spread + 1e-05)
    e_mean = jnp.sum(shares[:, 2], axis=0) / columns
    en_mean = rs * jnp.sum(shares[:, 3] + gap * shares[:, 2], axis=0) / columns
    return mean[:, None], rs[:, None], e_mean[:, None], en_mean[:, None]


def on_device(
    tokens,
    cotangent,
    seq_start,
    row_place,
    qkv_weight,
    qv_bias,
    out_weight,
    out_bias,
    first_gain,
    first_shift,
    up_weight,
    up_bias,
    down_weight,
    down_bias,
    second_gain,
    second_shift,
):
    row_count = tokens.shape[0]
    width = tokens.shape[1]
    columns = qkv_weight.shape[1]
    local_heads = qkv_weight.shape[2] // HEAD_DIM
    blocks = row_count // BLOCK
    part_index = lax.axis_index("tensor")
    score_scale = HEAD_DIM ** (-0.5)
    grad_scale = (row_count * lax.axis_size("dp")) ** (-0.5)

    def own(vector):
        return lax.dynamic_slice_in_dim(vector.astype(F32), part_index * width, width, 0)

    arr_tokens = lax.all_to_all(tokens, "dp", split_axis=0, concat_axis=0, tiled=True)
    arr_cot = lax.all_to_all(cotangent, "dp", split_axis=0, concat_axis=0, tiled=True)
    slot_index = row_place[0]
    row_ids = lax.broadcasted_iota(jnp.int32, (row_count, row_count), 0)
    placing = (row_ids == slot_index[None, :]).astype(BF)
    in_cols = dot(placing, arr_tokens, ((1,), (0,))).astype(BF)
    cot_cols = dot(placing, arr_cot, ((1,), (0,))).astype(BF)
    packed_in = gather_columns(in_cols)
    full_out = lax.all_gather(out_weight, "tensor", axis=0, tiled=True)

    alibi_bias = alibi_terms(part_index, local_heads, BLOCK)
    block_starts = seq_start.reshape(blocks, BLOCK)
    same_seq = block_starts[:, :, None] == block_starts[:, None, :]
    bias_rows = jnp.stack([qv_bias[0], jnp.zeros_like(qv_bias[0]), qv_bias[1]]).astype(F32)
    projected = jnp.einsum("td,kde->kte", packed_in, qkv_weight, preferred_element_type=F32)
    qkv_rows = (projected + bias_rows[:, None, :]).astype(BF)
    split_heads = qkv_rows.reshape(3, blocks, BLOCK, local_heads, HEAD_DIM)
    queries = split_heads[0]
    key_rows = split_heads[1]
    value_rows = split_heads[2]
    attn_probs, log_total = softmax_rows(block_scores(queries, key_rows, alibi_bias, same_seq, score_scale))
    context = jnp.einsum("bhqk,bkhe->bqhe", attn_probs.astype(BF), value_rows, preferred_element_type=F32)
    context = context.reshape(row_count, local_heads * HEAD_DIM).astype(BF)

    wide_context = gather_columns(context)
    attended = dot(wide_context, full_out, ((1,), (0,)))
    hidden = packed_in.astype(F32) + (attended + out_bias.astype(F32))
    center = hidden - jnp.mean(hidden, axis=1, keepdims=True)
    first_rs = lax.rsqrt(jnp.mean(center * center, axis=1, keepdims=True) + 1e-05)
    normed = center * first_rs * first_gain.astype(F32) + first_shift.astype(F32)
    normed_low = normed.astype(BF)
    first_unit = lax.dynamic_slice_in_dim(center * first_rs, part_index * width, width, 1)
    normed_cols = first_unit * own(first_gain) + own(first_shift)

    lifted = jnp.einsum("td,kdf->ktf", normed_low, up_weight, preferred_element_type=F32)
    lifted = lifted + up_bias.astype(F32)[:, None, :]
    half_erf = 0.5 * (1.0 + lax.erf(lifted[0] * (0.5**0.5)))
    gelu_gate = lifted[0] * half_erf
    gated_low = (gelu_gate * lifted[1]).astype(BF)
    ffn_part = dot(gated_low, down_weight, ((1,), (0,)))
    ffn_cols = scatter_columns(ffn_part.astype(BF)).astype(F32)
    mixed_cols = normed_cols + (ffn_cols + own(down_bias))
    cot_wide = cot_cols.astype(F32)
    weighted = cot_wide * own(second_gain)
    mean, rs, e_mean, en_mean = merge_stats(mixed_cols, weighted, columns)
    second_unit = (mixed_cols - mean) * rs
    result_cols = second_unit * own(second_gain) + own(second_shift)
    d_mixed_cols = rs * (weighted - e_mean - second_unit * en_mean)
    d_second_gain = jnp.sum(cot_wide * second_unit, axis=0)
    d_second_shift = jnp.sum(cot_wide, axis=0)
    g_down_bias = jnp.sum(d_mixed_cols, axis=0)

    def unpacked(rows):
        placed = dot(placing, rows, ((0,), (0,))).astype(BF)
        return lax.all_to_all(placed, "dp", split_axis=0, concat_axis=0, tiled=True)

    layer_out = unpacked(result_cols.astype(BF))

    d_mixed_low = gather_columns(d_mixed_cols.astype(BF))
    g_down = dot(d_mixed_low, gated_low, ((0,), (0,)))
    d_gated = dot(d_mixed_low, down_weight, ((1,), (1,)))
    gelu_slope = half_erf + lifted[0] * jnp.exp(-0.5 * lifted[0] * lifted[0]) * ((2.0 * jnp.pi) ** (-0.5))
    d_gate = (d_gated * lifted[1] * gelu_slope).astype(BF)
    d_value = (d_gated * gelu_gate).astype(BF)
    g_gate = dot(normed_low, d_gate, ((0,), (0,)))
    g_value = dot(normed_low, d_value, ((0,), (0,)))
    g_up_bias = jnp.stack([jnp.sum(d_gate, axis=0, dtype=F32), jnp.sum(d_value, axis=0, dtype=F32)])
    d_normed_part = dot(d_gate, up_weight[0], ((1,), (1,))) + dot(d_value, up_weight[1], ((1,), (1,)))
    d_normed_cols = d_mixed_cols + scatter_columns(d_normed_part.astype(BF)).astype(F32)

    first_weighted = d_normed_cols * own(first_gain)
    shares = lax.all_gather(
        jnp.stack([jnp.sum(first_weighted, axis=1), jnp.sum(first_weighted * first_unit, axis=1)]), "tensor", axis=0
    )
    totals = jnp.sum(shares, axis=0) / columns
    own_rs = first_rs
    d_hidden_cols = own_rs * (first_weighted - totals[0][:, None] - first_unit * totals[1][:, None])
    d_first_gain = jnp.sum(d_normed_cols * first_unit, axis=0)
    d_first_shift = jnp.sum(d_normed_cols, axis=0)
    g_out_bias = jnp.sum(d_hidden_cols, axis=0)
    d_hidden_low = gather_columns(d_hidden_cols.astype(BF))
    g_out = dot(d_hidden_low, context, ((0,), (0,)))
    d_context = dot(d_hidden_low, out_weight, ((1,), (1,)))
    d_context = d_context.astype(BF).reshape(blocks, BLOCK, local_heads, HEAD_DIM)
    probs_back = jnp.exp(block_scores(queries, key_rows, alibi_bias, same_seq, score_scale) - log_total)
    d_probs = jnp.einsum("bqhe,bkhe->bhqk", d_context, value_rows, preferred_element_type=F32)
    g_values = jnp.einsum("bhqk,bqhe->bkhe", probs_back.astype(BF), d_context, preferred_element_type=F32)
    center_term = jnp.sum(probs_back * d_probs, axis=-1, keepdims=True)
    d_scores = (probs_back * (d_probs - center_term)).astype(BF)
    g_queries = jnp.einsum("bhqk,bkhe->bqhe", d_scores, key_rows, preferred_element_type=F32) * score_scale
    g_keys = jnp.einsum("bhqk,bqhe->bkhe", d_scores, queries, preferred_element_type=F32) * score_scale
    d_query, d_key, d_value_rows = (
        part.astype(BF).reshape(row_count, local_heads * HEAD_DIM) for part in (g_queries, g_keys, g_values)
    )
    d_qkv = jnp.concatenate([d_query, d_key, d_value_rows], axis=1)
    side = qkv_weight.transpose(1, 0, 2).reshape(columns, 3 * width)
    g_qkv = dot(packed_in, d_qkv, ((0,), (0,)))
    g_qv_bias = jnp.stack([jnp.sum(d_query, axis=0, dtype=F32), jnp.sum(d_value_rows, axis=0, dtype=F32)])
    d_input_part = dot(d_qkv, side, ((1,), (1,)))
    grad_cols = d_hidden_cols + scatter_columns(d_input_part.astype(BF)).astype(F32)
    input_grad = unpacked(grad_cols.astype(BF))

    def over_groups(grad):
        return lax.psum_scatter((grad * grad_scale).astype(BF), "dp", scatter_dimension=0, tiled=True).astype(F32)

    down_grad = over_groups(g_down).T
    up_grad = jnp.stack([over_groups(g_gate), over_groups(g_value)])
    late = over_groups(jnp.concatenate([g_qkv, g_out], axis=1))
    qkv_grad = late[:, : 3 * width].reshape(-1, 3, width).transpose(1, 0, 2)
    out_grad = late[:, 3 * width :].T

    split_sums = jnp.stack([g_out_bias, d_first_gain, d_first_shift, g_down_bias, d_second_gain, d_second_shift])
    flat = jnp.concatenate([split_sums.reshape(-1), g_qv_bias.reshape(-1), g_up_bias.reshape(-1)]) * grad_scale
    flat = jnp.sum(lax.all_gather(flat, "dp", axis=0), axis=0)
    cut = 6 * width
    wide_sums = lax.all_gather(flat[:cut].reshape(6, width), "tensor", axis=1, tiled=True)
    rows_here = columns // lax.axis_size("dp")
    sums_here = lax.dynamic_slice_in_dim(wide_sums, lax.axis_index("dp") * rows_here, rows_here, 1)
    qv_bias_grad = flat[cut : cut + 2 * width].reshape(2, width)
    up_bias_grad = flat[cut + 2 * width :].reshape(2, -1)
    return (
        layer_out,
        input_grad,
        qkv_grad,
        qv_bias_grad,
        out_grad,
        sums_here[0],
        sums_here[1],
        sums_here[2],
        up_grad,
        up_bias_grad,
        down_grad,
        sums_here[3],
        sums_here[4],
        sums_here[5],
    )


def solution(mesh):
    return jax.shard_map(
        on_device,
        mesh=mesh,
        in_specs=(
            P("dp", "tensor"),
            P("dp", "tensor"),
            P("dp"),
            P("dp", None),
            P(None, None, "tensor"),
            P(None, "tensor"),
            P("tensor", None),
            P(),
            P(),
            P(),
            P(None, None, "tensor"),
            P(None, "tensor"),
            P("tensor", None),
            P(),
            P(),
            P(),
        ),
        out_specs=(
            P("dp", "tensor"),
            P("dp", "tensor"),
            P(None, "dp", "tensor"),
            P(None, "tensor"),
            P("tensor", "dp"),
            P("dp"),
            P("dp"),
            P("dp"),
            P(None, "dp", "tensor"),
            P(None, "tensor"),
            P("tensor", "dp"),
            P("dp"),
            P("dp"),
            P("dp"),
        ),
        check_vma=False,
    )
```

```python
import functools

import jax
import jax.numpy as jnp
from jax import lax
from jax.experimental import pallas as pl
from jax.experimental.pallas import tpu as pltpu
from jax.sharding import PartitionSpec as P

HEADS = 12
HEAD_DIM = 64
BLOCK = 512
BF = jnp.bfloat16
F32 = jnp.float32
MESH = pl.DeviceIdType.MESH
VMEM_LIMIT = 60 * 1024 * 1024


def dot(a, b, dims):
    return lax.dot_general(a, b, (dims, ((), ())), preferred_element_type=F32)


def place_of():
    me = lax.axis_index("tensor")
    core = me % 2
    side = me // 2
    sibling = side * 2 + (1 - core)
    across = (1 - side) * 2 + core
    diagonal = (1 - side) * 2 + (1 - core)
    return me, sibling, across, diagonal


def enter(devices, groups):
    barrier = pltpu.get_barrier_semaphore()
    count = len(devices)
    for device in devices:
        pl.semaphore_signal(barrier, inc=1, device_id={"tensor": device}, device_id_type=MESH)
    if groups:
        mine = lax.axis_index("dp")

        @pl.loop(1, groups)
        def _(step):
            pl.semaphore_signal(barrier, inc=1, device_id={"dp": (mine + step) % groups}, device_id_type=MESH)

        count += groups - 1
    pl.semaphore_wait(barrier, count)


def send(source, target, send_sem, recv_sem, **where):
    return pltpu.make_async_remote_copy(
        src_ref=source, dst_ref=target, send_sem=send_sem, recv_sem=recv_sem, device_id=where, device_id_type=MESH
    )


def fold_into(buffer, index, values, halves):
    width = values.shape[1]
    if not halves:
        buffer[index] = values
        return
    half = values.shape[0] // 2
    buffer[index + (slice(None), slice(0, width))] = values[:half]
    buffer[index + (slice(None), slice(width, 2 * width))] = values[half:]


def unfold(values, width, halves):
    if not halves:
        return values
    return jnp.concatenate([values[:, :width], values[:, width:]], axis=0)


def gather_rows_into(own, out, sems, count):
    me, sibling, across, _ = place_of()
    far, near, passed = [], [], []
    for b in range(count):
        far.append(send(own.at[b], out.at[b, me], sems.at[0, b], sems.at[1, b], tensor=across))
        near.append(send(own.at[b], out.at[b, me], sems.at[2, b], sems.at[3, b], tensor=sibling))
        far[b].start()
        near[b].start()
        out[b, me] = own[b]
    for b in range(count):
        far[b].wait_recv()
        passed.append(send(out.at[b, across], out.at[b, across], sems.at[4, b], sems.at[5, b], tensor=sibling))
        passed[b].start()
    for b in range(count):
        near[b].wait_recv()
        passed[b].wait_recv()
    for b in range(count):
        far[b].wait_send()
        near[b].wait_send()
        passed[b].wait_send()


def gather_rows_kernel(count, own, out, sems):
    _, sibling, across, _ = place_of()
    enter([sibling, across], 0)
    gather_rows_into(own, out, sems, count)


def whole(count):
    return [pl.BlockSpec(memory_space=pltpu.VMEM)] * count


def call(kernel, number, outs, scratch, args):
    return pl.pallas_call(
        kernel,
        out_shape=outs,
        in_specs=whole(len(args)),
        out_specs=jax.tree.map(lambda _: pl.BlockSpec(memory_space=pltpu.VMEM), outs),
        scratch_shapes=scratch,
        compiler_params=pltpu.CompilerParams(
            collective_id=number, has_side_effects=True, vmem_limit_bytes=VMEM_LIMIT
        ),
    )(*args)


def shape(dims, kind):
    return jax.ShapeDtypeStruct(dims, kind)


def gather_rows(own, number):
    count, rows, columns = own.shape
    return call(
        functools.partial(gather_rows_kernel, count),
        number,
        shape((count, 4, rows, columns), own.dtype),
        [pltpu.SemaphoreType.DMA((6, count))],
        (own,),
    )


def scatter_rows_kernel(count, part, out, first, second, third, sems):
    me, sibling, across, diagonal = place_of()
    enter([sibling, across], 0)
    near, cross, far = [], [], []
    for b in range(count):
        cross.append(send(part.at[b, diagonal], first.at[b], sems.at[0, b], sems.at[1, b], tensor=sibling))
        near.append(send(part.at[b, sibling], second.at[b], sems.at[2, b], sems.at[3, b], tensor=sibling))
        cross[b].start()
        near[b].start()
    for b in range(count):
        cross[b].wait()
        first[b] = (part[b, across].astype(F32) + first[b].astype(F32)).astype(BF)
        far.append(send(first.at[b], third.at[b], sems.at[4, b], sems.at[5, b], tensor=across))
        far[b].start()
    for b in range(count):
        near[b].wait()
        far[b].wait_recv()
        out[b] = part[b, me].astype(F32) + second[b].astype(F32) + third[b].astype(F32)
    for b in range(count):
        far[b].wait_send()


def scatter_rows(part, number):
    count, _, rows, columns = part.shape
    buffer = pltpu.VMEM((count, rows, columns), BF)
    return call(
        functools.partial(scatter_rows_kernel, count),
        number,
        shape((count, rows, columns), F32),
        [buffer, buffer, buffer, pltpu.SemaphoreType.DMA((6, count))],
        (part,),
    )


def place_rows(place_row, arrived, start, rows):
    ids = lax.broadcasted_iota(jnp.int32, (rows, arrived.shape[0]), 0) + start
    chosen = jnp.where(ids == place_row, 1.0, 0.0).astype(BF)
    return dot(chosen, arrived, ((1,), (0,))).astype(BF)


def take_rows(place_col, packed):
    ids = lax.broadcasted_iota(jnp.int32, (place_col.shape[0], packed.shape[0]), 1)
    chosen = jnp.where(ids == place_col, 1.0, 0.0).astype(BF)
    return dot(chosen, packed, ((1,), (0,))).astype(BF)


def dispatch_kernel(groups, blocks, tokens, cot, place_row, packed_out, cot_out, sent, recv, arrived, wide, csent, crecv,
                    group_sems, gather_sems, cot_sems):
    me, sibling, across, diagonal = place_of()
    mine = lax.axis_index("dp")
    rows, width = tokens.shape
    piece = rows // groups
    halves = (piece // 2) % 8 == 0
    enter([sibling, across, diagonal], groups)

    def pack(kind, source, peer):
        values = source[pl.ds(pl.multiple_of(peer * piece, 8), piece), :]
        fold_into(sent, (kind, peer), values, halves)

    def moved(kind, step):
        peer = (mine + step) % groups
        return send(sent.at[kind, peer], recv.at[kind, mine], group_sems.at[0, kind, step],
                    group_sems.at[1, kind, step], dp=peer)

    for kind, source in enumerate((tokens, cot)):
        @pl.loop(1, groups)
        def _(step):
            pack(kind, source, (mine + step) % groups)
            moved(kind, step).start()

    for kind, source in enumerate((tokens, cot)):
        values = source[pl.ds(pl.multiple_of(mine * piece, 8), piece), :]
        fold_into(recv, (kind, mine), values, halves)

    def land(kind):
        @pl.loop(1, groups)
        def _(step):
            moved(kind, step).wait_recv()

        @pl.loop(0, groups)
        def _(peer):
            arrived[pl.ds(pl.multiple_of(peer * piece, 8), piece), :] = unfold(recv[kind, peer], width, halves)

    land(0)
    far, near, passed = [], [], []
    for b in range(blocks):
        placed = place_rows(place_row[...], arrived[...], b * BLOCK, BLOCK)
        fold_into(wide, (me, b), placed, True)
        far.append(send(wide.at[me, b], wide.at[me, b], gather_sems.at[0, b], gather_sems.at[1, b], tensor=across))
        near.append(send(wide.at[me, b], wide.at[me, b], gather_sems.at[2, b], gather_sems.at[3, b], tensor=sibling))
        far[b].start()
        near[b].start()
    for b in range(blocks):
        far[b].wait_recv()
        passed.append(
            send(wide.at[across, b], wide.at[across, b], gather_sems.at[4, b], gather_sems.at[5, b], tensor=sibling))
        passed[b].start()
    land(1)
    quarter = BLOCK // 4
    for b in range(blocks):
        placed = place_rows(place_row[...], arrived[...], b * BLOCK, BLOCK)
        for u in range(4):
            fold_into(csent, (u, b), placed[u * quarter : (u + 1) * quarter], True)
    swaps = []
    for k, peer in enumerate((across, diagonal, sibling)):
        swaps.append(send(csent.at[peer], crecv.at[me], cot_sems.at[0, k], cot_sems.at[1, k], tensor=peer))
        swaps[k].start()
    crecv[me] = csent[me]
    for b in range(blocks):
        near[b].wait_recv()
        passed[b].wait_recv()
        for s in range(4):
            packed_out[b * BLOCK : (b + 1) * BLOCK, s * width : (s + 1) * width] = unfold(wide[s, b], width, True)
    for k in range(3):
        swaps[k].wait_recv()
    for b in range(blocks):
        for s in range(4):
            cot_out[b, :, s * width : (s + 1) * width] = unfold(crecv[s, b], width, True)
    for b in range(blocks):
        far[b].wait_send()
        near[b].wait_send()
        passed[b].wait_send()
    for k in range(3):
        swaps[k].wait_send()
    for kind in range(2):
        @pl.loop(1, groups)
        def _(step):
            moved(kind, step).wait_send()


def dispatch(tokens, cot, place_row, groups, number):
    rows, width = tokens.shape
    piece = rows // groups
    blocks = rows // BLOCK
    halves = (piece // 2) % 8 == 0
    slab = (2, groups, piece // 2, 2 * width) if halves else (2, groups, piece, width)
    return call(
        functools.partial(dispatch_kernel, groups, blocks),
        number,
        (shape((rows, 4 * width), BF), shape((blocks, BLOCK // 4, 4 * width), BF)),
        [
            pltpu.VMEM(slab, BF),
            pltpu.VMEM(slab, BF),
            pltpu.VMEM((rows, width), BF),
            pltpu.VMEM((4, blocks, BLOCK // 2, 2 * width), BF),
            pltpu.VMEM((4, blocks, BLOCK // 8, 2 * width), BF),
            pltpu.VMEM((4, blocks, BLOCK // 8, 2 * width), BF),
            pltpu.SemaphoreType.DMA((2, 2, groups)),
            pltpu.SemaphoreType.DMA((6, blocks)),
            pltpu.SemaphoreType.DMA((2, 3)),
        ],
        (tokens, cot, place_row),
    )


def gather_heads_kernel(blocks, context, out, wide, sems):
    me, sibling, across, _ = place_of()
    width = context.shape[1]
    enter([sibling, across], 0)
    far, near, passed = [], [], []
    for b in range(blocks):
        fold_into(wide, (me, b), context[b * BLOCK : (b + 1) * BLOCK, :], True)
        far.append(send(wide.at[me, b], wide.at[me, b], sems.at[0, b], sems.at[1, b], tensor=across))
        near.append(send(wide.at[me, b], wide.at[me, b], sems.at[2, b], sems.at[3, b], tensor=sibling))
        far[b].start()
        near[b].start()
    for b in range(blocks):
        far[b].wait_recv()
        passed.append(send(wide.at[across, b], wide.at[across, b], sems.at[4, b], sems.at[5, b], tensor=sibling))
        passed[b].start()
    for b in range(blocks):
        near[b].wait_recv()
        passed[b].wait_recv()
        for s in range(4):
            out[b * BLOCK : (b + 1) * BLOCK, s * width : (s + 1) * width] = unfold(wide[s, b], width, True)
    for b in range(blocks):
        far[b].wait_send()
        near[b].wait_send()
        passed[b].wait_send()


def gather_heads(context, number):
    rows, width = context.shape
    blocks = rows // BLOCK
    return call(
        functools.partial(gather_heads_kernel, blocks),
        number,
        shape((rows, 4 * width), BF),
        [pltpu.VMEM((4, blocks, BLOCK // 2, 2 * width), BF), pltpu.SemaphoreType.DMA((6, blocks))],
        (context,),
    )


def tail_kernel(groups, blocks, grads, result, part, place_col, small, layer_out, input_grad, summed, small_out,
                acc, recv1, recv2, cols, one, two, three, rrecv, packed, sent, recv, srecv, swide,
                pair_sems, group_sems, x_sems, r_sems, a_sems, s_sems, w_sems):
    me, sibling, across, diagonal = place_of()
    mine = lax.axis_index("dp")
    rows, width = layer_out.shape
    piece = rows // groups
    halves = (piece // 2) % 8 == 0
    pairs = groups // 2
    parity = mine % 2
    pair = mine + 1 - 2 * parity
    slot = mine // 2
    quarter = BLOCK // 4
    enter([sibling, across, diagonal], groups)

    def paired(step):
        m = (slot + step) % pairs
        return send(grads.at[2 * m + 1 - parity], recv1.at[m], pair_sems.at[0, step], pair_sems.at[1, step], dp=pair)

    @pl.loop(1, pairs + 1)
    def _(step):
        paired(step).start()

    swaps = [
        send(small, srecv.at[me], s_sems.at[0, k], s_sems.at[1, k], tensor=peer)
        for k, peer in enumerate((sibling, across, diagonal))
    ]
    for swap in swaps:
        swap.start()
    srecv[me] = small[...]

    for b in range(blocks):
        for u in range(4):
            fold_into(cols, (u, b), part[b * BLOCK : (b + 1) * BLOCK, u * width : (u + 1) * width], True)
    cross = send(cols.at[diagonal], one, x_sems.at[0], x_sems.at[1], tensor=sibling)
    cross.start()
    near = send(cols.at[sibling], two, x_sems.at[2], x_sems.at[3], tensor=sibling)
    near.start()
    cross.wait()
    one[...] = (cols[across].astype(F32) + one[...].astype(F32)).astype(BF)
    far = send(one, three, x_sems.at[4], x_sems.at[5], tensor=across)
    far.start()
    returns = [
        send(result.at[peer], rrecv.at[me], r_sems.at[0, k], r_sems.at[1, k], tensor=peer)
        for k, peer in enumerate((across, diagonal, sibling))
    ]
    for back in returns:
        back.start()
    rrecv[me] = result[me]

    for swap in swaps:
        swap.wait_recv()
    shared = small.shape[0] // 2
    swide[mine, 0:shared] = srecv[0, 0:shared] + srecv[1, 0:shared] + srecv[2, 0:shared] + srecv[3, 0:shared]
    swide[mine, shared:] = small[shared:, :]

    def spread(step):
        peer = (mine + step) % groups
        return send(swide.at[mine], swide.at[mine], w_sems.at[0, step], w_sems.at[1, step], dp=peer)

    @pl.loop(1, groups)
    def _(step):
        spread(step).start()

    def passed(step):
        m = (slot + step) % pairs
        return send(acc.at[m], recv2.at[slot], group_sems.at[0, step], group_sems.at[1, step], dp=2 * m + parity)

    def forward(step):
        m = (slot + step) % pairs
        paired(step).wait_recv()
        acc[m] = (grads[2 * m + parity].astype(F32) + recv1[m].astype(F32)).astype(BF)
        passed(step).start()

    def moved(kind, step):
        peer = (mine + step) % groups
        return send(sent.at[kind, peer], recv.at[kind, mine], a_sems.at[0, kind, step], a_sems.at[1, kind, step],
                    dp=peer)

    def give(kind, target):
        @pl.loop(0, groups)
        def _(step):
            peer = (mine + step) % groups
            columns = place_col[pl.ds(pl.multiple_of(peer * piece, 8), piece), :]
            values = take_rows(columns, packed[...])

            @pl.when(step > 0)
            def _():
                fold_into(sent, (kind, peer), values, halves)
                moved(kind, step).start()

            @pl.when(step == 0)
            def _():
                fold_into(recv, (kind, mine), values, halves)

    forward(1)
    near.wait()
    far.wait_recv()
    for b in range(blocks):
        total = cols[me, b].astype(F32) + two[b].astype(F32) + three[b].astype(F32)
        packed[b * BLOCK : (b + 1) * BLOCK, :] = unfold(total.astype(BF), width, True)
    give(1, input_grad)
    for back in returns:
        back.wait_recv()
    for b in range(blocks):
        for s in range(4):
            start = b * BLOCK + s * quarter
            packed[start : start + quarter, :] = unfold(rrecv[s, b], width, True)
    give(0, layer_out)

    @pl.loop(2, pairs)
    def _(step):
        forward(step)

    paired(pairs).wait_recv()
    summed[...] = grads[mine].astype(F32) + recv1[slot].astype(F32)

    @pl.loop(1, pairs)
    def _(step):
        passed(step).wait_recv()
        summed[...] += recv2[(slot + pairs - step) % pairs].astype(F32)

    @pl.loop(1, groups)
    def _(step):
        spread(step).wait_recv()

    small_out[...] = swide[0]

    @pl.loop(1, groups)
    def _(peer):
        small_out[...] += swide[peer]

    for kind, target in ((1, input_grad), (0, layer_out)):
        @pl.loop(1, groups)
        def _(step):
            moved(kind, step).wait_recv()

        @pl.loop(0, groups)
        def _(peer):
            target[pl.ds(pl.multiple_of(peer * piece, 8), piece), :] = unfold(recv[kind, peer], width, halves)

    far.wait_send()
    for copy in returns + swaps:
        copy.wait_send()

    @pl.loop(1, pairs + 1)
    def _(step):
        paired(step).wait_send()

    @pl.loop(1, pairs)
    def _(step):
        passed(step).wait_send()

    @pl.loop(1, groups)
    def _(step):
        spread(step).wait_send()
        moved(0, step).wait_send()
        moved(1, step).wait_send()


def tail(grads, result, part, place_col, small, number):
    groups, held, span = grads.shape
    rows, columns = part.shape
    width = columns // 4
    piece = rows // groups
    blocks = rows // BLOCK
    halves = (piece // 2) % 8 == 0
    slab = (2, groups, piece // 2, 2 * width) if halves else (2, groups, piece, width)
    pairs = groups // 2
    half = (blocks, BLOCK // 2, 2 * width)
    dma = pltpu.SemaphoreType.DMA
    return call(
        functools.partial(tail_kernel, groups, blocks),
        number,
        (shape((rows, width), BF), shape((rows, width), BF), shape((held, span), F32), shape(small.shape, F32)),
        [
            pltpu.VMEM((pairs, held, span), BF),
            pltpu.VMEM((pairs, held, span), BF),
            pltpu.VMEM((pairs, held, span), BF),
            pltpu.VMEM((4,) + half, BF),
            pltpu.VMEM(half, BF),
            pltpu.VMEM(half, BF),
            pltpu.VMEM(half, BF),
            pltpu.VMEM((4, blocks, BLOCK // 8, 2 * width), BF),
            pltpu.VMEM((rows, width), BF),
            pltpu.VMEM(slab, BF),
            pltpu.VMEM(slab, BF),
            pltpu.VMEM((4,) + small.shape, F32),
            pltpu.VMEM((groups,) + small.shape, F32),
            dma((2, pairs + 1)),
            dma((2, pairs + 1)),
            dma((6,)),
            dma((2, 3)),
            dma((2, 2, groups)),
            dma((2, 3)),
            dma((2, groups)),
        ],
        (grads, result, part, place_col, small),
    )


def alibi_terms(part_index, local_heads, block_rows):
    heads_idx = (part_index * local_heads + jnp.arange(local_heads)).astype(F32)
    slopes = 2.0 ** (-8.0 * (heads_idx + 1.0) / HEADS)
    position = jnp.arange(block_rows).astype(F32)
    distance = jnp.abs(position[:, None] - position[None, :])
    return -slopes[:, None, None] * distance[None]


def block_scores(queries, key_rows, alibi_bias, same_seq, score_scale):
    raw_scores = jnp.einsum("bqhe,bkhe->bhqk", queries, key_rows, preferred_element_type=F32)
    scored = raw_scores * score_scale + alibi_bias[None]
    return jnp.where(same_seq[:, None], scored, -1e30)


def softmax_rows(scored):
    row_max = jnp.max(scored, axis=-1, keepdims=True)
    exponent = jnp.exp(scored - row_max)
    denominator = jnp.sum(exponent, axis=-1, keepdims=True)
    return (exponent / denominator, row_max + jnp.log(denominator))


def norm_back(weighted, unit, rs):
    inner = jnp.mean(weighted * unit, axis=-1, keepdims=True)
    return rs * (weighted - jnp.mean(weighted, axis=-1, keepdims=True) - unit * inner)


def norm_unit(values):
    center = values - jnp.mean(values, axis=-1, keepdims=True)
    rs = lax.rsqrt(jnp.mean(center * center, axis=-1, keepdims=True) + 1e-05)
    return center * rs, rs


def on_device(
    tokens,
    cotangent,
    seq_start,
    row_place,
    qkv_weight,
    qv_bias,
    out_weight,
    out_bias,
    first_gain,
    first_shift,
    up_weight,
    up_bias,
    down_weight,
    down_bias,
    second_gain,
    second_shift,
):
    row_count, width = tokens.shape
    columns = qkv_weight.shape[1]
    hidden_units = down_weight.shape[0]
    local_heads = width // HEAD_DIM
    blocks = row_count // BLOCK
    groups = lax.axis_size("dp")
    quarter = BLOCK // 4
    me = lax.axis_index("tensor")
    score_scale = HEAD_DIM ** (-0.5)
    grad_scale = (row_count * groups) ** (-0.5)
    wide = lambda vector: vector.astype(F32)

    def own_rows(values):
        split = values.reshape(blocks, 4, quarter, columns)
        return lax.dynamic_slice_in_dim(split, me, 1, 1)[:, 0]

    packed_in, cot_own = dispatch(tokens, cotangent, row_place, groups, 0)
    full_out = lax.all_gather(out_weight, "tensor", axis=0, tiled=True)

    alibi_bias = alibi_terms(me, local_heads, BLOCK)
    block_starts = seq_start.reshape(blocks, BLOCK)
    same_seq = block_starts[:, :, None] == block_starts[:, None, :]
    bias_rows = jnp.stack([qv_bias[0], jnp.zeros_like(qv_bias[0]), qv_bias[1]]).astype(F32)
    projected = jnp.einsum("td,kde->kte", packed_in, qkv_weight, preferred_element_type=F32)
    qkv_rows = (projected + bias_rows[:, None, :]).astype(BF)
    split_heads = qkv_rows.reshape(3, blocks, BLOCK, local_heads, HEAD_DIM)
    queries = split_heads[0]
    key_rows = split_heads[1]
    value_rows = split_heads[2]
    attn_probs, log_total = softmax_rows(block_scores(queries, key_rows, alibi_bias, same_seq, score_scale))
    context = jnp.einsum("bhqk,bkhe->bqhe", attn_probs.astype(BF), value_rows, preferred_element_type=F32)
    context = context.reshape(row_count, width).astype(BF)

    wide_context = gather_heads(context, 1)
    attended = dot(wide_context, full_out, ((1,), (0,)))
    hidden = wide(packed_in) + (attended + wide(out_bias))
    first_unit, first_rs = norm_unit(hidden)
    normed = first_unit * wide(first_gain) + wide(first_shift)
    normed_low = normed.astype(BF)
    unit_own, _ = norm_unit(own_rows(hidden))
    rs_own = lax.dynamic_slice_in_dim(first_rs.reshape(blocks, 4, quarter, 1), me, 1, 1)[:, 0]
    normed_own = unit_own * wide(first_gain) + wide(first_shift)

    lifted = jnp.einsum("td,kdf->ktf", normed_low, up_weight, preferred_element_type=F32)
    lifted = lifted + wide(up_bias)[:, None, :]
    half_erf = 0.5 * (1.0 + lax.erf(lifted[0] * (0.5**0.5)))
    gelu_gate = lifted[0] * half_erf
    gated_low = (gelu_gate * lifted[1]).astype(BF)
    ffn_part = dot(gated_low, down_weight, ((1,), (0,))).astype(BF)
    ffn_own = scatter_rows(ffn_part.reshape(blocks, 4, quarter, columns), 2)
    mixed_own = normed_own + (ffn_own + wide(down_bias))
    cot_wide = wide(cot_own)
    weighted = cot_wide * wide(second_gain)
    second_unit, second_rs = norm_unit(mixed_own)
    result_own = (second_unit * wide(second_gain) + wide(second_shift)).astype(BF)
    d_mixed_own = norm_back(weighted, second_unit, second_rs)
    d_second_gain = jnp.sum(cot_wide * second_unit, axis=(0, 1))
    d_second_shift = jnp.sum(cot_wide, axis=(0, 1))
    g_down_bias = jnp.sum(d_mixed_own, axis=(0, 1))
    split_result = result_own.reshape(blocks, 2, quarter // 2, 4, width).transpose(3, 0, 2, 1, 4)
    split_result = split_result.reshape(4, blocks, quarter // 2, 2 * width)

    d_mixed_low = gather_rows(d_mixed_own.astype(BF), 3).reshape(row_count, columns)
    g_down = dot(d_mixed_low, gated_low, ((0,), (0,)))
    d_gated = dot(d_mixed_low, down_weight, ((1,), (1,)))
    gelu_slope = half_erf + lifted[0] * jnp.exp(-0.5 * lifted[0] * lifted[0]) * ((2.0 * jnp.pi) ** (-0.5))
    d_gate = (d_gated * lifted[1] * gelu_slope).astype(BF)
    d_value = (d_gated * gelu_gate).astype(BF)
    g_gate = dot(normed_low, d_gate, ((0,), (0,)))
    g_value = dot(normed_low, d_value, ((0,), (0,)))
    g_up_bias = jnp.stack([jnp.sum(d_gate, axis=0, dtype=F32), jnp.sum(d_value, axis=0, dtype=F32)])
    d_normed_part = dot(d_gate, up_weight[0], ((1,), (1,))) + dot(d_value, up_weight[1], ((1,), (1,)))
    d_ffn_own = scatter_rows(d_normed_part.astype(BF).reshape(blocks, 4, quarter, columns), 4)
    d_normed_own = d_mixed_own + d_ffn_own

    d_hidden_own = norm_back(d_normed_own * wide(first_gain), unit_own, rs_own)
    d_first_gain = jnp.sum(d_normed_own * unit_own, axis=(0, 1))
    d_first_shift = jnp.sum(d_normed_own, axis=(0, 1))
    g_out_bias = jnp.sum(d_hidden_own, axis=(0, 1))
    d_hidden_low = gather_rows(d_hidden_own.astype(BF), 5).reshape(row_count, columns)
    g_out = dot(d_hidden_low, context, ((0,), (0,)))
    d_context = dot(d_hidden_low, out_weight, ((1,), (1,)))
    d_context = d_context.astype(BF).reshape(blocks, BLOCK, local_heads, HEAD_DIM)
    probs_back = jnp.exp(block_scores(queries, key_rows, alibi_bias, same_seq, score_scale) - log_total)
    d_probs = jnp.einsum("bqhe,bkhe->bhqk", d_context, value_rows, preferred_element_type=F32)
    g_values = jnp.einsum("bhqk,bqhe->bkhe", probs_back.astype(BF), d_context, preferred_element_type=F32)
    center_term = jnp.sum(probs_back * d_probs, axis=-1, keepdims=True)
    d_scores = (probs_back * (d_probs - center_term)).astype(BF)
    g_queries = jnp.einsum("bhqk,bkhe->bqhe", d_scores, key_rows, preferred_element_type=F32) * score_scale
    g_keys = jnp.einsum("bhqk,bqhe->bkhe", d_scores, queries, preferred_element_type=F32) * score_scale
    d_query, d_key, d_value_rows = (
        part.astype(BF).reshape(row_count, width) for part in (g_queries, g_keys, g_values)
    )
    d_qkv = jnp.concatenate([d_query, d_key, d_value_rows], axis=1)
    side = qkv_weight.transpose(1, 0, 2).reshape(columns, 3 * width)
    g_qkv = dot(packed_in, d_qkv, ((0,), (0,)))
    g_qv_bias = jnp.stack([jnp.sum(d_query, axis=0, dtype=F32), jnp.sum(d_value_rows, axis=0, dtype=F32)])
    d_input_part = dot(d_qkv, side, ((1,), (1,))).reshape(blocks, 4, quarter, columns)
    mine = lax.broadcasted_iota(jnp.int32, (1, 4, 1, 1), 1) == me
    d_input_part = d_input_part + jnp.where(mine, d_hidden_own[:, None], 0.0)
    d_input_part = d_input_part.astype(BF).reshape(row_count, columns)

    grads = jnp.concatenate([g_down, g_gate, g_value, g_qkv, g_out], axis=1) * grad_scale
    grads = grads.astype(BF).reshape(groups, columns // groups, grads.shape[1])
    zero = jnp.zeros((2, columns), F32)
    small = jnp.stack([g_out_bias, d_first_gain, d_first_shift, g_down_bias, d_second_gain, d_second_shift])
    qv_row = jnp.pad(g_qv_bias.reshape(1, -1), ((0, 0), (0, columns - 2 * width)))
    small = jnp.concatenate([small, zero, g_up_bias, qv_row, jnp.zeros((5, columns), F32)], axis=0) * grad_scale
    layer_out, input_grad, summed, sums = tail(
        grads, split_result, d_input_part, row_place.reshape(row_count, 1), small, 6
    )

    edges = [0, hidden_units, 2 * hidden_units, 3 * hidden_units, 3 * hidden_units + 3 * width, summed.shape[1]]
    down_g, gate_g, value_g, qkv_g, out_g = (summed[:, a:b] for a, b in zip(edges[:-1], edges[1:]))
    rows_here = columns // groups
    sums_here = lax.dynamic_slice_in_dim(sums[:6], lax.axis_index("dp") * rows_here, rows_here, 1)
    return (
        layer_out,
        input_grad,
        qkv_g.reshape(rows_here, 3, width).transpose(1, 0, 2),
        sums[10, : 2 * width].reshape(2, width),
        out_g.T,
        sums_here[0],
        sums_here[1],
        sums_here[2],
        jnp.stack([gate_g, value_g]),
        sums[8:10],
        down_g.T,
        sums_here[3],
        sums_here[4],
        sums_here[5],
    )


def solution(mesh):
    return jax.shard_map(
        on_device,
        mesh=mesh,
        in_specs=(
            P("dp", "tensor"),
            P("dp", "tensor"),
            P("dp"),
            P("dp", None),
            P(None, None, "tensor"),
            P(None, "tensor"),
            P("tensor", None),
            P(),
            P(),
            P(),
            P(None, None, "tensor"),
            P(None, "tensor"),
            P("tensor", None),
            P(),
            P(),
            P(),
        ),
        out_specs=(
            P("dp", "tensor"),
            P("dp", "tensor"),
            P(None, "dp", "tensor"),
            P(None, "tensor"),
            P("tensor", "dp"),
            P("dp"),
            P("dp"),
            P("dp"),
            P(None, "dp", "tensor"),
            P(None, "tensor"),
            P("tensor", "dp"),
            P("dp"),
            P("dp"),
            P("dp"),
        ),
        check_vma=False,
    )
```

```python
import functools

import jax
import jax.numpy as jnp
from jax import lax
from jax.experimental import pallas as pl
from jax.experimental.pallas import tpu as pltpu
from jax.sharding import PartitionSpec as P

HEADS = 12
HEAD_DIM = 64
BLOCK = 512
BF = jnp.bfloat16
F32 = jnp.float32
MESH = pl.DeviceIdType.MESH
VMEM_LIMIT = 60 * 1024 * 1024


def dot(a, b, dims):
    return lax.dot_general(a, b, (dims, ((), ())), preferred_element_type=F32)


def place_of():
    me = lax.axis_index("tensor")
    core = me % 2
    side = me // 2
    sibling = side * 2 + (1 - core)
    across = (1 - side) * 2 + core
    diagonal = (1 - side) * 2 + (1 - core)
    return me, sibling, across, diagonal


def enter(devices, groups):
    barrier = pltpu.get_barrier_semaphore()
    count = len(devices)
    for device in devices:
        pl.semaphore_signal(barrier, inc=1, device_id={"tensor": device}, device_id_type=MESH)
    if groups:
        mine = lax.axis_index("dp")

        @pl.loop(1, groups)
        def _(step):
            pl.semaphore_signal(barrier, inc=1, device_id={"dp": (mine + step) % groups}, device_id_type=MESH)

        count += groups - 1
    pl.semaphore_wait(barrier, count)


def send(source, target, send_sem, recv_sem, **where):
    return pltpu.make_async_remote_copy(
        src_ref=source, dst_ref=target, send_sem=send_sem, recv_sem=recv_sem, device_id=where, device_id_type=MESH
    )


def fold_into(buffer, index, values, halves):
    width = values.shape[1]
    if not halves:
        buffer[index] = values
        return
    half = values.shape[0] // 2
    buffer[index + (slice(None), slice(0, width))] = values[:half]
    buffer[index + (slice(None), slice(width, 2 * width))] = values[half:]


def unfold(values, width, halves):
    if not halves:
        return values
    return jnp.concatenate([values[:, :width], values[:, width:]], axis=0)


def gather_rows_into(own, out, sems, count):
    me, sibling, across, _ = place_of()
    far, near, passed = [], [], []
    for b in range(count):
        far.append(send(own.at[b], out.at[b, me], sems.at[0, b], sems.at[1, b], tensor=across))
        near.append(send(own.at[b], out.at[b, me], sems.at[2, b], sems.at[3, b], tensor=sibling))
        far[b].start()
        near[b].start()
        out[b, me] = own[b]
    for b in range(count):
        far[b].wait_recv()
        passed.append(send(out.at[b, across], out.at[b, across], sems.at[4, b], sems.at[5, b], tensor=sibling))
        passed[b].start()
    for b in range(count):
        near[b].wait_recv()
        passed[b].wait_recv()
    for b in range(count):
        far[b].wait_send()
        near[b].wait_send()
        passed[b].wait_send()


def gather_rows_kernel(count, own, out, sems):
    _, sibling, across, _ = place_of()
    enter([sibling, across], 0)
    gather_rows_into(own, out, sems, count)


def whole(count):
    return [pl.BlockSpec(memory_space=pltpu.VMEM)] * count


def call(kernel, number, outs, scratch, args):
    return pl.pallas_call(
        kernel,
        out_shape=outs,
        in_specs=whole(len(args)),
        out_specs=jax.tree.map(lambda _: pl.BlockSpec(memory_space=pltpu.VMEM), outs),
        scratch_shapes=scratch,
        compiler_params=pltpu.CompilerParams(
            collective_id=number, has_side_effects=True, vmem_limit_bytes=VMEM_LIMIT
        ),
    )(*args)


def shape(dims, kind):
    return jax.ShapeDtypeStruct(dims, kind)


def gather_rows(own, number):
    count, rows, columns = own.shape
    return call(
        functools.partial(gather_rows_kernel, count),
        number,
        shape((count, 4, rows, columns), own.dtype),
        [pltpu.SemaphoreType.DMA((6, count))],
        (own,),
    )


def scatter_rows_kernel(count, part, out, first, second, third, sems):
    me, sibling, across, diagonal = place_of()
    enter([sibling, across], 0)
    near, cross, far = [], [], []
    for b in range(count):
        cross.append(send(part.at[b, diagonal], first.at[b], sems.at[0, b], sems.at[1, b], tensor=sibling))
        near.append(send(part.at[b, sibling], second.at[b], sems.at[2, b], sems.at[3, b], tensor=sibling))
        cross[b].start()
        near[b].start()
    for b in range(count):
        cross[b].wait()
        first[b] = (part[b, across].astype(F32) + first[b].astype(F32)).astype(BF)
        far.append(send(first.at[b], third.at[b], sems.at[4, b], sems.at[5, b], tensor=across))
        far[b].start()
    for b in range(count):
        near[b].wait()
        far[b].wait_recv()
        out[b] = part[b, me].astype(F32) + second[b].astype(F32) + third[b].astype(F32)
    for b in range(count):
        far[b].wait_send()


def scatter_rows(part, number):
    count, _, rows, columns = part.shape
    buffer = pltpu.VMEM((count, rows, columns), BF)
    return call(
        functools.partial(scatter_rows_kernel, count),
        number,
        shape((count, rows, columns), F32),
        [buffer, buffer, buffer, pltpu.SemaphoreType.DMA((6, count))],
        (part,),
    )


def place_rows(place_row, arrived, start, rows):
    ids = lax.broadcasted_iota(jnp.int32, (rows, arrived.shape[0]), 0) + start
    chosen = jnp.where(ids == place_row, 1.0, 0.0).astype(BF)
    return dot(chosen, arrived, ((1,), (0,))).astype(BF)


def take_rows(place_col, packed):
    ids = lax.broadcasted_iota(jnp.int32, (place_col.shape[0], packed.shape[0]), 1)
    chosen = jnp.where(ids == place_col, 1.0, 0.0).astype(BF)
    return dot(chosen, packed, ((1,), (0,))).astype(BF)


def dispatch_kernel(groups, blocks, tokens, cot, place_row, packed_out, cot_out, sent, recv, arrived, wide, csent, crecv,
                    group_sems, gather_sems, cot_sems):
    me, sibling, across, diagonal = place_of()
    mine = lax.axis_index("dp")
    rows, width = tokens.shape
    piece = rows // groups
    halves = (piece // 2) % 8 == 0
    enter([sibling, across, diagonal], groups)

    def pack(kind, source, peer):
        values = source[pl.ds(pl.multiple_of(peer * piece, 8), piece), :]
        fold_into(sent, (kind, peer), values, halves)

    def moved(kind, step):
        peer = (mine + step) % groups
        return send(sent.at[kind, peer], recv.at[kind, mine], group_sems.at[0, kind, step],
                    group_sems.at[1, kind, step], dp=peer)

    for kind, source in enumerate((tokens, cot)):
        @pl.loop(1, groups)
        def _(step):
            pack(kind, source, (mine + step) % groups)
            moved(kind, step).start()

    for kind, source in enumerate((tokens, cot)):
        values = source[pl.ds(pl.multiple_of(mine * piece, 8), piece), :]
        fold_into(recv, (kind, mine), values, halves)

    def land(kind):
        @pl.loop(1, groups)
        def _(step):
            moved(kind, step).wait_recv()

        @pl.loop(0, groups)
        def _(peer):
            arrived[pl.ds(pl.multiple_of(peer * piece, 8), piece), :] = unfold(recv[kind, peer], width, halves)

    land(0)
    far, near, passed = [], [], []
    for b in range(blocks):
        placed = place_rows(place_row[...], arrived[...], b * BLOCK, BLOCK)
        fold_into(wide, (me, b), placed, True)
        far.append(send(wide.at[me, b], wide.at[me, b], gather_sems.at[0, b], gather_sems.at[1, b], tensor=across))
        near.append(send(wide.at[me, b], wide.at[me, b], gather_sems.at[2, b], gather_sems.at[3, b], tensor=sibling))
        far[b].start()
        near[b].start()
    for b in range(blocks):
        far[b].wait_recv()
        passed.append(
            send(wide.at[across, b], wide.at[across, b], gather_sems.at[4, b], gather_sems.at[5, b], tensor=sibling))
        passed[b].start()
    land(1)
    quarter = BLOCK // 4
    for b in range(blocks):
        placed = place_rows(place_row[...], arrived[...], b * BLOCK, BLOCK)
        for u in range(4):
            fold_into(csent, (u, b), placed[u * quarter : (u + 1) * quarter], True)
    swaps = []
    for k, peer in enumerate((across, diagonal, sibling)):
        swaps.append(send(csent.at[peer], crecv.at[me], cot_sems.at[0, k], cot_sems.at[1, k], tensor=peer))
        swaps[k].start()
    crecv[me] = csent[me]
    for b in range(blocks):
        near[b].wait_recv()
        passed[b].wait_recv()
        for s in range(4):
            packed_out[b * BLOCK : (b + 1) * BLOCK, s * width : (s + 1) * width] = unfold(wide[s, b], width, True)
    for k in range(3):
        swaps[k].wait_recv()
    for b in range(blocks):
        for s in range(4):
            cot_out[b, :, s * width : (s + 1) * width] = unfold(crecv[s, b], width, True)
    for b in range(blocks):
        far[b].wait_send()
        near[b].wait_send()
        passed[b].wait_send()
    for k in range(3):
        swaps[k].wait_send()
    for kind in range(2):
        @pl.loop(1, groups)
        def _(step):
            moved(kind, step).wait_send()


def dispatch(tokens, cot, place_row, groups, number):
    rows, width = tokens.shape
    piece = rows // groups
    blocks = rows // BLOCK
    halves = (piece // 2) % 8 == 0
    slab = (2, groups, piece // 2, 2 * width) if halves else (2, groups, piece, width)
    return call(
        functools.partial(dispatch_kernel, groups, blocks),
        number,
        (shape((rows, 4 * width), BF), shape((blocks, BLOCK // 4, 4 * width), BF)),
        [
            pltpu.VMEM(slab, BF),
            pltpu.VMEM(slab, BF),
            pltpu.VMEM((rows, width), BF),
            pltpu.VMEM((4, blocks, BLOCK // 2, 2 * width), BF),
            pltpu.VMEM((4, blocks, BLOCK // 8, 2 * width), BF),
            pltpu.VMEM((4, blocks, BLOCK // 8, 2 * width), BF),
            pltpu.SemaphoreType.DMA((2, 2, groups)),
            pltpu.SemaphoreType.DMA((6, blocks)),
            pltpu.SemaphoreType.DMA((2, 3)),
        ],
        (tokens, cot, place_row),
    )


def gather_heads_kernel(blocks, context, out, wide, sems):
    me, sibling, across, _ = place_of()
    width = context.shape[1]
    enter([sibling, across], 0)
    far, near, passed = [], [], []
    for b in range(blocks):
        fold_into(wide, (me, b), context[b * BLOCK : (b + 1) * BLOCK, :], True)
        far.append(send(wide.at[me, b], wide.at[me, b], sems.at[0, b], sems.at[1, b], tensor=across))
        near.append(send(wide.at[me, b], wide.at[me, b], sems.at[2, b], sems.at[3, b], tensor=sibling))
        far[b].start()
        near[b].start()
    for b in range(blocks):
        far[b].wait_recv()
        passed.append(send(wide.at[across, b], wide.at[across, b], sems.at[4, b], sems.at[5, b], tensor=sibling))
        passed[b].start()
    for b in range(blocks):
        near[b].wait_recv()
        passed[b].wait_recv()
        for s in range(4):
            out[b * BLOCK : (b + 1) * BLOCK, s * width : (s + 1) * width] = unfold(wide[s, b], width, True)
    for b in range(blocks):
        far[b].wait_send()
        near[b].wait_send()
        passed[b].wait_send()


def gather_heads(context, number):
    rows, width = context.shape
    blocks = rows // BLOCK
    return call(
        functools.partial(gather_heads_kernel, blocks),
        number,
        shape((rows, 4 * width), BF),
        [pltpu.VMEM((4, blocks, BLOCK // 2, 2 * width), BF), pltpu.SemaphoreType.DMA((6, blocks))],
        (context,),
    )


def slope_of(index):
    value = jnp.float32(2.0 ** (-8.0 / HEADS))
    for head in range(1, HEADS):
        value = jnp.where(index == head, jnp.float32(2.0 ** (-8.0 * (head + 1) / HEADS)), value)
    return value


def key_distance():
    keys = lax.broadcasted_iota(jnp.int32, (BLOCK, BLOCK), 0)
    asks = lax.broadcasted_iota(jnp.int32, (BLOCK, BLOCK), 1)
    return jnp.abs(keys - asks).astype(F32)


def scores_by_key(keys, queries, slope, distance, same):
    raw = dot(keys, queries, ((1,), (1,))) * (HEAD_DIM**-0.5) - slope * distance
    return jnp.where(same, raw, -1e30)


def back_kernel(groups, blocks, grad_scale, dh_low, dh_own, qkv, lse, start_row, start_col, context, packed_in, qkv_w,
                out_w, grad0, grad1, grad2, result, small, place_col,
                layer_out, input_grad, up_grad, down_grad, qkv_grad, out_grad, small_out,
                d_rows, d_part, late_sum, late, acc, recv1, recv2, cols, one, two, three, rrecv, packed, sent, recv,
                ssent, srecv, swide, pair_sems, group_sems, x_sems, r_sems, a_sems, s_sems, w_sems):
    me, sibling, across, diagonal = place_of()
    mine = lax.axis_index("dp")
    rows, width = layer_out.shape
    heads = width // HEAD_DIM
    piece = rows // groups
    held = late.shape[1]
    halves = (piece // 2) % 8 == 0
    pairs = groups // 2
    parity = mine % 2
    pair = mine + 1 - 2 * parity
    slot = mine // 2
    quarter = BLOCK // 4
    grads = (grad0, grad1, grad2, late)
    enter([sibling, across, diagonal], groups)

    def paired(kind, step):
        m = (slot + step) % pairs
        return send(grads[kind].at[2 * m + 1 - parity], recv1.at[kind, m], pair_sems.at[0, kind, step],
                    pair_sems.at[1, kind, step], dp=pair)

    def passed(kind, step):
        m = (slot + step) % pairs
        return send(acc.at[kind, m], recv2.at[kind, slot], group_sems.at[0, kind, step], group_sems.at[1, kind, step],
                    dp=2 * m + parity)

    def forward(kind, step):
        m = (slot + step) % pairs
        paired(kind, step).wait_recv()
        acc[kind, m] = (grads[kind][2 * m + parity].astype(F32) + recv1[kind, m].astype(F32)).astype(BF)
        passed(kind, step).start()

    for kind in range(3):
        @pl.loop(1, pairs + 1)
        def _(step):
            paired(kind, step).start()

    returns = [
        send(result.at[peer], rrecv.at[me], r_sems.at[0, k], r_sems.at[1, k], tensor=peer)
        for k, peer in enumerate((across, diagonal, sibling))
    ]
    for back in returns:
        back.start()
    rrecv[me] = result[me]

    def cross(b):
        return send(cols.at[diagonal, b], one.at[b], x_sems.at[0, b], x_sems.at[1, b], tensor=sibling)

    def near(b):
        return send(cols.at[sibling, b], two.at[b], x_sems.at[2, b], x_sems.at[3, b], tensor=sibling)

    def far(b):
        return send(one.at[b], three.at[b], x_sems.at[4, b], x_sems.at[5, b], tensor=across)

    def relay(b):
        cross(b).wait()
        one[b] = (cols[across, b].astype(F32) + one[b].astype(F32)).astype(BF)
        far(b).start()

    late_sum[...] = jnp.zeros_like(late_sum)
    ssent[...] = small[...]

    @pl.loop(0, blocks)
    def _(b):
        here = pl.ds(pl.multiple_of(b * BLOCK, BLOCK), BLOCK)
        dh = dh_low[here, :]
        d_context = dot(dh, out_w[...], ((1,), (1,))).astype(BF)
        late_sum[:, 3 * width :] += dot(dh, context[here, :], ((0,), (0,)))
        same = start_col[here, :] == start_row[b]
        distance = key_distance()
        for h in range(heads):
            lanes = slice(h * HEAD_DIM, (h + 1) * HEAD_DIM)
            queries = qkv[0, here, lanes]
            keys = qkv[1, here, lanes]
            values = qkv[2, here, lanes]
            d_rows_out = d_context[:, lanes]
            scored = scores_by_key(keys, queries, slope_of(me * heads + h), distance, same)
            probs = jnp.exp(scored - lse[b, h : h + 1, :])
            d_probs = dot(values, d_rows_out, ((1,), (1,)))
            d_rows[2, :, lanes] = dot(probs.astype(BF), d_rows_out, ((1,), (0,))).astype(BF)
            center = jnp.sum(probs * d_probs, axis=0, keepdims=True)
            d_scores = (probs * (d_probs - center)).astype(BF)
            d_rows[1, :, lanes] = (dot(d_scores, queries, ((1,), (0,))) * (HEAD_DIM**-0.5)).astype(BF)
            turned = dot(keys.T, d_scores, ((1,), (0,))) * (HEAD_DIM**-0.5)
            d_rows[0, :, lanes] = turned.T.astype(BF)
        part = dot(d_rows[0], qkv_w[0], ((1,), (1,)))
        part += dot(d_rows[1], qkv_w[1], ((1,), (1,)))
        part += dot(d_rows[2], qkv_w[2], ((1,), (1,)))
        d_part[...] = part
        d_part[pl.ds(pl.multiple_of(me * quarter, quarter), quarter), :] += dh_own[b]
        for u in range(4):
            fold_into(cols, (u, b), d_part[:, u * width : (u + 1) * width].astype(BF), True)
        cross(b).start()
        near(b).start()
        for c in range(3):
            late_sum[:, c * width : (c + 1) * width] += dot(packed_in[here, :], d_rows[c], ((0,), (0,)))
        last = small.shape[0] - 6
        for k, c in enumerate((0, 2)):
            bias = jnp.sum(d_rows[c].astype(F32), axis=0, keepdims=True) * grad_scale
            ssent[last : last + 1, k * 2 * 128 : k * 2 * 128 + width] += bias
        relay(b)

    for g in range(groups):
        late[g] = (late_sum[g * held : (g + 1) * held, :] * grad_scale).astype(BF)

    @pl.loop(1, pairs + 1)
    def _(step):
        paired(3, step).start()

    swaps = [
        send(ssent, srecv.at[me], s_sems.at[0, k], s_sems.at[1, k], tensor=peer)
        for k, peer in enumerate((sibling, across, diagonal))
    ]
    for swap in swaps:
        swap.start()
    srecv[me] = ssent[...]

    def moved(kind, step):
        peer = (mine + step) % groups
        return send(sent.at[kind, peer], recv.at[kind, mine], a_sems.at[0, kind, step], a_sems.at[1, kind, step],
                    dp=peer)

    def give(kind):
        @pl.loop(0, groups)
        def _(step):
            peer = (mine + step) % groups
            columns = place_col[pl.ds(pl.multiple_of(peer * piece, 8), piece), :]
            values = take_rows(columns, packed[...])

            @pl.when(step > 0)
            def _():
                fold_into(sent, (kind, peer), values, halves)
                moved(kind, step).start()

            @pl.when(step == 0)
            def _():
                fold_into(recv, (kind, mine), values, halves)

    @pl.loop(1, pairs)
    def _(step):
        for kind in range(3):
            forward(kind, step)

    for back in returns:
        back.wait_recv()
    for b in range(blocks):
        for s in range(4):
            start = b * BLOCK + s * quarter
            packed[start : start + quarter, :] = unfold(rrecv[s, b], width, True)
    give(0)
    for b in range(blocks):
        near(b).wait()
        far(b).wait_recv()
        total = cols[me, b].astype(F32) + two[b].astype(F32) + three[b].astype(F32)
        packed[b * BLOCK : (b + 1) * BLOCK, :] = unfold(total.astype(BF), width, True)
    give(1)

    for swap in swaps:
        swap.wait_recv()
    shared = small.shape[0] // 2
    swide[mine, 0:shared] = srecv[0, 0:shared] + srecv[1, 0:shared] + srecv[2, 0:shared] + srecv[3, 0:shared]
    swide[mine, shared:] = ssent[shared:, :]

    def spread(step):
        peer = (mine + step) % groups
        return send(swide.at[mine], swide.at[mine], w_sems.at[0, step], w_sems.at[1, step], dp=peer)

    @pl.loop(1, groups)
    def _(step):
        spread(step).start()

    @pl.loop(1, pairs)
    def _(step):
        forward(3, step)

    def collect(kind):
        paired(kind, pairs).wait_recv()
        total = grads[kind][mine].astype(F32) + recv1[kind, slot].astype(F32)
        for step in range(1, pairs):
            passed(kind, step).wait_recv()
            total += recv2[kind, (slot + pairs - step) % pairs].astype(F32)
        return total

    down_grad[...] = collect(0).T
    up_grad[0] = collect(1)
    up_grad[1] = collect(2)
    total = collect(3)
    for c in range(3):
        qkv_grad[c] = total[:, c * width : (c + 1) * width]
    out_grad[...] = total[:, 3 * width :].T

    @pl.loop(1, groups)
    def _(step):
        spread(step).wait_recv()

    small_out[...] = swide[0]

    @pl.loop(1, groups)
    def _(peer):
        small_out[...] += swide[peer]

    for kind, target in ((0, layer_out), (1, input_grad)):
        @pl.loop(1, groups)
        def _(step):
            moved(kind, step).wait_recv()

        @pl.loop(0, groups)
        def _(peer):
            target[pl.ds(pl.multiple_of(peer * piece, 8), piece), :] = unfold(recv[kind, peer], width, halves)

    for b in range(blocks):
        far(b).wait_send()
    for copy in returns + swaps:
        copy.wait_send()
    for kind in range(4):
        @pl.loop(1, pairs + 1)
        def _(step):
            paired(kind, step).wait_send()

        @pl.loop(1, pairs)
        def _(step):
            passed(kind, step).wait_send()

    @pl.loop(1, groups)
    def _(step):
        spread(step).wait_send()
        moved(0, step).wait_send()
        moved(1, step).wait_send()


def back(groups, grad_scale, args, small, number):
    dh_low, qkv, grad = args[0], args[2], args[10]
    rows, columns = dh_low.shape
    width = qkv.shape[2]
    held, units = grad.shape[1:]
    piece = rows // groups
    blocks = rows // BLOCK
    halves = (piece // 2) % 8 == 0
    slab = (2, groups, piece // 2, 2 * width) if halves else (2, groups, piece, width)
    pairs = groups // 2
    half = (blocks, BLOCK // 2, 2 * width)
    dma = pltpu.SemaphoreType.DMA
    outs = (
        shape((rows, width), BF),
        shape((rows, width), BF),
        shape((2, held, units), F32),
        shape((units, held), F32),
        shape((3, held, width), F32),
        shape((width, held), F32),
        shape(small.shape, F32),
    )
    exchange = pltpu.VMEM((4, pairs, held, columns), BF)
    return call(
        functools.partial(back_kernel, groups, blocks, grad_scale),
        number,
        outs,
        [
            pltpu.VMEM((3, BLOCK, width), BF),
            pltpu.VMEM((BLOCK, columns), F32),
            pltpu.VMEM((columns, 4 * width), F32),
            pltpu.VMEM((groups, held, 4 * width), BF),
            exchange,
            exchange,
            exchange,
            pltpu.VMEM((4,) + half, BF),
            pltpu.VMEM(half, BF),
            pltpu.VMEM(half, BF),
            pltpu.VMEM(half, BF),
            pltpu.VMEM((4, blocks, BLOCK // 8, 2 * width), BF),
            pltpu.VMEM((rows, width), BF),
            pltpu.VMEM(slab, BF),
            pltpu.VMEM(slab, BF),
            pltpu.VMEM(small.shape, F32),
            pltpu.VMEM((4,) + small.shape, F32),
            pltpu.VMEM((groups,) + small.shape, F32),
            dma((2, 4, pairs + 1)),
            dma((2, 4, pairs + 1)),
            dma((6, blocks)),
            dma((2, 3)),
            dma((2, 2, groups)),
            dma((2, 3)),
            dma((2, groups)),
        ],
        args,
    )


def alibi_terms(part_index, local_heads, block_rows):
    heads_idx = (part_index * local_heads + jnp.arange(local_heads)).astype(F32)
    slopes = 2.0 ** (-8.0 * (heads_idx + 1.0) / HEADS)
    position = jnp.arange(block_rows).astype(F32)
    distance = jnp.abs(position[:, None] - position[None, :])
    return -slopes[:, None, None] * distance[None]


def block_scores(queries, key_rows, alibi_bias, same_seq, score_scale):
    raw_scores = jnp.einsum("bqhe,bkhe->bhqk", queries, key_rows, preferred_element_type=F32)
    scored = raw_scores * score_scale + alibi_bias[None]
    return jnp.where(same_seq[:, None], scored, -1e30)


def softmax_rows(scored):
    row_max = jnp.max(scored, axis=-1, keepdims=True)
    exponent = jnp.exp(scored - row_max)
    denominator = jnp.sum(exponent, axis=-1, keepdims=True)
    return (exponent / denominator, row_max + jnp.log(denominator))


def norm_back(weighted, unit, rs):
    inner = jnp.mean(weighted * unit, axis=-1, keepdims=True)
    return rs * (weighted - jnp.mean(weighted, axis=-1, keepdims=True) - unit * inner)


def norm_unit(values):
    center = values - jnp.mean(values, axis=-1, keepdims=True)
    rs = lax.rsqrt(jnp.mean(center * center, axis=-1, keepdims=True) + 1e-05)
    return center * rs, rs


def on_device(
    tokens,
    cotangent,
    seq_start,
    row_place,
    qkv_weight,
    qv_bias,
    out_weight,
    out_bias,
    first_gain,
    first_shift,
    up_weight,
    up_bias,
    down_weight,
    down_bias,
    second_gain,
    second_shift,
):
    row_count, width = tokens.shape
    columns = qkv_weight.shape[1]
    hidden_units = down_weight.shape[0]
    local_heads = width // HEAD_DIM
    blocks = row_count // BLOCK
    groups = lax.axis_size("dp")
    quarter = BLOCK // 4
    me = lax.axis_index("tensor")
    score_scale = HEAD_DIM ** (-0.5)
    grad_scale = (row_count * groups) ** (-0.5)
    wide = lambda vector: vector.astype(F32)

    def own_rows(values):
        split = values.reshape(blocks, 4, quarter, columns)
        return lax.dynamic_slice_in_dim(split, me, 1, 1)[:, 0]

    packed_in, cot_own = dispatch(tokens, cotangent, row_place, groups, 0)
    full_out = lax.all_gather(out_weight, "tensor", axis=0, tiled=True)

    alibi_bias = alibi_terms(me, local_heads, BLOCK)
    block_starts = seq_start.reshape(blocks, BLOCK)
    same_seq = block_starts[:, :, None] == block_starts[:, None, :]
    bias_rows = jnp.stack([qv_bias[0], jnp.zeros_like(qv_bias[0]), qv_bias[1]]).astype(F32)
    projected = jnp.einsum("td,kde->kte", packed_in, qkv_weight, preferred_element_type=F32)
    qkv_rows = (projected + bias_rows[:, None, :]).astype(BF)
    split_heads = qkv_rows.reshape(3, blocks, BLOCK, local_heads, HEAD_DIM)
    queries = split_heads[0]
    key_rows = split_heads[1]
    value_rows = split_heads[2]
    attn_probs, log_total = softmax_rows(block_scores(queries, key_rows, alibi_bias, same_seq, score_scale))
    context = jnp.einsum("bhqk,bkhe->bqhe", attn_probs.astype(BF), value_rows, preferred_element_type=F32)
    context = context.reshape(row_count, width).astype(BF)

    wide_context = gather_heads(context, 1)
    attended = dot(wide_context, full_out, ((1,), (0,)))
    hidden = wide(packed_in) + (attended + wide(out_bias))
    first_unit, first_rs = norm_unit(hidden)
    normed = first_unit * wide(first_gain) + wide(first_shift)
    normed_low = normed.astype(BF)
    unit_own, _ = norm_unit(own_rows(hidden))
    rs_own = lax.dynamic_slice_in_dim(first_rs.reshape(blocks, 4, quarter, 1), me, 1, 1)[:, 0]
    normed_own = unit_own * wide(first_gain) + wide(first_shift)

    lifted = jnp.einsum("td,kdf->ktf", normed_low, up_weight, preferred_element_type=F32)
    lifted = lifted + wide(up_bias)[:, None, :]
    half_erf = 0.5 * (1.0 + lax.erf(lifted[0] * (0.5**0.5)))
    gelu_gate = lifted[0] * half_erf
    gated_low = (gelu_gate * lifted[1]).astype(BF)
    ffn_part = dot(gated_low, down_weight, ((1,), (0,))).astype(BF)
    ffn_own = scatter_rows(ffn_part.reshape(blocks, 4, quarter, columns), 2)
    mixed_own = normed_own + (ffn_own + wide(down_bias))
    cot_wide = wide(cot_own)
    weighted = cot_wide * wide(second_gain)
    second_unit, second_rs = norm_unit(mixed_own)
    result_own = (second_unit * wide(second_gain) + wide(second_shift)).astype(BF)
    d_mixed_own = norm_back(weighted, second_unit, second_rs)
    d_second_gain = jnp.sum(cot_wide * second_unit, axis=(0, 1))
    d_second_shift = jnp.sum(cot_wide, axis=(0, 1))
    g_down_bias = jnp.sum(d_mixed_own, axis=(0, 1))
    split_result = result_own.reshape(blocks, 2, quarter // 2, 4, width).transpose(3, 0, 2, 1, 4)
    split_result = split_result.reshape(4, blocks, quarter // 2, 2 * width)

    d_mixed_low = gather_rows(d_mixed_own.astype(BF), 3).reshape(row_count, columns)
    g_down = dot(d_mixed_low, gated_low, ((0,), (0,)))
    d_gated = dot(d_mixed_low, down_weight, ((1,), (1,)))
    gelu_slope = half_erf + lifted[0] * jnp.exp(-0.5 * lifted[0] * lifted[0]) * ((2.0 * jnp.pi) ** (-0.5))
    d_gate = (d_gated * lifted[1] * gelu_slope).astype(BF)
    d_value = (d_gated * gelu_gate).astype(BF)
    g_gate = dot(normed_low, d_gate, ((0,), (0,)))
    g_value = dot(normed_low, d_value, ((0,), (0,)))
    g_up_bias = jnp.stack([jnp.sum(d_gate, axis=0, dtype=F32), jnp.sum(d_value, axis=0, dtype=F32)])
    d_normed_part = dot(d_gate, up_weight[0], ((1,), (1,))) + dot(d_value, up_weight[1], ((1,), (1,)))
    d_ffn_own = scatter_rows(d_normed_part.astype(BF).reshape(blocks, 4, quarter, columns), 4)
    d_normed_own = d_mixed_own + d_ffn_own

    d_hidden_own = norm_back(d_normed_own * wide(first_gain), unit_own, rs_own)
    d_first_gain = jnp.sum(d_normed_own * unit_own, axis=(0, 1))
    d_first_shift = jnp.sum(d_normed_own, axis=(0, 1))
    g_out_bias = jnp.sum(d_hidden_own, axis=(0, 1))
    d_hidden_low = gather_rows(d_hidden_own.astype(BF), 5).reshape(row_count, columns)
    def pieces(grad):
        return (grad * grad_scale).astype(BF).reshape(groups, columns // groups, grad.shape[1])

    zero = jnp.zeros((2, columns), F32)
    small = jnp.stack([g_out_bias, d_first_gain, d_first_shift, g_down_bias, d_second_gain, d_second_shift])
    small = jnp.concatenate([small, zero, g_up_bias], axis=0) * grad_scale
    small = jnp.pad(small, ((0, 6), (0, 0)))
    start_col = seq_start.reshape(row_count, 1)
    start_row = seq_start.reshape(blocks, 1, BLOCK)
    layer_out, input_grad, up_grad, down_grad, qkv_grad, out_grad, sums = back(
        groups,
        grad_scale,
        (
            d_hidden_low,
            d_hidden_own,
            qkv_rows,
            log_total.reshape(blocks, local_heads, BLOCK),
            start_row,
            start_col,
            context,
            packed_in,
            qkv_weight,
            out_weight,
            pieces(g_down),
            pieces(g_gate),
            pieces(g_value),
            split_result,
            small,
            row_place.reshape(row_count, 1),
        ),
        small,
        6,
    )

    rows_here = columns // groups
    sums_here = lax.dynamic_slice_in_dim(sums[:6], lax.axis_index("dp") * rows_here, rows_here, 1)
    return (
        layer_out,
        input_grad,
        qkv_grad,
        jnp.stack([sums[10, :width], sums[10, 256 : 256 + width]]),
        out_grad,
        sums_here[0],
        sums_here[1],
        sums_here[2],
        up_grad,
        sums[8:10],
        down_grad,
        sums_here[3],
        sums_here[4],
        sums_here[5],
    )


def solution(mesh):
    return jax.shard_map(
        on_device,
        mesh=mesh,
        in_specs=(
            P("dp", "tensor"),
            P("dp", "tensor"),
            P("dp"),
            P("dp", None),
            P(None, None, "tensor"),
            P(None, "tensor"),
            P("tensor", None),
            P(),
            P(),
            P(),
            P(None, None, "tensor"),
            P(None, "tensor"),
            P("tensor", None),
            P(),
            P(),
            P(),
        ),
        out_specs=(
            P("dp", "tensor"),
            P("dp", "tensor"),
            P(None, "dp", "tensor"),
            P(None, "tensor"),
            P("tensor", "dp"),
            P("dp"),
            P("dp"),
            P("dp"),
            P(None, "dp", "tensor"),
            P(None, "tensor"),
            P("tensor", "dp"),
            P("dp"),
            P("dp"),
            P("dp"),
        ),
        check_vma=False,
    )
```

```python
import functools

import jax
import jax.numpy as jnp
from jax import lax
from jax.experimental import pallas as pl
from jax.experimental.pallas import tpu as pltpu
from jax.sharding import PartitionSpec as P

HEADS = 12
HEAD_DIM = 64
BLOCK = 512
BF = jnp.bfloat16
F32 = jnp.float32
MESH = pl.DeviceIdType.MESH
VMEM_LIMIT = 67043328


def dot(a, b, dims):
    return lax.dot_general(a, b, (dims, ((), ())), preferred_element_type=F32)


def place_of():
    me = lax.axis_index("tensor")
    core = me % 2
    side = me // 2
    sibling = side * 2 + (1 - core)
    across = (1 - side) * 2 + core
    diagonal = (1 - side) * 2 + (1 - core)
    return me, sibling, across, diagonal


def enter(devices, groups):
    barrier = pltpu.get_barrier_semaphore()
    count = len(devices)
    for device in devices:
        pl.semaphore_signal(barrier, inc=1, device_id={"tensor": device}, device_id_type=MESH)
    if groups:
        mine = lax.axis_index("dp")

        @pl.loop(1, groups)
        def _(step):
            pl.semaphore_signal(barrier, inc=1, device_id={"dp": (mine + step) % groups}, device_id_type=MESH)

        count += groups - 1
    pl.semaphore_wait(barrier, count)


def send(source, target, send_sem, recv_sem, **where):
    return pltpu.make_async_remote_copy(
        src_ref=source, dst_ref=target, send_sem=send_sem, recv_sem=recv_sem, device_id=where, device_id_type=MESH
    )


def fold_into(buffer, index, values, halves):
    width = values.shape[1]
    if not halves:
        buffer[index] = values
        return
    half = values.shape[0] // 2
    buffer[index + (slice(None), slice(0, width))] = values[:half]
    buffer[index + (slice(None), slice(width, 2 * width))] = values[half:]


def unfold(values, width, halves):
    if not halves:
        return values
    return jnp.concatenate([values[:, :width], values[:, width:]], axis=0)


def whole(count):
    return [pl.BlockSpec(memory_space=pltpu.VMEM)] * count


def call(kernel, number, outs, scratch, args):
    return pl.pallas_call(
        kernel,
        out_shape=outs,
        in_specs=whole(len(args)),
        out_specs=jax.tree.map(lambda _: pl.BlockSpec(memory_space=pltpu.VMEM), outs),
        scratch_shapes=scratch,
        compiler_params=pltpu.CompilerParams(
            collective_id=number, has_side_effects=True, vmem_limit_bytes=VMEM_LIMIT
        ),
    )(*args)


def shape(dims, kind):
    return jax.ShapeDtypeStruct(dims, kind)


def place_rows(place_row, arrived, start, rows):
    ids = lax.broadcasted_iota(jnp.int32, (rows, arrived.shape[0]), 0) + start
    chosen = jnp.where(ids == place_row, 1.0, 0.0).astype(BF)
    return dot(chosen, arrived, ((1,), (0,))).astype(BF)


def take_rows(place_col, packed):
    ids = lax.broadcasted_iota(jnp.int32, (place_col.shape[0], packed.shape[0]), 1)
    chosen = jnp.where(ids == place_col, 1.0, 0.0).astype(BF)
    return dot(chosen, packed, ((1,), (0,))).astype(BF)


def dispatch_kernel(groups, blocks, tokens, cot, place_row, out_w, packed_out, cot_out, full_out, sent, recv, arrived, wide, csent, crecv,
                    group_sems, gather_sems, cot_sems, out_sems):
    me, sibling, across, diagonal = place_of()
    mine = lax.axis_index("dp")
    rows, width = tokens.shape
    piece = rows // groups
    halves = (piece // 2) % 8 == 0
    enter([sibling, across, diagonal], groups)

    def pack(kind, source, peer):
        values = source[pl.ds(pl.multiple_of(peer * piece, 8), piece), :]
        fold_into(sent, (kind, peer), values, halves)

    def moved(kind, step):
        peer = (mine + step) % groups
        return send(sent.at[kind, peer], recv.at[kind, mine], group_sems.at[0, kind, step],
                    group_sems.at[1, kind, step], dp=peer)

    out_far = send(out_w, full_out.at[me], out_sems.at[0], out_sems.at[1], tensor=across)
    out_near = send(out_w, full_out.at[me], out_sems.at[2], out_sems.at[3], tensor=sibling)
    out_far.start()
    out_near.start()
    for kind, source in enumerate((tokens, cot)):
        @pl.loop(1, groups)
        def _(step):
            pack(kind, source, (mine + step) % groups)
            moved(kind, step).start()

    for kind, source in enumerate((tokens, cot)):
        values = source[pl.ds(pl.multiple_of(mine * piece, 8), piece), :]
        fold_into(recv, (kind, mine), values, halves)

    def land(kind):
        @pl.loop(1, groups)
        def _(step):
            moved(kind, step).wait_recv()

        @pl.loop(0, groups)
        def _(peer):
            arrived[pl.ds(pl.multiple_of(peer * piece, 8), piece), :] = unfold(recv[kind, peer], width, halves)

    full_out[me] = out_w[...]
    out_far.wait_recv()
    out_pass = send(full_out.at[across], full_out.at[across], out_sems.at[4], out_sems.at[5], tensor=sibling)
    out_pass.start()
    land(0)
    far, near, passed = [], [], []
    for b in range(blocks):
        placed = place_rows(place_row[...], arrived[...], b * BLOCK, BLOCK)
        fold_into(wide, (me, b), placed, True)
        far.append(send(wide.at[me, b], wide.at[me, b], gather_sems.at[0, b], gather_sems.at[1, b], tensor=across))
        near.append(send(wide.at[me, b], wide.at[me, b], gather_sems.at[2, b], gather_sems.at[3, b], tensor=sibling))
        far[b].start()
        near[b].start()
    for b in range(blocks):
        far[b].wait_recv()
        passed.append(
            send(wide.at[across, b], wide.at[across, b], gather_sems.at[4, b], gather_sems.at[5, b], tensor=sibling))
        passed[b].start()
    land(1)
    quarter = BLOCK // 4
    for b in range(blocks):
        placed = place_rows(place_row[...], arrived[...], b * BLOCK, BLOCK)
        for u in range(4):
            fold_into(csent, (u, b), placed[u * quarter : (u + 1) * quarter], True)
    swaps = []
    for k, peer in enumerate((across, diagonal, sibling)):
        swaps.append(send(csent.at[peer], crecv.at[me], cot_sems.at[0, k], cot_sems.at[1, k], tensor=peer))
        swaps[k].start()
    crecv[me] = csent[me]
    for b in range(blocks):
        near[b].wait_recv()
        passed[b].wait_recv()
        for s in range(4):
            packed_out[b * BLOCK : (b + 1) * BLOCK, s * width : (s + 1) * width] = unfold(wide[s, b], width, True)
    for k in range(3):
        swaps[k].wait_recv()
    for b in range(blocks):
        for s in range(4):
            cot_out[b, :, s * width : (s + 1) * width] = unfold(crecv[s, b], width, True)
    for b in range(blocks):
        far[b].wait_send()
        near[b].wait_send()
        passed[b].wait_send()
    for k in range(3):
        swaps[k].wait_send()
    out_near.wait()
    out_pass.wait()
    out_far.wait_send()
    for kind in range(2):
        @pl.loop(1, groups)
        def _(step):
            moved(kind, step).wait_send()


def dispatch(tokens, cot, place_row, out_w, groups, number):
    rows, width = tokens.shape
    piece = rows // groups
    blocks = rows // BLOCK
    halves = (piece // 2) % 8 == 0
    slab = (2, groups, piece // 2, 2 * width) if halves else (2, groups, piece, width)
    return call(
        functools.partial(dispatch_kernel, groups, blocks),
        number,
        (
            shape((rows, 4 * width), BF),
            shape((blocks, BLOCK // 4, 4 * width), BF),
            shape((4,) + out_w.shape, BF),
        ),
        [
            pltpu.VMEM(slab, BF),
            pltpu.VMEM(slab, BF),
            pltpu.VMEM((rows, width), BF),
            pltpu.VMEM((4, blocks, BLOCK // 2, 2 * width), BF),
            pltpu.VMEM((4, blocks, BLOCK // 8, 2 * width), BF),
            pltpu.VMEM((4, blocks, BLOCK // 8, 2 * width), BF),
            pltpu.SemaphoreType.DMA((2, 2, groups)),
            pltpu.SemaphoreType.DMA((6, blocks)),
            pltpu.SemaphoreType.DMA((2, 3)),
            pltpu.SemaphoreType.DMA((6,)),
        ],
        (tokens, cot, place_row, out_w),
    )


def gather_heads_kernel(blocks, context, out, wide, sems):
    me, sibling, across, _ = place_of()
    width = context.shape[1]
    enter([sibling, across], 0)
    far, near, passed = [], [], []
    for b in range(blocks):
        fold_into(wide, (me, b), context[b * BLOCK : (b + 1) * BLOCK, :], True)
        far.append(send(wide.at[me, b], wide.at[me, b], sems.at[0, b], sems.at[1, b], tensor=across))
        near.append(send(wide.at[me, b], wide.at[me, b], sems.at[2, b], sems.at[3, b], tensor=sibling))
        far[b].start()
        near[b].start()
    for b in range(blocks):
        far[b].wait_recv()
        passed.append(send(wide.at[across, b], wide.at[across, b], sems.at[4, b], sems.at[5, b], tensor=sibling))
        passed[b].start()
    for b in range(blocks):
        near[b].wait_recv()
        passed[b].wait_recv()
        for s in range(4):
            out[b * BLOCK : (b + 1) * BLOCK, s * width : (s + 1) * width] = unfold(wide[s, b], width, True)
    for b in range(blocks):
        far[b].wait_send()
        near[b].wait_send()
        passed[b].wait_send()


def gather_heads(context, number):
    rows, width = context.shape
    blocks = rows // BLOCK
    return call(
        functools.partial(gather_heads_kernel, blocks),
        number,
        shape((rows, 4 * width), BF),
        [pltpu.VMEM((4, blocks, BLOCK // 2, 2 * width), BF), pltpu.SemaphoreType.DMA((6, blocks))],
        (context,),
    )


def norm_unit(values):
    center = values - jnp.mean(values, axis=-1, keepdims=True)
    rs = lax.rsqrt(jnp.mean(center * center, axis=-1, keepdims=True) + 1e-05)
    return center * rs, rs


def norm_back(weighted, unit, rs):
    inner = jnp.mean(weighted * unit, axis=-1, keepdims=True)
    return rs * (weighted - jnp.mean(weighted, axis=-1, keepdims=True) - unit * inner)


class GroupSum:
    def __init__(self, groups, grads, buffers, sems):
        self.acc, self.recv1, self.recv2 = buffers
        self.pair_sems, self.group_sems = sems
        self.grads = grads
        self.pairs = groups // 2
        self.mine = lax.axis_index("dp")
        self.parity = self.mine % 2
        self.pair = self.mine + 1 - 2 * self.parity
        self.slot = self.mine // 2

    def paired(self, kind, step):
        m = (self.slot + step) % self.pairs
        return send(self.grads[kind].at[2 * m + 1 - self.parity], self.recv1.at[kind, m],
                    self.pair_sems.at[0, kind, step], self.pair_sems.at[1, kind, step], dp=self.pair)

    def passed(self, kind, step):
        m = (self.slot + step) % self.pairs
        return send(self.acc.at[kind, m], self.recv2.at[kind, self.slot], self.group_sems.at[0, kind, step],
                    self.group_sems.at[1, kind, step], dp=2 * m + self.parity)

    def start(self, kind):
        @pl.loop(1, self.pairs + 1)
        def _(step):
            self.paired(kind, step).start()

    def forward(self, kinds):
        @pl.loop(1, self.pairs)
        def _(step):
            m = (self.slot + step) % self.pairs
            for kind in kinds:
                self.paired(kind, step).wait_recv()
                own = self.grads[kind][2 * m + self.parity].astype(F32)
                self.acc[kind, m] = (own + self.recv1[kind, m].astype(F32)).astype(BF)
                self.passed(kind, step).start()

    def collect(self, kind):
        self.paired(kind, self.pairs).wait_recv()
        total = self.grads[kind][self.mine].astype(F32) + self.recv1[kind, self.slot].astype(F32)
        for step in range(1, self.pairs):
            self.passed(kind, step).wait_recv()
            total += self.recv2[kind, (self.slot + self.pairs - step) % self.pairs].astype(F32)
        return total

    def end(self, kinds):
        for kind in kinds:
            @pl.loop(1, self.pairs + 1)
            def _(step):
                self.paired(kind, step).wait_send()

            @pl.loop(1, self.pairs)
            def _(step):
                self.passed(kind, step).wait_send()

    @staticmethod
    def scratch(kinds, groups, held, span):
        exchange = pltpu.VMEM((kinds, groups // 2, held, span), BF)
        sems = pltpu.SemaphoreType.DMA((2, kinds, groups // 2 + 1))
        return [exchange] * 3 + [sems] * 2


class GiveBack:
    def __init__(self, groups, rows, width, place_col, sent, recv, sems):
        self.groups, self.piece, self.width = groups, rows // groups, width
        self.halves = (self.piece // 2) % 8 == 0
        self.place_col, self.sent, self.recv, self.sems = place_col, sent, recv, sems
        self.mine = lax.axis_index("dp")

    def moved(self, step):
        peer = (self.mine + step) % self.groups
        return send(self.sent.at[peer], self.recv.at[self.mine], self.sems.at[0, step], self.sems.at[1, step], dp=peer)

    def start(self, packed):
        @pl.loop(0, self.groups)
        def _(step):
            peer = (self.mine + step) % self.groups
            columns = self.place_col[pl.ds(pl.multiple_of(peer * self.piece, 8), self.piece), :]
            values = take_rows(columns, packed[...])

            @pl.when(step > 0)
            def _():
                fold_into(self.sent, (peer,), values, self.halves)
                self.moved(step).start()

            @pl.when(step == 0)
            def _():
                fold_into(self.recv, (self.mine,), values, self.halves)

    def land(self, target):
        @pl.loop(1, self.groups)
        def _(step):
            self.moved(step).wait_recv()

        @pl.loop(0, self.groups)
        def _(peer):
            here = pl.ds(pl.multiple_of(peer * self.piece, 8), self.piece)
            target[here, :] = unfold(self.recv[peer], self.width, self.halves)

        @pl.loop(1, self.groups)
        def _(step):
            self.moved(step).wait_send()

    @staticmethod
    def scratch(groups, rows, width):
        piece = rows // groups
        halves = (piece // 2) % 8 == 0
        slab = (groups, piece // 2, 2 * width) if halves else (groups, piece, width)
        return [pltpu.VMEM(slab, BF)] * 2 + [pltpu.SemaphoreType.DMA((2, groups))]


class RowSum:
    def __init__(self, part, first, second, third, sems):
        self.part, self.first, self.second, self.third, self.sems = part, first, second, third, sems
        self.me, self.sibling, self.across, self.diagonal = place_of()

    def cross(self, b):
        return send(self.part.at[b, self.diagonal], self.first.at[b], self.sems.at[0, b], self.sems.at[1, b],
                    tensor=self.sibling)

    def near(self, b):
        return send(self.part.at[b, self.sibling], self.second.at[b], self.sems.at[2, b], self.sems.at[3, b],
                    tensor=self.sibling)

    def far(self, b):
        return send(self.first.at[b], self.third.at[b], self.sems.at[4, b], self.sems.at[5, b], tensor=self.across)

    def start(self, b):
        self.cross(b).start()
        self.near(b).start()

    def relay(self, b):
        self.cross(b).wait()
        self.first[b] = (self.part[b, self.across].astype(F32) + self.first[b].astype(F32)).astype(BF)
        self.far(b).start()

    def total(self, b):
        self.near(b).wait()
        self.far(b).wait()
        return self.part[b, self.me].astype(F32) + self.second[b].astype(F32) + self.third[b].astype(F32)

    @staticmethod
    def scratch(blocks, rows, columns):
        buffer = pltpu.VMEM((blocks, rows, columns), BF)
        return [pltpu.VMEM((blocks, 4, rows, columns), BF)] + [buffer] * 3 + [pltpu.SemaphoreType.DMA((6, blocks))]


class RowGather:
    def __init__(self, out, sems):
        self.out, self.sems = out, sems
        self.me, self.sibling, self.across, _ = place_of()

    def copy(self, b, kind, whose, peer):
        return send(self.out.at[b, whose], self.out.at[b, whose], self.sems.at[2 * kind, b],
                    self.sems.at[2 * kind + 1, b], tensor=peer)

    def start(self, b):
        self.copy(b, 0, self.me, self.across).start()
        self.copy(b, 1, self.me, self.sibling).start()

    def relay(self, b):
        self.copy(b, 0, self.me, self.across).wait_recv()
        self.copy(b, 2, self.across, self.sibling).start()

    def land(self, b):
        self.copy(b, 1, self.me, self.sibling).wait_recv()
        self.copy(b, 2, self.across, self.sibling).wait_recv()

    def end(self, b):
        self.copy(b, 0, self.me, self.across).wait_send()
        self.copy(b, 1, self.me, self.sibling).wait_send()
        self.copy(b, 2, self.across, self.sibling).wait_send()


CHUNK = 256


def mid_kernel(groups, blocks, grad_scale, context, packed, full_out, out_bias, first_gain, first_shift, up_w, up_bias,
               down_w, down_bias, second_gain, second_shift, cot, place_col,
               d_low, d_own, small, gate_grad, value_grad, down_grad, layer_out,
               normed_low, slope_term, gelu_term, gated, d_gate, d_value, unit_full, rs_full, unit_own, rs_own, d_mixed,
               mixed, whole_grad, down_pieces, folded, returned, result,
               part1, first1, second1, third1, sems1, part2, first2, second2, third2, sems2, sems3, sems4, r_sems,
               acc, recv1, recv2, pair_sems, group_sems, sent, recv, a_sems):
    me, sibling, across, diagonal = place_of()
    rows, width = layer_out.shape
    quarter = BLOCK // 4
    held = down_pieces.shape[1]
    enter([sibling, across, diagonal], groups)
    ffn = RowSum(part1, first1, second1, third1, sems1)
    back_sum = RowSum(part2, first2, second2, third2, sems2)
    mixed_gather = RowGather(mixed, sems3)
    hidden_gather = RowGather(d_low, sems4)
    sums = GroupSum(groups, (down_pieces,), (acc, recv1, recv2), (pair_sems, group_sems))
    giving = GiveBack(groups, rows, width, place_col, sent, recv, a_sems)
    small[...] = jnp.zeros_like(small)

    def add_small(row, values):
        small[row : row + 1, :] += jnp.sum(values, axis=0, keepdims=True) * grad_scale

    def ahead(b, c):
        here = slice(b * BLOCK + c * CHUNK, b * BLOCK + (c + 1) * CHUNK)
        inner = slice(c * CHUNK, (c + 1) * CHUNK)
        hidden = packed[here, :].astype(F32) + (dot(context[here, :], full_out[...], ((1,), (0,))) + out_bias[...])
        unit, rs = norm_unit(hidden)
        unit_full[inner, :] = unit
        rs_full[inner, :] = rs
        low = (unit * first_gain[...] + first_shift[...]).astype(BF)
        normed_low[here, :] = low
        gate = dot(low, up_w[0], ((1,), (0,))) + up_bias[0:1, :]
        value = dot(low, up_w[1], ((1,), (0,))) + up_bias[1:2, :]
        half_erf = 0.5 * (1.0 + lax.erf(gate * (0.5**0.5)))
        gelu = gate * half_erf
        slope = half_erf + gate * jnp.exp(-0.5 * gate * gate) * ((2.0 * jnp.pi) ** (-0.5))
        slope_term[here, :] = value * slope
        gelu_term[here, :] = gelu
        low_gated = (gelu * value).astype(BF)
        gated[here, :] = low_gated
        out = dot(low_gated, down_w[...], ((1,), (0,))).astype(BF)
        for k in range(CHUNK // quarter):
            part1[b, c * (CHUNK // quarter) + k] = out[k * quarter : (k + 1) * quarter]

    def keep_own(b):
        mine = pl.ds(pl.multiple_of(me * quarter, quarter), quarter)
        unit_own[b] = unit_full[mine, :]
        rs_own[b] = rs_full[mine, :]
        ffn.start(b)

    def turn(b):
        values = unit_own[b] * first_gain[...] + first_shift[...] + (ffn.total(b) + down_bias[...])
        unit, rs = norm_unit(values)
        out = (unit * second_gain[...] + second_shift[...]).astype(BF)
        for u in range(4):
            fold_into(folded, (u, b), out[:, u * width : (u + 1) * width], True)
        cot_rows = cot[b].astype(F32)
        d_rows = norm_back(cot_rows * second_gain[...], unit, rs)
        d_mixed[b] = d_rows
        mixed[b, me] = d_rows.astype(BF)
        mixed_gather.start(b)
        add_small(3, d_rows)
        add_small(4, cot_rows * unit)
        add_small(5, cot_rows)

    def astern(b):
        mixed_gather.land(b)
        for c in range(BLOCK // CHUNK):
            here = slice(b * BLOCK + c * CHUNK, b * BLOCK + (c + 1) * CHUNK)
            count = CHUNK // quarter
            d_rows = jnp.concatenate([mixed[b, c * count + k] for k in range(count)], axis=0)
            d_gated = dot(d_rows, down_w[...], ((1,), (1,)))
            gate_rows = (d_gated * slope_term[here, :]).astype(BF)
            value_rows = (d_gated * gelu_term[here, :]).astype(BF)
            d_gate[here, :] = gate_rows
            d_value[here, :] = value_rows
            add_small(8, gate_rows.astype(F32))
            add_small(9, value_rows.astype(F32))
            out = dot(gate_rows, up_w[0], ((1,), (1,))) + dot(value_rows, up_w[1], ((1,), (1,)))
            out = out.astype(BF)
            for k in range(count):
                part2[b, c * count + k] = out[k * quarter : (k + 1) * quarter]
        back_sum.start(b)

    def finish(b):
        d_normed = d_mixed[b] + back_sum.total(b)
        d_hidden = norm_back(d_normed * first_gain[...], unit_own[b], rs_own[b])
        d_own[b] = d_hidden
        d_low[b, me] = d_hidden.astype(BF)
        hidden_gather.start(b)
        add_small(0, d_hidden)
        add_small(1, d_normed * unit_own[b])
        add_small(2, d_normed)

    def weight_grad(left, right, pieces):
        span = right.shape[1]
        for c in range(span // CHUNK):
            lanes = slice(c * CHUNK, (c + 1) * CHUNK)
            whole_grad[:, lanes] = dot(left, right[:, lanes], ((0,), (0,)))
        for g in range(groups):
            pieces[g] = (whole_grad[g * held : (g + 1) * held, :] * grad_scale).astype(BF)

    last = blocks - 1
    for b in range(blocks):
        ahead(b, 0)
        if b >= 1:
            ffn.relay(b - 1)
        if b >= 2:
            turn(b - 2)
        ahead(b, 1)
        keep_own(b)
        if b >= 2:
            mixed_gather.relay(b - 2)
    ffn.relay(last)
    if blocks > 1:
        turn(last - 1)
    turn(last)
    if blocks > 1:
        mixed_gather.relay(last - 1)
    returns = [
        send(folded.at[peer], returned.at[me], r_sems.at[0, k], r_sems.at[1, k], tensor=peer)
        for k, peer in enumerate((across, diagonal, sibling))
    ]
    for b in range(blocks):
        if b == last:
            mixed_gather.relay(last)
        astern(b)
        if b >= 1:
            back_sum.relay(b - 1)
    for swap in returns:
        swap.start()
    returned[me] = folded[me]
    back_sum.relay(last)
    d_mixed_rows = jnp.concatenate([mixed[b, k] for b in range(blocks) for k in range(4)], axis=0)
    weight_grad(d_mixed_rows, gated, down_pieces)
    sums.start(0)
    finish(0)
    weight_grad(normed_low[...], d_gate, gate_grad)
    if blocks > 1:
        finish(1)
    weight_grad(normed_low[...], d_value, value_grad)
    for b in range(2, blocks):
        finish(b)
    for b in range(blocks):
        hidden_gather.relay(b)
    for swap in returns:
        swap.wait_recv()
    for b in range(blocks):
        for s in range(4):
            start = b * BLOCK + s * quarter
            result[start : start + quarter, :] = unfold(returned[s, b], width, True)
    giving.start(result)
    sums.forward((0,))
    for b in range(blocks):
        hidden_gather.land(b)
    down_grad[...] = sums.collect(0).T
    giving.land(layer_out)
    for b in range(blocks):
        mixed_gather.end(b)
        hidden_gather.end(b)
    for swap in returns:
        swap.wait_send()
    sums.end((0,))


def mid(groups, grad_scale, args, number):
    context, up_w, cot = args[0], args[6], args[12]
    rows, columns = context.shape
    units = up_w.shape[2]
    width = columns // 4
    held = columns // groups
    blocks = rows // BLOCK
    quarter = BLOCK // 4
    own = (blocks, quarter, columns)
    dma = pltpu.SemaphoreType.DMA
    outs = (
        shape((blocks, 4, quarter, columns), BF),
        shape(own, F32),
        shape((16, columns), F32),
        shape((groups, held, units), BF),
        shape((groups, held, units), BF),
        shape((units, held), F32),
        shape((rows, width), BF),
    )
    folded = pltpu.VMEM((4, blocks, quarter // 2, 2 * width), BF)
    return call(
        functools.partial(mid_kernel, groups, blocks, grad_scale),
        number,
        outs,
        [
            pltpu.VMEM((rows, columns), BF),
            pltpu.VMEM((rows, units), F32),
            pltpu.VMEM((rows, units), F32),
            pltpu.VMEM((rows, units), BF),
            pltpu.VMEM((rows, units), BF),
            pltpu.VMEM((rows, units), BF),
            pltpu.VMEM((BLOCK, columns), F32),
            pltpu.VMEM((BLOCK, 1), F32),
            pltpu.VMEM(own, F32),
            pltpu.VMEM((blocks, quarter, 1), F32),
            pltpu.VMEM(own, F32),
            pltpu.VMEM((blocks, 4, quarter, columns), BF),
            pltpu.VMEM((columns, units), F32),
            pltpu.VMEM((groups, held, units), BF),
            folded,
            folded,
            pltpu.VMEM((rows, width), BF),
        ]
        + RowSum.scratch(blocks, quarter, columns)
        + RowSum.scratch(blocks, quarter, columns)
        + [dma((6, blocks)), dma((6, blocks)), dma((2, 3))]
        + GroupSum.scratch(1, groups, held, units)
        + GiveBack.scratch(groups, rows, width),
        args,
    )


def slope_of(index):
    value = jnp.float32(2.0 ** (-8.0 / HEADS))
    for head in range(1, HEADS):
        value = jnp.where(index == head, jnp.float32(2.0 ** (-8.0 * (head + 1) / HEADS)), value)
    return value


def key_distance():
    keys = lax.broadcasted_iota(jnp.int32, (BLOCK, BLOCK), 0)
    asks = lax.broadcasted_iota(jnp.int32, (BLOCK, BLOCK), 1)
    return jnp.abs(keys - asks).astype(F32)


def scores_by_key(keys, queries, slope, distance, same):
    raw = dot(keys, queries, ((1,), (1,))) * (HEAD_DIM**-0.5) - slope * distance
    return jnp.where(same, raw, -1e30)


def back_kernel(groups, blocks, grad_scale, dh_low, dh_own, qkv, lse, start_row, start_col, context, packed_in, qkv_w,
                out_w, grad0, grad1, small, place_col,
                input_grad, up_grad, qkv_grad, out_grad, small_out,
                d_rows, d_part, late_sum, late, cols, one, two, three, packed, ssent, srecv, swide, x_sems, s_sems, w_sems,
                acc, recv1, recv2, pair_sems, group_sems, sent, recv, a_sems):
    me, sibling, across, diagonal = place_of()
    mine = lax.axis_index("dp")
    rows, width = input_grad.shape
    heads = width // HEAD_DIM
    held = late.shape[1]
    quarter = BLOCK // 4
    enter([sibling, across, diagonal], groups)
    sums = GroupSum(groups, (grad0, grad1, late), (acc, recv1, recv2), (pair_sems, group_sems))
    giving = GiveBack(groups, rows, width, place_col, sent, recv, a_sems)
    sums.start(0)
    sums.start(1)

    def cross(b):
        return send(cols.at[diagonal, b], one.at[b], x_sems.at[0, b], x_sems.at[1, b], tensor=sibling)

    def near(b):
        return send(cols.at[sibling, b], two.at[b], x_sems.at[2, b], x_sems.at[3, b], tensor=sibling)

    def far(b):
        return send(one.at[b], three.at[b], x_sems.at[4, b], x_sems.at[5, b], tensor=across)

    def relay(b):
        cross(b).wait()
        one[b] = (cols[across, b].astype(F32) + one[b].astype(F32)).astype(BF)
        far(b).start()

    late_sum[...] = jnp.zeros_like(late_sum)
    ssent[...] = small[...]

    @pl.loop(0, blocks)
    def _(b):
        here = pl.ds(pl.multiple_of(b * BLOCK, BLOCK), BLOCK)
        dh = dh_low[here, :]
        d_context = dot(dh, out_w[...], ((1,), (1,))).astype(BF)
        late_sum[:, 3 * width :] += dot(dh, context[here, :], ((0,), (0,)))
        same = start_col[here, :] == start_row[b]
        distance = key_distance()
        for h in range(heads):
            lanes = slice(h * HEAD_DIM, (h + 1) * HEAD_DIM)
            queries = qkv[0, here, lanes]
            keys = qkv[1, here, lanes]
            values = qkv[2, here, lanes]
            d_rows_out = d_context[:, lanes]
            scored = scores_by_key(keys, queries, slope_of(me * heads + h), distance, same)
            probs = jnp.exp(scored - lse[b, h : h + 1, :])
            d_probs = dot(values, d_rows_out, ((1,), (1,)))
            d_rows[2, :, lanes] = dot(probs.astype(BF), d_rows_out, ((1,), (0,))).astype(BF)
            center = jnp.sum(probs * d_probs, axis=0, keepdims=True)
            d_scores = (probs * (d_probs - center)).astype(BF)
            d_rows[1, :, lanes] = (dot(d_scores, queries, ((1,), (0,))) * (HEAD_DIM**-0.5)).astype(BF)
            turned = dot(keys.T, d_scores, ((1,), (0,))) * (HEAD_DIM**-0.5)
            d_rows[0, :, lanes] = turned.T.astype(BF)
        part = dot(d_rows[0], qkv_w[0], ((1,), (1,)))
        part += dot(d_rows[1], qkv_w[1], ((1,), (1,)))
        part += dot(d_rows[2], qkv_w[2], ((1,), (1,)))
        d_part[...] = part
        d_part[pl.ds(pl.multiple_of(me * quarter, quarter), quarter), :] += dh_own[b]
        for u in range(4):
            fold_into(cols, (u, b), d_part[:, u * width : (u + 1) * width].astype(BF), True)
        cross(b).start()
        near(b).start()
        for c in range(3):
            late_sum[:, c * width : (c + 1) * width] += dot(packed_in[here, :], d_rows[c], ((0,), (0,)))
        last = small.shape[0] - 6
        for k, c in enumerate((0, 2)):
            bias = jnp.sum(d_rows[c].astype(F32), axis=0, keepdims=True) * grad_scale
            ssent[last : last + 1, k * 2 * 128 : k * 2 * 128 + width] += bias
        relay(b)

    for g in range(groups):
        late[g] = (late_sum[g * held : (g + 1) * held, :] * grad_scale).astype(BF)

    sums.start(2)
    swaps = [
        send(ssent, srecv.at[me], s_sems.at[0, k], s_sems.at[1, k], tensor=peer)
        for k, peer in enumerate((sibling, across, diagonal))
    ]
    for swap in swaps:
        swap.start()
    srecv[me] = ssent[...]

    sums.forward((0, 1))
    for b in range(blocks):
        near(b).wait()
        far(b).wait_recv()
        total = cols[me, b].astype(F32) + two[b].astype(F32) + three[b].astype(F32)
        packed[b * BLOCK : (b + 1) * BLOCK, :] = unfold(total.astype(BF), width, True)
    giving.start(packed)

    for swap in swaps:
        swap.wait_recv()
    shared = small.shape[0] // 2
    swide[mine, 0:shared] = srecv[0, 0:shared] + srecv[1, 0:shared] + srecv[2, 0:shared] + srecv[3, 0:shared]
    swide[mine, shared:] = ssent[shared:, :]

    def spread(step):
        peer = (mine + step) % groups
        return send(swide.at[mine], swide.at[mine], w_sems.at[0, step], w_sems.at[1, step], dp=peer)

    @pl.loop(1, groups)
    def _(step):
        spread(step).start()

    sums.forward((2,))
    up_grad[0] = sums.collect(0)
    up_grad[1] = sums.collect(1)
    total = sums.collect(2)
    for c in range(3):
        qkv_grad[c] = total[:, c * width : (c + 1) * width]
    out_grad[...] = total[:, 3 * width :].T

    @pl.loop(1, groups)
    def _(step):
        spread(step).wait_recv()

    small_out[...] = swide[0]

    @pl.loop(1, groups)
    def _(peer):
        small_out[...] += swide[peer]

    giving.land(input_grad)
    for b in range(blocks):
        far(b).wait_send()
    for copy in swaps:
        copy.wait_send()
    sums.end((0, 1, 2))

    @pl.loop(1, groups)
    def _(step):
        spread(step).wait_send()


def back(groups, grad_scale, args, small, number):
    dh_low, qkv, grad = args[0], args[2], args[10]
    rows, columns = dh_low.shape
    width = qkv.shape[2]
    held, units = grad.shape[1:]
    blocks = rows // BLOCK
    half = (blocks, BLOCK // 2, 2 * width)
    dma = pltpu.SemaphoreType.DMA
    outs = (
        shape((rows, width), BF),
        shape((2, held, units), F32),
        shape((3, held, width), F32),
        shape((width, held), F32),
        shape(small.shape, F32),
    )
    return call(
        functools.partial(back_kernel, groups, blocks, grad_scale),
        number,
        outs,
        [
            pltpu.VMEM((3, BLOCK, width), BF),
            pltpu.VMEM((BLOCK, columns), F32),
            pltpu.VMEM((columns, 4 * width), F32),
            pltpu.VMEM((groups, held, 4 * width), BF),
            pltpu.VMEM((4,) + half, BF),
            pltpu.VMEM(half, BF),
            pltpu.VMEM(half, BF),
            pltpu.VMEM(half, BF),
            pltpu.VMEM((rows, width), BF),
            pltpu.VMEM(small.shape, F32),
            pltpu.VMEM((4,) + small.shape, F32),
            pltpu.VMEM((groups,) + small.shape, F32),
            dma((6, blocks)),
            dma((2, 3)),
            dma((2, groups)),
        ]
        + GroupSum.scratch(3, groups, held, columns)
        + GiveBack.scratch(groups, rows, width),
        args,
    )


def alibi_terms(part_index, local_heads, block_rows):
    heads_idx = (part_index * local_heads + jnp.arange(local_heads)).astype(F32)
    slopes = 2.0 ** (-8.0 * (heads_idx + 1.0) / HEADS)
    position = jnp.arange(block_rows).astype(F32)
    distance = jnp.abs(position[:, None] - position[None, :])
    return -slopes[:, None, None] * distance[None]


def block_scores(queries, key_rows, alibi_bias, same_seq, score_scale):
    raw_scores = jnp.einsum("bqhe,bkhe->bhqk", queries, key_rows, preferred_element_type=F32)
    scored = raw_scores * score_scale + alibi_bias[None]
    return jnp.where(same_seq[:, None], scored, -1e30)


def softmax_rows(scored):
    row_max = jnp.max(scored, axis=-1, keepdims=True)
    exponent = jnp.exp(scored - row_max)
    denominator = jnp.sum(exponent, axis=-1, keepdims=True)
    return (exponent / denominator, row_max + jnp.log(denominator))


def on_device(
    tokens,
    cotangent,
    seq_start,
    row_place,
    qkv_weight,
    qv_bias,
    out_weight,
    out_bias,
    first_gain,
    first_shift,
    up_weight,
    up_bias,
    down_weight,
    down_bias,
    second_gain,
    second_shift,
):
    row_count, width = tokens.shape
    columns = qkv_weight.shape[1]
    hidden_units = down_weight.shape[0]
    local_heads = width // HEAD_DIM
    blocks = row_count // BLOCK
    groups = lax.axis_size("dp")
    quarter = BLOCK // 4
    me = lax.axis_index("tensor")
    score_scale = HEAD_DIM ** (-0.5)
    grad_scale = (row_count * groups) ** (-0.5)
    wide = lambda vector: vector.astype(F32)

    packed_in, cot_own, full_out = dispatch(tokens, cotangent, row_place, out_weight, groups, 0)
    place_col = row_place.reshape(row_count, 1)

    alibi_bias = alibi_terms(me, local_heads, BLOCK)
    block_starts = seq_start.reshape(blocks, BLOCK)
    same_seq = block_starts[:, :, None] == block_starts[:, None, :]
    bias_rows = jnp.stack([qv_bias[0], jnp.zeros_like(qv_bias[0]), qv_bias[1]]).astype(F32)
    projected = jnp.einsum("td,kde->kte", packed_in, qkv_weight, preferred_element_type=F32)
    qkv_rows = (projected + bias_rows[:, None, :]).astype(BF)
    split_heads = qkv_rows.reshape(3, blocks, BLOCK, local_heads, HEAD_DIM)
    queries = split_heads[0]
    key_rows = split_heads[1]
    value_rows = split_heads[2]
    attn_probs, log_total = softmax_rows(block_scores(queries, key_rows, alibi_bias, same_seq, score_scale))
    context = jnp.einsum("bhqk,bkhe->bqhe", attn_probs.astype(BF), value_rows, preferred_element_type=F32)
    context = context.reshape(row_count, width).astype(BF)

    wide_context = gather_heads(context, 1)
    row = lambda vector: wide(vector).reshape(1, columns)
    d_low, d_own, small, gate_grad, value_grad, down_grad, layer_out = mid(
        groups,
        grad_scale,
        (
            wide_context,
            packed_in,
            full_out.reshape(columns, columns),
            row(out_bias),
            row(first_gain),
            row(first_shift),
            up_weight,
            wide(up_bias),
            down_weight,
            row(down_bias),
            row(second_gain),
            row(second_shift),
            cot_own,
            place_col,
        ),
        2,
    )
    start_col = seq_start.reshape(row_count, 1)
    start_row = seq_start.reshape(blocks, 1, BLOCK)
    input_grad, up_grad, qkv_grad, out_grad, sums = back(
        groups,
        grad_scale,
        (
            d_low.reshape(row_count, columns),
            d_own,
            qkv_rows,
            log_total.reshape(blocks, local_heads, BLOCK),
            start_row,
            start_col,
            context,
            packed_in,
            qkv_weight,
            out_weight,
            gate_grad,
            value_grad,
            small,
            place_col,
        ),
        small,
        3,
    )
    rows_here = columns // groups
    sums_here = lax.dynamic_slice_in_dim(sums[:6], lax.axis_index("dp") * rows_here, rows_here, 1)
    return (
        layer_out,
        input_grad,
        qkv_grad,
        jnp.stack([sums[10, :width], sums[10, 256 : 256 + width]]),
        out_grad,
        sums_here[0],
        sums_here[1],
        sums_here[2],
        up_grad,
        sums[8:10],
        down_grad,
        sums_here[3],
        sums_here[4],
        sums_here[5],
    )


def solution(mesh):
    return jax.shard_map(
        on_device,
        mesh=mesh,
        in_specs=(
            P("dp", "tensor"),
            P("dp", "tensor"),
            P("dp"),
            P("dp", None),
            P(None, None, "tensor"),
            P(None, "tensor"),
            P("tensor", None),
            P(),
            P(),
            P(),
            P(None, None, "tensor"),
            P(None, "tensor"),
            P("tensor", None),
            P(),
            P(),
            P(),
        ),
        out_specs=(
            P("dp", "tensor"),
            P("dp", "tensor"),
            P(None, "dp", "tensor"),
            P(None, "tensor"),
            P("tensor", "dp"),
            P("dp"),
            P("dp"),
            P("dp"),
            P(None, "dp", "tensor"),
            P(None, "tensor"),
            P("tensor", "dp"),
            P("dp"),
            P("dp"),
            P("dp"),
        ),
        check_vma=False,
    )
```

```python
import functools

import jax
import jax.numpy as jnp
from jax import lax
from jax.experimental import pallas as pl
from jax.experimental.pallas import tpu as pltpu
from jax.sharding import PartitionSpec as P

HEADS = 12
HEAD_DIM = 64
BLOCK = 512
BF = jnp.bfloat16
F32 = jnp.float32
MESH = pl.DeviceIdType.MESH
VMEM_LIMIT = 67043328


def dot(a, b, dims):
    return lax.dot_general(a, b, (dims, ((), ())), preferred_element_type=F32)


def place_of():
    me = lax.axis_index("tensor")
    core = me % 2
    side = me // 2
    sibling = side * 2 + (1 - core)
    across = (1 - side) * 2 + core
    diagonal = (1 - side) * 2 + (1 - core)
    return me, sibling, across, diagonal


def enter(devices, groups):
    barrier = pltpu.get_barrier_semaphore()
    count = len(devices)
    for device in devices:
        pl.semaphore_signal(barrier, inc=1, device_id={"tensor": device}, device_id_type=MESH)
    if groups:
        mine = lax.axis_index("dp")

        @pl.loop(1, groups)
        def _(step):
            pl.semaphore_signal(barrier, inc=1, device_id={"dp": (mine + step) % groups}, device_id_type=MESH)

        count += groups - 1
    pl.semaphore_wait(barrier, count)


def send(source, target, send_sem, recv_sem, **where):
    return pltpu.make_async_remote_copy(
        src_ref=source, dst_ref=target, send_sem=send_sem, recv_sem=recv_sem, device_id=where, device_id_type=MESH
    )


def fold_into(buffer, index, values, halves):
    width = values.shape[1]
    if not halves:
        buffer[index] = values
        return
    half = values.shape[0] // 2
    buffer[index + (slice(None), slice(0, width))] = values[:half]
    buffer[index + (slice(None), slice(width, 2 * width))] = values[half:]


def unfold(values, width, halves):
    if not halves:
        return values
    return jnp.concatenate([values[:, :width], values[:, width:]], axis=0)


def call(kernel, number, outs, scratch, args, apart=()):
    specs = [pl.BlockSpec(memory_space=pl.ANY if k in apart else pltpu.VMEM) for k in range(len(args))]
    return pl.pallas_call(
        kernel,
        out_shape=outs,
        in_specs=specs,
        out_specs=jax.tree.map(lambda _: pl.BlockSpec(memory_space=pltpu.VMEM), outs),
        scratch_shapes=scratch,
        compiler_params=pltpu.CompilerParams(
            collective_id=number, has_side_effects=True, vmem_limit_bytes=VMEM_LIMIT
        ),
    )(*args)


def shape(dims, kind):
    return jax.ShapeDtypeStruct(dims, kind)


def place_rows(place_row, arrived, start, rows):
    ids = lax.broadcasted_iota(jnp.int32, (rows, arrived.shape[0]), 0) + start
    chosen = jnp.where(ids == place_row, 1.0, 0.0).astype(BF)
    return dot(chosen, arrived, ((1,), (0,))).astype(BF)


def take_rows(place_col, packed):
    ids = lax.broadcasted_iota(jnp.int32, (place_col.shape[0], packed.shape[0]), 1)
    chosen = jnp.where(ids == place_col, 1.0, 0.0).astype(BF)
    return dot(chosen, packed, ((1,), (0,))).astype(BF)


def to_column(row, column):
    for k in range(row.shape[1] // 128):
        piece = jnp.broadcast_to(row[0:1, k * 128 : (k + 1) * 128], (8, 128))
        column[k * 128 : (k + 1) * 128, :] = piece.T


def slope_of(index):
    value = jnp.float32(2.0 ** (-8.0 / HEADS))
    for head in range(1, HEADS):
        value = jnp.where(index == head, jnp.float32(2.0 ** (-8.0 * (head + 1) / HEADS)), value)
    return value


def key_distance():
    keys = lax.broadcasted_iota(jnp.int32, (BLOCK, BLOCK), 0)
    asks = lax.broadcasted_iota(jnp.int32, (BLOCK, BLOCK), 1)
    return jnp.abs(keys - asks).astype(F32)


def scores_by_key(keys, queries, slope, distance, same):
    raw = dot(keys, queries, ((1,), (1,))) * (HEAD_DIM**-0.5) - slope * distance
    return jnp.where(same, raw, -1e30)


class HeadGather:
    def __init__(self, wide, sems):
        self.wide, self.sems = wide, sems
        self.me, self.sibling, self.across, _ = place_of()

    def copy(self, b, kind, whose, peer):
        return send(self.wide.at[whose, b], self.wide.at[whose, b], self.sems.at[2 * kind, b],
                    self.sems.at[2 * kind + 1, b], tensor=peer)

    def start(self, b, values):
        fold_into(self.wide, (self.me, b), values, True)
        self.copy(b, 0, self.me, self.across).start()
        self.copy(b, 1, self.me, self.sibling).start()

    def relay(self, b):
        self.copy(b, 0, self.me, self.across).wait_recv()
        self.copy(b, 2, self.across, self.sibling).start()

    def land(self, b, out, width):
        self.copy(b, 1, self.me, self.sibling).wait_recv()
        self.copy(b, 2, self.across, self.sibling).wait_recv()
        for s in range(4):
            out[b * BLOCK : (b + 1) * BLOCK, s * width : (s + 1) * width] = unfold(self.wide[s, b], width, True)

    def end(self, b):
        self.copy(b, 0, self.me, self.across).wait_send()
        self.copy(b, 1, self.me, self.sibling).wait_send()
        self.copy(b, 2, self.across, self.sibling).wait_send()


def front_kernel(groups, blocks, tokens, cot, place_row, seq_row, qkv_w, qv_bias, out_w,
                 packed_out, cot_out, full_out, qkv, lse, context, wide_context,
                 tokens_here, cot_here, weight_here, start_col, sent, recv, arrived, wide, wide_heads, csent, crecv,
                 local_sems, group_sems, gather_sems, head_sems, cot_sems, out_sems):
    me, sibling, across, diagonal = place_of()
    mine = lax.axis_index("dp")
    rows, width = tokens_here.shape
    heads = width // HEAD_DIM
    piece = rows // groups
    halves = (piece // 2) % 8 == 0
    quarter = BLOCK // 4
    loads = [
        pltpu.make_async_copy(source, target, local_sems.at[k])
        for k, (source, target) in enumerate(((tokens, tokens_here), (cot, cot_here), (qkv_w, weight_here)))
    ]
    for load in loads:
        load.start()
    enter([sibling, across, diagonal], groups)

    def moved(kind, step):
        peer = (mine + step) % groups
        return send(sent.at[kind, peer], recv.at[kind, mine], group_sems.at[0, kind, step],
                    group_sems.at[1, kind, step], dp=peer)

    def give(kind, source):
        @pl.loop(1, groups)
        def _(step):
            peer = (mine + step) % groups
            values = source[pl.ds(pl.multiple_of(peer * piece, 8), piece), :]
            fold_into(sent, (kind, peer), values, halves)
            moved(kind, step).start()

        values = source[pl.ds(pl.multiple_of(mine * piece, 8), piece), :]
        fold_into(recv, (kind, mine), values, halves)

    loads[0].wait()
    give(0, tokens_here)
    out_far = send(out_w, full_out.at[me], out_sems.at[0], out_sems.at[1], tensor=across)
    out_near = send(out_w, full_out.at[me], out_sems.at[2], out_sems.at[3], tensor=sibling)
    out_pass = send(full_out.at[across], full_out.at[across], out_sems.at[4], out_sems.at[5], tensor=sibling)
    out_far.start()
    out_near.start()
    loads[1].wait()
    give(1, cot_here)
    full_out[me] = out_w[...]
    to_column(seq_row, start_col)
    out_far.wait_recv()
    out_pass.start()

    def land(kind):
        @pl.loop(1, groups)
        def _(step):
            moved(kind, step).wait_recv()

        @pl.loop(0, groups)
        def _(peer):
            arrived[pl.ds(pl.multiple_of(peer * piece, 8), piece), :] = unfold(recv[kind, peer], width, halves)

    token_gather = HeadGather(wide, gather_sems)
    head_gather = HeadGather(wide_heads, head_sems)
    land(0)
    for b in range(blocks):
        token_gather.start(b, place_rows(place_row[...], arrived[...], b * BLOCK, BLOCK))
        if b >= 1:
            token_gather.relay(b - 1)
    loads[2].wait()

    def attend(b):
        here = slice(b * BLOCK, (b + 1) * BLOCK)
        token_gather.land(b, packed_out, width)
        for k in range(3):
            part = dot(packed_out[here, :], weight_here[k], ((1,), (0,)))
            if k != 1:
                part += qv_bias[k // 2 : k // 2 + 1, :].astype(F32)
            qkv[k, here, :] = part.astype(BF)
        same = start_col[here, 0:1] == seq_row[0:1, here]
        distance = key_distance()
        for h in range(heads):
            lanes = slice(h * HEAD_DIM, (h + 1) * HEAD_DIM)
            scored = scores_by_key(qkv[1, here, lanes], qkv[0, here, lanes], slope_of(me * heads + h), distance, same)
            top = jnp.max(scored, axis=0, keepdims=True)
            raised = jnp.exp(scored - top)
            total = jnp.sum(raised, axis=0, keepdims=True)
            lse[b, h : h + 1, :] = top + jnp.log(total)
            probs = (raised * (1.0 / total)).astype(BF)
            turned = dot(qkv[2, here, lanes].T, probs, ((1,), (0,)))
            context[here, lanes] = turned.T.astype(BF)
        head_gather.start(b, context[here, :])

    def swap(k):
        peer = (across, diagonal, sibling)[k]
        return send(csent.at[peer], crecv.at[me], cot_sems.at[0, k], cot_sems.at[1, k], tensor=peer)

    def place_cot():
        land(1)
        for b in range(blocks):
            placed = place_rows(place_row[...], arrived[...], b * BLOCK, BLOCK)
            for u in range(4):
                fold_into(csent, (u, b), placed[u * quarter : (u + 1) * quarter], True)
        for k in range(3):
            swap(k).start()
        crecv[me] = csent[me]

    for b in range(blocks):
        if b == blocks - 1:
            token_gather.relay(b)
            place_cot()
        attend(b)
        if b >= 1:
            head_gather.relay(b - 1)
    for b in range(blocks - 1):
        head_gather.land(b, wide_context, width)
    for k in range(3):
        swap(k).wait_recv()
    for b in range(blocks):
        for s in range(4):
            cot_out[b, :, s * width : (s + 1) * width] = unfold(crecv[s, b], width, True)
    head_gather.relay(blocks - 1)
    head_gather.land(blocks - 1, wide_context, width)
    for b in range(blocks):
        token_gather.end(b)
        head_gather.end(b)
    for k in range(3):
        swap(k).wait_send()
    out_near.wait()
    out_pass.wait()
    out_far.wait_send()
    for kind in range(2):
        @pl.loop(1, groups)
        def _(step):
            moved(kind, step).wait_send()


def front(groups, args, number):
    tokens, qkv_w, out_w = args[0], args[4], args[6]
    rows, width = tokens.shape
    piece = rows // groups
    blocks = rows // BLOCK
    heads = width // HEAD_DIM
    halves = (piece // 2) % 8 == 0
    slab = (2, groups, piece // 2, 2 * width) if halves else (2, groups, piece, width)
    here = pltpu.VMEM((rows, width), BF)
    wide = pltpu.VMEM((4, blocks, BLOCK // 2, 2 * width), BF)
    folded = pltpu.VMEM((4, blocks, BLOCK // 8, 2 * width), BF)
    dma = pltpu.SemaphoreType.DMA
    return call(
        functools.partial(front_kernel, groups, blocks),
        number,
        (
            shape((rows, 4 * width), BF),
            shape((blocks, BLOCK // 4, 4 * width), BF),
            shape((4,) + out_w.shape, BF),
            shape((3, rows, width), BF),
            shape((blocks, heads, BLOCK), F32),
            shape((rows, width), BF),
            shape((rows, 4 * width), BF),
        ),
        [
            here,
            here,
            pltpu.VMEM(qkv_w.shape, BF),
            pltpu.VMEM((rows, 8), jnp.int32),
            pltpu.VMEM(slab, BF),
            pltpu.VMEM(slab, BF),
            here,
            wide,
            wide,
            folded,
            folded,
            dma((3,)),
            dma((2, 2, groups)),
            dma((6, blocks)),
            dma((6, blocks)),
            dma((2, 3)),
            dma((6,)),
        ],
        args,
        apart=(0, 1, 4),
    )


def norm_unit(values):
    center = values - jnp.mean(values, axis=-1, keepdims=True)
    rs = lax.rsqrt(jnp.mean(center * center, axis=-1, keepdims=True) + 1e-05)
    return center * rs, rs


def norm_back(weighted, unit, rs):
    inner = jnp.mean(weighted * unit, axis=-1, keepdims=True)
    return rs * (weighted - jnp.mean(weighted, axis=-1, keepdims=True) - unit * inner)


class GroupSum:
    def __init__(self, groups, grads, buffers, sems):
        self.acc, self.recv1, self.recv2 = buffers
        self.pair_sems, self.group_sems = sems
        self.grads = grads
        self.pairs = groups // 2
        self.mine = lax.axis_index("dp")
        self.parity = self.mine % 2
        self.pair = self.mine + 1 - 2 * self.parity
        self.slot = self.mine // 2

    def paired(self, kind, step):
        m = (self.slot + step) % self.pairs
        return send(self.grads[kind].at[2 * m + 1 - self.parity], self.recv1.at[kind, m],
                    self.pair_sems.at[0, kind, step], self.pair_sems.at[1, kind, step], dp=self.pair)

    def passed(self, kind, step):
        m = (self.slot + step) % self.pairs
        return send(self.acc.at[kind, m], self.recv2.at[kind, self.slot], self.group_sems.at[0, kind, step],
                    self.group_sems.at[1, kind, step], dp=2 * m + self.parity)

    def start(self, kind):
        @pl.loop(1, self.pairs + 1)
        def _(step):
            self.paired(kind, step).start()

    def forward(self, kinds):
        @pl.loop(1, self.pairs)
        def _(step):
            m = (self.slot + step) % self.pairs
            for kind in kinds:
                self.paired(kind, step).wait_recv()
                own = self.grads[kind][2 * m + self.parity].astype(F32)
                self.acc[kind, m] = (own + self.recv1[kind, m].astype(F32)).astype(BF)
                self.passed(kind, step).start()

    def collect(self, kind):
        self.paired(kind, self.pairs).wait_recv()
        total = self.grads[kind][self.mine].astype(F32) + self.recv1[kind, self.slot].astype(F32)
        for step in range(1, self.pairs):
            self.passed(kind, step).wait_recv()
            total += self.recv2[kind, (self.slot + self.pairs - step) % self.pairs].astype(F32)
        return total

    def end(self, kinds):
        for kind in kinds:
            @pl.loop(1, self.pairs + 1)
            def _(step):
                self.paired(kind, step).wait_send()

            @pl.loop(1, self.pairs)
            def _(step):
                self.passed(kind, step).wait_send()

    @staticmethod
    def scratch(kinds, groups, held, span):
        exchange = pltpu.VMEM((kinds, groups // 2, held, span), BF)
        sems = pltpu.SemaphoreType.DMA((2, kinds, groups // 2 + 1))
        return [exchange] * 3 + [sems] * 2


class GiveBack:
    def __init__(self, groups, rows, width, place_col, sent, recv, sems):
        self.groups, self.piece, self.width = groups, rows // groups, width
        self.halves = (self.piece // 2) % 8 == 0
        self.place_col, self.sent, self.recv, self.sems = place_col, sent, recv, sems
        self.mine = lax.axis_index("dp")

    def moved(self, step):
        peer = (self.mine + step) % self.groups
        return send(self.sent.at[peer], self.recv.at[self.mine], self.sems.at[0, step], self.sems.at[1, step], dp=peer)

    def start(self, packed):
        @pl.loop(0, self.groups)
        def _(step):
            peer = (self.mine + step) % self.groups
            columns = self.place_col[pl.ds(pl.multiple_of(peer * self.piece, 8), self.piece), 0:1]
            values = take_rows(columns, packed[...])

            @pl.when(step > 0)
            def _():
                fold_into(self.sent, (peer,), values, self.halves)
                self.moved(step).start()

            @pl.when(step == 0)
            def _():
                fold_into(self.recv, (self.mine,), values, self.halves)

    def land(self, target):
        @pl.loop(1, self.groups)
        def _(step):
            self.moved(step).wait_recv()

        @pl.loop(0, self.groups)
        def _(peer):
            here = pl.ds(pl.multiple_of(peer * self.piece, 8), self.piece)
            target[here, :] = unfold(self.recv[peer], self.width, self.halves)

        @pl.loop(1, self.groups)
        def _(step):
            self.moved(step).wait_send()

    @staticmethod
    def scratch(groups, rows, width):
        piece = rows // groups
        halves = (piece // 2) % 8 == 0
        slab = (groups, piece // 2, 2 * width) if halves else (groups, piece, width)
        return [pltpu.VMEM(slab, BF)] * 2 + [pltpu.SemaphoreType.DMA((2, groups))]


class RowSum:
    def __init__(self, part, first, second, third, sems):
        self.part, self.first, self.second, self.third, self.sems = part, first, second, third, sems
        self.me, self.sibling, self.across, self.diagonal = place_of()

    def cross(self, b):
        return send(self.part.at[b, self.diagonal], self.first.at[b], self.sems.at[0, b], self.sems.at[1, b],
                    tensor=self.sibling)

    def near(self, b):
        return send(self.part.at[b, self.sibling], self.second.at[b], self.sems.at[2, b], self.sems.at[3, b],
                    tensor=self.sibling)

    def far(self, b):
        return send(self.first.at[b], self.third.at[b], self.sems.at[4, b], self.sems.at[5, b], tensor=self.across)

    def start(self, b):
        self.cross(b).start()
        self.near(b).start()

    def relay(self, b):
        self.cross(b).wait()
        self.first[b] = (self.part[b, self.across].astype(F32) + self.first[b].astype(F32)).astype(BF)
        self.far(b).start()

    def total(self, b):
        self.near(b).wait()
        self.far(b).wait()
        return self.part[b, self.me].astype(F32) + self.second[b].astype(F32) + self.third[b].astype(F32)

    @staticmethod
    def scratch(blocks, rows, columns):
        buffer = pltpu.VMEM((blocks, rows, columns), BF)
        return [pltpu.VMEM((blocks, 4, rows, columns), BF)] + [buffer] * 3 + [pltpu.SemaphoreType.DMA((6, blocks))]


class RowGather:
    def __init__(self, out, sems):
        self.out, self.sems = out, sems
        self.me, self.sibling, self.across, _ = place_of()

    def copy(self, b, kind, whose, peer):
        return send(self.out.at[b, whose], self.out.at[b, whose], self.sems.at[2 * kind, b],
                    self.sems.at[2 * kind + 1, b], tensor=peer)

    def start(self, b):
        self.copy(b, 0, self.me, self.across).start()
        self.copy(b, 1, self.me, self.sibling).start()

    def relay(self, b):
        self.copy(b, 0, self.me, self.across).wait_recv()
        self.copy(b, 2, self.across, self.sibling).start()

    def land(self, b):
        self.copy(b, 1, self.me, self.sibling).wait_recv()
        self.copy(b, 2, self.across, self.sibling).wait_recv()

    def end(self, b):
        self.copy(b, 0, self.me, self.across).wait_send()
        self.copy(b, 1, self.me, self.sibling).wait_send()
        self.copy(b, 2, self.across, self.sibling).wait_send()


CHUNK = 256


def mid_kernel(groups, blocks, grad_scale, context, packed, full_out, vectors, up_w, up_bias, down_w, cot, place_row,
               d_low, d_own, small, gate_grad, value_grad, down_grad, layer_out,
               normed_low, slope_term, gelu_term, gated, d_gate, d_value, unit_full, rs_full, unit_own, rs_own, d_mixed,
               mixed, whole_grad, down_pieces, folded, returned, result,
               part1, first1, second1, third1, sems1, part2, first2, second2, third2, sems2, sems3, sems4, r_sems,
               place_col, vector_rows, acc, recv1, recv2, pair_sems, group_sems, sent, recv, a_sems):
    me, sibling, across, diagonal = place_of()
    rows, width = layer_out.shape
    quarter = BLOCK // 4
    held = down_pieces.shape[1]
    enter([sibling, across, diagonal], groups)
    ffn = RowSum(part1, first1, second1, third1, sems1)
    back_sum = RowSum(part2, first2, second2, third2, sems2)
    mixed_gather = RowGather(mixed, sems3)
    hidden_gather = RowGather(d_low, sems4)
    sums = GroupSum(groups, (down_pieces,), (acc, recv1, recv2), (pair_sems, group_sems))
    giving = GiveBack(groups, rows, width, place_col, sent, recv, a_sems)
    small[...] = jnp.zeros_like(small)
    to_column(place_row, place_col)
    vector_rows[...] = vectors[...].astype(F32)
    out_bias, first_gain, first_shift, down_bias, second_gain, second_shift = (
        vector_rows.at[k : k + 1] for k in range(6)
    )

    def add_small(row, values):
        small[row : row + 1, :] += jnp.sum(values, axis=0, keepdims=True) * grad_scale

    def ahead(b, c):
        here = slice(b * BLOCK + c * CHUNK, b * BLOCK + (c + 1) * CHUNK)
        inner = slice(c * CHUNK, (c + 1) * CHUNK)
        hidden = packed[here, :].astype(F32) + (dot(context[here, :], full_out[...], ((1,), (0,))) + out_bias[...])
        unit, rs = norm_unit(hidden)
        unit_full[inner, :] = unit
        rs_full[inner, :] = rs
        low = (unit * first_gain[...] + first_shift[...]).astype(BF)
        normed_low[here, :] = low
        gate = dot(low, up_w[0], ((1,), (0,))) + up_bias[0:1, :].astype(F32)
        value = dot(low, up_w[1], ((1,), (0,))) + up_bias[1:2, :].astype(F32)
        half_erf = 0.5 * (1.0 + lax.erf(gate * (0.5**0.5)))
        gelu = gate * half_erf
        slope = half_erf + gate * jnp.exp(-0.5 * gate * gate) * ((2.0 * jnp.pi) ** (-0.5))
        slope_term[here, :] = value * slope
        gelu_term[here, :] = gelu
        low_gated = (gelu * value).astype(BF)
        gated[here, :] = low_gated
        out = dot(low_gated, down_w[...], ((1,), (0,))).astype(BF)
        for k in range(CHUNK // quarter):
            part1[b, c * (CHUNK // quarter) + k] = out[k * quarter : (k + 1) * quarter]

    def keep_own(b):
        mine = pl.ds(pl.multiple_of(me * quarter, quarter), quarter)
        unit_own[b] = unit_full[mine, :]
        rs_own[b] = rs_full[mine, :]
        ffn.start(b)

    def turn(b):
        values = unit_own[b] * first_gain[...] + first_shift[...] + (ffn.total(b) + down_bias[...])
        unit, rs = norm_unit(values)
        out = (unit * second_gain[...] + second_shift[...]).astype(BF)
        for u in range(4):
            fold_into(folded, (u, b), out[:, u * width : (u + 1) * width], True)
        cot_rows = cot[b].astype(F32)
        d_rows = norm_back(cot_rows * second_gain[...], unit, rs)
        d_mixed[b] = d_rows
        mixed[b, me] = d_rows.astype(BF)
        mixed_gather.start(b)
        add_small(3, d_rows)
        add_small(4, cot_rows * unit)
        add_small(5, cot_rows)

    def astern(b):
        mixed_gather.land(b)
        for c in range(BLOCK // CHUNK):
            here = slice(b * BLOCK + c * CHUNK, b * BLOCK + (c + 1) * CHUNK)
            count = CHUNK // quarter
            d_rows = jnp.concatenate([mixed[b, c * count + k] for k in range(count)], axis=0)
            d_gated = dot(d_rows, down_w[...], ((1,), (1,)))
            gate_rows = (d_gated * slope_term[here, :]).astype(BF)
            value_rows = (d_gated * gelu_term[here, :]).astype(BF)
            d_gate[here, :] = gate_rows
            d_value[here, :] = value_rows
            add_small(8, gate_rows.astype(F32))
            add_small(9, value_rows.astype(F32))
            out = dot(gate_rows, up_w[0], ((1,), (1,))) + dot(value_rows, up_w[1], ((1,), (1,)))
            out = out.astype(BF)
            for k in range(count):
                part2[b, c * count + k] = out[k * quarter : (k + 1) * quarter]
        back_sum.start(b)

    def finish(b):
        d_normed = d_mixed[b] + back_sum.total(b)
        d_hidden = norm_back(d_normed * first_gain[...], unit_own[b], rs_own[b])
        d_own[b] = d_hidden
        d_low[b, me] = d_hidden.astype(BF)
        hidden_gather.start(b)
        add_small(0, d_hidden)
        add_small(1, d_normed * unit_own[b])
        add_small(2, d_normed)

    def weight_grad(left, right, pieces):
        span = right.shape[1]
        for c in range(span // CHUNK):
            lanes = slice(c * CHUNK, (c + 1) * CHUNK)
            whole_grad[:, lanes] = dot(left, right[:, lanes], ((0,), (0,)))
        for g in range(groups):
            pieces[g] = (whole_grad[g * held : (g + 1) * held, :] * grad_scale).astype(BF)

    last = blocks - 1
    for b in range(blocks):
        ahead(b, 0)
        if b >= 1:
            ffn.relay(b - 1)
        if b >= 2:
            turn(b - 2)
        ahead(b, 1)
        keep_own(b)
        if b >= 2:
            mixed_gather.relay(b - 2)
    ffn.relay(last)
    if blocks > 1:
        turn(last - 1)
    turn(last)
    if blocks > 1:
        mixed_gather.relay(last - 1)
    returns = [
        send(folded.at[peer], returned.at[me], r_sems.at[0, k], r_sems.at[1, k], tensor=peer)
        for k, peer in enumerate((across, diagonal, sibling))
    ]
    returned[me] = folded[me]
    for b in range(blocks):
        if b == last:
            mixed_gather.relay(last)
        astern(b)
        if b == 0:
            for swap in returns:
                swap.start()
        if b >= 1:
            back_sum.relay(b - 1)
    back_sum.relay(last)
    d_mixed_rows = jnp.concatenate([mixed[b, k] for b in range(blocks) for k in range(4)], axis=0)
    weight_grad(d_mixed_rows, gated, down_pieces)
    sums.start(0)
    for swap in returns:
        swap.wait_recv()
    for b in range(blocks):
        for s in range(4):
            start = b * BLOCK + s * quarter
            result[start : start + quarter, :] = unfold(returned[s, b], width, True)
    giving.start(result)
    finish(0)
    weight_grad(normed_low[...], d_gate, gate_grad)
    if blocks > 1:
        finish(1)
    weight_grad(normed_low[...], d_value, value_grad)
    for b in range(2, blocks):
        finish(b)
    for b in range(blocks):
        hidden_gather.relay(b)
    sums.forward((0,))
    for b in range(blocks):
        hidden_gather.land(b)
    down_grad[...] = sums.collect(0).T
    giving.land(layer_out)
    for b in range(blocks):
        mixed_gather.end(b)
        hidden_gather.end(b)
    for swap in returns:
        swap.wait_send()
    sums.end((0,))


def mid(groups, grad_scale, args, number):
    context, up_w = args[0], args[4]
    rows, columns = context.shape
    units = up_w.shape[2]
    width = columns // 4
    held = columns // groups
    blocks = rows // BLOCK
    quarter = BLOCK // 4
    own = (blocks, quarter, columns)
    dma = pltpu.SemaphoreType.DMA
    outs = (
        shape((blocks, 4, quarter, columns), BF),
        shape(own, F32),
        shape((16, columns), F32),
        shape((groups, held, units), BF),
        shape((groups, held, units), BF),
        shape((units, held), F32),
        shape((rows, width), BF),
    )
    folded = pltpu.VMEM((4, blocks, quarter // 2, 2 * width), BF)
    return call(
        functools.partial(mid_kernel, groups, blocks, grad_scale),
        number,
        outs,
        [
            pltpu.VMEM((rows, columns), BF),
            pltpu.VMEM((rows, units), F32),
            pltpu.VMEM((rows, units), F32),
            pltpu.VMEM((rows, units), BF),
            pltpu.VMEM((rows, units), BF),
            pltpu.VMEM((rows, units), BF),
            pltpu.VMEM((BLOCK, columns), F32),
            pltpu.VMEM((BLOCK, 1), F32),
            pltpu.VMEM(own, F32),
            pltpu.VMEM((blocks, quarter, 1), F32),
            pltpu.VMEM(own, F32),
            pltpu.VMEM((blocks, 4, quarter, columns), BF),
            pltpu.VMEM((columns, units), F32),
            pltpu.VMEM((groups, held, units), BF),
            folded,
            folded,
            pltpu.VMEM((rows, width), BF),
        ]
        + RowSum.scratch(blocks, quarter, columns)
        + RowSum.scratch(blocks, quarter, columns)
        + [dma((6, blocks)), dma((6, blocks)), dma((2, 3))]
        + [pltpu.VMEM((rows, 8), jnp.int32), pltpu.VMEM((6, columns), F32)]
        + GroupSum.scratch(1, groups, held, units)
        + GiveBack.scratch(groups, rows, width),
        args,
    )


def back_kernel(groups, blocks, grad_scale, dh_low, dh_own, qkv, lse, seq_row, context, packed_in, qkv_w,
                out_w, grad0, grad1, small, place_row,
                input_grad, up_grad, qkv_grad, out_grad, small_out,
                d_rows, d_part, late_sum, late, cols, one, two, three, packed, ssent, srecv, swide, x_sems, s_sems, w_sems,
                start_col, place_col, weight_here, load_sem,
                acc, recv1, recv2, pair_sems, group_sems, sent, recv, a_sems):
    me, sibling, across, diagonal = place_of()
    mine = lax.axis_index("dp")
    rows, width = input_grad.shape
    heads = width // HEAD_DIM
    held = late.shape[1]
    quarter = BLOCK // 4
    load = pltpu.make_async_copy(qkv_w, weight_here, load_sem)
    load.start()
    enter([sibling, across, diagonal], groups)
    sums = GroupSum(groups, (grad0, grad1, late), (acc, recv1, recv2), (pair_sems, group_sems))
    giving = GiveBack(groups, rows, width, place_col, sent, recv, a_sems)
    sums.start(0)
    sums.start(1)

    def cross(b):
        return send(cols.at[diagonal, b], one.at[b], x_sems.at[0, b], x_sems.at[1, b], tensor=sibling)

    def near(b):
        return send(cols.at[sibling, b], two.at[b], x_sems.at[2, b], x_sems.at[3, b], tensor=sibling)

    def far(b):
        return send(one.at[b], three.at[b], x_sems.at[4, b], x_sems.at[5, b], tensor=across)

    def relay(b):
        cross(b).wait()
        one[b] = (cols[across, b].astype(F32) + one[b].astype(F32)).astype(BF)
        far(b).start()

    late_sum[...] = jnp.zeros_like(late_sum)
    to_column(seq_row, start_col)
    to_column(place_row, place_col)
    load.wait()
    ssent[...] = small[...]

    @pl.loop(0, blocks)
    def _(b):
        here = pl.ds(pl.multiple_of(b * BLOCK, BLOCK), BLOCK)
        dh = dh_low[here, :]
        d_context = dot(dh, out_w[...], ((1,), (1,))).astype(BF)
        late_sum[:, 3 * width :] += dot(dh, context[here, :], ((0,), (0,)))
        same = start_col[here, 0:1] == seq_row[0:1, here]
        distance = key_distance()
        for h in range(heads):
            lanes = slice(h * HEAD_DIM, (h + 1) * HEAD_DIM)
            queries = qkv[0, here, lanes]
            keys = qkv[1, here, lanes]
            values = qkv[2, here, lanes]
            d_rows_out = d_context[:, lanes]
            scored = scores_by_key(keys, queries, slope_of(me * heads + h), distance, same)
            probs = jnp.exp(scored - lse[b, h : h + 1, :])
            d_probs = dot(values, d_rows_out, ((1,), (1,)))
            d_rows[2, :, lanes] = dot(probs.astype(BF), d_rows_out, ((1,), (0,))).astype(BF)
            center = jnp.sum(probs * d_probs, axis=0, keepdims=True)
            d_scores = (probs * (d_probs - center)).astype(BF)
            d_rows[1, :, lanes] = (dot(d_scores, queries, ((1,), (0,))) * (HEAD_DIM**-0.5)).astype(BF)
            turned = dot(keys.T, d_scores, ((1,), (0,))) * (HEAD_DIM**-0.5)
            d_rows[0, :, lanes] = turned.T.astype(BF)
        part = dot(d_rows[0], weight_here[0], ((1,), (1,)))
        part += dot(d_rows[1], weight_here[1], ((1,), (1,)))
        part += dot(d_rows[2], weight_here[2], ((1,), (1,)))
        d_part[...] = part
        d_part[pl.ds(pl.multiple_of(me * quarter, quarter), quarter), :] += dh_own[b]
        for u in range(4):
            fold_into(cols, (u, b), d_part[:, u * width : (u + 1) * width].astype(BF), True)
        cross(b).start()
        near(b).start()
        for c in range(3):
            late_sum[:, c * width : (c + 1) * width] += dot(packed_in[here, :], d_rows[c], ((0,), (0,)))
        last = small.shape[0] - 6
        for k, c in enumerate((0, 2)):
            bias = jnp.sum(d_rows[c].astype(F32), axis=0, keepdims=True) * grad_scale
            ssent[last : last + 1, k * 2 * 128 : k * 2 * 128 + width] += bias
        relay(b)

    for g in range(groups):
        late[g] = (late_sum[g * held : (g + 1) * held, :] * grad_scale).astype(BF)

    sums.start(2)
    swaps = [
        send(ssent, srecv.at[me], s_sems.at[0, k], s_sems.at[1, k], tensor=peer)
        for k, peer in enumerate((sibling, across, diagonal))
    ]
    for swap in swaps:
        swap.start()
    srecv[me] = ssent[...]

    sums.forward((0, 1))
    for b in range(blocks):
        near(b).wait()
        far(b).wait_recv()
        total = cols[me, b].astype(F32) + two[b].astype(F32) + three[b].astype(F32)
        packed[b * BLOCK : (b + 1) * BLOCK, :] = unfold(total.astype(BF), width, True)
    giving.start(packed)

    for swap in swaps:
        swap.wait_recv()
    shared = small.shape[0] // 2
    swide[mine, 0:shared] = srecv[0, 0:shared] + srecv[1, 0:shared] + srecv[2, 0:shared] + srecv[3, 0:shared]
    swide[mine, shared:] = ssent[shared:, :]

    def spread(step):
        peer = (mine + step) % groups
        return send(swide.at[mine], swide.at[mine], w_sems.at[0, step], w_sems.at[1, step], dp=peer)

    @pl.loop(1, groups)
    def _(step):
        spread(step).start()

    sums.forward((2,))
    up_grad[0] = sums.collect(0)
    up_grad[1] = sums.collect(1)
    total = sums.collect(2)
    for c in range(3):
        qkv_grad[c] = total[:, c * width : (c + 1) * width]
    out_grad[...] = total[:, 3 * width :].T

    @pl.loop(1, groups)
    def _(step):
        spread(step).wait_recv()

    small_out[...] = swide[0]

    @pl.loop(1, groups)
    def _(peer):
        small_out[...] += swide[peer]

    giving.land(input_grad)
    for b in range(blocks):
        far(b).wait_send()
    for copy in swaps:
        copy.wait_send()
    sums.end((0, 1, 2))

    @pl.loop(1, groups)
    def _(step):
        spread(step).wait_send()


def back(groups, grad_scale, args, small, number):
    dh_low, qkv, qkv_w, grad = args[0], args[2], args[7], args[9]
    rows, columns = dh_low.shape
    width = qkv.shape[2]
    held, units = grad.shape[1:]
    blocks = rows // BLOCK
    half = (blocks, BLOCK // 2, 2 * width)
    dma = pltpu.SemaphoreType.DMA
    outs = (
        shape((rows, width), BF),
        shape((2, held, units), F32),
        shape((3, held, width), F32),
        shape((width, held), F32),
        shape(small.shape, F32),
    )
    return call(
        functools.partial(back_kernel, groups, blocks, grad_scale),
        number,
        outs,
        [
            pltpu.VMEM((3, BLOCK, width), BF),
            pltpu.VMEM((BLOCK, columns), F32),
            pltpu.VMEM((columns, 4 * width), F32),
            pltpu.VMEM((groups, held, 4 * width), BF),
            pltpu.VMEM((4,) + half, BF),
            pltpu.VMEM(half, BF),
            pltpu.VMEM(half, BF),
            pltpu.VMEM(half, BF),
            pltpu.VMEM((rows, width), BF),
            pltpu.VMEM(small.shape, F32),
            pltpu.VMEM((4,) + small.shape, F32),
            pltpu.VMEM((groups,) + small.shape, F32),
            dma((6, blocks)),
            dma((2, 3)),
            dma((2, groups)),
            pltpu.VMEM((rows, 8), jnp.int32),
            pltpu.VMEM((rows, 8), jnp.int32),
            pltpu.VMEM(qkv_w.shape, BF),
            dma,
        ]
        + GroupSum.scratch(3, groups, held, columns)
        + GiveBack.scratch(groups, rows, width),
        args,
        apart=(7,),
    )


def on_device(
    tokens,
    cotangent,
    seq_start,
    row_place,
    qkv_weight,
    qv_bias,
    out_weight,
    out_bias,
    first_gain,
    first_shift,
    up_weight,
    up_bias,
    down_weight,
    down_bias,
    second_gain,
    second_shift,
):
    row_count, width = tokens.shape
    columns = qkv_weight.shape[1]
    groups = lax.axis_size("dp")
    grad_scale = (row_count * groups) ** (-0.5)
    seq_row = seq_start.reshape(1, row_count)
    packed_in, cot_own, full_out, qkv_rows, log_total, context, wide_context = front(
        groups, (tokens, cotangent, row_place, seq_row, qkv_weight, qv_bias, out_weight), 0
    )
    vectors = jnp.stack([out_bias, first_gain, first_shift, down_bias, second_gain, second_shift])
    d_low, d_own, small, gate_grad, value_grad, down_grad, layer_out = mid(
        groups,
        grad_scale,
        (
            wide_context,
            packed_in,
            full_out.reshape(columns, columns),
            vectors,
            up_weight,
            up_bias,
            down_weight,
            cot_own,
            row_place,
        ),
        1,
    )
    input_grad, up_grad, qkv_grad, out_grad, sums = back(
        groups,
        grad_scale,
        (
            d_low.reshape(row_count, columns),
            d_own,
            qkv_rows,
            log_total,
            seq_row,
            context,
            packed_in,
            qkv_weight,
            out_weight,
            gate_grad,
            value_grad,
            small,
            row_place,
        ),
        small,
        2,
    )
    rows_here = columns // groups
    sums_here = lax.dynamic_slice_in_dim(sums[:6], lax.axis_index("dp") * rows_here, rows_here, 1)
    return (
        layer_out,
        input_grad,
        qkv_grad,
        jnp.stack([sums[10, :width], sums[10, 256 : 256 + width]]),
        out_grad,
        sums_here[0],
        sums_here[1],
        sums_here[2],
        up_grad,
        sums[8:10],
        down_grad,
        sums_here[3],
        sums_here[4],
        sums_here[5],
    )


def solution(mesh):
    return jax.shard_map(
        on_device,
        mesh=mesh,
        in_specs=(
            P("dp", "tensor"),
            P("dp", "tensor"),
            P("dp"),
            P("dp", None),
            P(None, None, "tensor"),
            P(None, "tensor"),
            P("tensor", None),
            P(),
            P(),
            P(),
            P(None, None, "tensor"),
            P(None, "tensor"),
            P("tensor", None),
            P(),
            P(),
            P(),
        ),
        out_specs=(
            P("dp", "tensor"),
            P("dp", "tensor"),
            P(None, "dp", "tensor"),
            P(None, "tensor"),
            P("tensor", "dp"),
            P("dp"),
            P("dp"),
            P("dp"),
            P(None, "dp", "tensor"),
            P(None, "tensor"),
            P("tensor", "dp"),
            P("dp"),
            P("dp"),
            P("dp"),
        ),
        check_vma=False,
    )
```

```python
import functools

import jax
import jax.numpy as jnp
from jax import lax
from jax.experimental import pallas as pl
from jax.experimental.pallas import tpu as pltpu
from jax.sharding import PartitionSpec as P

HEADS = 12
HEAD_DIM = 64
BLOCK = 512
BF = jnp.bfloat16
F32 = jnp.float32
MESH = pl.DeviceIdType.MESH
VMEM_LIMIT = 67043328


def dot(a, b, dims):
    return lax.dot_general(a, b, (dims, ((), ())), preferred_element_type=F32)


def place_of():
    me = lax.axis_index("tensor")
    core = me % 2
    side = me // 2
    sibling = side * 2 + (1 - core)
    across = (1 - side) * 2 + core
    diagonal = (1 - side) * 2 + (1 - core)
    return me, sibling, across, diagonal


def enter(devices, groups):
    barrier = pltpu.get_barrier_semaphore()
    count = len(devices)
    for device in devices:
        pl.semaphore_signal(barrier, inc=1, device_id={"tensor": device}, device_id_type=MESH)
    if groups:
        mine = lax.axis_index("dp")

        @pl.loop(1, groups)
        def _(step):
            pl.semaphore_signal(barrier, inc=1, device_id={"dp": (mine + step) % groups}, device_id_type=MESH)

        count += groups - 1
    pl.semaphore_wait(barrier, count)


def send(source, target, send_sem, recv_sem, **where):
    return pltpu.make_async_remote_copy(
        src_ref=source, dst_ref=target, send_sem=send_sem, recv_sem=recv_sem, device_id=where, device_id_type=MESH
    )


def fold_into(buffer, index, values, halves):
    width = values.shape[1]
    if not halves:
        buffer[index] = values
        return
    half = values.shape[0] // 2
    buffer[index + (slice(None), slice(0, width))] = values[:half]
    buffer[index + (slice(None), slice(width, 2 * width))] = values[half:]


def unfold(values, width, halves):
    if not halves:
        return values
    return jnp.concatenate([values[:, :width], values[:, width:]], axis=0)


def call(kernel, number, outs, scratch, args, apart=()):
    specs = [pl.BlockSpec(memory_space=pl.ANY if k in apart else pltpu.VMEM) for k in range(len(args))]
    return pl.pallas_call(
        kernel,
        out_shape=outs,
        in_specs=specs,
        out_specs=jax.tree.map(lambda _: pl.BlockSpec(memory_space=pltpu.VMEM), outs),
        scratch_shapes=scratch,
        compiler_params=pltpu.CompilerParams(
            collective_id=number, has_side_effects=True, vmem_limit_bytes=VMEM_LIMIT
        ),
    )(*args)


def shape(dims, kind):
    return jax.ShapeDtypeStruct(dims, kind)


def to_column(row, column, where):
    for k in range(row.shape[1] // 128):
        piece = jnp.broadcast_to(row[0:1, k * 128 : (k + 1) * 128], (8, 128))
        column[k * 128 : (k + 1) * 128, where : where + 1] = piece.T[:, 0:1]


def slope_of(index):
    value = jnp.float32(2.0 ** (-8.0 / HEADS))
    for head in range(1, HEADS):
        value = jnp.where(index == head, jnp.float32(2.0 ** (-8.0 * (head + 1) / HEADS)), value)
    return value


def key_distance():
    keys = lax.broadcasted_iota(jnp.int32, (BLOCK, BLOCK), 0)
    asks = lax.broadcasted_iota(jnp.int32, (BLOCK, BLOCK), 1)
    return jnp.abs(keys - asks).astype(F32)


def scores_by_key(keys, queries, slope, distance, same):
    raw = dot(keys, queries, ((1,), (1,))) * (HEAD_DIM**-0.5) - slope * distance
    return jnp.where(same, raw, -1e30)


class HeadGather:
    def __init__(self, wide, sems):
        self.wide, self.sems = wide, sems
        self.me, self.sibling, self.across, _ = place_of()

    def copy(self, b, kind, whose, peer):
        return send(self.wide.at[whose, b], self.wide.at[whose, b], self.sems.at[2 * kind, b],
                    self.sems.at[2 * kind + 1, b], tensor=peer)

    def start(self, b, values):
        fold_into(self.wide, (self.me, b), values, True)
        self.copy(b, 0, self.me, self.across).start()
        self.copy(b, 1, self.me, self.sibling).start()

    def relay(self, b):
        self.copy(b, 0, self.me, self.across).wait_recv()
        self.copy(b, 2, self.across, self.sibling).start()

    def land(self, b, out, width):
        self.copy(b, 1, self.me, self.sibling).wait_recv()
        self.copy(b, 2, self.across, self.sibling).wait_recv()
        for s in range(4):
            out[b * BLOCK : (b + 1) * BLOCK, s * width : (s + 1) * width] = unfold(self.wide[s, b], width, True)

    def end(self, b):
        self.copy(b, 0, self.me, self.across).wait_send()
        self.copy(b, 1, self.me, self.sibling).wait_send()
        self.copy(b, 2, self.across, self.sibling).wait_send()


def front_kernel(groups, blocks, tokens, cot, place_row, seq_row, qkv_w, qv_bias, out_w,
                 packed_out, cot_out, full_out, qkv, lse, context, wide_context,
                 tokens_turned, cot_turned, tokens_here, cot_here, weight_here, start_col, chosen, sent, recv, arrived,
                 wide, wide_heads, local_sems, group_sems, gather_sems, head_sems, out_sems):
    me, sibling, across, diagonal = place_of()
    mine = lax.axis_index("dp")
    rows, width = tokens_here.shape
    heads = width // HEAD_DIM
    piece = rows // groups
    halves = (piece // 2) % 8 == 0
    quarter = BLOCK // 4
    loads = [
        pltpu.make_async_copy(source, target, local_sems.at[k])
        for k, (source, target) in enumerate(((tokens, tokens_turned), (cot, cot_turned), (qkv_w, weight_here)))
    ]
    for load in loads:
        load.start()
    enter([sibling, across, diagonal], groups)

    def moved(kind, step):
        peer = (mine + step) % groups
        return send(sent.at[kind, peer], recv.at[kind, mine], group_sems.at[0, kind, step],
                    group_sems.at[1, kind, step], dp=peer)

    def give(kind, source):
        @pl.loop(1, groups)
        def _(step):
            peer = (mine + step) % groups
            values = source[pl.ds(pl.multiple_of(peer * piece, 8), piece), :]
            fold_into(sent, (kind, peer), values, halves)
            moved(kind, step).start()

        values = source[pl.ds(pl.multiple_of(mine * piece, 8), piece), :]
        fold_into(recv, (kind, mine), values, halves)

    loads[0].wait()
    tokens_here[...] = tokens_turned[...].T
    give(0, tokens_here)
    out_far = send(out_w, full_out.at[me], out_sems.at[0], out_sems.at[1], tensor=across)
    out_near = send(out_w, full_out.at[me], out_sems.at[2], out_sems.at[3], tensor=sibling)
    out_pass = send(full_out.at[across], full_out.at[across], out_sems.at[4], out_sems.at[5], tensor=sibling)
    out_far.start()
    out_near.start()
    loads[1].wait()
    cot_here[...] = cot_turned[...].T
    give(1, cot_here)
    full_out[me] = out_w[...]
    to_column(seq_row, start_col, 0)
    for b in range(blocks):
        ids = lax.broadcasted_iota(jnp.int32, (BLOCK, rows), 0) + b * BLOCK
        chosen[b * BLOCK : (b + 1) * BLOCK, :] = jnp.where(ids == place_row[...], 1.0, 0.0).astype(BF)

    def placed(b):
        return dot(chosen[b * BLOCK : (b + 1) * BLOCK, :], arrived[...], ((1,), (0,))).astype(BF)

    out_far.wait_recv()
    out_pass.start()

    def land(kind):
        @pl.loop(1, groups)
        def _(step):
            moved(kind, step).wait_recv()

        @pl.loop(0, groups)
        def _(peer):
            arrived[pl.ds(pl.multiple_of(peer * piece, 8), piece), :] = unfold(recv[kind, peer], width, halves)

    token_gather = HeadGather(wide, gather_sems)
    head_gather = HeadGather(wide_heads, head_sems)
    land(0)
    for b in range(blocks):
        token_gather.start(b, placed(b))
        if b >= 1:
            token_gather.relay(b - 1)
    loads[2].wait()

    def attend(b):
        here = slice(b * BLOCK, (b + 1) * BLOCK)
        token_gather.land(b, packed_out, width)
        for k in range(3):
            part = dot(packed_out[here, :], weight_here[k], ((1,), (1,)))
            if k != 1:
                part += qv_bias[k // 2 : k // 2 + 1, :].astype(F32)
            qkv[k, here, :] = part.astype(BF)
        same = start_col[here, 0:1] == seq_row[0:1, here]
        distance = key_distance()
        for h in range(heads):
            lanes = slice(h * HEAD_DIM, (h + 1) * HEAD_DIM)
            scored = scores_by_key(qkv[1, here, lanes], qkv[0, here, lanes], slope_of(me * heads + h), distance, same)
            top = jnp.max(scored, axis=0, keepdims=True)
            raised = jnp.exp(scored - top)
            total = jnp.sum(raised, axis=0, keepdims=True)
            lse[b, h : h + 1, :] = top + jnp.log(total)
            probs = (raised * (1.0 / total)).astype(BF)
            turned = dot(qkv[2, here, lanes].T, probs, ((1,), (0,)))
            context[here, lanes] = turned.T.astype(BF)
        head_gather.start(b, context[here, :])

    for b in range(blocks):
        if b == blocks - 1:
            token_gather.relay(b)
        attend(b)
        if b >= 1:
            head_gather.relay(b - 1)
    for b in range(blocks - 1):
        head_gather.land(b, wide_context, width)
    land(1)
    for b in range(blocks):
        cot_block = placed(b)
        for u in range(4):
            fold_into(cot_out, (u, b), cot_block[u * quarter : (u + 1) * quarter], True)
    head_gather.relay(blocks - 1)
    head_gather.land(blocks - 1, wide_context, width)
    for b in range(blocks):
        token_gather.end(b)
        head_gather.end(b)
    out_near.wait()
    out_pass.wait()
    out_far.wait_send()
    for kind in range(2):
        @pl.loop(1, groups)
        def _(step):
            moved(kind, step).wait_send()


def front(groups, args, number):
    tokens, qkv_w, out_w = args[0], args[4], args[6]
    width, rows = tokens.shape
    piece = rows // groups
    blocks = rows // BLOCK
    heads = width // HEAD_DIM
    halves = (piece // 2) % 8 == 0
    slab = (2, groups, piece // 2, 2 * width) if halves else (2, groups, piece, width)
    here = pltpu.VMEM((rows, width), BF)
    wide = pltpu.VMEM((4, blocks, BLOCK // 2, 2 * width), BF)
    turned = pltpu.VMEM((width, rows), BF)
    dma = pltpu.SemaphoreType.DMA
    return call(
        functools.partial(front_kernel, groups, blocks),
        number,
        (
            shape((rows, 4 * width), BF),
            shape((4, blocks, BLOCK // 8, 2 * width), BF),
            shape((4,) + out_w.shape, BF),
            shape((3, rows, width), BF),
            shape((blocks, heads, BLOCK), F32),
            shape((rows, width), BF),
            shape((rows, 4 * width), BF),
        ),
        [
            turned,
            turned,
            here,
            here,
            pltpu.VMEM(qkv_w.shape, BF),
            pltpu.VMEM((rows, 8), jnp.int32),
            pltpu.VMEM((rows, rows), BF),
            pltpu.VMEM(slab, BF),
            pltpu.VMEM(slab, BF),
            here,
            wide,
            wide,
            dma((3,)),
            dma((2, 2, groups)),
            dma((6, blocks)),
            dma((6, blocks)),
            dma((6,)),
        ],
        args,
        apart=(0, 1, 4),
    )


def norm_unit(values):
    center = values - jnp.mean(values, axis=-1, keepdims=True)
    rs = lax.rsqrt(jnp.mean(center * center, axis=-1, keepdims=True) + 1e-05)
    return center * rs, rs


def norm_back(weighted, unit, rs):
    inner = jnp.mean(weighted * unit, axis=-1, keepdims=True)
    return rs * (weighted - jnp.mean(weighted, axis=-1, keepdims=True) - unit * inner)


class GroupSum:
    def __init__(self, groups, grads, buffers, sems):
        self.acc, self.recv1, self.recv2 = buffers
        self.pair_sems, self.group_sems = sems
        self.grads = grads
        self.pairs = groups // 2
        self.mine = lax.axis_index("dp")
        self.parity = self.mine % 2
        self.pair = self.mine + 1 - 2 * self.parity
        self.slot = self.mine // 2

    def paired(self, kind, step):
        m = (self.slot + step) % self.pairs
        return send(self.grads[kind].at[2 * m + 1 - self.parity], self.recv1.at[kind, m],
                    self.pair_sems.at[0, kind, step], self.pair_sems.at[1, kind, step], dp=self.pair)

    def passed(self, kind, step):
        m = (self.slot + step) % self.pairs
        return send(self.acc.at[kind, m], self.recv2.at[kind, self.slot], self.group_sems.at[0, kind, step],
                    self.group_sems.at[1, kind, step], dp=2 * m + self.parity)

    def start(self, kind):
        @pl.loop(1, self.pairs + 1)
        def _(step):
            self.paired(kind, step).start()

    def forward(self, kinds):
        @pl.loop(1, self.pairs)
        def _(step):
            m = (self.slot + step) % self.pairs
            for kind in kinds:
                self.paired(kind, step).wait_recv()
                own = self.grads[kind][2 * m + self.parity].astype(F32)
                self.acc[kind, m] = (own + self.recv1[kind, m].astype(F32)).astype(BF)
                self.passed(kind, step).start()

    def collect(self, kind):
        self.paired(kind, self.pairs).wait_recv()
        total = self.grads[kind][self.mine].astype(F32) + self.recv1[kind, self.slot].astype(F32)
        for step in range(1, self.pairs):
            self.passed(kind, step).wait_recv()
            total += self.recv2[kind, (self.slot + self.pairs - step) % self.pairs].astype(F32)
        return total

    def end(self, kinds):
        for kind in kinds:
            @pl.loop(1, self.pairs + 1)
            def _(step):
                self.paired(kind, step).wait_send()

            @pl.loop(1, self.pairs)
            def _(step):
                self.passed(kind, step).wait_send()

    @staticmethod
    def scratch(kinds, groups, held, span):
        exchange = pltpu.VMEM((kinds, groups // 2, held, span), BF)
        sems = pltpu.SemaphoreType.DMA((2, kinds, groups // 2 + 1))
        return [exchange] * 3 + [sems] * 2


class GiveBack:
    def __init__(self, groups, rows, width, chosen, sent, recv, sems):
        self.groups, self.piece, self.width = groups, rows // groups, width
        self.halves = (self.piece // 2) % 8 == 0
        self.chosen, self.sent, self.recv, self.sems = chosen, sent, recv, sems
        self.mine = lax.axis_index("dp")

    def moved(self, step):
        peer = (self.mine + step) % self.groups
        return send(self.sent.at[peer], self.recv.at[self.mine], self.sems.at[0, step], self.sems.at[1, step], dp=peer)

    def start(self, packed):
        @pl.loop(0, self.groups)
        def _(step):
            peer = (self.mine + step) % self.groups
            rows = self.chosen[pl.ds(pl.multiple_of(peer * self.piece, 8), self.piece), :]
            values = dot(rows, packed[...], ((1,), (0,))).astype(BF)

            @pl.when(step > 0)
            def _():
                fold_into(self.sent, (peer,), values, self.halves)
                self.moved(step).start()

            @pl.when(step == 0)
            def _():
                fold_into(self.recv, (self.mine,), values, self.halves)

    def land(self, target):
        @pl.loop(1, self.groups)
        def _(step):
            self.moved(step).wait_recv()

        @pl.loop(0, self.groups)
        def _(peer):
            here = pl.ds(pl.multiple_of(peer * self.piece, 8), self.piece)
            target[here, :] = unfold(self.recv[peer], self.width, self.halves)

        @pl.loop(1, self.groups)
        def _(step):
            self.moved(step).wait_send()

    @staticmethod
    def scratch(groups, rows, width):
        piece = rows // groups
        halves = (piece // 2) % 8 == 0
        slab = (groups, piece // 2, 2 * width) if halves else (groups, piece, width)
        return [pltpu.VMEM(slab, BF)] * 2 + [pltpu.SemaphoreType.DMA((2, groups))]


class RowSum:
    def __init__(self, part, first, second, third, sems):
        self.part, self.first, self.second, self.third, self.sems = part, first, second, third, sems
        self.me, self.sibling, self.across, self.diagonal = place_of()

    def cross(self, b):
        return send(self.part.at[b, self.diagonal], self.first.at[b], self.sems.at[0, b], self.sems.at[1, b],
                    tensor=self.sibling)

    def near(self, b):
        return send(self.part.at[b, self.sibling], self.second.at[b], self.sems.at[2, b], self.sems.at[3, b],
                    tensor=self.sibling)

    def far(self, b):
        return send(self.first.at[b], self.third.at[b], self.sems.at[4, b], self.sems.at[5, b], tensor=self.across)

    def start(self, b):
        self.cross(b).start()
        self.near(b).start()

    def relay(self, b):
        self.cross(b).wait()
        self.first[b] = (self.part[b, self.across].astype(F32) + self.first[b].astype(F32)).astype(BF)
        self.far(b).start()

    def total(self, b):
        self.near(b).wait()
        self.far(b).wait()
        return self.part[b, self.me].astype(F32) + self.second[b].astype(F32) + self.third[b].astype(F32)

    @staticmethod
    def scratch(blocks, rows, columns):
        buffer = pltpu.VMEM((blocks, rows, columns), BF)
        return [pltpu.VMEM((blocks, 4, rows, columns), BF)] + [buffer] * 3 + [pltpu.SemaphoreType.DMA((6, blocks))]


class RowGather:
    def __init__(self, out, sems):
        self.out, self.sems = out, sems
        self.me, self.sibling, self.across, _ = place_of()

    def copy(self, b, kind, whose, peer):
        return send(self.out.at[b, whose], self.out.at[b, whose], self.sems.at[2 * kind, b],
                    self.sems.at[2 * kind + 1, b], tensor=peer)

    def start(self, b):
        self.copy(b, 0, self.me, self.across).start()
        self.copy(b, 1, self.me, self.sibling).start()

    def relay(self, b):
        self.copy(b, 0, self.me, self.across).wait_recv()
        self.copy(b, 2, self.across, self.sibling).start()

    def land(self, b):
        self.copy(b, 1, self.me, self.sibling).wait_recv()
        self.copy(b, 2, self.across, self.sibling).wait_recv()

    def end(self, b):
        self.copy(b, 0, self.me, self.across).wait_send()
        self.copy(b, 1, self.me, self.sibling).wait_send()
        self.copy(b, 2, self.across, self.sibling).wait_send()


CHUNK = 256


def mid_kernel(groups, blocks, grad_scale, context, packed, full_out, vectors, up_w, up_bias, down_w, cot_folded,
               d_low, d_own, small, value_grad, down_grad, gate_sum, folded,
               normed_low, slope_term, gelu_term, gated, d_gate, d_value, unit_full, rs_full, unit_own, rs_own, d_mixed,
               mixed, whole_grad, down_pieces, gate_pieces, cot_recv,
               part1, first1, second1, third1, sems1, part2, first2, second2, third2, sems2, sems3, sems4, c_sems,
               vector_rows, acc, recv1, recv2, pair_sems, group_sems):
    me, sibling, across, diagonal = place_of()
    columns = packed.shape[1]
    width = columns // 4
    quarter = BLOCK // 4
    held = down_pieces.shape[1]
    enter([sibling, across, diagonal], groups)
    swaps = [
        send(cot_folded.at[peer], cot_recv.at[me], c_sems.at[0, k], c_sems.at[1, k], tensor=peer)
        for k, peer in enumerate((across, diagonal, sibling))
    ]
    for swap in swaps:
        swap.start()
    cot_recv[me] = cot_folded[me]
    ffn = RowSum(part1, first1, second1, third1, sems1)
    back_sum = RowSum(part2, first2, second2, third2, sems2)
    mixed_gather = RowGather(mixed, sems3)
    hidden_gather = RowGather(d_low, sems4)
    sums = GroupSum(groups, (down_pieces, gate_pieces), (acc, recv1, recv2), (pair_sems, group_sems))
    small[...] = jnp.zeros_like(small)
    vector_rows[...] = vectors[...].astype(F32)
    out_bias, first_gain, first_shift, down_bias, second_gain, second_shift = (
        vector_rows.at[k : k + 1] for k in range(6)
    )

    def add_small(row, values):
        small[row : row + 1, :] += jnp.sum(values, axis=0, keepdims=True) * grad_scale

    def ahead(b, c):
        here = slice(b * BLOCK + c * CHUNK, b * BLOCK + (c + 1) * CHUNK)
        inner = slice(c * CHUNK, (c + 1) * CHUNK)
        hidden = packed[here, :].astype(F32) + (dot(context[here, :], full_out[...], ((1,), (0,))) + out_bias[...])
        unit, rs = norm_unit(hidden)
        unit_full[inner, :] = unit
        rs_full[inner, :] = rs
        low = (unit * first_gain[...] + first_shift[...]).astype(BF)
        normed_low[here, :] = low
        gate = dot(low, up_w[0], ((1,), (0,))) + up_bias[0:1, :].astype(F32)
        value = dot(low, up_w[1], ((1,), (0,))) + up_bias[1:2, :].astype(F32)
        half_erf = 0.5 * (1.0 + lax.erf(gate * (0.5**0.5)))
        gelu = gate * half_erf
        slope = half_erf + gate * jnp.exp(-0.5 * gate * gate) * ((2.0 * jnp.pi) ** (-0.5))
        slope_term[here, :] = value * slope
        gelu_term[here, :] = gelu
        low_gated = (gelu * value).astype(BF)
        gated[here, :] = low_gated
        out = dot(low_gated, down_w[...], ((1,), (0,))).astype(BF)
        for k in range(CHUNK // quarter):
            part1[b, c * (CHUNK // quarter) + k] = out[k * quarter : (k + 1) * quarter]

    def keep_own(b):
        mine = pl.ds(pl.multiple_of(me * quarter, quarter), quarter)
        unit_own[b] = unit_full[mine, :]
        rs_own[b] = rs_full[mine, :]
        ffn.start(b)

    def turn(b):
        if b == 0:
            for swap in swaps:
                swap.wait_recv()
        values = unit_own[b] * first_gain[...] + first_shift[...] + (ffn.total(b) + down_bias[...])
        unit, rs = norm_unit(values)
        out = (unit * second_gain[...] + second_shift[...]).astype(BF)
        for u in range(4):
            fold_into(folded, (u, b), out[:, u * width : (u + 1) * width], True)
        cot_rows = jnp.concatenate([unfold(cot_recv[s, b], width, True) for s in range(4)], axis=1).astype(F32)
        d_rows = norm_back(cot_rows * second_gain[...], unit, rs)
        d_mixed[b] = d_rows
        mixed[b, me] = d_rows.astype(BF)
        mixed_gather.start(b)
        add_small(3, d_rows)
        add_small(4, cot_rows * unit)
        add_small(5, cot_rows)

    def astern(b):
        mixed_gather.land(b)
        for c in range(BLOCK // CHUNK):
            here = slice(b * BLOCK + c * CHUNK, b * BLOCK + (c + 1) * CHUNK)
            count = CHUNK // quarter
            d_rows = jnp.concatenate([mixed[b, c * count + k] for k in range(count)], axis=0)
            d_gated = dot(d_rows, down_w[...], ((1,), (1,)))
            gate_rows = (d_gated * slope_term[here, :]).astype(BF)
            value_rows = (d_gated * gelu_term[here, :]).astype(BF)
            d_gate[here, :] = gate_rows
            d_value[here, :] = value_rows
            add_small(8, gate_rows.astype(F32))
            add_small(9, value_rows.astype(F32))
            out = dot(gate_rows, up_w[0], ((1,), (1,))) + dot(value_rows, up_w[1], ((1,), (1,)))
            out = out.astype(BF)
            for k in range(count):
                part2[b, c * count + k] = out[k * quarter : (k + 1) * quarter]
        back_sum.start(b)

    def finish(b):
        d_normed = d_mixed[b] + back_sum.total(b)
        d_hidden = norm_back(d_normed * first_gain[...], unit_own[b], rs_own[b])
        d_own[b] = d_hidden
        d_low[b, me] = d_hidden.astype(BF)
        hidden_gather.start(b)
        add_small(0, d_hidden)
        add_small(1, d_normed * unit_own[b])
        add_small(2, d_normed)

    def weight_grad(left, right, pieces):
        span = right.shape[1]
        for c in range(span // CHUNK):
            lanes = slice(c * CHUNK, (c + 1) * CHUNK)
            whole_grad[:, lanes] = dot(left, right[:, lanes], ((0,), (0,)))
        for g in range(groups):
            pieces[g] = (whole_grad[g * held : (g + 1) * held, :] * grad_scale).astype(BF)

    last = blocks - 1
    for b in range(blocks):
        ahead(b, 0)
        if b >= 1:
            ffn.relay(b - 1)
        if b >= 2:
            turn(b - 2)
        ahead(b, 1)
        keep_own(b)
        if b >= 2:
            mixed_gather.relay(b - 2)
    ffn.relay(last)
    if blocks > 1:
        turn(last - 1)
    turn(last)
    if blocks > 1:
        mixed_gather.relay(last - 1)
    for b in range(blocks):
        if b == last:
            mixed_gather.relay(last)
        astern(b)
        if b >= 1:
            back_sum.relay(b - 1)
    back_sum.relay(last)
    d_mixed_rows = jnp.concatenate([mixed[b, k] for b in range(blocks) for k in range(4)], axis=0)
    weight_grad(d_mixed_rows, gated, down_pieces)
    sums.start(0)
    finish(0)
    weight_grad(normed_low[...], d_gate, gate_pieces)
    sums.start(1)
    if blocks > 1:
        finish(1)
    weight_grad(normed_low[...], d_value, value_grad)
    for b in range(2, blocks):
        finish(b)
    for b in range(blocks):
        hidden_gather.relay(b)
    sums.forward((0,))
    sums.forward((1,))
    for b in range(blocks):
        hidden_gather.land(b)
    down_grad[...] = sums.collect(0)
    gate_sum[...] = sums.collect(1)
    for b in range(blocks):
        mixed_gather.end(b)
        hidden_gather.end(b)
    for swap in swaps:
        swap.wait_send()
    sums.end((0, 1))


def mid(groups, grad_scale, args, number):
    context, up_w, cot_folded = args[0], args[4], args[7]
    rows, columns = context.shape
    units = up_w.shape[2]
    held = columns // groups
    blocks = rows // BLOCK
    quarter = BLOCK // 4
    own = (blocks, quarter, columns)
    dma = pltpu.SemaphoreType.DMA
    outs = (
        shape((blocks, 4, quarter, columns), BF),
        shape(own, F32),
        shape((16, columns), F32),
        shape((groups, held, units), BF),
        shape((held, units), F32),
        shape((held, units), F32),
        shape(cot_folded.shape, BF),
    )
    return call(
        functools.partial(mid_kernel, groups, blocks, grad_scale),
        number,
        outs,
        [
            pltpu.VMEM((rows, columns), BF),
            pltpu.VMEM((rows, units), F32),
            pltpu.VMEM((rows, units), F32),
            pltpu.VMEM((rows, units), BF),
            pltpu.VMEM((rows, units), BF),
            pltpu.VMEM((rows, units), BF),
            pltpu.VMEM((BLOCK, columns), F32),
            pltpu.VMEM((BLOCK, 1), F32),
            pltpu.VMEM(own, F32),
            pltpu.VMEM((blocks, quarter, 1), F32),
            pltpu.VMEM(own, F32),
            pltpu.VMEM((blocks, 4, quarter, columns), BF),
            pltpu.VMEM((columns, units), F32),
            pltpu.VMEM((groups, held, units), BF),
            pltpu.VMEM((groups, held, units), BF),
            pltpu.VMEM(cot_folded.shape, BF),
        ]
        + RowSum.scratch(blocks, quarter, columns)
        + RowSum.scratch(blocks, quarter, columns)
        + [dma((6, blocks)), dma((6, blocks)), dma((2, 3)), pltpu.VMEM((6, columns), F32)]
        + GroupSum.scratch(2, groups, held, units),
        args,
    )


def back_kernel(groups, blocks, grad_scale, dh_low, dh_own, qkv, lse, seq_row, context, packed_in, qkv_w,
                out_w, value_grad, gate_sum, folded, small, place_row,
                layer_out, input_grad, up_grad, qkv_grad, out_grad, small_out,
                d_rows, d_part, late_sum, late, cols, one, two, three, packed, ssent, srecv, swide, x_sems, s_sems, w_sems,
                start_col, chosen, weight_here, returned, landed, load_sem, r_sems,
                acc, recv1, recv2, pair_sems, group_sems, acc2, recv3, recv4, pair_sems2, group_sems2,
                sent, recv, a_sems, sent2, recv5, a_sems2):
    me, sibling, across, diagonal = place_of()
    mine = lax.axis_index("dp")
    width, rows = input_grad.shape
    heads = width // HEAD_DIM
    held = late.shape[1]
    quarter = BLOCK // 4
    load = pltpu.make_async_copy(qkv_w, weight_here, load_sem)
    load.start()
    enter([sibling, across, diagonal], groups)
    sums = GroupSum(groups, (value_grad,), (acc, recv1, recv2), (pair_sems, group_sems))
    late_sums = GroupSum(groups, (late,), (acc2, recv3, recv4), (pair_sems2, group_sems2))
    giving = GiveBack(groups, rows, width, chosen, sent, recv, a_sems)
    giving_result = GiveBack(groups, rows, width, chosen, sent2, recv5, a_sems2)
    sums.start(0)
    returns = [
        send(folded.at[peer], returned.at[me], r_sems.at[0, k], r_sems.at[1, k], tensor=peer)
        for k, peer in enumerate((across, diagonal, sibling))
    ]
    for swap in returns:
        swap.start()
    returned[me] = folded[me]
    up_grad[0] = gate_sum[...]

    def choose(step):
        half = rows // 2
        ids = lax.broadcasted_iota(jnp.int32, (half, rows), 1)
        here = slice(step * half, (step + 1) * half)
        chosen[here, :] = jnp.where(ids == start_col[here, 1:2], 1.0, 0.0).astype(BF)

    def cross(b):
        return send(cols.at[diagonal, b], one.at[b], x_sems.at[0, b], x_sems.at[1, b], tensor=sibling)

    def near(b):
        return send(cols.at[sibling, b], two.at[b], x_sems.at[2, b], x_sems.at[3, b], tensor=sibling)

    def far(b):
        return send(one.at[b], three.at[b], x_sems.at[4, b], x_sems.at[5, b], tensor=across)

    def relay(b):
        cross(b).wait()
        one[b] = (cols[across, b].astype(F32) + one[b].astype(F32)).astype(BF)
        far(b).start()

    to_column(seq_row, start_col, 0)
    to_column(place_row, start_col, 1)
    choose(0)
    choose(1)
    late_sum[:, 3 * width :] = dot(dh_low[...], context[...], ((0,), (0,)))
    load.wait()
    ssent[...] = small[...]

    @pl.loop(0, blocks)
    def _(b):
        here = pl.ds(pl.multiple_of(b * BLOCK, BLOCK), BLOCK)
        dh = dh_low[here, :]
        d_context = dot(dh, out_w[...], ((1,), (1,))).astype(BF)
        same = start_col[here, 0:1] == seq_row[0:1, here]
        distance = key_distance()
        for h in range(heads):
            lanes = slice(h * HEAD_DIM, (h + 1) * HEAD_DIM)
            queries = qkv[0, here, lanes]
            keys = qkv[1, here, lanes]
            values = qkv[2, here, lanes]
            d_rows_out = d_context[:, lanes]
            scored = scores_by_key(keys, queries, slope_of(me * heads + h), distance, same)
            probs = jnp.exp(scored - lse[b, h : h + 1, :])
            d_probs = dot(values, d_rows_out, ((1,), (1,)))
            d_rows[2, here, lanes] = dot(probs.astype(BF), d_rows_out, ((1,), (0,))).astype(BF)
            center = jnp.sum(probs * d_probs, axis=0, keepdims=True)
            d_scores = (probs * (d_probs - center)).astype(BF)
            d_rows[1, here, lanes] = (dot(d_scores, queries, ((1,), (0,))) * (HEAD_DIM**-0.5)).astype(BF)
            turned = dot(keys.T, d_scores, ((1,), (0,))) * (HEAD_DIM**-0.5)
            d_rows[0, here, lanes] = turned.T.astype(BF)
        part = dot(d_rows[0, here, :], weight_here[0], ((1,), (0,)))
        part += dot(d_rows[1, here, :], weight_here[1], ((1,), (0,)))
        part += dot(d_rows[2, here, :], weight_here[2], ((1,), (0,)))
        d_part[...] = part
        d_part[pl.ds(pl.multiple_of(me * quarter, quarter), quarter), :] += dh_own[b]
        for u in range(4):
            fold_into(cols, (u, b), d_part[:, u * width : (u + 1) * width].astype(BF), True)
        cross(b).start()
        near(b).start()
        last = small.shape[0] - 6
        for k, c in enumerate((0, 2)):
            bias = jnp.sum(d_rows[c, here, :].astype(F32), axis=0, keepdims=True) * grad_scale
            ssent[last : last + 1, k * 2 * 128 : k * 2 * 128 + width] += bias
        relay(b)

        @pl.when(b == 0)
        def _():
            for swap in returns:
                swap.wait_recv()
            for q in range(blocks):
                for s in range(4):
                    start = q * BLOCK + s * quarter
                    packed[start : start + quarter, :] = unfold(returned[s, q], width, True)
            giving_result.start(packed)

        @pl.when(b == 1)
        def _():
            sums.forward((0,))

    for c in range(3):
        late_sum[:, c * width : (c + 1) * width] = dot(packed_in[...], d_rows[c], ((0,), (0,)))
    for g in range(groups):
        late[g] = (late_sum[g * held : (g + 1) * held, :] * grad_scale).astype(BF)

    late_sums.start(0)
    swaps = [
        send(ssent, srecv.at[me], s_sems.at[0, k], s_sems.at[1, k], tensor=peer)
        for k, peer in enumerate((sibling, across, diagonal))
    ]
    for swap in swaps:
        swap.start()
    srecv[me] = ssent[...]

    for b in range(blocks):
        near(b).wait()
        far(b).wait_recv()
        total = cols[me, b].astype(F32) + two[b].astype(F32) + three[b].astype(F32)
        packed[b * BLOCK : (b + 1) * BLOCK, :] = unfold(total.astype(BF), width, True)
    giving.start(packed)

    for swap in swaps:
        swap.wait_recv()
    shared = small.shape[0] // 2
    swide[mine, 0:shared] = srecv[0, 0:shared] + srecv[1, 0:shared] + srecv[2, 0:shared] + srecv[3, 0:shared]
    swide[mine, shared:] = ssent[shared:, :]

    def spread(step):
        peer = (mine + step) % groups
        return send(swide.at[mine], swide.at[mine], w_sems.at[0, step], w_sems.at[1, step], dp=peer)

    @pl.loop(1, groups)
    def _(step):
        spread(step).start()

    late_sums.forward((0,))
    up_grad[1] = sums.collect(0)
    giving_result.land(landed)
    layer_out[...] = landed[...].T

    @pl.loop(1, groups)
    def _(step):
        spread(step).wait_recv()

    small_out[...] = swide[0]

    @pl.loop(1, groups)
    def _(peer):
        small_out[...] += swide[peer]

    total = late_sums.collect(0)
    for c in range(3):
        qkv_grad[c] = total[:, c * width : (c + 1) * width]
    out_grad[...] = total[:, 3 * width :].T
    giving.land(landed)
    input_grad[...] = landed[...].T
    for b in range(blocks):
        far(b).wait_send()
    for copy in swaps + returns:
        copy.wait_send()
    sums.end((0,))
    late_sums.end((0,))

    @pl.loop(1, groups)
    def _(step):
        spread(step).wait_send()


def back(groups, grad_scale, args, small, number):
    dh_low, qkv, qkv_w, grad, folded = args[0], args[2], args[7], args[9], args[11]
    rows, columns = dh_low.shape
    width = qkv.shape[2]
    held, units = grad.shape[1:]
    blocks = rows // BLOCK
    half = (blocks, BLOCK // 2, 2 * width)
    dma = pltpu.SemaphoreType.DMA
    outs = (
        shape((width, rows), BF),
        shape((width, rows), BF),
        shape((2, held, units), F32),
        shape((3, held, width), F32),
        shape((width, held), F32),
        shape(small.shape, F32),
    )
    return call(
        functools.partial(back_kernel, groups, blocks, grad_scale),
        number,
        outs,
        [
            pltpu.VMEM((3, rows, width), BF),
            pltpu.VMEM((BLOCK, columns), F32),
            pltpu.VMEM((columns, 4 * width), F32),
            pltpu.VMEM((groups, held, 4 * width), BF),
            pltpu.VMEM((4,) + half, BF),
            pltpu.VMEM(half, BF),
            pltpu.VMEM(half, BF),
            pltpu.VMEM(half, BF),
            pltpu.VMEM((rows, width), BF),
            pltpu.VMEM(small.shape, F32),
            pltpu.VMEM((4,) + small.shape, F32),
            pltpu.VMEM((groups,) + small.shape, F32),
            dma((6, blocks)),
            dma((2, 3)),
            dma((2, groups)),
            pltpu.VMEM((rows, 8), jnp.int32),
            pltpu.VMEM((rows, rows), BF),
            pltpu.VMEM(qkv_w.shape, BF),
            pltpu.VMEM(folded.shape, BF),
            pltpu.VMEM((rows, width), BF),
            dma,
            dma((2, 3)),
        ]
        + GroupSum.scratch(1, groups, held, units)
        + GroupSum.scratch(1, groups, held, 4 * width)
        + GiveBack.scratch(groups, rows, width)
        + GiveBack.scratch(groups, rows, width),
        args,
        apart=(7,),
    )


def on_device(
    tokens,
    cotangent,
    seq_start,
    row_place,
    qkv_weight,
    qv_bias,
    out_weight,
    out_bias,
    first_gain,
    first_shift,
    up_weight,
    up_bias,
    down_weight,
    down_bias,
    second_gain,
    second_shift,
):
    row_count, width = tokens.shape
    columns = qkv_weight.shape[1]
    groups = lax.axis_size("dp")
    grad_scale = (row_count * groups) ** (-0.5)
    seq_row = seq_start.reshape(1, row_count)
    weight_turned = qkv_weight.transpose(0, 2, 1)
    packed_in, cot_folded, full_out, qkv_rows, log_total, context, wide_context = front(
        groups, (tokens.T, cotangent.T, row_place, seq_row, weight_turned, qv_bias, out_weight), 0
    )
    vectors = jnp.stack([out_bias, first_gain, first_shift, down_bias, second_gain, second_shift])
    d_low, d_own, small, value_grad, down_grad, gate_sum, folded = mid(
        groups,
        grad_scale,
        (
            wide_context,
            packed_in,
            full_out.reshape(columns, columns),
            vectors,
            up_weight,
            up_bias,
            down_weight,
            cot_folded,
        ),
        1,
    )
    layer_out, input_grad, up_grad, qkv_grad, out_grad, sums = back(
        groups,
        grad_scale,
        (
            d_low.reshape(row_count, columns),
            d_own,
            qkv_rows,
            log_total,
            seq_row,
            context,
            packed_in,
            weight_turned,
            out_weight,
            value_grad,
            gate_sum,
            folded,
            small,
            row_place,
        ),
        small,
        2,
    )
    rows_here = columns // groups
    sums_here = lax.dynamic_slice_in_dim(sums[:6], lax.axis_index("dp") * rows_here, rows_here, 1)
    return (
        layer_out.T,
        input_grad.T,
        qkv_grad,
        jnp.stack([sums[10, :width], sums[10, 256 : 256 + width]]),
        out_grad,
        sums_here[0],
        sums_here[1],
        sums_here[2],
        up_grad,
        sums[8:10],
        down_grad.T,
        sums_here[3],
        sums_here[4],
        sums_here[5],
    )


def solution(mesh):
    return jax.shard_map(
        on_device,
        mesh=mesh,
        in_specs=(
            P("dp", "tensor"),
            P("dp", "tensor"),
            P("dp"),
            P("dp", None),
            P(None, None, "tensor"),
            P(None, "tensor"),
            P("tensor", None),
            P(),
            P(),
            P(),
            P(None, None, "tensor"),
            P(None, "tensor"),
            P("tensor", None),
            P(),
            P(),
            P(),
        ),
        out_specs=(
            P("dp", "tensor"),
            P("dp", "tensor"),
            P(None, "dp", "tensor"),
            P(None, "tensor"),
            P("tensor", "dp"),
            P("dp"),
            P("dp"),
            P("dp"),
            P(None, "dp", "tensor"),
            P(None, "tensor"),
            P("tensor", "dp"),
            P("dp"),
            P("dp"),
            P("dp"),
        ),
        check_vma=False,
    )
```

```python
import functools

import jax
import jax.numpy as jnp
from jax import lax
from jax.experimental import pallas as pl
from jax.experimental.pallas import tpu as pltpu
from jax.sharding import PartitionSpec as P

HEADS = 12
HEAD_DIM = 64
BLOCK = 512
BF = jnp.bfloat16
F32 = jnp.float32
MESH = pl.DeviceIdType.MESH
VMEM_LIMIT = 67043328


def dot(a, b, dims):
    return lax.dot_general(a, b, (dims, ((), ())), preferred_element_type=F32)


def place_of():
    me = lax.axis_index("tensor")
    core = me % 2
    side = me // 2
    sibling = side * 2 + (1 - core)
    across = (1 - side) * 2 + core
    diagonal = (1 - side) * 2 + (1 - core)
    return me, sibling, across, diagonal


def enter(devices, groups):
    barrier = pltpu.get_barrier_semaphore()
    count = len(devices)
    for device in devices:
        pl.semaphore_signal(barrier, inc=1, device_id={"tensor": device}, device_id_type=MESH)
    if groups:
        mine = lax.axis_index("dp")

        @pl.loop(1, groups)
        def _(step):
            pl.semaphore_signal(barrier, inc=1, device_id={"dp": (mine + step) % groups}, device_id_type=MESH)

        count += groups - 1
    pl.semaphore_wait(barrier, count)


def send(source, target, send_sem, recv_sem, **where):
    return pltpu.make_async_remote_copy(
        src_ref=source, dst_ref=target, send_sem=send_sem, recv_sem=recv_sem, device_id=where, device_id_type=MESH
    )


def fold_into(buffer, index, values, halves):
    width = values.shape[1]
    if not halves:
        buffer[index] = values
        return
    half = values.shape[0] // 2
    buffer[index + (slice(None), slice(0, width))] = values[:half]
    buffer[index + (slice(None), slice(width, 2 * width))] = values[half:]


def unfold(values, width, halves):
    if not halves:
        return values
    return jnp.concatenate([values[:, :width], values[:, width:]], axis=0)


def call(kernel, number, outs, scratch, args, apart=(), apart_outs=()):
    specs = [pl.BlockSpec(memory_space=pl.ANY if k in apart else pltpu.VMEM) for k in range(len(args))]
    return pl.pallas_call(
        kernel,
        out_shape=outs,
        in_specs=specs,
        out_specs=tuple(
            pl.BlockSpec(memory_space=pl.ANY if k in apart_outs else pltpu.VMEM) for k in range(len(outs))
        ),
        scratch_shapes=scratch,
        compiler_params=pltpu.CompilerParams(
            collective_id=number, has_side_effects=True, vmem_limit_bytes=VMEM_LIMIT
        ),
    )(*args)


def shape(dims, kind):
    return jax.ShapeDtypeStruct(dims, kind)


def to_column(row, column, where):
    for k in range(row.shape[1] // 128):
        piece = jnp.broadcast_to(row[0:1, k * 128 : (k + 1) * 128], (8, 128))
        column[k * 128 : (k + 1) * 128, where : where + 1] = piece.T[:, 0:1]


def slope_of(index):
    value = jnp.float32(2.0 ** (-8.0 / HEADS))
    for head in range(1, HEADS):
        value = jnp.where(index == head, jnp.float32(2.0 ** (-8.0 * (head + 1) / HEADS)), value)
    return value


def key_distance():
    keys = lax.broadcasted_iota(jnp.int32, (BLOCK, BLOCK), 0)
    asks = lax.broadcasted_iota(jnp.int32, (BLOCK, BLOCK), 1)
    return jnp.abs(keys - asks).astype(F32)


def scores_by_key(keys, queries, slope, distance, same):
    raw = dot(keys, queries, ((1,), (1,))) * (HEAD_DIM**-0.5) - slope * distance
    return jnp.where(same, raw, -1e30)


class HeadGather:
    def __init__(self, wide, sems):
        self.wide, self.sems = wide, sems
        self.me, self.sibling, self.across, _ = place_of()

    def copy(self, b, kind, whose, peer):
        return send(self.wide.at[whose, b], self.wide.at[whose, b], self.sems.at[2 * kind, b],
                    self.sems.at[2 * kind + 1, b], tensor=peer)

    def start(self, b, values):
        fold_into(self.wide, (self.me, b), values, True)
        self.copy(b, 0, self.me, self.across).start()
        self.copy(b, 1, self.me, self.sibling).start()

    def relay(self, b):
        self.copy(b, 0, self.me, self.across).wait_recv()
        self.copy(b, 2, self.across, self.sibling).start()

    def land(self, b, out, width):
        self.copy(b, 1, self.me, self.sibling).wait_recv()
        self.copy(b, 2, self.across, self.sibling).wait_recv()
        for s in range(4):
            out[b * BLOCK : (b + 1) * BLOCK, s * width : (s + 1) * width] = unfold(self.wide[s, b], width, True)

    def end(self, b):
        self.copy(b, 0, self.me, self.across).wait_send()
        self.copy(b, 1, self.me, self.sibling).wait_send()
        self.copy(b, 2, self.across, self.sibling).wait_send()


def front_kernel(groups, blocks, tokens, cot, place_row, seq_row, qkv_w, qv_bias, out_w,
                 packed_out, cot_out, full_out, qkv, lse, context, wide_context, taking,
                 tokens_turned, cot_turned, tokens_here, cot_here, weight_here, start_col, chosen, taken, sent, recv, arrived,
                 wide, wide_heads, local_sems, group_sems, gather_sems, head_sems, out_sems):
    me, sibling, across, diagonal = place_of()
    mine = lax.axis_index("dp")
    rows, width = tokens_here.shape
    heads = width // HEAD_DIM
    piece = rows // groups
    halves = (piece // 2) % 8 == 0
    quarter = BLOCK // 4
    loads = [
        pltpu.make_async_copy(source, target, local_sems.at[k])
        for k, (source, target) in enumerate(((tokens, tokens_turned), (cot, cot_turned), (qkv_w, weight_here)))
    ]
    for load in loads:
        load.start()
    enter([sibling, across, diagonal], groups)

    def moved(kind, step):
        peer = (mine + step) % groups
        return send(sent.at[kind, peer], recv.at[kind, mine], group_sems.at[0, kind, step],
                    group_sems.at[1, kind, step], dp=peer)

    def give(kind, source):
        @pl.loop(1, groups)
        def _(step):
            peer = (mine + step) % groups
            values = source[pl.ds(pl.multiple_of(peer * piece, 8), piece), :]
            fold_into(sent, (kind, peer), values, halves)
            moved(kind, step).start()

        values = source[pl.ds(pl.multiple_of(mine * piece, 8), piece), :]
        fold_into(recv, (kind, mine), values, halves)

    loads[0].wait()
    tokens_here[...] = tokens_turned[...].T
    give(0, tokens_here)
    out_far = send(out_w, full_out.at[me], out_sems.at[0], out_sems.at[1], tensor=across)
    out_near = send(out_w, full_out.at[me], out_sems.at[2], out_sems.at[3], tensor=sibling)
    out_pass = send(full_out.at[across], full_out.at[across], out_sems.at[4], out_sems.at[5], tensor=sibling)
    out_far.start()
    out_near.start()
    loads[1].wait()
    cot_here[...] = cot_turned[...].T
    give(1, cot_here)
    full_out[me] = out_w[...]
    to_column(seq_row, start_col, 0)
    for b in range(blocks):
        ids = lax.broadcasted_iota(jnp.int32, (BLOCK, rows), 0) + b * BLOCK
        chosen[b * BLOCK : (b + 1) * BLOCK, :] = jnp.where(ids == place_row[...], 1.0, 0.0).astype(BF)

    to_column(place_row, start_col, 1)
    for b in range(blocks):
        ids = lax.broadcasted_iota(jnp.int32, (BLOCK, rows), 1)
        here = slice(b * BLOCK, (b + 1) * BLOCK)
        taken[here, :] = jnp.where(ids == start_col[here, 1:2], 1.0, 0.0).astype(BF)
    store = pltpu.make_async_copy(taken, taking, local_sems.at[3])
    store.start()

    def placed(b):
        return dot(chosen[b * BLOCK : (b + 1) * BLOCK, :], arrived[...], ((1,), (0,))).astype(BF)

    out_far.wait_recv()
    out_pass.start()

    def land(kind):
        @pl.loop(1, groups)
        def _(step):
            moved(kind, step).wait_recv()

        @pl.loop(0, groups)
        def _(peer):
            arrived[pl.ds(pl.multiple_of(peer * piece, 8), piece), :] = unfold(recv[kind, peer], width, halves)

    token_gather = HeadGather(wide, gather_sems)
    head_gather = HeadGather(wide_heads, head_sems)
    land(0)
    for b in range(blocks):
        token_gather.start(b, placed(b))
        if b >= 1:
            token_gather.relay(b - 1)
    loads[2].wait()

    def attend(b):
        here = slice(b * BLOCK, (b + 1) * BLOCK)
        token_gather.land(b, packed_out, width)
        for k in range(3):
            part = dot(packed_out[here, :], weight_here[k], ((1,), (1,)))
            if k != 1:
                part += qv_bias[k // 2 : k // 2 + 1, :].astype(F32)
            qkv[k, here, :] = part.astype(BF)
        same = start_col[here, 0:1] == seq_row[0:1, here]
        distance = key_distance()
        for h in range(heads):
            lanes = slice(h * HEAD_DIM, (h + 1) * HEAD_DIM)
            scored = scores_by_key(qkv[1, here, lanes], qkv[0, here, lanes], slope_of(me * heads + h), distance, same)
            top = jnp.max(scored, axis=0, keepdims=True)
            raised = jnp.exp(scored - top)
            total = jnp.sum(raised, axis=0, keepdims=True)
            lse[b, h : h + 1, :] = top + jnp.log(total)
            probs = (raised * (1.0 / total)).astype(BF)
            turned = dot(qkv[2, here, lanes].T, probs, ((1,), (0,)))
            context[here, lanes] = turned.T.astype(BF)
        head_gather.start(b, context[here, :])

    for b in range(blocks):
        if b == blocks - 1:
            token_gather.relay(b)
        attend(b)
        if b >= 1:
            head_gather.relay(b - 1)
    for b in range(blocks - 1):
        head_gather.land(b, wide_context, width)
    land(1)
    for b in range(blocks):
        cot_block = placed(b)
        for u in range(4):
            fold_into(cot_out, (u, b), cot_block[u * quarter : (u + 1) * quarter], True)
    head_gather.relay(blocks - 1)
    head_gather.land(blocks - 1, wide_context, width)
    for b in range(blocks):
        token_gather.end(b)
        head_gather.end(b)
    store.wait()
    out_near.wait()
    out_pass.wait()
    out_far.wait_send()
    for kind in range(2):
        @pl.loop(1, groups)
        def _(step):
            moved(kind, step).wait_send()


def front(groups, args, number):
    tokens, qkv_w, out_w = args[0], args[4], args[6]
    width, rows = tokens.shape
    piece = rows // groups
    blocks = rows // BLOCK
    heads = width // HEAD_DIM
    halves = (piece // 2) % 8 == 0
    slab = (2, groups, piece // 2, 2 * width) if halves else (2, groups, piece, width)
    here = pltpu.VMEM((rows, width), BF)
    wide = pltpu.VMEM((4, blocks, BLOCK // 2, 2 * width), BF)
    turned = pltpu.VMEM((width, rows), BF)
    dma = pltpu.SemaphoreType.DMA
    return call(
        functools.partial(front_kernel, groups, blocks),
        number,
        (
            shape((rows, 4 * width), BF),
            shape((4, blocks, BLOCK // 8, 2 * width), BF),
            shape((4,) + out_w.shape, BF),
            shape((3, rows, width), BF),
            shape((blocks, heads, BLOCK), F32),
            shape((rows, width), BF),
            shape((rows, 4 * width), BF),
            shape((rows, rows), BF),
        ),
        [
            turned,
            turned,
            here,
            here,
            pltpu.VMEM(qkv_w.shape, BF),
            pltpu.VMEM((rows, 8), jnp.int32),
            pltpu.VMEM((rows, rows), BF),
            pltpu.VMEM((rows, rows), BF),
            pltpu.VMEM(slab, BF),
            pltpu.VMEM(slab, BF),
            here,
            wide,
            wide,
            dma((4,)),
            dma((2, 2, groups)),
            dma((6, blocks)),
            dma((6, blocks)),
            dma((6,)),
        ],
        args,
        apart=(0, 1, 4),
        apart_outs=(7,),
    )


def norm_unit(values):
    center = values - jnp.mean(values, axis=-1, keepdims=True)
    rs = lax.rsqrt(jnp.mean(center * center, axis=-1, keepdims=True) + 1e-05)
    return center * rs, rs


def norm_back(weighted, unit, rs):
    inner = jnp.mean(weighted * unit, axis=-1, keepdims=True)
    return rs * (weighted - jnp.mean(weighted, axis=-1, keepdims=True) - unit * inner)


class GroupSum:
    def __init__(self, groups, grads, buffers, sems):
        self.acc, self.recv1, self.recv2 = buffers
        self.pair_sems, self.group_sems = sems
        self.grads = grads
        self.pairs = groups // 2
        self.mine = lax.axis_index("dp")
        self.parity = self.mine % 2
        self.pair = self.mine + 1 - 2 * self.parity
        self.slot = self.mine // 2

    def paired(self, kind, step):
        m = (self.slot + step) % self.pairs
        return send(self.grads[kind].at[2 * m + 1 - self.parity], self.recv1.at[kind, m],
                    self.pair_sems.at[0, kind, step], self.pair_sems.at[1, kind, step], dp=self.pair)

    def passed(self, kind, step):
        m = (self.slot + step) % self.pairs
        return send(self.acc.at[kind, m], self.recv2.at[kind, self.slot], self.group_sems.at[0, kind, step],
                    self.group_sems.at[1, kind, step], dp=2 * m + self.parity)

    def start(self, kind):
        @pl.loop(1, self.pairs + 1)
        def _(step):
            self.paired(kind, step).start()

    def forward(self, kinds):
        @pl.loop(1, self.pairs)
        def _(step):
            m = (self.slot + step) % self.pairs
            for kind in kinds:
                self.paired(kind, step).wait_recv()
                own = self.grads[kind][2 * m + self.parity].astype(F32)
                self.acc[kind, m] = (own + self.recv1[kind, m].astype(F32)).astype(BF)
                self.passed(kind, step).start()

    def pair_only(self, kind, shares, own):
        @pl.loop(1, self.pairs)
        def _(step):
            m = (self.slot + step) % self.pairs
            self.paired(kind, step).wait_recv()
            mine = self.grads[kind][2 * m + self.parity].astype(F32)
            shares[m] = (mine + self.recv1[kind, m].astype(F32)).astype(BF)

        self.paired(kind, self.pairs).wait_recv()
        shares[self.slot] = jnp.zeros_like(shares[0])
        own[...] = self.grads[kind][self.mine].astype(F32) + self.recv1[kind, self.slot].astype(F32)

        @pl.loop(1, self.pairs + 1)
        def _(step):
            self.paired(kind, step).wait_send()

    def collect(self, kind):
        self.paired(kind, self.pairs).wait_recv()
        total = self.grads[kind][self.mine].astype(F32) + self.recv1[kind, self.slot].astype(F32)
        for step in range(1, self.pairs):
            self.passed(kind, step).wait_recv()
            total += self.recv2[kind, (self.slot + self.pairs - step) % self.pairs].astype(F32)
        return total

    def end(self, kinds):
        for kind in kinds:
            @pl.loop(1, self.pairs + 1)
            def _(step):
                self.paired(kind, step).wait_send()

            @pl.loop(1, self.pairs)
            def _(step):
                self.passed(kind, step).wait_send()

    @staticmethod
    def scratch(kinds, groups, held, span):
        exchange = pltpu.VMEM((kinds, groups // 2, held, span), BF)
        sems = pltpu.SemaphoreType.DMA((2, kinds, groups // 2 + 1))
        return [exchange] * 3 + [sems] * 2


class ShareSum:
    def __init__(self, groups, shares, recv, sems):
        self.shares, self.recv, self.sems = shares, recv, sems
        self.pairs = groups // 2
        mine = lax.axis_index("dp")
        self.parity, self.slot = mine % 2, mine // 2

    def passed(self, step):
        m = (self.slot + step) % self.pairs
        return send(self.shares.at[m], self.recv.at[self.slot], self.sems.at[0, step], self.sems.at[1, step],
                    dp=2 * m + self.parity)

    def start(self):
        @pl.loop(1, self.pairs)
        def _(step):
            self.passed(step).start()

    def collect(self, own):
        total = own[...]
        for step in range(1, self.pairs):
            self.passed(step).wait()
            total += self.recv[(self.slot + self.pairs - step) % self.pairs].astype(F32)
        return total


class GiveBack:
    def __init__(self, groups, rows, width, chosen, sent, recv, sems):
        self.groups, self.piece, self.width = groups, rows // groups, width
        self.halves = (self.piece // 2) % 8 == 0
        self.chosen, self.sent, self.recv, self.sems = chosen, sent, recv, sems
        self.mine = lax.axis_index("dp")

    def moved(self, step):
        peer = (self.mine + step) % self.groups
        return send(self.sent.at[peer], self.recv.at[self.mine], self.sems.at[0, step], self.sems.at[1, step], dp=peer)

    def start(self, packed):
        @pl.loop(0, self.groups)
        def _(step):
            peer = (self.mine + step) % self.groups
            rows = self.chosen[pl.ds(pl.multiple_of(peer * self.piece, 8), self.piece), :]
            values = dot(rows, packed[...], ((1,), (0,))).astype(BF)

            @pl.when(step > 0)
            def _():
                fold_into(self.sent, (peer,), values, self.halves)
                self.moved(step).start()

            @pl.when(step == 0)
            def _():
                fold_into(self.recv, (self.mine,), values, self.halves)

    def land(self, target):
        @pl.loop(1, self.groups)
        def _(step):
            self.moved(step).wait_recv()

        @pl.loop(0, self.groups)
        def _(peer):
            here = pl.ds(pl.multiple_of(peer * self.piece, 8), self.piece)
            target[here, :] = unfold(self.recv[peer], self.width, self.halves)

        @pl.loop(1, self.groups)
        def _(step):
            self.moved(step).wait_send()

    @staticmethod
    def scratch(groups, rows, width):
        piece = rows // groups
        halves = (piece // 2) % 8 == 0
        slab = (groups, piece // 2, 2 * width) if halves else (groups, piece, width)
        return [pltpu.VMEM(slab, BF)] * 2 + [pltpu.SemaphoreType.DMA((2, groups))]


class RowSum:
    def __init__(self, part, first, second, third, sems):
        self.part, self.first, self.second, self.third, self.sems = part, first, second, third, sems
        self.me, self.sibling, self.across, self.diagonal = place_of()

    def cross(self, b):
        return send(self.part.at[b, self.diagonal], self.first.at[b], self.sems.at[0, b], self.sems.at[1, b],
                    tensor=self.sibling)

    def near(self, b):
        return send(self.part.at[b, self.sibling], self.second.at[b], self.sems.at[2, b], self.sems.at[3, b],
                    tensor=self.sibling)

    def far(self, b):
        return send(self.first.at[b], self.third.at[b], self.sems.at[4, b], self.sems.at[5, b], tensor=self.across)

    def start(self, b):
        self.cross(b).start()
        self.near(b).start()

    def relay(self, b):
        self.cross(b).wait()
        self.first[b] = (self.part[b, self.across].astype(F32) + self.first[b].astype(F32)).astype(BF)
        self.far(b).start()

    def total(self, b):
        self.near(b).wait()
        self.far(b).wait()
        return self.part[b, self.me].astype(F32) + self.second[b].astype(F32) + self.third[b].astype(F32)

    @staticmethod
    def scratch(blocks, rows, columns):
        buffer = pltpu.VMEM((blocks, rows, columns), BF)
        return [pltpu.VMEM((blocks, 4, rows, columns), BF)] + [buffer] * 3 + [pltpu.SemaphoreType.DMA((6, blocks))]


class RowGather:
    def __init__(self, out, sems):
        self.out, self.sems = out, sems
        self.me, self.sibling, self.across, _ = place_of()

    def copy(self, b, kind, whose, peer):
        return send(self.out.at[b, whose], self.out.at[b, whose], self.sems.at[2 * kind, b],
                    self.sems.at[2 * kind + 1, b], tensor=peer)

    def start(self, b):
        self.copy(b, 0, self.me, self.across).start()
        self.copy(b, 1, self.me, self.sibling).start()

    def relay(self, b):
        self.copy(b, 0, self.me, self.across).wait_recv()
        self.copy(b, 2, self.across, self.sibling).start()

    def land(self, b):
        self.copy(b, 1, self.me, self.sibling).wait_recv()
        self.copy(b, 2, self.across, self.sibling).wait_recv()

    def end(self, b):
        self.copy(b, 0, self.me, self.across).wait_send()
        self.copy(b, 1, self.me, self.sibling).wait_send()
        self.copy(b, 2, self.across, self.sibling).wait_send()


CHUNK = 256


def mid_kernel(groups, blocks, grad_scale, context, packed, full_out, up_w, up_bias, down_w, cot_folded, v0, v1, v2, v3, v4, v5,
               d_low, d_own, small, value_grad, down_grad, gate_shares, gate_sum, folded,
               normed_low, slope_term, gelu_term, gated, d_gate, d_value, unit_full, rs_full, unit_own, rs_own, d_mixed,
               mixed, whole_grad, down_pieces, gate_pieces, cot_recv,
               part1, first1, second1, third1, sems1, part2, first2, second2, third2, sems2, sems3, sems4, c_sems,
               vector_rows, acc, recv1, recv2, pair_sems, group_sems):
    me, sibling, across, diagonal = place_of()
    columns = packed.shape[1]
    width = columns // 4
    quarter = BLOCK // 4
    held = down_pieces.shape[1]
    enter([sibling, across, diagonal], groups)
    swaps = [
        send(cot_folded.at[peer], cot_recv.at[me], c_sems.at[0, k], c_sems.at[1, k], tensor=peer)
        for k, peer in enumerate((across, diagonal, sibling))
    ]
    for swap in swaps:
        swap.start()
    cot_recv[me] = cot_folded[me]
    ffn = RowSum(part1, first1, second1, third1, sems1)
    back_sum = RowSum(part2, first2, second2, third2, sems2)
    mixed_gather = RowGather(mixed, sems3)
    hidden_gather = RowGather(d_low, sems4)
    sums = GroupSum(groups, (down_pieces, gate_pieces), (acc, recv1, recv2), (pair_sems, group_sems))
    small[...] = jnp.zeros_like(small)
    for k, vector in enumerate((v0, v1, v2, v3, v4, v5)):
        vector_rows[k : k + 1, :] = vector[...].astype(F32).reshape(1, columns)
    out_bias, first_gain, first_shift, down_bias, second_gain, second_shift = (
        vector_rows.at[k : k + 1] for k in range(6)
    )

    def add_small(row, values):
        small[row : row + 1, :] += jnp.sum(values, axis=0, keepdims=True) * grad_scale

    def ahead(b, c):
        here = slice(b * BLOCK + c * CHUNK, b * BLOCK + (c + 1) * CHUNK)
        inner = slice(c * CHUNK, (c + 1) * CHUNK)
        hidden = packed[here, :].astype(F32) + (dot(context[here, :], full_out[...], ((1,), (0,))) + out_bias[...])
        unit, rs = norm_unit(hidden)
        unit_full[inner, :] = unit
        rs_full[inner, :] = rs
        low = (unit * first_gain[...] + first_shift[...]).astype(BF)
        normed_low[here, :] = low
        gate = dot(low, up_w[0], ((1,), (0,))) + up_bias[0:1, :].astype(F32)
        value = dot(low, up_w[1], ((1,), (0,))) + up_bias[1:2, :].astype(F32)
        half_erf = 0.5 * (1.0 + lax.erf(gate * (0.5**0.5)))
        gelu = gate * half_erf
        slope = half_erf + gate * jnp.exp(-0.5 * gate * gate) * ((2.0 * jnp.pi) ** (-0.5))
        slope_term[here, :] = value * slope
        gelu_term[here, :] = gelu
        low_gated = (gelu * value).astype(BF)
        gated[here, :] = low_gated
        out = dot(low_gated, down_w[...], ((1,), (0,))).astype(BF)
        for k in range(CHUNK // quarter):
            part1[b, c * (CHUNK // quarter) + k] = out[k * quarter : (k + 1) * quarter]

    def keep_own(b):
        mine = pl.ds(pl.multiple_of(me * quarter, quarter), quarter)
        unit_own[b] = unit_full[mine, :]
        rs_own[b] = rs_full[mine, :]
        ffn.start(b)

    def turn(b):
        if b == 0:
            for swap in swaps:
                swap.wait_recv()
        values = unit_own[b] * first_gain[...] + first_shift[...] + (ffn.total(b) + down_bias[...])
        unit, rs = norm_unit(values)
        out = (unit * second_gain[...] + second_shift[...]).astype(BF)
        for u in range(4):
            fold_into(folded, (u, b), out[:, u * width : (u + 1) * width], True)
        cot_rows = jnp.concatenate([unfold(cot_recv[s, b], width, True) for s in range(4)], axis=1).astype(F32)
        d_rows = norm_back(cot_rows * second_gain[...], unit, rs)
        d_mixed[b] = d_rows
        mixed[b, me] = d_rows.astype(BF)
        mixed_gather.start(b)
        add_small(3, d_rows)
        add_small(4, cot_rows * unit)
        add_small(5, cot_rows)

    def astern(b):
        mixed_gather.land(b)
        for c in range(BLOCK // CHUNK):
            here = slice(b * BLOCK + c * CHUNK, b * BLOCK + (c + 1) * CHUNK)
            count = CHUNK // quarter
            d_rows = jnp.concatenate([mixed[b, c * count + k] for k in range(count)], axis=0)
            d_gated = dot(d_rows, down_w[...], ((1,), (1,)))
            gate_rows = (d_gated * slope_term[here, :]).astype(BF)
            value_rows = (d_gated * gelu_term[here, :]).astype(BF)
            d_gate[here, :] = gate_rows
            d_value[here, :] = value_rows
            add_small(8, gate_rows.astype(F32))
            add_small(9, value_rows.astype(F32))
            out = dot(gate_rows, up_w[0], ((1,), (1,))) + dot(value_rows, up_w[1], ((1,), (1,)))
            out = out.astype(BF)
            for k in range(count):
                part2[b, c * count + k] = out[k * quarter : (k + 1) * quarter]
        back_sum.start(b)

    def finish(b):
        d_normed = d_mixed[b] + back_sum.total(b)
        d_hidden = norm_back(d_normed * first_gain[...], unit_own[b], rs_own[b])
        d_own[b] = d_hidden
        d_low[b, me] = d_hidden.astype(BF)
        hidden_gather.start(b)
        add_small(0, d_hidden)
        add_small(1, d_normed * unit_own[b])
        add_small(2, d_normed)

    def weight_grad(left, right, pieces):
        span = right.shape[1]
        for c in range(span // CHUNK):
            lanes = slice(c * CHUNK, (c + 1) * CHUNK)
            whole_grad[:, lanes] = dot(left, right[:, lanes], ((0,), (0,)))
        for g in range(groups):
            pieces[g] = (whole_grad[g * held : (g + 1) * held, :] * grad_scale).astype(BF)

    last = blocks - 1
    for b in range(blocks):
        ahead(b, 0)
        if b >= 1:
            ffn.relay(b - 1)
        if b >= 2:
            turn(b - 2)
        ahead(b, 1)
        keep_own(b)
        if b >= 2:
            mixed_gather.relay(b - 2)
    ffn.relay(last)
    if blocks > 1:
        turn(last - 1)
    turn(last)
    if blocks > 1:
        mixed_gather.relay(last - 1)
    for b in range(blocks):
        if b == last:
            mixed_gather.relay(last)
        astern(b)
        if b >= 1:
            back_sum.relay(b - 1)
    back_sum.relay(last)
    d_mixed_rows = jnp.concatenate([mixed[b, k] for b in range(blocks) for k in range(4)], axis=0)
    weight_grad(d_mixed_rows, gated, down_pieces)
    sums.start(0)
    finish(0)
    weight_grad(normed_low[...], d_gate, gate_pieces)
    sums.start(1)
    if blocks > 1:
        finish(1)
    weight_grad(normed_low[...], d_value, value_grad)
    for b in range(2, blocks):
        finish(b)
    for b in range(blocks):
        hidden_gather.relay(b)
    sums.forward((0,))
    for b in range(blocks):
        hidden_gather.land(b)
    sums.pair_only(1, gate_shares, gate_sum)
    down_grad[...] = sums.collect(0)
    for b in range(blocks):
        mixed_gather.end(b)
        hidden_gather.end(b)
    for swap in swaps:
        swap.wait_send()
    sums.end((0,))


def mid(groups, grad_scale, args, number):
    context, up_w, cot_folded = args[0], args[3], args[6]
    rows, columns = context.shape
    units = up_w.shape[2]
    held = columns // groups
    blocks = rows // BLOCK
    quarter = BLOCK // 4
    own = (blocks, quarter, columns)
    dma = pltpu.SemaphoreType.DMA
    outs = (
        shape((blocks, 4, quarter, columns), BF),
        shape(own, F32),
        shape((16, columns), F32),
        shape((groups, held, units), BF),
        shape((held, units), F32),
        shape((groups // 2, held, units), BF),
        shape((held, units), F32),
        shape(cot_folded.shape, BF),
    )
    return call(
        functools.partial(mid_kernel, groups, blocks, grad_scale),
        number,
        outs,
        [
            pltpu.VMEM((rows, columns), BF),
            pltpu.VMEM((rows, units), F32),
            pltpu.VMEM((rows, units), F32),
            pltpu.VMEM((rows, units), BF),
            pltpu.VMEM((rows, units), BF),
            pltpu.VMEM((rows, units), BF),
            pltpu.VMEM((BLOCK, columns), F32),
            pltpu.VMEM((BLOCK, 1), F32),
            pltpu.VMEM(own, F32),
            pltpu.VMEM((blocks, quarter, 1), F32),
            pltpu.VMEM(own, F32),
            pltpu.VMEM((blocks, 4, quarter, columns), BF),
            pltpu.VMEM((columns, units), F32),
            pltpu.VMEM((groups, held, units), BF),
            pltpu.VMEM((groups, held, units), BF),
            pltpu.VMEM(cot_folded.shape, BF),
        ]
        + RowSum.scratch(blocks, quarter, columns)
        + RowSum.scratch(blocks, quarter, columns)
        + [dma((6, blocks)), dma((6, blocks)), dma((2, 3)), pltpu.VMEM((6, columns), F32)]
        + GroupSum.scratch(2, groups, held, units),
        args,
    )


def back_kernel(groups, blocks, grad_scale, dh_low, dh_own, qkv, lse, seq_row, context, packed_in, qkv_w,
                out_w, value_grad, gate_shares, gate_sum, folded, small, taking,
                layer_out, input_grad, up_grad, qkv_grad, out_grad, small_out,
                d_rows, d_part, late_sum, late, cols, one, two, three, packed, ssent, srecv, swide, x_sems, s_sems, w_sems,
                start_col, chosen, weight_here, returned, landed, load_sem, r_sems,
                acc, recv1, recv2, pair_sems, group_sems, acc2, recv3, recv4, pair_sems2, group_sems2, share_recv, share_sems,
                sent, recv, a_sems, sent2, recv5, a_sems2):
    me, sibling, across, diagonal = place_of()
    mine = lax.axis_index("dp")
    width, rows = input_grad.shape
    heads = width // HEAD_DIM
    held = late.shape[1]
    quarter = BLOCK // 4
    load = pltpu.make_async_copy(qkv_w, weight_here, load_sem.at[0])
    load.start()
    load_rows = pltpu.make_async_copy(taking, chosen, load_sem.at[1])
    load_rows.start()
    enter([sibling, across, diagonal], groups)
    sums = GroupSum(groups, (value_grad,), (acc, recv1, recv2), (pair_sems, group_sems))
    late_sums = GroupSum(groups, (late,), (acc2, recv3, recv4), (pair_sems2, group_sems2))
    giving = GiveBack(groups, rows, width, chosen, sent, recv, a_sems)
    giving_result = GiveBack(groups, rows, width, chosen, sent2, recv5, a_sems2)
    gate = ShareSum(groups, gate_shares, share_recv, share_sems)
    gate.start()
    sums.start(0)
    returns = [
        send(folded.at[peer], returned.at[me], r_sems.at[0, k], r_sems.at[1, k], tensor=peer)
        for k, peer in enumerate((across, diagonal, sibling))
    ]
    for swap in returns:
        swap.start()
    returned[me] = folded[me]
    def cross(b):
        return send(cols.at[diagonal, b], one.at[b], x_sems.at[0, b], x_sems.at[1, b], tensor=sibling)

    def near(b):
        return send(cols.at[sibling, b], two.at[b], x_sems.at[2, b], x_sems.at[3, b], tensor=sibling)

    def far(b):
        return send(one.at[b], three.at[b], x_sems.at[4, b], x_sems.at[5, b], tensor=across)

    def relay(b):
        cross(b).wait()
        one[b] = (cols[across, b].astype(F32) + one[b].astype(F32)).astype(BF)
        far(b).start()

    to_column(seq_row, start_col, 0)
    late_sum[:, 3 * width :] = dot(dh_low[...], context[...], ((0,), (0,)))
    load.wait()
    ssent[...] = small[...]

    @pl.loop(0, blocks)
    def _(b):
        here = pl.ds(pl.multiple_of(b * BLOCK, BLOCK), BLOCK)
        dh = dh_low[here, :]
        d_context = dot(dh, out_w[...], ((1,), (1,))).astype(BF)
        same = start_col[here, 0:1] == seq_row[0:1, here]
        distance = key_distance()
        for h in range(heads):
            lanes = slice(h * HEAD_DIM, (h + 1) * HEAD_DIM)
            queries = qkv[0, here, lanes]
            keys = qkv[1, here, lanes]
            values = qkv[2, here, lanes]
            d_rows_out = d_context[:, lanes]
            scored = scores_by_key(keys, queries, slope_of(me * heads + h), distance, same)
            probs = jnp.exp(scored - lse[b, h : h + 1, :])
            d_probs = dot(values, d_rows_out, ((1,), (1,)))
            d_rows[2, here, lanes] = dot(probs.astype(BF), d_rows_out, ((1,), (0,))).astype(BF)
            center = jnp.sum(probs * d_probs, axis=0, keepdims=True)
            d_scores = (probs * (d_probs - center)).astype(BF)
            d_rows[1, here, lanes] = (dot(d_scores, queries, ((1,), (0,))) * (HEAD_DIM**-0.5)).astype(BF)
            turned = dot(keys.T, d_scores, ((1,), (0,))) * (HEAD_DIM**-0.5)
            d_rows[0, here, lanes] = turned.T.astype(BF)
        part = dot(d_rows[0, here, :], weight_here[0], ((1,), (0,)))
        part += dot(d_rows[1, here, :], weight_here[1], ((1,), (0,)))
        part += dot(d_rows[2, here, :], weight_here[2], ((1,), (0,)))
        d_part[...] = part
        d_part[pl.ds(pl.multiple_of(me * quarter, quarter), quarter), :] += dh_own[b]
        for u in range(4):
            fold_into(cols, (u, b), d_part[:, u * width : (u + 1) * width].astype(BF), True)
        cross(b).start()
        near(b).start()
        last = small.shape[0] - 6
        for k, c in enumerate((0, 2)):
            bias = jnp.sum(d_rows[c, here, :].astype(F32), axis=0, keepdims=True) * grad_scale
            ssent[last : last + 1, k * 2 * 128 : k * 2 * 128 + width] += bias
        relay(b)

        @pl.when(b == 0)
        def _():
            sums.forward((0,))

        @pl.when(b == 1)
        def _():
            load_rows.wait()
            for swap in returns:
                swap.wait_recv()
            for q in range(blocks):
                for s in range(4):
                    start = q * BLOCK + s * quarter
                    packed[start : start + quarter, :] = unfold(returned[s, q], width, True)
            giving_result.start(packed)

    for c in range(3):
        late_sum[:, c * width : (c + 1) * width] = dot(packed_in[...], d_rows[c], ((0,), (0,)))
    for g in range(groups):
        late[g] = (late_sum[g * held : (g + 1) * held, :] * grad_scale).astype(BF)

    late_sums.start(0)
    swaps = [
        send(ssent, srecv.at[me], s_sems.at[0, k], s_sems.at[1, k], tensor=peer)
        for k, peer in enumerate((sibling, across, diagonal))
    ]
    for swap in swaps:
        swap.start()
    srecv[me] = ssent[...]

    for b in range(blocks):
        near(b).wait()
        far(b).wait_recv()
        total = cols[me, b].astype(F32) + two[b].astype(F32) + three[b].astype(F32)
        packed[b * BLOCK : (b + 1) * BLOCK, :] = unfold(total.astype(BF), width, True)
    giving.start(packed)

    for swap in swaps:
        swap.wait_recv()
    shared = small.shape[0] // 2
    swide[mine, 0:shared] = srecv[0, 0:shared] + srecv[1, 0:shared] + srecv[2, 0:shared] + srecv[3, 0:shared]
    swide[mine, shared:] = ssent[shared:, :]

    def spread(step):
        peer = (mine + step) % groups
        return send(swide.at[mine], swide.at[mine], w_sems.at[0, step], w_sems.at[1, step], dp=peer)

    @pl.loop(1, groups)
    def _(step):
        spread(step).start()

    late_sums.forward((0,))
    up_grad[0] = gate.collect(gate_sum)
    up_grad[1] = sums.collect(0)
    giving_result.land(landed)
    layer_out[...] = landed[...].T

    @pl.loop(1, groups)
    def _(step):
        spread(step).wait_recv()

    small_out[...] = swide[0]

    @pl.loop(1, groups)
    def _(peer):
        small_out[...] += swide[peer]

    total = late_sums.collect(0)
    for c in range(3):
        qkv_grad[c] = total[:, c * width : (c + 1) * width]
    out_grad[...] = total[:, 3 * width :].T
    giving.land(landed)
    input_grad[...] = landed[...].T
    for b in range(blocks):
        far(b).wait_send()
    for copy in swaps + returns:
        copy.wait_send()
    sums.end((0,))
    late_sums.end((0,))

    @pl.loop(1, groups)
    def _(step):
        spread(step).wait_send()


def back(groups, grad_scale, args, small, number):
    dh_low, qkv, qkv_w, grad, folded = args[0], args[2], args[7], args[9], args[12]
    rows, columns = dh_low.shape
    width = qkv.shape[2]
    held, units = grad.shape[1:]
    blocks = rows // BLOCK
    half = (blocks, BLOCK // 2, 2 * width)
    dma = pltpu.SemaphoreType.DMA
    outs = (
        shape((width, rows), BF),
        shape((width, rows), BF),
        shape((2, held, units), F32),
        shape((3, held, width), F32),
        shape((width, held), F32),
        shape(small.shape, F32),
    )
    return call(
        functools.partial(back_kernel, groups, blocks, grad_scale),
        number,
        outs,
        [
            pltpu.VMEM((3, rows, width), BF),
            pltpu.VMEM((BLOCK, columns), F32),
            pltpu.VMEM((columns, 4 * width), F32),
            pltpu.VMEM((groups, held, 4 * width), BF),
            pltpu.VMEM((4,) + half, BF),
            pltpu.VMEM(half, BF),
            pltpu.VMEM(half, BF),
            pltpu.VMEM(half, BF),
            pltpu.VMEM((rows, width), BF),
            pltpu.VMEM(small.shape, F32),
            pltpu.VMEM((4,) + small.shape, F32),
            pltpu.VMEM((groups,) + small.shape, F32),
            dma((6, blocks)),
            dma((2, 3)),
            dma((2, groups)),
            pltpu.VMEM((rows, 8), jnp.int32),
            pltpu.VMEM((rows, rows), BF),
            pltpu.VMEM(qkv_w.shape, BF),
            pltpu.VMEM(folded.shape, BF),
            pltpu.VMEM((rows, width), BF),
            dma((2,)),
            dma((2, 3)),
        ]
        + GroupSum.scratch(1, groups, held, units)
        + GroupSum.scratch(1, groups, held, 4 * width)
        + [pltpu.VMEM((groups // 2, held, units), BF), dma((2, groups // 2))]
        + GiveBack.scratch(groups, rows, width)
        + GiveBack.scratch(groups, rows, width),
        args,
        apart=(7, 14),
    )


def on_device(
    tokens,
    cotangent,
    seq_start,
    row_place,
    qkv_weight,
    qv_bias,
    out_weight,
    out_bias,
    first_gain,
    first_shift,
    up_weight,
    up_bias,
    down_weight,
    down_bias,
    second_gain,
    second_shift,
):
    row_count, width = tokens.shape
    columns = qkv_weight.shape[1]
    groups = lax.axis_size("dp")
    grad_scale = (row_count * groups) ** (-0.5)
    seq_row = seq_start.reshape(1, row_count)
    weight_turned = qkv_weight.transpose(0, 2, 1)
    packed_in, cot_folded, full_out, qkv_rows, log_total, context, wide_context, taking = front(
        groups, (tokens.T, cotangent.T, row_place, seq_row, weight_turned, qv_bias, out_weight), 0
    )
    d_low, d_own, small, value_grad, down_grad, gate_shares, gate_sum, folded = mid(
        groups,
        grad_scale,
        (
            wide_context,
            packed_in,
            full_out.reshape(columns, columns),
            up_weight,
            up_bias,
            down_weight,
            cot_folded,
            out_bias,
            first_gain,
            first_shift,
            down_bias,
            second_gain,
            second_shift,
        ),
        1,
    )
    layer_out, input_grad, up_grad, qkv_grad, out_grad, sums = back(
        groups,
        grad_scale,
        (
            d_low.reshape(row_count, columns),
            d_own,
            qkv_rows,
            log_total,
            seq_row,
            context,
            packed_in,
            weight_turned,
            out_weight,
            value_grad,
            gate_shares,
            gate_sum,
            folded,
            small,
            taking,
        ),
        small,
        2,
    )
    rows_here = columns // groups
    sums_here = lax.dynamic_slice_in_dim(sums[:6], lax.axis_index("dp") * rows_here, rows_here, 1)
    return (
        layer_out.T,
        input_grad.T,
        qkv_grad,
        jnp.stack([sums[10, :width], sums[10, 256 : 256 + width]]),
        out_grad,
        sums_here[0],
        sums_here[1],
        sums_here[2],
        up_grad,
        sums[8:10],
        down_grad.T,
        sums_here[3],
        sums_here[4],
        sums_here[5],
    )


def solution(mesh):
    return jax.shard_map(
        on_device,
        mesh=mesh,
        in_specs=(
            P("dp", "tensor"),
            P("dp", "tensor"),
            P("dp"),
            P("dp", None),
            P(None, None, "tensor"),
            P(None, "tensor"),
            P("tensor", None),
            P(),
            P(),
            P(),
            P(None, None, "tensor"),
            P(None, "tensor"),
            P("tensor", None),
            P(),
            P(),
            P(),
        ),
        out_specs=(
            P("dp", "tensor"),
            P("dp", "tensor"),
            P(None, "dp", "tensor"),
            P(None, "tensor"),
            P("tensor", "dp"),
            P("dp"),
            P("dp"),
            P("dp"),
            P(None, "dp", "tensor"),
            P(None, "tensor"),
            P("tensor", "dp"),
            P("dp"),
            P("dp"),
            P("dp"),
        ),
        check_vma=False,
    )
```

```python
import functools

import jax
import jax.numpy as jnp
from jax import lax
from jax.experimental import pallas as pl
from jax.experimental.pallas import tpu as pltpu
from jax.sharding import PartitionSpec as P

HEADS = 12
HEAD_DIM = 64
BLOCK = 512
BF = jnp.bfloat16
F32 = jnp.float32
MESH = pl.DeviceIdType.MESH
VMEM_LIMIT = 67043328


def dot(a, b, dims):
    return lax.dot_general(a, b, (dims, ((), ())), preferred_element_type=F32)


def place_of():
    me = lax.axis_index("tensor")
    core = me % 2
    side = me // 2
    sibling = side * 2 + (1 - core)
    across = (1 - side) * 2 + core
    diagonal = (1 - side) * 2 + (1 - core)
    return me, sibling, across, diagonal


def enter(devices, groups):
    barrier = pltpu.get_barrier_semaphore()
    count = len(devices)
    for device in devices:
        pl.semaphore_signal(barrier, inc=1, device_id={"tensor": device}, device_id_type=MESH)
    if groups:
        mine = lax.axis_index("dp")

        @pl.loop(1, groups)
        def _(step):
            pl.semaphore_signal(barrier, inc=1, device_id={"dp": (mine + step) % groups}, device_id_type=MESH)

        count += groups - 1
    pl.semaphore_wait(barrier, count)


def send(source, target, send_sem, recv_sem, **where):
    return pltpu.make_async_remote_copy(
        src_ref=source, dst_ref=target, send_sem=send_sem, recv_sem=recv_sem, device_id=where, device_id_type=MESH
    )


def fold_into(buffer, index, values, halves):
    width = values.shape[1]
    if not halves:
        buffer[index] = values
        return
    half = values.shape[0] // 2
    buffer[index + (slice(None), slice(0, width))] = values[:half]
    buffer[index + (slice(None), slice(width, 2 * width))] = values[half:]


def unfold(values, width, halves):
    if not halves:
        return values
    return jnp.concatenate([values[:, :width], values[:, width:]], axis=0)


def call(kernel, number, outs, scratch, args, apart=(), apart_outs=()):
    specs = [pl.BlockSpec(memory_space=pl.ANY if k in apart else pltpu.VMEM) for k in range(len(args))]
    return pl.pallas_call(
        kernel,
        out_shape=outs,
        in_specs=specs,
        out_specs=tuple(
            pl.BlockSpec(memory_space=pl.ANY if k in apart_outs else pltpu.VMEM) for k in range(len(outs))
        ),
        scratch_shapes=scratch,
        compiler_params=pltpu.CompilerParams(
            collective_id=number, has_side_effects=True, vmem_limit_bytes=VMEM_LIMIT
        ),
    )(*args)


def shape(dims, kind):
    return jax.ShapeDtypeStruct(dims, kind)


def to_column(row, column, where):
    for k in range(row.shape[1] // 128):
        piece = jnp.broadcast_to(row[0:1, k * 128 : (k + 1) * 128], (8, 128))
        column[k * 128 : (k + 1) * 128, where : where + 1] = piece.T[:, 0:1]


def slope_of(index):
    value = jnp.float32(2.0 ** (-8.0 / HEADS))
    for head in range(1, HEADS):
        value = jnp.where(index == head, jnp.float32(2.0 ** (-8.0 * (head + 1) / HEADS)), value)
    return value


def key_distance():
    keys = lax.broadcasted_iota(jnp.int32, (BLOCK, BLOCK), 0)
    asks = lax.broadcasted_iota(jnp.int32, (BLOCK, BLOCK), 1)
    return jnp.abs(keys - asks).astype(F32)


def scores_by_key(keys, queries, slope, distance, same):
    raw = dot(keys, queries, ((1,), (1,))) * (HEAD_DIM**-0.5) - slope * distance
    return jnp.where(same, raw, -1e30)


class HeadGather:
    def __init__(self, wide, sems):
        self.wide, self.sems = wide, sems
        self.me, self.sibling, self.across, _ = place_of()

    def copy(self, b, kind, whose, peer):
        return send(self.wide.at[whose, b], self.wide.at[whose, b], self.sems.at[2 * kind, b],
                    self.sems.at[2 * kind + 1, b], tensor=peer)

    def start(self, b, values):
        fold_into(self.wide, (self.me, b), values, True)
        self.copy(b, 0, self.me, self.across).start()
        self.copy(b, 1, self.me, self.sibling).start()

    def relay(self, b):
        self.copy(b, 0, self.me, self.across).wait_recv()
        self.copy(b, 2, self.across, self.sibling).start()

    def land(self, b, out, width):
        self.copy(b, 1, self.me, self.sibling).wait_recv()
        self.copy(b, 2, self.across, self.sibling).wait_recv()
        for s in range(4):
            out[b * BLOCK : (b + 1) * BLOCK, s * width : (s + 1) * width] = unfold(self.wide[s, b], width, True)

    def end(self, b):
        self.copy(b, 0, self.me, self.across).wait_send()
        self.copy(b, 1, self.me, self.sibling).wait_send()
        self.copy(b, 2, self.across, self.sibling).wait_send()


def front_kernel(groups, blocks, tokens, cot, place_row, seq_row, qkv_w, qv_bias, out_w,
                 packed_out, cot_out, full_out, qkv, lse, context, wide_context, taking,
                 tokens_turned, cot_turned, tokens_here, cot_here, weight_here, start_col, chosen, taken, sent, recv, arrived,
                 wide, wide_heads, local_sems, group_sems, gather_sems, head_sems, out_sems):
    me, sibling, across, diagonal = place_of()
    mine = lax.axis_index("dp")
    rows, width = tokens_here.shape
    heads = width // HEAD_DIM
    piece = rows // groups
    halves = (piece // 2) % 8 == 0
    quarter = BLOCK // 4
    loads = [
        pltpu.make_async_copy(source, target, local_sems.at[k])
        for k, (source, target) in enumerate(((tokens, tokens_turned), (cot, cot_turned), (qkv_w, weight_here)))
    ]
    for load in loads:
        load.start()
    enter([sibling, across, diagonal], groups)

    def moved(kind, step):
        peer = (mine + step) % groups
        return send(sent.at[kind, peer], recv.at[kind, mine], group_sems.at[0, kind, step],
                    group_sems.at[1, kind, step], dp=peer)

    def give(kind, source):
        @pl.loop(1, groups)
        def _(step):
            peer = (mine + step) % groups
            values = source[pl.ds(pl.multiple_of(peer * piece, 8), piece), :]
            fold_into(sent, (kind, peer), values, halves)
            moved(kind, step).start()

        values = source[pl.ds(pl.multiple_of(mine * piece, 8), piece), :]
        fold_into(recv, (kind, mine), values, halves)

    loads[0].wait()
    tokens_here[...] = tokens_turned[...].T
    give(0, tokens_here)
    out_far = send(out_w, full_out.at[me], out_sems.at[0], out_sems.at[1], tensor=across)
    out_near = send(out_w, full_out.at[me], out_sems.at[2], out_sems.at[3], tensor=sibling)
    out_pass = send(full_out.at[across], full_out.at[across], out_sems.at[4], out_sems.at[5], tensor=sibling)
    out_far.start()
    out_near.start()
    loads[1].wait()
    cot_here[...] = cot_turned[...].T
    give(1, cot_here)
    full_out[me] = out_w[...]
    to_column(seq_row, start_col, 0)
    for b in range(blocks):
        ids = lax.broadcasted_iota(jnp.int32, (BLOCK, rows), 0) + b * BLOCK
        chosen[b * BLOCK : (b + 1) * BLOCK, :] = jnp.where(ids == place_row[...], 1.0, 0.0).astype(BF)

    to_column(place_row, start_col, 1)
    for b in range(blocks):
        ids = lax.broadcasted_iota(jnp.int32, (BLOCK, rows), 1)
        here = slice(b * BLOCK, (b + 1) * BLOCK)
        taken[here, :] = jnp.where(ids == start_col[here, 1:2], 1.0, 0.0).astype(BF)
    store = pltpu.make_async_copy(taken, taking, local_sems.at[3])
    store.start()

    def placed(b):
        return dot(chosen[b * BLOCK : (b + 1) * BLOCK, :], arrived[...], ((1,), (0,))).astype(BF)

    out_far.wait_recv()
    out_pass.start()

    def land(kind):
        @pl.loop(1, groups)
        def _(step):
            moved(kind, step).wait_recv()

        @pl.loop(0, groups)
        def _(peer):
            arrived[pl.ds(pl.multiple_of(peer * piece, 8), piece), :] = unfold(recv[kind, peer], width, halves)

    token_gather = HeadGather(wide, gather_sems)
    head_gather = HeadGather(wide_heads, head_sems)
    land(0)
    for b in range(blocks):
        token_gather.start(b, placed(b))
        if b >= 1:
            token_gather.relay(b - 1)
    loads[2].wait()

    def attend(b):
        here = slice(b * BLOCK, (b + 1) * BLOCK)
        token_gather.land(b, packed_out, width)
        for k in range(3):
            part = dot(packed_out[here, :], weight_here[k], ((1,), (1,)))
            if k != 1:
                part += qv_bias[k // 2 : k // 2 + 1, :].astype(F32)
            qkv[k, here, :] = part.astype(BF)
        same = start_col[here, 0:1] == seq_row[0:1, here]
        distance = key_distance()
        for h in range(heads):
            lanes = slice(h * HEAD_DIM, (h + 1) * HEAD_DIM)
            scored = scores_by_key(qkv[1, here, lanes], qkv[0, here, lanes], slope_of(me * heads + h), distance, same)
            top = jnp.max(scored, axis=0, keepdims=True)
            raised = jnp.exp(scored - top)
            total = jnp.sum(raised, axis=0, keepdims=True)
            lse[b, h : h + 1, :] = top + jnp.log(total)
            probs = (raised * (1.0 / total)).astype(BF)
            turned = dot(qkv[2, here, lanes].T, probs, ((1,), (0,)))
            context[here, lanes] = turned.T.astype(BF)
        head_gather.start(b, context[here, :])

    for b in range(blocks):
        if b == blocks - 1:
            token_gather.relay(b)
        attend(b)
        if b >= 1:
            head_gather.relay(b - 1)
    for b in range(blocks - 1):
        head_gather.land(b, wide_context, width)
    land(1)
    for b in range(blocks):
        cot_block = placed(b)
        for u in range(4):
            fold_into(cot_out, (u, b), cot_block[u * quarter : (u + 1) * quarter], True)
    head_gather.relay(blocks - 1)
    head_gather.land(blocks - 1, wide_context, width)
    for b in range(blocks):
        token_gather.end(b)
        head_gather.end(b)
    store.wait()
    out_near.wait()
    out_pass.wait()
    out_far.wait_send()
    for kind in range(2):
        @pl.loop(1, groups)
        def _(step):
            moved(kind, step).wait_send()


def front(groups, args, number):
    tokens, qkv_w, out_w = args[0], args[4], args[6]
    width, rows = tokens.shape
    piece = rows // groups
    blocks = rows // BLOCK
    heads = width // HEAD_DIM
    halves = (piece // 2) % 8 == 0
    slab = (2, groups, piece // 2, 2 * width) if halves else (2, groups, piece, width)
    here = pltpu.VMEM((rows, width), BF)
    wide = pltpu.VMEM((4, blocks, BLOCK // 2, 2 * width), BF)
    turned = pltpu.VMEM((width, rows), BF)
    dma = pltpu.SemaphoreType.DMA
    return call(
        functools.partial(front_kernel, groups, blocks),
        number,
        (
            shape((rows, 4 * width), BF),
            shape((4, blocks, BLOCK // 8, 2 * width), BF),
            shape((4,) + out_w.shape, BF),
            shape((3, rows, width), BF),
            shape((blocks, heads, BLOCK), F32),
            shape((rows, width), BF),
            shape((rows, 4 * width), BF),
            shape((rows, rows), BF),
        ),
        [
            turned,
            turned,
            here,
            here,
            pltpu.VMEM(qkv_w.shape, BF),
            pltpu.VMEM((rows, 8), jnp.int32),
            pltpu.VMEM((rows, rows), BF),
            pltpu.VMEM((rows, rows), BF),
            pltpu.VMEM(slab, BF),
            pltpu.VMEM(slab, BF),
            here,
            wide,
            wide,
            dma((4,)),
            dma((2, 2, groups)),
            dma((6, blocks)),
            dma((6, blocks)),
            dma((6,)),
        ],
        args,
        apart=(0, 1, 4),
        apart_outs=(7,),
    )


def norm_unit(values):
    center = values - jnp.mean(values, axis=-1, keepdims=True)
    rs = lax.rsqrt(jnp.mean(center * center, axis=-1, keepdims=True) + 1e-05)
    return center * rs, rs


def norm_back(weighted, unit, rs):
    inner = jnp.mean(weighted * unit, axis=-1, keepdims=True)
    return rs * (weighted - jnp.mean(weighted, axis=-1, keepdims=True) - unit * inner)


class GroupSum:
    def __init__(self, groups, grads, scratch):
        self.groups, self.grads = groups, grads
        self.stages = groups.bit_length() - 1
        self.recv = scratch[: self.stages]
        self.held = (None,) + tuple(scratch[self.stages : 2 * self.stages - 1])
        self.sems = scratch[-1]
        self.mine = lax.axis_index("dp")

    def count(self, stage):
        return self.groups >> (stage + 1)

    def index(self, stage, step):
        return (self.mine // (2 << stage) + step) % self.count(stage)

    def given(self, stage, step):
        bit = (self.mine // (1 << stage)) % 2
        low = self.mine % (1 << stage)
        return self.index(stage, step) * (2 << stage) + (1 - bit) * (1 << stage) + low

    def copy(self, kind, stage, step):
        bit = (self.mine // (1 << stage)) % 2
        partner = self.mine + (1 - 2 * bit) * (1 << stage)
        at = self.index(stage, step)
        source = self.held[stage].at[kind, at] if stage else self.grads[kind].at[self.given(0, step)]
        return send(source, self.recv[stage].at[kind, at], self.sems.at[0, kind, stage, step],
                    self.sems.at[1, kind, stage, step], dp=partner)

    def start(self, kind):
        @pl.loop(1, self.count(0) + 1)
        def _(step):
            self.copy(kind, 0, step).start()

    def total(self, kind, stages, piece):
        total = self.grads[kind][piece].astype(F32)
        for stage in range(stages):
            count = self.count(stage)
            at = piece // (2 << stage)
            step = (at + 2 * count - 1 - self.mine // (2 << stage)) % count + 1
            self.copy(kind, stage, step).wait_recv()
            total += self.recv[stage][kind, at].astype(F32)
        return total

    def stage(self, kind, stage):
        @pl.loop(1, self.count(stage) + 1)
        def _(step):
            at = self.index(stage, step)
            self.held[stage][kind, at] = self.total(kind, stage, self.given(stage, step)).astype(BF)
            self.copy(kind, stage, step).start()

    def rest(self, kind, first):
        for stage in range(first, self.stages):
            self.stage(kind, stage)

    def collect(self, kind):
        return self.total(kind, self.stages, self.mine)

    def end(self, kinds):
        for kind in kinds:
            for stage in range(self.stages):
                @pl.loop(1, self.count(stage) + 1)
                def _(step):
                    self.copy(kind, stage, step).wait_send()

    @staticmethod
    def scratch(kinds, groups, held, span):
        stages = groups.bit_length() - 1
        buffers = [pltpu.VMEM((kinds, groups >> (k + 1), held, span), BF) for k in range(stages)]
        return buffers + buffers[1:] + [pltpu.SemaphoreType.DMA((2, kinds, stages, groups // 2 + 1))]


class GiveBack:
    def __init__(self, groups, rows, width, chosen, sent, recv, sems):
        self.groups, self.piece, self.width = groups, rows // groups, width
        self.halves = (self.piece // 2) % 8 == 0
        self.chosen, self.sent, self.recv, self.sems = chosen, sent, recv, sems
        self.mine = lax.axis_index("dp")

    def moved(self, step):
        peer = (self.mine + step) % self.groups
        return send(self.sent.at[peer], self.recv.at[self.mine], self.sems.at[0, step], self.sems.at[1, step], dp=peer)

    def start(self, packed):
        @pl.loop(0, self.groups)
        def _(step):
            peer = (self.mine + step) % self.groups
            rows = self.chosen[pl.ds(pl.multiple_of(peer * self.piece, 8), self.piece), :]
            values = dot(rows, packed[...], ((1,), (0,))).astype(BF)

            @pl.when(step > 0)
            def _():
                fold_into(self.sent, (peer,), values, self.halves)
                self.moved(step).start()

            @pl.when(step == 0)
            def _():
                fold_into(self.recv, (self.mine,), values, self.halves)

    def land(self, target):
        @pl.loop(1, self.groups)
        def _(step):
            self.moved(step).wait_recv()

        @pl.loop(0, self.groups)
        def _(peer):
            here = pl.ds(pl.multiple_of(peer * self.piece, 8), self.piece)
            target[here, :] = unfold(self.recv[peer], self.width, self.halves)

        @pl.loop(1, self.groups)
        def _(step):
            self.moved(step).wait_send()

    @staticmethod
    def scratch(groups, rows, width):
        piece = rows // groups
        halves = (piece // 2) % 8 == 0
        slab = (groups, piece // 2, 2 * width) if halves else (groups, piece, width)
        return [pltpu.VMEM(slab, BF)] * 2 + [pltpu.SemaphoreType.DMA((2, groups))]


class RowSum:
    def __init__(self, part, first, second, third, sems):
        self.part, self.first, self.second, self.third, self.sems = part, first, second, third, sems
        self.me, self.sibling, self.across, self.diagonal = place_of()

    def cross(self, b):
        return send(self.part.at[b, self.diagonal], self.first.at[b], self.sems.at[0, b], self.sems.at[1, b],
                    tensor=self.sibling)

    def near(self, b):
        return send(self.part.at[b, self.sibling], self.second.at[b], self.sems.at[2, b], self.sems.at[3, b],
                    tensor=self.sibling)

    def far(self, b):
        return send(self.first.at[b], self.third.at[b], self.sems.at[4, b], self.sems.at[5, b], tensor=self.across)

    def start(self, b):
        self.cross(b).start()
        self.near(b).start()

    def relay(self, b):
        self.cross(b).wait()
        self.first[b] = (self.part[b, self.across].astype(F32) + self.first[b].astype(F32)).astype(BF)
        self.far(b).start()

    def total(self, b):
        self.near(b).wait()
        self.far(b).wait()
        return self.part[b, self.me].astype(F32) + self.second[b].astype(F32) + self.third[b].astype(F32)

    @staticmethod
    def scratch(blocks, rows, columns):
        buffer = pltpu.VMEM((blocks, rows, columns), BF)
        return [pltpu.VMEM((blocks, 4, rows, columns), BF)] + [buffer] * 3 + [pltpu.SemaphoreType.DMA((6, blocks))]


class RowGather:
    def __init__(self, out, sems):
        self.out, self.sems = out, sems
        self.me, self.sibling, self.across, _ = place_of()

    def copy(self, b, kind, whose, peer):
        return send(self.out.at[b, whose], self.out.at[b, whose], self.sems.at[2 * kind, b],
                    self.sems.at[2 * kind + 1, b], tensor=peer)

    def start(self, b):
        self.copy(b, 0, self.me, self.across).start()
        self.copy(b, 1, self.me, self.sibling).start()

    def relay(self, b):
        self.copy(b, 0, self.me, self.across).wait_recv()
        self.copy(b, 2, self.across, self.sibling).start()

    def land(self, b):
        self.copy(b, 1, self.me, self.sibling).wait_recv()
        self.copy(b, 2, self.across, self.sibling).wait_recv()

    def end(self, b):
        self.copy(b, 0, self.me, self.across).wait_send()
        self.copy(b, 1, self.me, self.sibling).wait_send()
        self.copy(b, 2, self.across, self.sibling).wait_send()


CHUNK = 256


def mid_kernel(groups, blocks, grad_scale, context, packed, full_out, up_w, up_bias, down_w, cot_folded, v0, v1, v2, v3, v4, v5,
               d_low, d_own, small, gate_grad, value_grad, down_grad, folded,
               normed_low, slope_term, gelu_term, gated, d_gate, d_value, unit_full, rs_full, unit_own, rs_own, d_mixed,
               mixed, whole_grad, down_pieces, cot_recv,
               part1, first1, second1, third1, sems1, part2, first2, second2, third2, sems2, sems3, sems4, c_sems,
               vector_rows, *sum_scratch):
    me, sibling, across, diagonal = place_of()
    columns = packed.shape[1]
    width = columns // 4
    quarter = BLOCK // 4
    held = down_pieces.shape[1]
    enter([sibling, across, diagonal], groups)
    swaps = [
        send(cot_folded.at[peer], cot_recv.at[me], c_sems.at[0, k], c_sems.at[1, k], tensor=peer)
        for k, peer in enumerate((across, diagonal, sibling))
    ]
    for swap in swaps:
        swap.start()
    cot_recv[me] = cot_folded[me]
    ffn = RowSum(part1, first1, second1, third1, sems1)
    back_sum = RowSum(part2, first2, second2, third2, sems2)
    mixed_gather = RowGather(mixed, sems3)
    hidden_gather = RowGather(d_low, sems4)
    sums = GroupSum(groups, (down_pieces,), sum_scratch)
    small[...] = jnp.zeros_like(small)
    for k, vector in enumerate((v0, v1, v2, v3, v4, v5)):
        vector_rows[k : k + 1, :] = vector[...].astype(F32).reshape(1, columns)
    out_bias, first_gain, first_shift, down_bias, second_gain, second_shift = (
        vector_rows.at[k : k + 1] for k in range(6)
    )

    def add_small(row, values):
        small[row : row + 1, :] += jnp.sum(values, axis=0, keepdims=True) * grad_scale

    def ahead(b, c):
        here = slice(b * BLOCK + c * CHUNK, b * BLOCK + (c + 1) * CHUNK)
        inner = slice(c * CHUNK, (c + 1) * CHUNK)
        hidden = packed[here, :].astype(F32) + (dot(context[here, :], full_out[...], ((1,), (0,))) + out_bias[...])
        unit, rs = norm_unit(hidden)
        unit_full[inner, :] = unit
        rs_full[inner, :] = rs
        low = (unit * first_gain[...] + first_shift[...]).astype(BF)
        normed_low[here, :] = low
        gate = dot(low, up_w[0], ((1,), (0,))) + up_bias[0:1, :].astype(F32)
        value = dot(low, up_w[1], ((1,), (0,))) + up_bias[1:2, :].astype(F32)
        half_erf = 0.5 * (1.0 + lax.erf(gate * (0.5**0.5)))
        gelu = gate * half_erf
        slope = half_erf + gate * jnp.exp(-0.5 * gate * gate) * ((2.0 * jnp.pi) ** (-0.5))
        slope_term[here, :] = value * slope
        gelu_term[here, :] = gelu
        low_gated = (gelu * value).astype(BF)
        gated[here, :] = low_gated
        out = dot(low_gated, down_w[...], ((1,), (0,))).astype(BF)
        for k in range(CHUNK // quarter):
            part1[b, c * (CHUNK // quarter) + k] = out[k * quarter : (k + 1) * quarter]

    def keep_own(b):
        mine = pl.ds(pl.multiple_of(me * quarter, quarter), quarter)
        unit_own[b] = unit_full[mine, :]
        rs_own[b] = rs_full[mine, :]
        ffn.start(b)

    def turn(b):
        if b == 0:
            for swap in swaps:
                swap.wait_recv()
        values = unit_own[b] * first_gain[...] + first_shift[...] + (ffn.total(b) + down_bias[...])
        unit, rs = norm_unit(values)
        out = (unit * second_gain[...] + second_shift[...]).astype(BF)
        for u in range(4):
            fold_into(folded, (u, b), out[:, u * width : (u + 1) * width], True)
        cot_rows = jnp.concatenate([unfold(cot_recv[s, b], width, True) for s in range(4)], axis=1).astype(F32)
        d_rows = norm_back(cot_rows * second_gain[...], unit, rs)
        d_mixed[b] = d_rows
        mixed[b, me] = d_rows.astype(BF)
        mixed_gather.start(b)
        add_small(3, d_rows)
        add_small(4, cot_rows * unit)
        add_small(5, cot_rows)

    def astern(b):
        mixed_gather.land(b)
        for c in range(BLOCK // CHUNK):
            here = slice(b * BLOCK + c * CHUNK, b * BLOCK + (c + 1) * CHUNK)
            count = CHUNK // quarter
            d_rows = jnp.concatenate([mixed[b, c * count + k] for k in range(count)], axis=0)
            d_gated = dot(d_rows, down_w[...], ((1,), (1,)))
            gate_rows = (d_gated * slope_term[here, :]).astype(BF)
            value_rows = (d_gated * gelu_term[here, :]).astype(BF)
            d_gate[here, :] = gate_rows
            d_value[here, :] = value_rows
            add_small(8, gate_rows.astype(F32))
            add_small(9, value_rows.astype(F32))
            out = dot(gate_rows, up_w[0], ((1,), (1,))) + dot(value_rows, up_w[1], ((1,), (1,)))
            out = out.astype(BF)
            for k in range(count):
                part2[b, c * count + k] = out[k * quarter : (k + 1) * quarter]
        back_sum.start(b)

    def finish(b):
        d_normed = d_mixed[b] + back_sum.total(b)
        d_hidden = norm_back(d_normed * first_gain[...], unit_own[b], rs_own[b])
        d_own[b] = d_hidden
        d_low[b, me] = d_hidden.astype(BF)
        hidden_gather.start(b)
        add_small(0, d_hidden)
        add_small(1, d_normed * unit_own[b])
        add_small(2, d_normed)

    def weight_grad(left, right, pieces):
        span = right.shape[1]
        for c in range(span // CHUNK):
            lanes = slice(c * CHUNK, (c + 1) * CHUNK)
            whole_grad[:, lanes] = dot(left, right[:, lanes], ((0,), (0,)))
        for g in range(groups):
            pieces[g] = (whole_grad[g * held : (g + 1) * held, :] * grad_scale).astype(BF)

    last = blocks - 1
    for b in range(blocks):
        ahead(b, 0)
        if b >= 1:
            ffn.relay(b - 1)
        if b >= 2:
            turn(b - 2)
        ahead(b, 1)
        keep_own(b)
        if b >= 2:
            mixed_gather.relay(b - 2)
    ffn.relay(last)
    if blocks > 1:
        turn(last - 1)
    turn(last)
    if blocks > 1:
        mixed_gather.relay(last - 1)
    for b in range(blocks):
        if b == last:
            mixed_gather.relay(last)
        astern(b)
        if b >= 1:
            back_sum.relay(b - 1)
    back_sum.relay(last)
    d_mixed_rows = jnp.concatenate([mixed[b, k] for b in range(blocks) for k in range(4)], axis=0)
    weight_grad(d_mixed_rows, gated, down_pieces)
    sums.start(0)
    finish(0)
    weight_grad(normed_low[...], d_gate, gate_grad)
    if blocks > 1:
        finish(1)
    weight_grad(normed_low[...], d_value, value_grad)
    for b in range(2, blocks):
        finish(b)
    sums.stage(0, 1)
    for b in range(blocks):
        hidden_gather.relay(b)
    sums.rest(0, 2)
    for b in range(blocks):
        hidden_gather.land(b)
    down_grad[...] = sums.collect(0)
    for b in range(blocks):
        mixed_gather.end(b)
        hidden_gather.end(b)
    for swap in swaps:
        swap.wait_send()
    sums.end((0,))


def mid(groups, grad_scale, args, number):
    context, up_w, cot_folded = args[0], args[3], args[6]
    rows, columns = context.shape
    units = up_w.shape[2]
    held = columns // groups
    blocks = rows // BLOCK
    quarter = BLOCK // 4
    own = (blocks, quarter, columns)
    dma = pltpu.SemaphoreType.DMA
    outs = (
        shape((blocks, 4, quarter, columns), BF),
        shape(own, F32),
        shape((16, columns), F32),
        shape((groups, held, units), BF),
        shape((groups, held, units), BF),
        shape((held, units), F32),
        shape(cot_folded.shape, BF),
    )
    return call(
        functools.partial(mid_kernel, groups, blocks, grad_scale),
        number,
        outs,
        [
            pltpu.VMEM((rows, columns), BF),
            pltpu.VMEM((rows, units), F32),
            pltpu.VMEM((rows, units), F32),
            pltpu.VMEM((rows, units), BF),
            pltpu.VMEM((rows, units), BF),
            pltpu.VMEM((rows, units), BF),
            pltpu.VMEM((BLOCK, columns), F32),
            pltpu.VMEM((BLOCK, 1), F32),
            pltpu.VMEM(own, F32),
            pltpu.VMEM((blocks, quarter, 1), F32),
            pltpu.VMEM(own, F32),
            pltpu.VMEM((blocks, 4, quarter, columns), BF),
            pltpu.VMEM((columns, units), F32),
            pltpu.VMEM((groups, held, units), BF),
            pltpu.VMEM(cot_folded.shape, BF),
        ]
        + RowSum.scratch(blocks, quarter, columns)
        + RowSum.scratch(blocks, quarter, columns)
        + [dma((6, blocks)), dma((6, blocks)), dma((2, 3)), pltpu.VMEM((6, columns), F32)]
        + GroupSum.scratch(1, groups, held, units),
        args,
    )


def back_kernel(groups, blocks, grad_scale, dh_low, dh_own, qkv, lse, seq_row, context, packed_in, qkv_w,
                out_w, gate_grad, value_grad, folded, small, taking,
                layer_out, input_grad, up_grad, qkv_grad, out_grad, small_out, qv_out, up_out,
                d_rows, d_part, late_sum, late, cols, one, two, three, packed, ssent, srecv, swide, x_sems, s_sems, w_sems,
                start_col, chosen, weight_here, returned, landed, load_sem, r_sems,
                sent, recv, a_sems, sent2, recv5, a_sems2, *sum_scratch):
    me, sibling, across, diagonal = place_of()
    mine = lax.axis_index("dp")
    width, rows = input_grad.shape
    heads = width // HEAD_DIM
    held = late.shape[1]
    quarter = BLOCK // 4
    load = pltpu.make_async_copy(qkv_w, weight_here, load_sem.at[0])
    load.start()
    load_rows = pltpu.make_async_copy(taking, chosen, load_sem.at[1])
    load_rows.start()
    enter([sibling, across, diagonal], groups)
    half_scratch = len(sum_scratch) // 2
    sums = GroupSum(groups, (gate_grad, value_grad), sum_scratch[:half_scratch])
    late_sums = GroupSum(groups, (late,), sum_scratch[half_scratch:])
    giving = GiveBack(groups, rows, width, chosen, sent, recv, a_sems)
    giving_result = GiveBack(groups, rows, width, chosen, sent2, recv5, a_sems2)
    sums.start(0)
    sums.start(1)
    returns = [
        send(folded.at[peer], returned.at[me], r_sems.at[0, k], r_sems.at[1, k], tensor=peer)
        for k, peer in enumerate((across, diagonal, sibling))
    ]
    for swap in returns:
        swap.start()
    returned[me] = folded[me]
    def cross(b):
        return send(cols.at[diagonal, b], one.at[b], x_sems.at[0, b], x_sems.at[1, b], tensor=sibling)

    def near(b):
        return send(cols.at[sibling, b], two.at[b], x_sems.at[2, b], x_sems.at[3, b], tensor=sibling)

    def far(b):
        return send(one.at[b], three.at[b], x_sems.at[4, b], x_sems.at[5, b], tensor=across)

    def relay(b):
        cross(b).wait()
        one[b] = (cols[across, b].astype(F32) + one[b].astype(F32)).astype(BF)
        far(b).start()

    to_column(seq_row, start_col, 0)
    late_sum[:, 3 * width :] = dot(dh_low[...], context[...], ((0,), (0,)))
    load.wait()
    ssent[...] = small[...]

    @pl.loop(0, blocks)
    def _(b):
        here = pl.ds(pl.multiple_of(b * BLOCK, BLOCK), BLOCK)
        dh = dh_low[here, :]
        d_context = dot(dh, out_w[...], ((1,), (1,))).astype(BF)
        same = start_col[here, 0:1] == seq_row[0:1, here]
        distance = key_distance()
        for h in range(heads):
            lanes = slice(h * HEAD_DIM, (h + 1) * HEAD_DIM)
            queries = qkv[0, here, lanes]
            keys = qkv[1, here, lanes]
            values = qkv[2, here, lanes]
            d_rows_out = d_context[:, lanes]
            scored = scores_by_key(keys, queries, slope_of(me * heads + h), distance, same)
            probs = jnp.exp(scored - lse[b, h : h + 1, :])
            d_probs = dot(values, d_rows_out, ((1,), (1,)))
            d_rows[2, here, lanes] = dot(probs.astype(BF), d_rows_out, ((1,), (0,))).astype(BF)
            center = jnp.sum(probs * d_probs, axis=0, keepdims=True)
            d_scores = (probs * (d_probs - center)).astype(BF)
            d_rows[1, here, lanes] = (dot(d_scores, queries, ((1,), (0,))) * (HEAD_DIM**-0.5)).astype(BF)
            turned = dot(keys.T, d_scores, ((1,), (0,))) * (HEAD_DIM**-0.5)
            d_rows[0, here, lanes] = turned.T.astype(BF)
        part = dot(d_rows[0, here, :], weight_here[0], ((1,), (0,)))
        part += dot(d_rows[1, here, :], weight_here[1], ((1,), (0,)))
        part += dot(d_rows[2, here, :], weight_here[2], ((1,), (0,)))
        d_part[...] = part
        d_part[pl.ds(pl.multiple_of(me * quarter, quarter), quarter), :] += dh_own[b]
        for u in range(4):
            fold_into(cols, (u, b), d_part[:, u * width : (u + 1) * width].astype(BF), True)
        cross(b).start()
        near(b).start()
        last = small.shape[0] - 6
        for k, c in enumerate((0, 2)):
            bias = jnp.sum(d_rows[c, here, :].astype(F32), axis=0, keepdims=True) * grad_scale
            ssent[last : last + 1, k * 2 * 128 : k * 2 * 128 + width] += bias
        relay(b)

        @pl.when(b == 0)
        def _():
            sums.stage(0, 1)

        @pl.when(b == 1)
        def _():
            load_rows.wait()
            for swap in returns:
                swap.wait_recv()
            for q in range(blocks):
                for s in range(4):
                    start = q * BLOCK + s * quarter
                    packed[start : start + quarter, :] = unfold(returned[s, q], width, True)
            sums.rest(0, 2)
            giving_result.start(packed)

        @pl.when(b == 2)
        def _():
            sums.stage(1, 1)

    for c in range(3):
        late_sum[:, c * width : (c + 1) * width] = dot(packed_in[...], d_rows[c], ((0,), (0,)))
    for g in range(groups):
        late[g] = (late_sum[g * held : (g + 1) * held, :] * grad_scale).astype(BF)

    late_sums.start(0)
    sums.rest(1, 2)
    swaps = [
        send(ssent, srecv.at[me], s_sems.at[0, k], s_sems.at[1, k], tensor=peer)
        for k, peer in enumerate((sibling, across, diagonal))
    ]
    for swap in swaps:
        swap.start()
    srecv[me] = ssent[...]

    for b in range(blocks):
        near(b).wait()
        far(b).wait_recv()
        total = cols[me, b].astype(F32) + two[b].astype(F32) + three[b].astype(F32)
        packed[b * BLOCK : (b + 1) * BLOCK, :] = unfold(total.astype(BF), width, True)
    giving.start(packed)

    for swap in swaps:
        swap.wait_recv()
    shared = small.shape[0] // 2
    swide[mine, 0:shared] = srecv[0, 0:shared] + srecv[1, 0:shared] + srecv[2, 0:shared] + srecv[3, 0:shared]
    swide[mine, shared:] = ssent[shared:, :]

    def spread(step):
        peer = (mine + step) % groups
        return send(swide.at[mine], swide.at[mine], w_sems.at[0, step], w_sems.at[1, step], dp=peer)

    @pl.loop(1, groups)
    def _(step):
        spread(step).start()

    late_sums.rest(0, 1)
    up_grad[0] = sums.collect(0)
    up_grad[1] = sums.collect(1)
    giving_result.land(landed)
    layer_out[...] = landed[...].T

    @pl.loop(1, groups)
    def _(step):
        spread(step).wait_recv()

    for swap in swaps:
        swap.wait_send()
    ssent[...] = swide[0]

    @pl.loop(1, groups)
    def _(peer):
        ssent[...] += swide[peer]

    small_out[...] = ssent[0:8, :]
    up_out[...] = ssent[8:10, :]
    for k in range(2):
        qv_out[k : k + 1, :] = ssent[10:11, k * 256 : k * 256 + width]
    total = late_sums.collect(0)
    for c in range(3):
        qkv_grad[c] = total[:, c * width : (c + 1) * width]
    out_grad[...] = total[:, 3 * width :].T
    giving.land(landed)
    input_grad[...] = landed[...].T
    for b in range(blocks):
        far(b).wait_send()
    for copy in returns:
        copy.wait_send()
    sums.end((0, 1))
    late_sums.end((0,))

    @pl.loop(1, groups)
    def _(step):
        spread(step).wait_send()


def back(groups, grad_scale, args, small, number):
    dh_low, qkv, qkv_w, grad, folded = args[0], args[2], args[7], args[9], args[11]
    rows, columns = dh_low.shape
    width = qkv.shape[2]
    held, units = grad.shape[1:]
    blocks = rows // BLOCK
    half = (blocks, BLOCK // 2, 2 * width)
    dma = pltpu.SemaphoreType.DMA
    outs = (
        shape((width, rows), BF),
        shape((width, rows), BF),
        shape((2, held, units), F32),
        shape((3, held, width), F32),
        shape((width, held), F32),
        shape((8, columns), F32),
        shape((2, width), F32),
        shape((2, units), F32),
    )
    return call(
        functools.partial(back_kernel, groups, blocks, grad_scale),
        number,
        outs,
        [
            pltpu.VMEM((3, rows, width), BF),
            pltpu.VMEM((BLOCK, columns), F32),
            pltpu.VMEM((columns, 4 * width), F32),
            pltpu.VMEM((groups, held, 4 * width), BF),
            pltpu.VMEM((4,) + half, BF),
            pltpu.VMEM(half, BF),
            pltpu.VMEM(half, BF),
            pltpu.VMEM(half, BF),
            pltpu.VMEM((rows, width), BF),
            pltpu.VMEM(small.shape, F32),
            pltpu.VMEM((4,) + small.shape, F32),
            pltpu.VMEM((groups,) + small.shape, F32),
            dma((6, blocks)),
            dma((2, 3)),
            dma((2, groups)),
            pltpu.VMEM((rows, 8), jnp.int32),
            pltpu.VMEM((rows, rows), BF),
            pltpu.VMEM(qkv_w.shape, BF),
            pltpu.VMEM(folded.shape, BF),
            pltpu.VMEM((rows, width), BF),
            dma((2,)),
            dma((2, 3)),
        ]
        + GiveBack.scratch(groups, rows, width)
        + GiveBack.scratch(groups, rows, width)
        + GroupSum.scratch(2, groups, held, units)
        + GroupSum.scratch(1, groups, held, 4 * width),
        args,
        apart=(7, 13),
    )


def on_device(
    tokens,
    cotangent,
    seq_start,
    row_place,
    qkv_weight,
    qv_bias,
    out_weight,
    out_bias,
    first_gain,
    first_shift,
    up_weight,
    up_bias,
    down_weight,
    down_bias,
    second_gain,
    second_shift,
):
    row_count, width = tokens.shape
    columns = qkv_weight.shape[1]
    groups = lax.axis_size("dp")
    grad_scale = (row_count * groups) ** (-0.5)
    seq_row = seq_start.reshape(1, row_count)
    weight_turned = qkv_weight.transpose(0, 2, 1)
    packed_in, cot_folded, full_out, qkv_rows, log_total, context, wide_context, taking = front(
        groups, (tokens.T, cotangent.T, row_place, seq_row, weight_turned, qv_bias, out_weight), 0
    )
    d_low, d_own, small, gate_grad, value_grad, down_grad, folded = mid(
        groups,
        grad_scale,
        (
            wide_context,
            packed_in,
            full_out.reshape(columns, columns),
            up_weight,
            up_bias,
            down_weight,
            cot_folded,
            out_bias,
            first_gain,
            first_shift,
            down_bias,
            second_gain,
            second_shift,
        ),
        1,
    )
    layer_out, input_grad, up_grad, qkv_grad, out_grad, sums, qv_bias_grad, up_bias_grad = back(
        groups,
        grad_scale,
        (
            d_low.reshape(row_count, columns),
            d_own,
            qkv_rows,
            log_total,
            seq_row,
            context,
            packed_in,
            weight_turned,
            out_weight,
            gate_grad,
            value_grad,
            folded,
            small,
            taking,
        ),
        small,
        2,
    )
    rows_here = columns // groups
    sums_here = lax.dynamic_slice_in_dim(sums[:6], lax.axis_index("dp") * rows_here, rows_here, 1)
    return (
        layer_out.T,
        input_grad.T,
        qkv_grad,
        qv_bias_grad,
        out_grad,
        sums_here[0],
        sums_here[1],
        sums_here[2],
        up_grad,
        up_bias_grad,
        down_grad.T,
        sums_here[3],
        sums_here[4],
        sums_here[5],
    )


def solution(mesh):
    return jax.shard_map(
        on_device,
        mesh=mesh,
        in_specs=(
            P("dp", "tensor"),
            P("dp", "tensor"),
            P("dp"),
            P("dp", None),
            P(None, None, "tensor"),
            P(None, "tensor"),
            P("tensor", None),
            P(),
            P(),
            P(),
            P(None, None, "tensor"),
            P(None, "tensor"),
            P("tensor", None),
            P(),
            P(),
            P(),
        ),
        out_specs=(
            P("dp", "tensor"),
            P("dp", "tensor"),
            P(None, "dp", "tensor"),
            P(None, "tensor"),
            P("tensor", "dp"),
            P("dp"),
            P("dp"),
            P("dp"),
            P(None, "dp", "tensor"),
            P(None, "tensor"),
            P("tensor", "dp"),
            P("dp"),
            P("dp"),
            P("dp"),
        ),
        check_vma=False,
    )
```

```python
import functools

import jax
import jax.numpy as jnp
from jax import lax
from jax.experimental import pallas as pl
from jax.experimental.pallas import tpu as pltpu
from jax.sharding import PartitionSpec as P

HEADS = 12
HEAD_DIM = 64
BLOCK = 512
BF = jnp.bfloat16
F32 = jnp.float32
MESH = pl.DeviceIdType.MESH
VMEM_LIMIT = 67043328


def dot(a, b, dims):
    return lax.dot_general(a, b, (dims, ((), ())), preferred_element_type=F32)


def place_of():
    me = lax.axis_index("tensor")
    core = me % 2
    side = me // 2
    sibling = side * 2 + (1 - core)
    across = (1 - side) * 2 + core
    diagonal = (1 - side) * 2 + (1 - core)
    return me, sibling, across, diagonal


def enter(devices, groups):
    barrier = pltpu.get_barrier_semaphore()
    count = len(devices)
    for device in devices:
        pl.semaphore_signal(barrier, inc=1, device_id={"tensor": device}, device_id_type=MESH)
    if groups:
        mine = lax.axis_index("dp")

        @pl.loop(1, groups)
        def _(step):
            pl.semaphore_signal(barrier, inc=1, device_id={"dp": (mine + step) % groups}, device_id_type=MESH)

        count += groups - 1
    pl.semaphore_wait(barrier, count)


def send(source, target, send_sem, recv_sem, **where):
    return pltpu.make_async_remote_copy(
        src_ref=source, dst_ref=target, send_sem=send_sem, recv_sem=recv_sem, device_id=where, device_id_type=MESH
    )


def fold_into(buffer, index, values, halves):
    width = values.shape[1]
    if not halves:
        buffer[index] = values
        return
    half = values.shape[0] // 2
    buffer[index + (slice(None), slice(0, width))] = values[:half]
    buffer[index + (slice(None), slice(width, 2 * width))] = values[half:]


def unfold(values, width, halves):
    if not halves:
        return values
    return jnp.concatenate([values[:, :width], values[:, width:]], axis=0)


def call(kernel, number, outs, scratch, args, apart=(), apart_outs=()):
    specs = [pl.BlockSpec(memory_space=pl.ANY if k in apart else pltpu.VMEM) for k in range(len(args))]
    return pl.pallas_call(
        kernel,
        out_shape=outs,
        in_specs=specs,
        out_specs=tuple(
            pl.BlockSpec(memory_space=pl.ANY if k in apart_outs else pltpu.VMEM) for k in range(len(outs))
        ),
        scratch_shapes=scratch,
        compiler_params=pltpu.CompilerParams(
            collective_id=number, has_side_effects=True, vmem_limit_bytes=VMEM_LIMIT
        ),
    )(*args)


def shape(dims, kind):
    return jax.ShapeDtypeStruct(dims, kind)


def to_column(row, column, where):
    for k in range(row.shape[1] // 128):
        piece = jnp.broadcast_to(row[0:1, k * 128 : (k + 1) * 128], (8, 128))
        column[k * 128 : (k + 1) * 128, where : where + 1] = piece.T[:, 0:1]


def slope_of(index):
    value = jnp.float32(2.0 ** (-8.0 / HEADS))
    for head in range(1, HEADS):
        value = jnp.where(index == head, jnp.float32(2.0 ** (-8.0 * (head + 1) / HEADS)), value)
    return value


def key_distance():
    keys = lax.broadcasted_iota(jnp.int32, (BLOCK, BLOCK), 0)
    asks = lax.broadcasted_iota(jnp.int32, (BLOCK, BLOCK), 1)
    return jnp.abs(keys - asks).astype(F32)


def scores_by_key(keys, queries, slope, distance, same):
    raw = dot(keys, queries, ((1,), (1,))) * (HEAD_DIM**-0.5) - slope * distance
    return jnp.where(same, raw, -1e30)


class HeadGather:
    def __init__(self, wide, sems):
        self.wide, self.sems = wide, sems
        self.me, self.sibling, self.across, _ = place_of()

    def copy(self, b, kind, whose, peer):
        return send(self.wide.at[whose, b], self.wide.at[whose, b], self.sems.at[2 * kind, b],
                    self.sems.at[2 * kind + 1, b], tensor=peer)

    def start(self, b, values):
        fold_into(self.wide, (self.me, b), values, True)
        self.copy(b, 0, self.me, self.across).start()
        self.copy(b, 1, self.me, self.sibling).start()

    def relay(self, b):
        self.copy(b, 0, self.me, self.across).wait_recv()
        self.copy(b, 2, self.across, self.sibling).start()

    def land(self, b, out, width):
        self.copy(b, 1, self.me, self.sibling).wait_recv()
        self.copy(b, 2, self.across, self.sibling).wait_recv()
        for s in range(4):
            out[b * BLOCK : (b + 1) * BLOCK, s * width : (s + 1) * width] = unfold(self.wide[s, b], width, True)

    def end(self, b):
        self.copy(b, 0, self.me, self.across).wait_send()
        self.copy(b, 1, self.me, self.sibling).wait_send()
        self.copy(b, 2, self.across, self.sibling).wait_send()


def front_kernel(groups, blocks, tokens, cot, place_row, seq_row, qkv_w, qv_bias, out_w,
                 packed_out, cot_out, full_out, qkv, lse, context, wide_context, taking,
                 tokens_turned, cot_turned, tokens_here, cot_here, weight_here, start_col, chosen, taken, sent, recv, arrived,
                 wide, wide_heads, local_sems, group_sems, gather_sems, head_sems, out_sems):
    me, sibling, across, diagonal = place_of()
    mine = lax.axis_index("dp")
    rows, width = tokens_here.shape
    heads = width // HEAD_DIM
    piece = rows // groups
    halves = (piece // 2) % 8 == 0
    quarter = BLOCK // 4
    loads = [
        pltpu.make_async_copy(source, target, local_sems.at[k])
        for k, (source, target) in enumerate(((tokens, tokens_turned), (cot, cot_turned), (qkv_w, weight_here)))
    ]
    for load in loads:
        load.start()
    enter([sibling, across, diagonal], groups)

    def moved(kind, step):
        peer = (mine + step) % groups
        return send(sent.at[kind, peer], recv.at[kind, mine], group_sems.at[0, kind, step],
                    group_sems.at[1, kind, step], dp=peer)

    def give(kind, source):
        @pl.loop(1, groups)
        def _(step):
            peer = (mine + step) % groups
            values = source[pl.ds(pl.multiple_of(peer * piece, 8), piece), :]
            fold_into(sent, (kind, peer), values, halves)
            moved(kind, step).start()

        values = source[pl.ds(pl.multiple_of(mine * piece, 8), piece), :]
        fold_into(recv, (kind, mine), values, halves)

    loads[0].wait()
    tokens_here[...] = tokens_turned[...].T
    give(0, tokens_here)
    out_far = send(out_w, full_out.at[me], out_sems.at[0], out_sems.at[1], tensor=across)
    out_near = send(out_w, full_out.at[me], out_sems.at[2], out_sems.at[3], tensor=sibling)
    out_pass = send(full_out.at[across], full_out.at[across], out_sems.at[4], out_sems.at[5], tensor=sibling)
    out_far.start()
    out_near.start()
    loads[1].wait()
    cot_here[...] = cot_turned[...].T
    full_out[me] = out_w[...]
    to_column(seq_row, start_col, 0)
    for b in range(blocks):
        ids = lax.broadcasted_iota(jnp.int32, (BLOCK, rows), 0) + b * BLOCK
        chosen[b * BLOCK : (b + 1) * BLOCK, :] = jnp.where(ids == place_row[...], 1.0, 0.0).astype(BF)

    to_column(place_row, start_col, 1)
    for b in range(blocks):
        ids = lax.broadcasted_iota(jnp.int32, (BLOCK, rows), 1)
        here = slice(b * BLOCK, (b + 1) * BLOCK)
        taken[here, :] = jnp.where(ids == start_col[here, 1:2], 1.0, 0.0).astype(BF)
    store = pltpu.make_async_copy(taken, taking, local_sems.at[3])
    store.start()

    def placed(b):
        return dot(chosen[b * BLOCK : (b + 1) * BLOCK, :], arrived[...], ((1,), (0,))).astype(BF)

    out_far.wait_recv()
    out_pass.start()

    def land(kind):
        @pl.loop(1, groups)
        def _(step):
            moved(kind, step).wait_recv()

        @pl.loop(0, groups)
        def _(peer):
            arrived[pl.ds(pl.multiple_of(peer * piece, 8), piece), :] = unfold(recv[kind, peer], width, halves)

    token_gather = HeadGather(wide, gather_sems)
    head_gather = HeadGather(wide_heads, head_sems)
    land(0)
    for b in range(blocks):
        token_gather.start(b, placed(b))
        if b >= 1:
            token_gather.relay(b - 1)
    give(1, cot_here)
    loads[2].wait()

    def attend(b):
        here = slice(b * BLOCK, (b + 1) * BLOCK)
        token_gather.land(b, packed_out, width)
        for k in range(3):
            part = dot(packed_out[here, :], weight_here[k], ((1,), (1,)))
            if k != 1:
                part += qv_bias[k // 2 : k // 2 + 1, :].astype(F32)
            qkv[k, here, :] = part.astype(BF)
        same = start_col[here, 0:1] == seq_row[0:1, here]
        distance = key_distance()
        for h in range(heads):
            lanes = slice(h * HEAD_DIM, (h + 1) * HEAD_DIM)
            scored = scores_by_key(qkv[1, here, lanes], qkv[0, here, lanes], slope_of(me * heads + h), distance, same)
            top = jnp.max(scored, axis=0, keepdims=True)
            raised = jnp.exp(scored - top)
            total = jnp.sum(raised, axis=0, keepdims=True)
            lse[b, h : h + 1, :] = top + jnp.log(total)
            probs = (raised * (1.0 / total)).astype(BF)
            turned = dot(qkv[2, here, lanes].T, probs, ((1,), (0,)))
            context[here, lanes] = turned.T.astype(BF)
        head_gather.start(b, context[here, :])

    for b in range(blocks):
        if b == blocks - 1:
            token_gather.relay(b)
        attend(b)
        if b >= 1:
            head_gather.relay(b - 1)
    for b in range(blocks - 1):
        head_gather.land(b, wide_context, width)
    land(1)
    for b in range(blocks):
        cot_block = placed(b)
        for u in range(4):
            fold_into(cot_out, (u, b), cot_block[u * quarter : (u + 1) * quarter], True)
    head_gather.relay(blocks - 1)
    head_gather.land(blocks - 1, wide_context, width)
    for b in range(blocks):
        token_gather.end(b)
        head_gather.end(b)
    store.wait()
    out_near.wait()
    out_pass.wait()
    out_far.wait_send()
    for kind in range(2):
        @pl.loop(1, groups)
        def _(step):
            moved(kind, step).wait_send()


def front(groups, args, number):
    tokens, qkv_w, out_w = args[0], args[4], args[6]
    width, rows = tokens.shape
    piece = rows // groups
    blocks = rows // BLOCK
    heads = width // HEAD_DIM
    halves = (piece // 2) % 8 == 0
    slab = (2, groups, piece // 2, 2 * width) if halves else (2, groups, piece, width)
    here = pltpu.VMEM((rows, width), BF)
    wide = pltpu.VMEM((4, blocks, BLOCK // 2, 2 * width), BF)
    turned = pltpu.VMEM((width, rows), BF)
    dma = pltpu.SemaphoreType.DMA
    return call(
        functools.partial(front_kernel, groups, blocks),
        number,
        (
            shape((rows, 4 * width), BF),
            shape((4, blocks, BLOCK // 8, 2 * width), BF),
            shape((4,) + out_w.shape, BF),
            shape((3, rows, width), BF),
            shape((blocks, heads, BLOCK), F32),
            shape((rows, width), BF),
            shape((rows, 4 * width), BF),
            shape((rows, rows), BF),
        ),
        [
            turned,
            turned,
            here,
            here,
            pltpu.VMEM(qkv_w.shape, BF),
            pltpu.VMEM((rows, 8), jnp.int32),
            pltpu.VMEM((rows, rows), BF),
            pltpu.VMEM((rows, rows), BF),
            pltpu.VMEM(slab, BF),
            pltpu.VMEM(slab, BF),
            here,
            wide,
            wide,
            dma((4,)),
            dma((2, 2, groups)),
            dma((6, blocks)),
            dma((6, blocks)),
            dma((6,)),
        ],
        args,
        apart=(0, 1, 4),
        apart_outs=(7,),
    )


def norm_unit(values):
    center = values - jnp.mean(values, axis=-1, keepdims=True)
    rs = lax.rsqrt(jnp.mean(center * center, axis=-1, keepdims=True) + 1e-05)
    return center * rs, rs


def norm_back(weighted, unit, rs):
    inner = jnp.mean(weighted * unit, axis=-1, keepdims=True)
    return rs * (weighted - jnp.mean(weighted, axis=-1, keepdims=True) - unit * inner)


class GroupSum:
    def __init__(self, groups, grads, scratch, turned):
        self.groups, self.grads, self.turned = groups, grads, turned
        self.stages = groups.bit_length() - 1
        self.recv = scratch[: self.stages]
        self.held = (None,) + tuple(scratch[self.stages : 2 * self.stages - 1])
        self.sems = scratch[-1]
        mine = lax.axis_index("dp")
        self.mine = mine // 2 + mine % 2 * (groups // 2) if turned else mine

    def real(self, device):
        half = self.groups // 2
        return device % half * 2 + device // half if self.turned else device

    def count(self, stage):
        return self.groups >> (stage + 1)

    def index(self, stage, step):
        return (self.mine // (2 << stage) + step) % self.count(stage)

    def given(self, stage, step):
        bit = (self.mine // (1 << stage)) % 2
        low = self.mine % (1 << stage)
        return self.index(stage, step) * (2 << stage) + (1 - bit) * (1 << stage) + low

    def copy(self, stage, step):
        bit = (self.mine // (1 << stage)) % 2
        partner = self.mine + (1 - 2 * bit) * (1 << stage)
        at = self.index(stage, step)
        source = self.held[stage].at[at] if stage else self.grads.at[self.real(self.given(0, step))]
        return send(source, self.recv[stage].at[at], self.sems.at[0, stage, step], self.sems.at[1, stage, step],
                    dp=self.real(partner))

    def start(self):
        @pl.loop(1, self.count(0) + 1)
        def _(step):
            self.copy(0, step).start()

    def total(self, stages, piece):
        total = self.grads[self.real(piece)].astype(F32)
        for stage in range(stages):
            count = self.count(stage)
            at = piece // (2 << stage)
            step = (at + 2 * count - 1 - self.mine // (2 << stage)) % count + 1
            self.copy(stage, step).wait_recv()
            total += self.recv[stage][at].astype(F32)
        return total

    def stage(self, stage):
        @pl.loop(1, self.count(stage) + 1)
        def _(step):
            at = self.index(stage, step)
            self.held[stage][at] = self.total(stage, self.given(stage, step)).astype(BF)
            self.copy(stage, step).start()

    def rest(self, first):
        for stage in range(first, self.stages):
            self.stage(stage)

    def collect(self):
        return self.total(self.stages, self.mine)

    def end(self):
        for stage in range(self.stages):
            @pl.loop(1, self.count(stage) + 1)
            def _(step):
                self.copy(stage, step).wait_send()

    @staticmethod
    def scratch(groups, held, span):
        stages = groups.bit_length() - 1
        buffers = [pltpu.VMEM((groups >> (k + 1), held, span), BF) for k in range(stages)]
        return buffers + buffers[1:] + [pltpu.SemaphoreType.DMA((2, stages, groups // 2 + 1))]


def both_ways(groups, pair, scratch):
    half = len(scratch) // 2
    return [
        GroupSum(groups, grads, scratch[k * half : (k + 1) * half], k == 1) for k, grads in enumerate(pair)
    ]


class GiveBack:
    def __init__(self, groups, rows, width, chosen, sent, recv, sems):
        self.groups, self.piece, self.width = groups, rows // groups, width
        self.halves = (self.piece // 2) % 8 == 0
        self.chosen, self.sent, self.recv, self.sems = chosen, sent, recv, sems
        self.mine = lax.axis_index("dp")

    def moved(self, step):
        peer = (self.mine + step) % self.groups
        return send(self.sent.at[peer], self.recv.at[self.mine], self.sems.at[0, step], self.sems.at[1, step], dp=peer)

    def start(self, packed):
        @pl.loop(0, self.groups)
        def _(step):
            peer = (self.mine + step) % self.groups
            rows = self.chosen[pl.ds(pl.multiple_of(peer * self.piece, 8), self.piece), :]
            values = dot(rows, packed[...], ((1,), (0,))).astype(BF)

            @pl.when(step > 0)
            def _():
                fold_into(self.sent, (peer,), values, self.halves)
                self.moved(step).start()

            @pl.when(step == 0)
            def _():
                fold_into(self.recv, (self.mine,), values, self.halves)

    def land(self, target):
        @pl.loop(1, self.groups)
        def _(step):
            self.moved(step).wait_recv()

        @pl.loop(0, self.groups)
        def _(peer):
            here = pl.ds(pl.multiple_of(peer * self.piece, 8), self.piece)
            target[here, :] = unfold(self.recv[peer], self.width, self.halves)

        @pl.loop(1, self.groups)
        def _(step):
            self.moved(step).wait_send()

    @staticmethod
    def scratch(groups, rows, width):
        piece = rows // groups
        halves = (piece // 2) % 8 == 0
        slab = (groups, piece // 2, 2 * width) if halves else (groups, piece, width)
        return [pltpu.VMEM(slab, BF)] * 2 + [pltpu.SemaphoreType.DMA((2, groups))]


class RowSum:
    def __init__(self, part, first, second, third, sems):
        self.part, self.first, self.second, self.third, self.sems = part, first, second, third, sems
        self.me, self.sibling, self.across, self.diagonal = place_of()

    def cross(self, b):
        return send(self.part.at[b, self.diagonal], self.first.at[b], self.sems.at[0, b], self.sems.at[1, b],
                    tensor=self.sibling)

    def near(self, b):
        return send(self.part.at[b, self.sibling], self.second.at[b], self.sems.at[2, b], self.sems.at[3, b],
                    tensor=self.sibling)

    def far(self, b):
        return send(self.first.at[b], self.third.at[b], self.sems.at[4, b], self.sems.at[5, b], tensor=self.across)

    def start(self, b):
        self.cross(b).start()
        self.near(b).start()

    def relay(self, b):
        self.cross(b).wait()
        self.first[b] = (self.part[b, self.across].astype(F32) + self.first[b].astype(F32)).astype(BF)
        self.far(b).start()

    def total(self, b):
        self.near(b).wait()
        self.far(b).wait()
        return self.part[b, self.me].astype(F32) + self.second[b].astype(F32) + self.third[b].astype(F32)

    @staticmethod
    def scratch(blocks, rows, columns):
        buffer = pltpu.VMEM((blocks, rows, columns), BF)
        return [pltpu.VMEM((blocks, 4, rows, columns), BF)] + [buffer] * 3 + [pltpu.SemaphoreType.DMA((6, blocks))]


class RowGather:
    def __init__(self, out, sems):
        self.out, self.sems = out, sems
        self.me, self.sibling, self.across, _ = place_of()

    def copy(self, b, kind, whose, peer):
        return send(self.out.at[b, whose], self.out.at[b, whose], self.sems.at[2 * kind, b],
                    self.sems.at[2 * kind + 1, b], tensor=peer)

    def start(self, b):
        self.copy(b, 0, self.me, self.across).start()
        self.copy(b, 1, self.me, self.sibling).start()

    def relay(self, b):
        self.copy(b, 0, self.me, self.across).wait_recv()
        self.copy(b, 2, self.across, self.sibling).start()

    def land(self, b):
        self.copy(b, 1, self.me, self.sibling).wait_recv()
        self.copy(b, 2, self.across, self.sibling).wait_recv()

    def end(self, b):
        self.copy(b, 0, self.me, self.across).wait_send()
        self.copy(b, 1, self.me, self.sibling).wait_send()
        self.copy(b, 2, self.across, self.sibling).wait_send()


CHUNK = 256


def mid_kernel(groups, blocks, grad_scale, context, packed, full_out, up_w, up_bias, down_w, cot_folded, v0, v1, v2, v3, v4, v5,
               d_low, d_own, small, gate_grad, value_grad, down_grad, folded,
               normed_low, slope_term, gelu_term, gated, d_gate, d_value, unit_full, rs_full, unit_own, rs_own, d_mixed,
               mixed, whole_grad, down_left, down_right, cot_recv,
               part1, first1, second1, third1, sems1, part2, first2, second2, third2, sems2, sems3, sems4, c_sems,
               vector_rows, *sum_scratch):
    me, sibling, across, diagonal = place_of()
    columns = packed.shape[1]
    width = columns // 4
    quarter = BLOCK // 4
    held = down_left.shape[1]
    enter([sibling, across, diagonal], groups)
    swaps = [
        send(cot_folded.at[peer], cot_recv.at[me], c_sems.at[0, k], c_sems.at[1, k], tensor=peer)
        for k, peer in enumerate((across, diagonal, sibling))
    ]
    for swap in swaps:
        swap.start()
    cot_recv[me] = cot_folded[me]
    ffn = RowSum(part1, first1, second1, third1, sems1)
    back_sum = RowSum(part2, first2, second2, third2, sems2)
    mixed_gather = RowGather(mixed, sems3)
    hidden_gather = RowGather(d_low, sems4)
    sums = both_ways(groups, (down_left, down_right), sum_scratch)
    small[...] = jnp.zeros_like(small)
    for k, vector in enumerate((v0, v1, v2, v3, v4, v5)):
        vector_rows[k : k + 1, :] = vector[...].astype(F32).reshape(1, columns)
    out_bias, first_gain, first_shift, down_bias, second_gain, second_shift = (
        vector_rows.at[k : k + 1] for k in range(6)
    )

    def add_small(row, values):
        small[row : row + 1, :] += jnp.sum(values, axis=0, keepdims=True) * grad_scale

    def ahead(b, c):
        here = slice(b * BLOCK + c * CHUNK, b * BLOCK + (c + 1) * CHUNK)
        inner = slice(c * CHUNK, (c + 1) * CHUNK)
        hidden = packed[here, :].astype(F32) + (dot(context[here, :], full_out[...], ((1,), (0,))) + out_bias[...])
        unit, rs = norm_unit(hidden)
        unit_full[inner, :] = unit
        rs_full[inner, :] = rs
        low = (unit * first_gain[...] + first_shift[...]).astype(BF)
        normed_low[here, :] = low
        gate = dot(low, up_w[0], ((1,), (0,))) + up_bias[0:1, :].astype(F32)
        value = dot(low, up_w[1], ((1,), (0,))) + up_bias[1:2, :].astype(F32)
        half_erf = 0.5 * (1.0 + lax.erf(gate * (0.5**0.5)))
        gelu = gate * half_erf
        slope = half_erf + gate * jnp.exp(-0.5 * gate * gate) * ((2.0 * jnp.pi) ** (-0.5))
        slope_term[here, :] = value * slope
        gelu_term[here, :] = gelu
        low_gated = (gelu * value).astype(BF)
        gated[here, :] = low_gated
        out = dot(low_gated, down_w[...], ((1,), (0,))).astype(BF)
        for k in range(CHUNK // quarter):
            part1[b, c * (CHUNK // quarter) + k] = out[k * quarter : (k + 1) * quarter]

    def keep_own(b):
        mine = pl.ds(pl.multiple_of(me * quarter, quarter), quarter)
        unit_own[b] = unit_full[mine, :]
        rs_own[b] = rs_full[mine, :]
        ffn.start(b)

    def turn(b):
        if b == 0:
            for swap in swaps:
                swap.wait_recv()
        values = unit_own[b] * first_gain[...] + first_shift[...] + (ffn.total(b) + down_bias[...])
        unit, rs = norm_unit(values)
        out = (unit * second_gain[...] + second_shift[...]).astype(BF)
        for u in range(4):
            fold_into(folded, (u, b), out[:, u * width : (u + 1) * width], True)
        cot_rows = jnp.concatenate([unfold(cot_recv[s, b], width, True) for s in range(4)], axis=1).astype(F32)
        d_rows = norm_back(cot_rows * second_gain[...], unit, rs)
        d_mixed[b] = d_rows
        mixed[b, me] = d_rows.astype(BF)
        mixed_gather.start(b)
        add_small(3, d_rows)
        add_small(4, cot_rows * unit)
        add_small(5, cot_rows)

    def astern(b):
        mixed_gather.land(b)
        for c in range(BLOCK // CHUNK):
            here = slice(b * BLOCK + c * CHUNK, b * BLOCK + (c + 1) * CHUNK)
            count = CHUNK // quarter
            d_rows = jnp.concatenate([mixed[b, c * count + k] for k in range(count)], axis=0)
            d_gated = dot(d_rows, down_w[...], ((1,), (1,)))
            gate_rows = (d_gated * slope_term[here, :]).astype(BF)
            value_rows = (d_gated * gelu_term[here, :]).astype(BF)
            d_gate[here, :] = gate_rows
            d_value[here, :] = value_rows
            add_small(8, gate_rows.astype(F32))
            add_small(9, value_rows.astype(F32))
            out = dot(gate_rows, up_w[0], ((1,), (1,))) + dot(value_rows, up_w[1], ((1,), (1,)))
            out = out.astype(BF)
            for k in range(count):
                part2[b, c * count + k] = out[k * quarter : (k + 1) * quarter]
        back_sum.start(b)

    def finish(b):
        d_normed = d_mixed[b] + back_sum.total(b)
        d_hidden = norm_back(d_normed * first_gain[...], unit_own[b], rs_own[b])
        d_own[b] = d_hidden
        d_low[b, me] = d_hidden.astype(BF)
        hidden_gather.start(b)
        add_small(0, d_hidden)
        add_small(1, d_normed * unit_own[b])
        add_small(2, d_normed)

    def weight_grad(left, right, pieces):
        span = right.shape[1]
        for c in range(span // CHUNK):
            lanes = slice(c * CHUNK, (c + 1) * CHUNK)
            whole_grad[:, lanes] = dot(left, right[:, lanes], ((0,), (0,)))
        for g in range(groups):
            rows_here = (whole_grad[g * held : (g + 1) * held, :] * grad_scale).astype(BF)
            for k, target in enumerate(pieces):
                target[g] = rows_here[:, k * target.shape[2] : (k + 1) * target.shape[2]]

    last = blocks - 1
    for b in range(blocks):
        ahead(b, 0)
        if b >= 1:
            ffn.relay(b - 1)
        if b >= 2:
            turn(b - 2)
        ahead(b, 1)
        keep_own(b)
        if b >= 2:
            mixed_gather.relay(b - 2)
    ffn.relay(last)
    if blocks > 1:
        turn(last - 1)
    turn(last)
    if blocks > 1:
        mixed_gather.relay(last - 1)
    for b in range(blocks):
        if b == last:
            mixed_gather.relay(last)
        astern(b)
        if b >= 1:
            back_sum.relay(b - 1)
    back_sum.relay(last)
    d_mixed_rows = jnp.concatenate([mixed[b, k] for b in range(blocks) for k in range(4)], axis=0)
    weight_grad(d_mixed_rows, gated, (down_left, down_right))
    for half in sums:
        half.start()
    finish(0)
    weight_grad(normed_low[...], d_gate, (gate_grad,))
    if blocks > 1:
        finish(1)
    weight_grad(normed_low[...], d_value, (value_grad,))
    for b in range(2, blocks):
        finish(b)
    for half in sums:
        half.stage(1)
    for b in range(blocks):
        hidden_gather.relay(b)
    for half in sums:
        half.rest(2)
    for b in range(blocks):
        hidden_gather.land(b)
    for k, half in enumerate(sums):
        span = half.grads.shape[2]
        down_grad[:, k * span : (k + 1) * span] = half.collect()
    for b in range(blocks):
        mixed_gather.end(b)
        hidden_gather.end(b)
    for swap in swaps:
        swap.wait_send()
    for half in sums:
        half.end()


def mid(groups, grad_scale, args, number):
    context, up_w, cot_folded = args[0], args[3], args[6]
    rows, columns = context.shape
    units = up_w.shape[2]
    held = columns // groups
    blocks = rows // BLOCK
    quarter = BLOCK // 4
    own = (blocks, quarter, columns)
    dma = pltpu.SemaphoreType.DMA
    outs = (
        shape((blocks, 4, quarter, columns), BF),
        shape(own, F32),
        shape((16, columns), F32),
        shape((groups, held, units), BF),
        shape((groups, held, units), BF),
        shape((held, units), F32),
        shape(cot_folded.shape, BF),
    )
    return call(
        functools.partial(mid_kernel, groups, blocks, grad_scale),
        number,
        outs,
        [
            pltpu.VMEM((rows, columns), BF),
            pltpu.VMEM((rows, units), F32),
            pltpu.VMEM((rows, units), F32),
            pltpu.VMEM((rows, units), BF),
            pltpu.VMEM((rows, units), BF),
            pltpu.VMEM((rows, units), BF),
            pltpu.VMEM((BLOCK, columns), F32),
            pltpu.VMEM((BLOCK, 1), F32),
            pltpu.VMEM(own, F32),
            pltpu.VMEM((blocks, quarter, 1), F32),
            pltpu.VMEM(own, F32),
            pltpu.VMEM((blocks, 4, quarter, columns), BF),
            pltpu.VMEM((columns, units), F32),
            pltpu.VMEM((groups, held, units // 2), BF),
            pltpu.VMEM((groups, held, units // 2), BF),
            pltpu.VMEM(cot_folded.shape, BF),
        ]
        + RowSum.scratch(blocks, quarter, columns)
        + RowSum.scratch(blocks, quarter, columns)
        + [dma((6, blocks)), dma((6, blocks)), dma((2, 3)), pltpu.VMEM((6, columns), F32)]
        + GroupSum.scratch(groups, held, units // 2)
        + GroupSum.scratch(groups, held, units // 2),
        args,
    )


def back_kernel(groups, blocks, grad_scale, dh_low, dh_own, qkv, lse, seq_row, context, packed_in, qkv_w,
                out_w, gate_grad, value_grad, folded, small, taking,
                layer_out, input_grad, up_grad, qkv_grad, out_grad, small_out, qv_out, up_out,
                d_rows, d_part, late_sum, late_left, late_right, cols, one, two, three, packed, ssent, srecv, swide, x_sems, s_sems, w_sems,
                start_col, chosen, weight_here, returned, landed, load_sem, r_sems,
                sent, recv, a_sems, sent2, recv5, a_sems2, *sum_scratch):
    me, sibling, across, diagonal = place_of()
    mine = lax.axis_index("dp")
    width, rows = input_grad.shape
    heads = width // HEAD_DIM
    held = late_left.shape[1]
    quarter = BLOCK // 4
    load = pltpu.make_async_copy(qkv_w, weight_here, load_sem.at[0])
    load.start()
    load_rows = pltpu.make_async_copy(taking, chosen, load_sem.at[1])
    load_rows.start()
    enter([sibling, across, diagonal], groups)
    half_scratch = len(sum_scratch) // 2
    sums = both_ways(groups, (gate_grad, value_grad), sum_scratch[:half_scratch])
    late_sums = both_ways(groups, (late_left, late_right), sum_scratch[half_scratch:])
    giving = GiveBack(groups, rows, width, chosen, sent, recv, a_sems)
    giving_result = GiveBack(groups, rows, width, chosen, sent2, recv5, a_sems2)
    for each in sums:
        each.start()
    returns = [
        send(folded.at[peer], returned.at[me], r_sems.at[0, k], r_sems.at[1, k], tensor=peer)
        for k, peer in enumerate((across, diagonal, sibling))
    ]
    for swap in returns:
        swap.start()
    returned[me] = folded[me]
    def cross(b):
        return send(cols.at[diagonal, b], one.at[b], x_sems.at[0, b], x_sems.at[1, b], tensor=sibling)

    def near(b):
        return send(cols.at[sibling, b], two.at[b], x_sems.at[2, b], x_sems.at[3, b], tensor=sibling)

    def far(b):
        return send(one.at[b], three.at[b], x_sems.at[4, b], x_sems.at[5, b], tensor=across)

    def relay(b):
        cross(b).wait()
        one[b] = (cols[across, b].astype(F32) + one[b].astype(F32)).astype(BF)
        far(b).start()

    to_column(seq_row, start_col, 0)
    late_sum[:, 3 * width :] = dot(dh_low[...], context[...], ((0,), (0,)))
    load.wait()
    ssent[...] = small[...]

    @pl.loop(0, blocks)
    def _(b):
        here = pl.ds(pl.multiple_of(b * BLOCK, BLOCK), BLOCK)
        dh = dh_low[here, :]
        d_context = dot(dh, out_w[...], ((1,), (1,))).astype(BF)
        same = start_col[here, 0:1] == seq_row[0:1, here]
        distance = key_distance()
        for h in range(heads):
            lanes = slice(h * HEAD_DIM, (h + 1) * HEAD_DIM)
            queries = qkv[0, here, lanes]
            keys = qkv[1, here, lanes]
            values = qkv[2, here, lanes]
            d_rows_out = d_context[:, lanes]
            scored = scores_by_key(keys, queries, slope_of(me * heads + h), distance, same)
            probs = jnp.exp(scored - lse[b, h : h + 1, :])
            d_probs = dot(values, d_rows_out, ((1,), (1,)))
            d_rows[2, here, lanes] = dot(probs.astype(BF), d_rows_out, ((1,), (0,))).astype(BF)
            center = jnp.sum(probs * d_probs, axis=0, keepdims=True)
            d_scores = (probs * (d_probs - center)).astype(BF)
            d_rows[1, here, lanes] = (dot(d_scores, queries, ((1,), (0,))) * (HEAD_DIM**-0.5)).astype(BF)
            turned = dot(keys.T, d_scores, ((1,), (0,))) * (HEAD_DIM**-0.5)
            d_rows[0, here, lanes] = turned.T.astype(BF)
        part = dot(d_rows[0, here, :], weight_here[0], ((1,), (0,)))
        part += dot(d_rows[1, here, :], weight_here[1], ((1,), (0,)))
        part += dot(d_rows[2, here, :], weight_here[2], ((1,), (0,)))
        d_part[...] = part
        d_part[pl.ds(pl.multiple_of(me * quarter, quarter), quarter), :] += dh_own[b]
        for u in range(4):
            fold_into(cols, (u, b), d_part[:, u * width : (u + 1) * width].astype(BF), True)
        cross(b).start()
        near(b).start()
        last = small.shape[0] - 6
        for k, c in enumerate((0, 2)):
            bias = jnp.sum(d_rows[c, here, :].astype(F32), axis=0, keepdims=True) * grad_scale
            ssent[last : last + 1, k * 2 * 128 : k * 2 * 128 + width] += bias
        relay(b)

        @pl.when(b == 0)
        def _():
            for each in sums:
                each.stage(1)

        @pl.when(b == 1)
        def _():
            load_rows.wait()
            for swap in returns:
                swap.wait_recv()
            for q in range(blocks):
                for s in range(4):
                    start = q * BLOCK + s * quarter
                    packed[start : start + quarter, :] = unfold(returned[s, q], width, True)
            for each in sums:
                each.rest(2)
            giving_result.start(packed)

    for c in range(3):
        late_sum[:, c * width : (c + 1) * width] = dot(packed_in[...], d_rows[c], ((0,), (0,)))
    for g in range(groups):
        rows_here = (late_sum[g * held : (g + 1) * held, :] * grad_scale).astype(BF)
        late_left[g] = rows_here[:, : 2 * width]
        late_right[g] = rows_here[:, 2 * width :]

    for each in late_sums:
        each.start()
    swaps = [
        send(ssent, srecv.at[me], s_sems.at[0, k], s_sems.at[1, k], tensor=peer)
        for k, peer in enumerate((sibling, across, diagonal))
    ]
    for swap in swaps:
        swap.start()
    srecv[me] = ssent[...]

    for b in range(blocks):
        near(b).wait()
        far(b).wait_recv()
        total = cols[me, b].astype(F32) + two[b].astype(F32) + three[b].astype(F32)
        packed[b * BLOCK : (b + 1) * BLOCK, :] = unfold(total.astype(BF), width, True)
    giving.start(packed)

    for swap in swaps:
        swap.wait_recv()
    shared = small.shape[0] // 2
    swide[mine, 0:shared] = srecv[0, 0:shared] + srecv[1, 0:shared] + srecv[2, 0:shared] + srecv[3, 0:shared]
    swide[mine, shared:] = ssent[shared:, :]

    def spread(step):
        peer = (mine + step) % groups
        return send(swide.at[mine], swide.at[mine], w_sems.at[0, step], w_sems.at[1, step], dp=peer)

    @pl.loop(1, groups)
    def _(step):
        spread(step).start()

    for stage in range(1, late_sums[0].stages):
        for each in late_sums:
            each.stage(stage)
    for k, each in enumerate(sums):
        up_grad[k] = each.collect()
    giving_result.land(landed)
    layer_out[...] = landed[...].T

    @pl.loop(1, groups)
    def _(step):
        spread(step).wait_recv()

    for swap in swaps:
        swap.wait_send()
    ssent[...] = swide[0]

    @pl.loop(1, groups)
    def _(peer):
        ssent[...] += swide[peer]

    small_out[...] = ssent[0:8, :]
    up_out[...] = ssent[8:10, :]
    for k in range(2):
        qv_out[k : k + 1, :] = ssent[10:11, k * 256 : k * 256 + width]
    for k, each in enumerate(late_sums):
        total = each.collect()
        qkv_grad[2 * k] = total[:, :width]
        if k == 0:
            qkv_grad[1] = total[:, width:]
        else:
            out_grad[...] = total[:, width:].T
    giving.land(landed)
    input_grad[...] = landed[...].T
    for b in range(blocks):
        far(b).wait_send()
    for copy in returns:
        copy.wait_send()
    for each in sums + late_sums:
        each.end()

    @pl.loop(1, groups)
    def _(step):
        spread(step).wait_send()


def back(groups, grad_scale, args, small, number):
    dh_low, qkv, qkv_w, grad, folded = args[0], args[2], args[7], args[9], args[11]
    rows, columns = dh_low.shape
    width = qkv.shape[2]
    held, units = grad.shape[1:]
    blocks = rows // BLOCK
    half = (blocks, BLOCK // 2, 2 * width)
    dma = pltpu.SemaphoreType.DMA
    outs = (
        shape((width, rows), BF),
        shape((width, rows), BF),
        shape((2, held, units), F32),
        shape((3, held, width), F32),
        shape((width, held), F32),
        shape((8, columns), F32),
        shape((2, width), F32),
        shape((2, units), F32),
    )
    return call(
        functools.partial(back_kernel, groups, blocks, grad_scale),
        number,
        outs,
        [
            pltpu.VMEM((3, rows, width), BF),
            pltpu.VMEM((BLOCK, columns), F32),
            pltpu.VMEM((columns, 4 * width), F32),
            pltpu.VMEM((groups, held, 2 * width), BF),
            pltpu.VMEM((groups, held, 2 * width), BF),
            pltpu.VMEM((4,) + half, BF),
            pltpu.VMEM(half, BF),
            pltpu.VMEM(half, BF),
            pltpu.VMEM(half, BF),
            pltpu.VMEM((rows, width), BF),
            pltpu.VMEM(small.shape, F32),
            pltpu.VMEM((4,) + small.shape, F32),
            pltpu.VMEM((groups,) + small.shape, F32),
            dma((6, blocks)),
            dma((2, 3)),
            dma((2, groups)),
            pltpu.VMEM((rows, 8), jnp.int32),
            pltpu.VMEM((rows, rows), BF),
            pltpu.VMEM(qkv_w.shape, BF),
            pltpu.VMEM(folded.shape, BF),
            pltpu.VMEM((rows, width), BF),
            dma((2,)),
            dma((2, 3)),
        ]
        + GiveBack.scratch(groups, rows, width)
        + GiveBack.scratch(groups, rows, width)
        + GroupSum.scratch(groups, held, units) * 2
        + GroupSum.scratch(groups, held, 2 * width) * 2,
        args,
        apart=(7, 13),
    )


def on_device(
    tokens,
    cotangent,
    seq_start,
    row_place,
    qkv_weight,
    qv_bias,
    out_weight,
    out_bias,
    first_gain,
    first_shift,
    up_weight,
    up_bias,
    down_weight,
    down_bias,
    second_gain,
    second_shift,
):
    row_count, width = tokens.shape
    columns = qkv_weight.shape[1]
    groups = lax.axis_size("dp")
    grad_scale = (row_count * groups) ** (-0.5)
    seq_row = seq_start.reshape(1, row_count)
    weight_turned = qkv_weight.transpose(0, 2, 1)
    packed_in, cot_folded, full_out, qkv_rows, log_total, context, wide_context, taking = front(
        groups, (tokens.T, cotangent.T, row_place, seq_row, weight_turned, qv_bias, out_weight), 0
    )
    d_low, d_own, small, gate_grad, value_grad, down_grad, folded = mid(
        groups,
        grad_scale,
        (
            wide_context,
            packed_in,
            full_out.reshape(columns, columns),
            up_weight,
            up_bias,
            down_weight,
            cot_folded,
            out_bias,
            first_gain,
            first_shift,
            down_bias,
            second_gain,
            second_shift,
        ),
        1,
    )
    layer_out, input_grad, up_grad, qkv_grad, out_grad, sums, qv_bias_grad, up_bias_grad = back(
        groups,
        grad_scale,
        (
            d_low.reshape(row_count, columns),
            d_own,
            qkv_rows,
            log_total,
            seq_row,
            context,
            packed_in,
            weight_turned,
            out_weight,
            gate_grad,
            value_grad,
            folded,
            small,
            taking,
        ),
        small,
        2,
    )
    rows_here = columns // groups
    sums_here = lax.dynamic_slice_in_dim(sums[:6], lax.axis_index("dp") * rows_here, rows_here, 1)
    return (
        layer_out.T,
        input_grad.T,
        qkv_grad,
        qv_bias_grad,
        out_grad,
        sums_here[0],
        sums_here[1],
        sums_here[2],
        up_grad,
        up_bias_grad,
        down_grad.T,
        sums_here[3],
        sums_here[4],
        sums_here[5],
    )


def solution(mesh):
    return jax.shard_map(
        on_device,
        mesh=mesh,
        in_specs=(
            P("dp", "tensor"),
            P("dp", "tensor"),
            P("dp"),
            P("dp", None),
            P(None, None, "tensor"),
            P(None, "tensor"),
            P("tensor", None),
            P(),
            P(),
            P(),
            P(None, None, "tensor"),
            P(None, "tensor"),
            P("tensor", None),
            P(),
            P(),
            P(),
        ),
        out_specs=(
            P("dp", "tensor"),
            P("dp", "tensor"),
            P(None, "dp", "tensor"),
            P(None, "tensor"),
            P("tensor", "dp"),
            P("dp"),
            P("dp"),
            P("dp"),
            P(None, "dp", "tensor"),
            P(None, "tensor"),
            P("tensor", "dp"),
            P("dp"),
            P("dp"),
            P("dp"),
        ),
        check_vma=False,
    )
```

```python
import functools

import jax
import jax.numpy as jnp
from jax import lax
from jax.experimental import pallas as pl
from jax.experimental.pallas import tpu as pltpu
from jax.sharding import PartitionSpec as P

HEADS = 12
HEAD_DIM = 64
BLOCK = 512
BF = jnp.bfloat16
F32 = jnp.float32
MESH = pl.DeviceIdType.MESH
VMEM_LIMIT = 67043328


def dot(a, b, dims):
    return lax.dot_general(a, b, (dims, ((), ())), preferred_element_type=F32)


def place_of():
    me = lax.axis_index("tensor")
    core = me % 2
    side = me // 2
    sibling = side * 2 + (1 - core)
    across = (1 - side) * 2 + core
    diagonal = (1 - side) * 2 + (1 - core)
    return me, sibling, across, diagonal


def enter(devices, groups):
    barrier = pltpu.get_barrier_semaphore()
    count = len(devices)
    for device in devices:
        pl.semaphore_signal(barrier, inc=1, device_id={"tensor": device}, device_id_type=MESH)
    if groups:
        mine = lax.axis_index("dp")

        @pl.loop(1, groups)
        def _(step):
            pl.semaphore_signal(barrier, inc=1, device_id={"dp": (mine + step) % groups}, device_id_type=MESH)

        count += groups - 1
    pl.semaphore_wait(barrier, count)


def send(source, target, send_sem, recv_sem, **where):
    return pltpu.make_async_remote_copy(
        src_ref=source, dst_ref=target, send_sem=send_sem, recv_sem=recv_sem, device_id=where, device_id_type=MESH
    )


def fold_into(buffer, index, values, halves):
    width = values.shape[1]
    if not halves:
        buffer[index] = values
        return
    half = values.shape[0] // 2
    buffer[index + (slice(None), slice(0, width))] = values[:half]
    buffer[index + (slice(None), slice(width, 2 * width))] = values[half:]


def unfold(values, width, halves):
    if not halves:
        return values
    return jnp.concatenate([values[:, :width], values[:, width:]], axis=0)


def call(kernel, number, outs, scratch, args, apart=(), apart_outs=()):
    specs = [pl.BlockSpec(memory_space=pl.ANY if k in apart else pltpu.VMEM) for k in range(len(args))]
    return pl.pallas_call(
        kernel,
        out_shape=outs,
        in_specs=specs,
        out_specs=tuple(
            pl.BlockSpec(memory_space=pl.ANY if k in apart_outs else pltpu.VMEM) for k in range(len(outs))
        ),
        scratch_shapes=scratch,
        compiler_params=pltpu.CompilerParams(
            collective_id=number, has_side_effects=True, vmem_limit_bytes=VMEM_LIMIT
        ),
    )(*args)


def shape(dims, kind):
    return jax.ShapeDtypeStruct(dims, kind)


def to_column(row, column, where):
    for k in range(row.shape[1] // 128):
        piece = jnp.broadcast_to(row[0:1, k * 128 : (k + 1) * 128], (8, 128))
        column[k * 128 : (k + 1) * 128, where : where + 1] = piece.T[:, 0:1]


def slope_of(index):
    value = jnp.float32(2.0 ** (-8.0 / HEADS))
    for head in range(1, HEADS):
        value = jnp.where(index == head, jnp.float32(2.0 ** (-8.0 * (head + 1) / HEADS)), value)
    return value


def key_distance():
    keys = lax.broadcasted_iota(jnp.int32, (BLOCK, BLOCK), 0)
    asks = lax.broadcasted_iota(jnp.int32, (BLOCK, BLOCK), 1)
    return jnp.abs(keys - asks).astype(F32)


def scores_by_key(keys, queries, slope, distance, same):
    raw = dot(keys, queries, ((1,), (1,))) * (HEAD_DIM**-0.5) - slope * distance
    return jnp.where(same, raw, -1e30)


class HeadGather:
    def __init__(self, wide, sems):
        self.wide, self.sems = wide, sems
        self.me, self.sibling, self.across, _ = place_of()

    def copy(self, b, kind, whose, peer):
        return send(self.wide.at[whose, b], self.wide.at[whose, b], self.sems.at[2 * kind, b],
                    self.sems.at[2 * kind + 1, b], tensor=peer)

    def start(self, b, values):
        fold_into(self.wide, (self.me, b), values, True)
        self.copy(b, 0, self.me, self.across).start()
        self.copy(b, 1, self.me, self.sibling).start()

    def relay(self, b):
        self.copy(b, 0, self.me, self.across).wait_recv()
        self.copy(b, 2, self.across, self.sibling).start()

    def land(self, b, out, width):
        self.copy(b, 1, self.me, self.sibling).wait_recv()
        self.copy(b, 2, self.across, self.sibling).wait_recv()
        for s in range(4):
            out[b * BLOCK : (b + 1) * BLOCK, s * width : (s + 1) * width] = unfold(self.wide[s, b], width, True)

    def end(self, b):
        self.copy(b, 0, self.me, self.across).wait_send()
        self.copy(b, 1, self.me, self.sibling).wait_send()
        self.copy(b, 2, self.across, self.sibling).wait_send()


def front_kernel(groups, blocks, tokens, cot, place_row, seq_row, qkv_w, qv_bias, out_w,
                 packed_out, cot_out, full_out, qkv, lse, context, wide_context, taking,
                 tokens_turned, cot_turned, tokens_here, cot_here, weight_here, start_col, chosen, taken, sent, recv, arrived,
                 wide, wide_heads, local_sems, group_sems, gather_sems, head_sems, out_sems):
    me, sibling, across, diagonal = place_of()
    mine = lax.axis_index("dp")
    rows, width = tokens_here.shape
    heads = width // HEAD_DIM
    piece = rows // groups
    halves = (piece // 2) % 8 == 0
    quarter = BLOCK // 4
    loads = [
        pltpu.make_async_copy(source, target, local_sems.at[k])
        for k, (source, target) in enumerate(((tokens, tokens_turned), (cot, cot_turned), (qkv_w, weight_here)))
    ]
    for load in loads:
        load.start()
    enter([sibling, across, diagonal], groups)

    def moved(kind, step):
        peer = (mine + step) % groups
        return send(sent.at[kind, peer], recv.at[kind, mine], group_sems.at[0, kind, step],
                    group_sems.at[1, kind, step], dp=peer)

    def give(kind, source):
        @pl.loop(1, groups)
        def _(step):
            peer = (mine + step) % groups
            values = source[pl.ds(pl.multiple_of(peer * piece, 8), piece), :]
            fold_into(sent, (kind, peer), values, halves)
            moved(kind, step).start()

        values = source[pl.ds(pl.multiple_of(mine * piece, 8), piece), :]
        fold_into(recv, (kind, mine), values, halves)

    loads[0].wait()
    tokens_here[...] = tokens_turned[...].T
    give(0, tokens_here)
    out_far = send(out_w, full_out.at[me], out_sems.at[0], out_sems.at[1], tensor=across)
    out_near = send(out_w, full_out.at[me], out_sems.at[2], out_sems.at[3], tensor=sibling)
    out_pass = send(full_out.at[across], full_out.at[across], out_sems.at[4], out_sems.at[5], tensor=sibling)
    out_far.start()
    out_near.start()
    loads[1].wait()
    cot_here[...] = cot_turned[...].T
    full_out[me] = out_w[...]
    to_column(seq_row, start_col, 0)
    for b in range(blocks):
        ids = lax.broadcasted_iota(jnp.int32, (BLOCK, rows), 0) + b * BLOCK
        chosen[b * BLOCK : (b + 1) * BLOCK, :] = jnp.where(ids == place_row[...], 1.0, 0.0).astype(BF)

    to_column(place_row, start_col, 1)
    for b in range(blocks):
        ids = lax.broadcasted_iota(jnp.int32, (BLOCK, rows), 1)
        here = slice(b * BLOCK, (b + 1) * BLOCK)
        taken[here, :] = jnp.where(ids == start_col[here, 1:2], 1.0, 0.0).astype(BF)
    store = pltpu.make_async_copy(taken, taking, local_sems.at[3])
    store.start()

    def placed(b):
        return dot(chosen[b * BLOCK : (b + 1) * BLOCK, :], arrived[...], ((1,), (0,))).astype(BF)

    out_far.wait_recv()
    out_pass.start()

    def land(kind):
        @pl.loop(1, groups)
        def _(step):
            moved(kind, step).wait_recv()

        @pl.loop(0, groups)
        def _(peer):
            arrived[pl.ds(pl.multiple_of(peer * piece, 8), piece), :] = unfold(recv[kind, peer], width, halves)

    token_gather = HeadGather(wide, gather_sems)
    head_gather = HeadGather(wide_heads, head_sems)
    land(0)
    for b in range(blocks):
        token_gather.start(b, placed(b))
        if b >= 1:
            token_gather.relay(b - 1)
    give(1, cot_here)
    loads[2].wait()

    def attend(b):
        here = slice(b * BLOCK, (b + 1) * BLOCK)
        token_gather.land(b, packed_out, width)
        for k in range(3):
            part = dot(packed_out[here, :], weight_here[k], ((1,), (1,)))
            if k != 1:
                part += qv_bias[k // 2 : k // 2 + 1, :].astype(F32)
            qkv[k, here, :] = part.astype(BF)
        same = start_col[here, 0:1] == seq_row[0:1, here]
        distance = key_distance()
        for h in range(heads):
            lanes = slice(h * HEAD_DIM, (h + 1) * HEAD_DIM)
            scored = scores_by_key(qkv[1, here, lanes], qkv[0, here, lanes], slope_of(me * heads + h), distance, same)
            top = jnp.max(scored, axis=0, keepdims=True)
            raised = jnp.exp(scored - top)
            total = jnp.sum(raised, axis=0, keepdims=True)
            lse[b, h : h + 1, :] = top + jnp.log(total)
            probs = (raised * (1.0 / total)).astype(BF)
            turned = dot(qkv[2, here, lanes].T, probs, ((1,), (0,)))
            context[here, lanes] = turned.T.astype(BF)
        head_gather.start(b, context[here, :])

    for b in range(blocks):
        if b == blocks - 1:
            token_gather.relay(b)
        attend(b)
        if b >= 1:
            head_gather.relay(b - 1)
    for b in range(blocks - 1):
        head_gather.land(b, wide_context, width)
    land(1)
    for b in range(blocks):
        cot_block = placed(b)
        for u in range(4):
            fold_into(cot_out, (u, b), cot_block[u * quarter : (u + 1) * quarter], True)
    head_gather.relay(blocks - 1)
    head_gather.land(blocks - 1, wide_context, width)
    for b in range(blocks):
        token_gather.end(b)
        head_gather.end(b)
    store.wait()
    out_near.wait()
    out_pass.wait()
    out_far.wait_send()
    for kind in range(2):
        @pl.loop(1, groups)
        def _(step):
            moved(kind, step).wait_send()


def front(groups, args, number):
    tokens, qkv_w, out_w = args[0], args[4], args[6]
    width, rows = tokens.shape
    piece = rows // groups
    blocks = rows // BLOCK
    heads = width // HEAD_DIM
    halves = (piece // 2) % 8 == 0
    slab = (2, groups, piece // 2, 2 * width) if halves else (2, groups, piece, width)
    here = pltpu.VMEM((rows, width), BF)
    wide = pltpu.VMEM((4, blocks, BLOCK // 2, 2 * width), BF)
    turned = pltpu.VMEM((width, rows), BF)
    dma = pltpu.SemaphoreType.DMA
    return call(
        functools.partial(front_kernel, groups, blocks),
        number,
        (
            shape((rows, 4 * width), BF),
            shape((4, blocks, BLOCK // 8, 2 * width), BF),
            shape((4,) + out_w.shape, BF),
            shape((3, rows, width), BF),
            shape((blocks, heads, BLOCK), F32),
            shape((rows, width), BF),
            shape((rows, 4 * width), BF),
            shape((rows, rows), BF),
        ),
        [
            turned,
            turned,
            here,
            here,
            pltpu.VMEM(qkv_w.shape, BF),
            pltpu.VMEM((rows, 8), jnp.int32),
            pltpu.VMEM((rows, rows), BF),
            pltpu.VMEM((rows, rows), BF),
            pltpu.VMEM(slab, BF),
            pltpu.VMEM(slab, BF),
            here,
            wide,
            wide,
            dma((4,)),
            dma((2, 2, groups)),
            dma((6, blocks)),
            dma((6, blocks)),
            dma((6,)),
        ],
        args,
        apart=(0, 1, 4),
        apart_outs=(7,),
    )


def norm_unit(values):
    center = values - jnp.mean(values, axis=-1, keepdims=True)
    rs = lax.rsqrt(jnp.mean(center * center, axis=-1, keepdims=True) + 1e-05)
    return center * rs, rs


def norm_back(weighted, unit, rs):
    inner = jnp.mean(weighted * unit, axis=-1, keepdims=True)
    return rs * (weighted - jnp.mean(weighted, axis=-1, keepdims=True) - unit * inner)


class GroupSum:
    def __init__(self, groups, grads, scratch, turned):
        self.groups, self.grads, self.turned = groups, grads, turned
        self.stages = groups.bit_length() - 1
        self.recv = scratch[: self.stages]
        self.held = (None,) + tuple(scratch[self.stages : 2 * self.stages - 1])
        self.sems = scratch[-1]
        mine = lax.axis_index("dp")
        self.mine = mine // 2 + mine % 2 * (groups // 2) if turned else mine

    def real(self, device):
        half = self.groups // 2
        return device % half * 2 + device // half if self.turned else device

    def count(self, stage):
        return self.groups >> (stage + 1)

    def index(self, stage, step):
        return (self.mine // (2 << stage) + step) % self.count(stage)

    def given(self, stage, step):
        bit = (self.mine // (1 << stage)) % 2
        low = self.mine % (1 << stage)
        return self.index(stage, step) * (2 << stage) + (1 - bit) * (1 << stage) + low

    def copy(self, stage, step):
        bit = (self.mine // (1 << stage)) % 2
        partner = self.mine + (1 - 2 * bit) * (1 << stage)
        at = self.index(stage, step)
        source = self.held[stage].at[at] if stage else self.grads.at[self.real(self.given(0, step))]
        return send(source, self.recv[stage].at[at], self.sems.at[0, stage, step], self.sems.at[1, stage, step],
                    dp=self.real(partner))

    def start(self):
        @pl.loop(1, self.count(0) + 1)
        def _(step):
            self.copy(0, step).start()

    def total(self, stages, piece):
        total = self.grads[self.real(piece)].astype(F32)
        for stage in range(stages):
            count = self.count(stage)
            at = piece // (2 << stage)
            step = (at + 2 * count - 1 - self.mine // (2 << stage)) % count + 1
            self.copy(stage, step).wait_recv()
            total += self.recv[stage][at].astype(F32)
        return total

    def stage(self, stage):
        @pl.loop(1, self.count(stage) + 1)
        def _(step):
            at = self.index(stage, step)
            self.held[stage][at] = self.total(stage, self.given(stage, step)).astype(BF)
            self.copy(stage, step).start()

    def rest(self, first):
        for stage in range(first, self.stages):
            self.stage(stage)

    def collect(self):
        return self.total(self.stages, self.mine)

    def end(self):
        for stage in range(self.stages):
            @pl.loop(1, self.count(stage) + 1)
            def _(step):
                self.copy(stage, step).wait_send()

    @staticmethod
    def scratch(groups, held, span):
        stages = groups.bit_length() - 1
        buffers = [pltpu.VMEM((groups >> (k + 1), held, span), BF) for k in range(stages)]
        return buffers + buffers[1:] + [pltpu.SemaphoreType.DMA((2, stages, groups // 2 + 1))]


def both_ways(groups, pair, scratch, turned=True):
    half = len(scratch) // 2
    return [
        GroupSum(groups, grads, scratch[k * half : (k + 1) * half], turned and k == 1) for k, grads in enumerate(pair)
    ]


class GiveBack:
    def __init__(self, groups, rows, width, chosen, sent, recv, sems):
        self.groups, self.piece, self.width = groups, rows // groups, width
        self.halves = (self.piece // 2) % 8 == 0
        self.chosen, self.sent, self.recv, self.sems = chosen, sent, recv, sems
        self.mine = lax.axis_index("dp")

    def moved(self, step):
        peer = (self.mine + step) % self.groups
        return send(self.sent.at[peer], self.recv.at[self.mine], self.sems.at[0, step], self.sems.at[1, step], dp=peer)

    def start(self, packed):
        @pl.loop(0, self.groups)
        def _(step):
            peer = (self.mine + step) % self.groups
            rows = self.chosen[pl.ds(pl.multiple_of(peer * self.piece, 8), self.piece), :]
            values = dot(rows, packed[...], ((1,), (0,))).astype(BF)

            @pl.when(step > 0)
            def _():
                fold_into(self.sent, (peer,), values, self.halves)
                self.moved(step).start()

            @pl.when(step == 0)
            def _():
                fold_into(self.recv, (self.mine,), values, self.halves)

    def land(self, target):
        @pl.loop(1, self.groups)
        def _(step):
            self.moved(step).wait_recv()

        @pl.loop(0, self.groups)
        def _(peer):
            here = pl.ds(pl.multiple_of(peer * self.piece, 8), self.piece)
            target[here, :] = unfold(self.recv[peer], self.width, self.halves)

        @pl.loop(1, self.groups)
        def _(step):
            self.moved(step).wait_send()

    @staticmethod
    def scratch(groups, rows, width):
        piece = rows // groups
        halves = (piece // 2) % 8 == 0
        slab = (groups, piece // 2, 2 * width) if halves else (groups, piece, width)
        return [pltpu.VMEM(slab, BF)] * 2 + [pltpu.SemaphoreType.DMA((2, groups))]


class RowSum:
    def __init__(self, part, first, second, third, sems):
        self.part, self.first, self.second, self.third, self.sems = part, first, second, third, sems
        self.me, self.sibling, self.across, self.diagonal = place_of()

    def cross(self, b):
        return send(self.part.at[b, self.diagonal], self.first.at[b], self.sems.at[0, b], self.sems.at[1, b],
                    tensor=self.sibling)

    def near(self, b):
        return send(self.part.at[b, self.sibling], self.second.at[b], self.sems.at[2, b], self.sems.at[3, b],
                    tensor=self.sibling)

    def far(self, b):
        return send(self.first.at[b], self.third.at[b], self.sems.at[4, b], self.sems.at[5, b], tensor=self.across)

    def start(self, b):
        self.cross(b).start()
        self.near(b).start()

    def relay(self, b):
        self.cross(b).wait()
        self.first[b] = (self.part[b, self.across].astype(F32) + self.first[b].astype(F32)).astype(BF)
        self.far(b).start()

    def total(self, b):
        self.near(b).wait()
        self.far(b).wait()
        return self.part[b, self.me].astype(F32) + self.second[b].astype(F32) + self.third[b].astype(F32)

    @staticmethod
    def scratch(blocks, rows, columns):
        buffer = pltpu.VMEM((blocks, rows, columns), BF)
        return [pltpu.VMEM((blocks, 4, rows, columns), BF)] + [buffer] * 3 + [pltpu.SemaphoreType.DMA((6, blocks))]


class RowGather:
    def __init__(self, out, sems):
        self.out, self.sems = out, sems
        self.me, self.sibling, self.across, _ = place_of()

    def copy(self, b, kind, whose, peer):
        return send(self.out.at[b, whose], self.out.at[b, whose], self.sems.at[2 * kind, b],
                    self.sems.at[2 * kind + 1, b], tensor=peer)

    def start(self, b):
        self.copy(b, 0, self.me, self.across).start()
        self.copy(b, 1, self.me, self.sibling).start()

    def relay(self, b):
        self.copy(b, 0, self.me, self.across).wait_recv()
        self.copy(b, 2, self.across, self.sibling).start()

    def land(self, b):
        self.copy(b, 1, self.me, self.sibling).wait_recv()
        self.copy(b, 2, self.across, self.sibling).wait_recv()

    def end(self, b):
        self.copy(b, 0, self.me, self.across).wait_send()
        self.copy(b, 1, self.me, self.sibling).wait_send()
        self.copy(b, 2, self.across, self.sibling).wait_send()


CHUNK = 256


def mid_kernel(groups, blocks, grad_scale, context, packed, full_out, up_w, up_bias, down_w, cot_folded, v0, v1, v2, v3, v4, v5,
               d_low, d_own, small, gate_grad, value_grad, down_grad, folded,
               normed_low, slope_term, gelu_term, gated, d_gate, d_value, unit_full, rs_full, unit_own, rs_own, d_mixed,
               mixed, whole_grad, down_left, down_right, cot_recv,
               part1, first1, second1, third1, sems1, part2, first2, second2, third2, sems2, sems3, sems4, c_sems,
               vector_rows, *sum_scratch):
    me, sibling, across, diagonal = place_of()
    columns = packed.shape[1]
    width = columns // 4
    quarter = BLOCK // 4
    held = down_left.shape[1]
    enter([sibling, across, diagonal], groups)
    swaps = [
        send(cot_folded.at[peer], cot_recv.at[me], c_sems.at[0, k], c_sems.at[1, k], tensor=peer)
        for k, peer in enumerate((across, diagonal, sibling))
    ]
    for swap in swaps:
        swap.start()
    cot_recv[me] = cot_folded[me]
    ffn = RowSum(part1, first1, second1, third1, sems1)
    back_sum = RowSum(part2, first2, second2, third2, sems2)
    mixed_gather = RowGather(mixed, sems3)
    hidden_gather = RowGather(d_low, sems4)
    sums = both_ways(groups, (down_left, down_right), sum_scratch)
    small[...] = jnp.zeros_like(small)
    for k, vector in enumerate((v0, v1, v2, v3, v4, v5)):
        vector_rows[k : k + 1, :] = vector[...].astype(F32).reshape(1, columns)
    out_bias, first_gain, first_shift, down_bias, second_gain, second_shift = (
        vector_rows.at[k : k + 1] for k in range(6)
    )

    def add_small(row, values):
        small[row : row + 1, :] += jnp.sum(values, axis=0, keepdims=True) * grad_scale

    def ahead(b, c):
        here = slice(b * BLOCK + c * CHUNK, b * BLOCK + (c + 1) * CHUNK)
        inner = slice(c * CHUNK, (c + 1) * CHUNK)
        hidden = packed[here, :].astype(F32) + (dot(context[here, :], full_out[...], ((1,), (0,))) + out_bias[...])
        unit, rs = norm_unit(hidden)
        unit_full[inner, :] = unit
        rs_full[inner, :] = rs
        low = (unit * first_gain[...] + first_shift[...]).astype(BF)
        normed_low[here, :] = low
        gate = dot(low, up_w[0], ((1,), (0,))) + up_bias[0:1, :].astype(F32)
        value = dot(low, up_w[1], ((1,), (0,))) + up_bias[1:2, :].astype(F32)
        half_erf = 0.5 * (1.0 + lax.erf(gate * (0.5**0.5)))
        gelu = gate * half_erf
        slope = half_erf + gate * jnp.exp(-0.5 * gate * gate) * ((2.0 * jnp.pi) ** (-0.5))
        slope_term[here, :] = value * slope
        gelu_term[here, :] = gelu
        low_gated = (gelu * value).astype(BF)
        gated[here, :] = low_gated
        out = dot(low_gated, down_w[...], ((1,), (0,))).astype(BF)
        for k in range(CHUNK // quarter):
            part1[b, c * (CHUNK // quarter) + k] = out[k * quarter : (k + 1) * quarter]

    def keep_own(b):
        mine = pl.ds(pl.multiple_of(me * quarter, quarter), quarter)
        unit_own[b] = unit_full[mine, :]
        rs_own[b] = rs_full[mine, :]
        ffn.start(b)

    def turn(b):
        if b == 0:
            for swap in swaps:
                swap.wait_recv()
        values = unit_own[b] * first_gain[...] + first_shift[...] + (ffn.total(b) + down_bias[...])
        unit, rs = norm_unit(values)
        out = (unit * second_gain[...] + second_shift[...]).astype(BF)
        for u in range(4):
            fold_into(folded, (u, b), out[:, u * width : (u + 1) * width], True)
        cot_rows = jnp.concatenate([unfold(cot_recv[s, b], width, True) for s in range(4)], axis=1).astype(F32)
        d_rows = norm_back(cot_rows * second_gain[...], unit, rs)
        d_mixed[b] = d_rows
        mixed[b, me] = d_rows.astype(BF)
        mixed_gather.start(b)
        add_small(3, d_rows)
        add_small(4, cot_rows * unit)
        add_small(5, cot_rows)

    def astern(b):
        mixed_gather.land(b)
        for c in range(BLOCK // CHUNK):
            here = slice(b * BLOCK + c * CHUNK, b * BLOCK + (c + 1) * CHUNK)
            count = CHUNK // quarter
            d_rows = jnp.concatenate([mixed[b, c * count + k] for k in range(count)], axis=0)
            d_gated = dot(d_rows, down_w[...], ((1,), (1,)))
            gate_rows = (d_gated * slope_term[here, :]).astype(BF)
            value_rows = (d_gated * gelu_term[here, :]).astype(BF)
            d_gate[here, :] = gate_rows
            d_value[here, :] = value_rows
            add_small(8, gate_rows.astype(F32))
            add_small(9, value_rows.astype(F32))
            out = dot(gate_rows, up_w[0], ((1,), (1,))) + dot(value_rows, up_w[1], ((1,), (1,)))
            out = out.astype(BF)
            for k in range(count):
                part2[b, c * count + k] = out[k * quarter : (k + 1) * quarter]
        back_sum.start(b)

    def finish(b):
        d_normed = d_mixed[b] + back_sum.total(b)
        d_hidden = norm_back(d_normed * first_gain[...], unit_own[b], rs_own[b])
        d_own[b] = d_hidden
        d_low[b, me] = d_hidden.astype(BF)
        hidden_gather.start(b)
        add_small(0, d_hidden)
        add_small(1, d_normed * unit_own[b])
        add_small(2, d_normed)

    def weight_grad(left, right, pieces):
        span = right.shape[1]
        for c in range(span // CHUNK):
            lanes = slice(c * CHUNK, (c + 1) * CHUNK)
            whole_grad[:, lanes] = dot(left, right[:, lanes], ((0,), (0,)))
        for g in range(groups):
            rows_here = (whole_grad[g * held : (g + 1) * held, :] * grad_scale).astype(BF)
            for k, target in enumerate(pieces):
                target[g] = rows_here[:, k * target.shape[2] : (k + 1) * target.shape[2]]

    last = blocks - 1
    for b in range(blocks):
        ahead(b, 0)
        if b >= 1:
            ffn.relay(b - 1)
        if b >= 2:
            turn(b - 2)
        ahead(b, 1)
        keep_own(b)
        if b >= 2:
            mixed_gather.relay(b - 2)
    ffn.relay(last)
    if blocks > 1:
        turn(last - 1)
    turn(last)
    if blocks > 1:
        mixed_gather.relay(last - 1)
    for b in range(blocks):
        if b == last:
            mixed_gather.relay(last)
        astern(b)
        if b >= 1:
            back_sum.relay(b - 1)
    back_sum.relay(last)
    d_mixed_rows = jnp.concatenate([mixed[b, k] for b in range(blocks) for k in range(4)], axis=0)
    weight_grad(d_mixed_rows, gated, (down_left, down_right))
    for half in sums:
        half.start()
    finish(0)
    weight_grad(normed_low[...], d_gate, (gate_grad,))
    if blocks > 1:
        finish(1)
    weight_grad(normed_low[...], d_value, (value_grad,))
    for b in range(2, blocks):
        finish(b)
    for half in sums:
        half.stage(1)
    for b in range(blocks):
        hidden_gather.relay(b)
    for half in sums:
        half.rest(2)
    for b in range(blocks):
        hidden_gather.land(b)
    for k, half in enumerate(sums):
        span = half.grads.shape[2]
        down_grad[:, k * span : (k + 1) * span] = half.collect()
    for b in range(blocks):
        mixed_gather.end(b)
        hidden_gather.end(b)
    for swap in swaps:
        swap.wait_send()
    for half in sums:
        half.end()


def mid(groups, grad_scale, args, number):
    context, up_w, cot_folded = args[0], args[3], args[6]
    rows, columns = context.shape
    units = up_w.shape[2]
    held = columns // groups
    blocks = rows // BLOCK
    quarter = BLOCK // 4
    own = (blocks, quarter, columns)
    dma = pltpu.SemaphoreType.DMA
    outs = (
        shape((blocks, 4, quarter, columns), BF),
        shape(own, F32),
        shape((16, columns), F32),
        shape((groups, held, units), BF),
        shape((groups, held, units), BF),
        shape((held, units), F32),
        shape(cot_folded.shape, BF),
    )
    return call(
        functools.partial(mid_kernel, groups, blocks, grad_scale),
        number,
        outs,
        [
            pltpu.VMEM((rows, columns), BF),
            pltpu.VMEM((rows, units), F32),
            pltpu.VMEM((rows, units), F32),
            pltpu.VMEM((rows, units), BF),
            pltpu.VMEM((rows, units), BF),
            pltpu.VMEM((rows, units), BF),
            pltpu.VMEM((BLOCK, columns), F32),
            pltpu.VMEM((BLOCK, 1), F32),
            pltpu.VMEM(own, F32),
            pltpu.VMEM((blocks, quarter, 1), F32),
            pltpu.VMEM(own, F32),
            pltpu.VMEM((blocks, 4, quarter, columns), BF),
            pltpu.VMEM((columns, units), F32),
            pltpu.VMEM((groups, held, units // 2), BF),
            pltpu.VMEM((groups, held, units // 2), BF),
            pltpu.VMEM(cot_folded.shape, BF),
        ]
        + RowSum.scratch(blocks, quarter, columns)
        + RowSum.scratch(blocks, quarter, columns)
        + [dma((6, blocks)), dma((6, blocks)), dma((2, 3)), pltpu.VMEM((6, columns), F32)]
        + GroupSum.scratch(groups, held, units // 2)
        + GroupSum.scratch(groups, held, units // 2),
        args,
    )


def back_kernel(groups, blocks, grad_scale, dh_low, dh_own, qkv, lse, seq_row, context, packed_in, qkv_w,
                out_w, gate_grad, value_grad, folded, small, taking,
                layer_out, input_grad, up_grad, qkv_grad, out_grad, small_out, qv_out, up_out,
                d_rows, d_part, late_sum, late_left, late_right, cols, one, two, three, packed, ssent, srecv, swide, x_sems, s_sems, w_sems,
                start_col, chosen, weight_here, returned, landed, load_sem, r_sems,
                sent, recv, a_sems, sent2, recv5, a_sems2, *sum_scratch):
    me, sibling, across, diagonal = place_of()
    mine = lax.axis_index("dp")
    width, rows = input_grad.shape
    heads = width // HEAD_DIM
    held = late_left.shape[1]
    quarter = BLOCK // 4
    load = pltpu.make_async_copy(qkv_w, weight_here, load_sem.at[0])
    load.start()
    load_rows = pltpu.make_async_copy(taking, chosen, load_sem.at[1])
    load_rows.start()
    enter([sibling, across, diagonal], groups)
    half_scratch = len(sum_scratch) // 2
    sums = both_ways(groups, (gate_grad, value_grad), sum_scratch[:half_scratch], False)
    late_sums = both_ways(groups, (late_left, late_right), sum_scratch[half_scratch:])
    giving = GiveBack(groups, rows, width, chosen, sent, recv, a_sems)
    giving_result = GiveBack(groups, rows, width, chosen, sent2, recv5, a_sems2)
    for each in sums:
        each.start()
    returns = [
        send(folded.at[peer], returned.at[me], r_sems.at[0, k], r_sems.at[1, k], tensor=peer)
        for k, peer in enumerate((across, diagonal, sibling))
    ]
    for swap in returns:
        swap.start()
    returned[me] = folded[me]
    def cross(b):
        return send(cols.at[diagonal, b], one.at[b], x_sems.at[0, b], x_sems.at[1, b], tensor=sibling)

    def near(b):
        return send(cols.at[sibling, b], two.at[b], x_sems.at[2, b], x_sems.at[3, b], tensor=sibling)

    def far(b):
        return send(one.at[b], three.at[b], x_sems.at[4, b], x_sems.at[5, b], tensor=across)

    def relay(b):
        cross(b).wait()
        one[b] = (cols[across, b].astype(F32) + one[b].astype(F32)).astype(BF)
        far(b).start()

    to_column(seq_row, start_col, 0)
    late_sum[:, 3 * width :] = dot(dh_low[...], context[...], ((0,), (0,)))
    load.wait()
    ssent[...] = small[...]

    @pl.loop(0, blocks)
    def _(b):
        here = pl.ds(pl.multiple_of(b * BLOCK, BLOCK), BLOCK)
        dh = dh_low[here, :]
        d_context = dot(dh, out_w[...], ((1,), (1,))).astype(BF)
        same = start_col[here, 0:1] == seq_row[0:1, here]
        distance = key_distance()
        for h in range(heads):
            lanes = slice(h * HEAD_DIM, (h + 1) * HEAD_DIM)
            queries = qkv[0, here, lanes]
            keys = qkv[1, here, lanes]
            values = qkv[2, here, lanes]
            d_rows_out = d_context[:, lanes]
            scored = scores_by_key(keys, queries, slope_of(me * heads + h), distance, same)
            probs = jnp.exp(scored - lse[b, h : h + 1, :])
            d_probs = dot(values, d_rows_out, ((1,), (1,)))
            d_rows[2, here, lanes] = dot(probs.astype(BF), d_rows_out, ((1,), (0,))).astype(BF)
            center = jnp.sum(probs * d_probs, axis=0, keepdims=True)
            d_scores = (probs * (d_probs - center)).astype(BF)
            d_rows[1, here, lanes] = (dot(d_scores, queries, ((1,), (0,))) * (HEAD_DIM**-0.5)).astype(BF)
            turned = dot(keys.T, d_scores, ((1,), (0,))) * (HEAD_DIM**-0.5)
            d_rows[0, here, lanes] = turned.T.astype(BF)
        last = small.shape[0] - 6
        for k, c in enumerate((0, 2)):
            bias = jnp.sum(d_rows[c, here, :].astype(F32), axis=0, keepdims=True) * grad_scale
            ssent[last : last + 1, k * 2 * 128 : k * 2 * 128 + width] += bias
        @pl.when(b == 1)
        def _():
            load_rows.wait()
            for swap in returns:
                swap.wait_recv()
            for q in range(blocks):
                for s in range(4):
                    start = q * BLOCK + s * quarter
                    packed[start : start + quarter, :] = unfold(returned[s, q], width, True)
            giving_result.start(packed)
            sums[0].stage(1)

    for c in range(3):
        late_sum[:, c * width : (c + 1) * width] = dot(packed_in[...], d_rows[c], ((0,), (0,)))
    for g in range(groups):
        rows_here = (late_sum[g * held : (g + 1) * held, :] * grad_scale).astype(BF)
        late_left[g] = rows_here[:, : 2 * width]
        late_right[g] = rows_here[:, 2 * width :]

    for each in late_sums:
        each.start()
    sums[0].rest(2)

    @pl.loop(0, blocks)
    def _(b):
        here = pl.ds(pl.multiple_of(b * BLOCK, BLOCK), BLOCK)
        part = dot(d_rows[0, here, :], weight_here[0], ((1,), (0,)))
        part += dot(d_rows[1, here, :], weight_here[1], ((1,), (0,)))
        part += dot(d_rows[2, here, :], weight_here[2], ((1,), (0,)))
        d_part[...] = part
        d_part[pl.ds(pl.multiple_of(me * quarter, quarter), quarter), :] += dh_own[b]
        for u in range(4):
            fold_into(cols, (u, b), d_part[:, u * width : (u + 1) * width].astype(BF), True)
        cross(b).start()
        near(b).start()
        relay(b)

    sums[1].stage(1)
    swaps = [
        send(ssent, srecv.at[me], s_sems.at[0, k], s_sems.at[1, k], tensor=peer)
        for k, peer in enumerate((sibling, across, diagonal))
    ]
    for swap in swaps:
        swap.start()
    srecv[me] = ssent[...]

    sums[1].rest(2)
    for each in late_sums:
        each.stage(1)
    for b in range(blocks):
        near(b).wait()
        far(b).wait_recv()
        total = cols[me, b].astype(F32) + two[b].astype(F32) + three[b].astype(F32)
        packed[b * BLOCK : (b + 1) * BLOCK, :] = unfold(total.astype(BF), width, True)
    giving.start(packed)
    for each in late_sums:
        each.rest(2)

    for swap in swaps:
        swap.wait_recv()
    shared = small.shape[0] // 2
    swide[mine, 0:shared] = srecv[0, 0:shared] + srecv[1, 0:shared] + srecv[2, 0:shared] + srecv[3, 0:shared]
    swide[mine, shared:] = ssent[shared:, :]

    def spread(step):
        peer = (mine + step) % groups
        return send(swide.at[mine], swide.at[mine], w_sems.at[0, step], w_sems.at[1, step], dp=peer)

    @pl.loop(1, groups)
    def _(step):
        spread(step).start()

    for k, each in enumerate(sums):
        up_grad[k] = each.collect()
    giving_result.land(landed)
    layer_out[...] = landed[...].T

    @pl.loop(1, groups)
    def _(step):
        spread(step).wait_recv()

    for swap in swaps:
        swap.wait_send()
    ssent[...] = swide[0]

    @pl.loop(1, groups)
    def _(peer):
        ssent[...] += swide[peer]

    small_out[...] = ssent[0:8, :]
    up_out[...] = ssent[8:10, :]
    for k in range(2):
        qv_out[k : k + 1, :] = ssent[10:11, k * 256 : k * 256 + width]
    for k, each in enumerate(late_sums):
        total = each.collect()
        qkv_grad[2 * k] = total[:, :width]
        if k == 0:
            qkv_grad[1] = total[:, width:]
        else:
            out_grad[...] = total[:, width:].T
    giving.land(landed)
    input_grad[...] = landed[...].T
    for b in range(blocks):
        far(b).wait_send()
    for copy in returns:
        copy.wait_send()
    for each in sums + late_sums:
        each.end()

    @pl.loop(1, groups)
    def _(step):
        spread(step).wait_send()


def back(groups, grad_scale, args, small, number):
    dh_low, qkv, qkv_w, grad, folded = args[0], args[2], args[7], args[9], args[11]
    rows, columns = dh_low.shape
    width = qkv.shape[2]
    held, units = grad.shape[1:]
    blocks = rows // BLOCK
    half = (blocks, BLOCK // 2, 2 * width)
    dma = pltpu.SemaphoreType.DMA
    outs = (
        shape((width, rows), BF),
        shape((width, rows), BF),
        shape((2, held, units), F32),
        shape((3, held, width), F32),
        shape((width, held), F32),
        shape((8, columns), F32),
        shape((2, width), F32),
        shape((2, units), F32),
    )
    return call(
        functools.partial(back_kernel, groups, blocks, grad_scale),
        number,
        outs,
        [
            pltpu.VMEM((3, rows, width), BF),
            pltpu.VMEM((BLOCK, columns), F32),
            pltpu.VMEM((columns, 4 * width), F32),
            pltpu.VMEM((groups, held, 2 * width), BF),
            pltpu.VMEM((groups, held, 2 * width), BF),
            pltpu.VMEM((4,) + half, BF),
            pltpu.VMEM(half, BF),
            pltpu.VMEM(half, BF),
            pltpu.VMEM(half, BF),
            pltpu.VMEM((rows, width), BF),
            pltpu.VMEM(small.shape, F32),
            pltpu.VMEM((4,) + small.shape, F32),
            pltpu.VMEM((groups,) + small.shape, F32),
            dma((6, blocks)),
            dma((2, 3)),
            dma((2, groups)),
            pltpu.VMEM((rows, 8), jnp.int32),
            pltpu.VMEM((rows, rows), BF),
            pltpu.VMEM(qkv_w.shape, BF),
            pltpu.VMEM(folded.shape, BF),
            pltpu.VMEM((rows, width), BF),
            dma((2,)),
            dma((2, 3)),
        ]
        + GiveBack.scratch(groups, rows, width)
        + GiveBack.scratch(groups, rows, width)
        + GroupSum.scratch(groups, held, units) * 2
        + GroupSum.scratch(groups, held, 2 * width) * 2,
        args,
        apart=(7, 13),
    )


def on_device(
    tokens,
    cotangent,
    seq_start,
    row_place,
    qkv_weight,
    qv_bias,
    out_weight,
    out_bias,
    first_gain,
    first_shift,
    up_weight,
    up_bias,
    down_weight,
    down_bias,
    second_gain,
    second_shift,
):
    row_count, width = tokens.shape
    columns = qkv_weight.shape[1]
    groups = lax.axis_size("dp")
    grad_scale = (row_count * groups) ** (-0.5)
    seq_row = seq_start.reshape(1, row_count)
    weight_turned = qkv_weight.transpose(0, 2, 1)
    packed_in, cot_folded, full_out, qkv_rows, log_total, context, wide_context, taking = front(
        groups, (tokens.T, cotangent.T, row_place, seq_row, weight_turned, qv_bias, out_weight), 0
    )
    d_low, d_own, small, gate_grad, value_grad, down_grad, folded = mid(
        groups,
        grad_scale,
        (
            wide_context,
            packed_in,
            full_out.reshape(columns, columns),
            up_weight,
            up_bias,
            down_weight,
            cot_folded,
            out_bias,
            first_gain,
            first_shift,
            down_bias,
            second_gain,
            second_shift,
        ),
        1,
    )
    layer_out, input_grad, up_grad, qkv_grad, out_grad, sums, qv_bias_grad, up_bias_grad = back(
        groups,
        grad_scale,
        (
            d_low.reshape(row_count, columns),
            d_own,
            qkv_rows,
            log_total,
            seq_row,
            context,
            packed_in,
            weight_turned,
            out_weight,
            gate_grad,
            value_grad,
            folded,
            small,
            taking,
        ),
        small,
        2,
    )
    rows_here = columns // groups
    sums_here = lax.dynamic_slice_in_dim(sums[:6], lax.axis_index("dp") * rows_here, rows_here, 1)
    return (
        layer_out.T,
        input_grad.T,
        qkv_grad,
        qv_bias_grad,
        out_grad,
        sums_here[0],
        sums_here[1],
        sums_here[2],
        up_grad,
        up_bias_grad,
        down_grad.T,
        sums_here[3],
        sums_here[4],
        sums_here[5],
    )


def solution(mesh):
    return jax.shard_map(
        on_device,
        mesh=mesh,
        in_specs=(
            P("dp", "tensor"),
            P("dp", "tensor"),
            P("dp"),
            P("dp", None),
            P(None, None, "tensor"),
            P(None, "tensor"),
            P("tensor", None),
            P(),
            P(),
            P(),
            P(None, None, "tensor"),
            P(None, "tensor"),
            P("tensor", None),
            P(),
            P(),
            P(),
        ),
        out_specs=(
            P("dp", "tensor"),
            P("dp", "tensor"),
            P(None, "dp", "tensor"),
            P(None, "tensor"),
            P("tensor", "dp"),
            P("dp"),
            P("dp"),
            P("dp"),
            P(None, "dp", "tensor"),
            P(None, "tensor"),
            P("tensor", "dp"),
            P("dp"),
            P("dp"),
            P("dp"),
        ),
        check_vma=False,
    )
```

```python
import functools

import jax
import jax.numpy as jnp
from jax import lax
from jax.experimental import pallas as pl
from jax.experimental.pallas import tpu as pltpu
from jax.sharding import PartitionSpec as P

HEADS = 12
HEAD_DIM = 64
BLOCK = 512
BF = jnp.bfloat16
F32 = jnp.float32
MESH = pl.DeviceIdType.MESH
VMEM_LIMIT = 67043328


def dot(a, b, dims):
    return lax.dot_general(a, b, (dims, ((), ())), preferred_element_type=F32)


def place_of():
    me = lax.axis_index("tensor")
    core = me % 2
    side = me // 2
    sibling = side * 2 + (1 - core)
    across = (1 - side) * 2 + core
    diagonal = (1 - side) * 2 + (1 - core)
    return me, sibling, across, diagonal


def enter(devices, groups):
    barrier = pltpu.get_barrier_semaphore()
    count = len(devices)
    for device in devices:
        pl.semaphore_signal(barrier, inc=1, device_id={"tensor": device}, device_id_type=MESH)
    if groups:
        mine = lax.axis_index("dp")

        @pl.loop(1, groups)
        def _(step):
            pl.semaphore_signal(barrier, inc=1, device_id={"dp": (mine + step) % groups}, device_id_type=MESH)

        count += groups - 1
    pl.semaphore_wait(barrier, count)


def send(source, target, send_sem, recv_sem, **where):
    return pltpu.make_async_remote_copy(
        src_ref=source, dst_ref=target, send_sem=send_sem, recv_sem=recv_sem, device_id=where, device_id_type=MESH
    )


def fold_into(buffer, index, values, halves):
    width = values.shape[1]
    if not halves:
        buffer[index] = values
        return
    half = values.shape[0] // 2
    buffer[index + (slice(None), slice(0, width))] = values[:half]
    buffer[index + (slice(None), slice(width, 2 * width))] = values[half:]


def unfold(values, width, halves):
    if not halves:
        return values
    return jnp.concatenate([values[:, :width], values[:, width:]], axis=0)


def call(kernel, number, outs, scratch, args, apart=(), apart_outs=()):
    specs = [pl.BlockSpec(memory_space=pl.ANY if k in apart else pltpu.VMEM) for k in range(len(args))]
    return pl.pallas_call(
        kernel,
        out_shape=outs,
        in_specs=specs,
        out_specs=tuple(
            pl.BlockSpec(memory_space=pl.ANY if k in apart_outs else pltpu.VMEM) for k in range(len(outs))
        ),
        scratch_shapes=scratch,
        compiler_params=pltpu.CompilerParams(
            collective_id=number, has_side_effects=True, vmem_limit_bytes=VMEM_LIMIT
        ),
    )(*args)


def shape(dims, kind):
    return jax.ShapeDtypeStruct(dims, kind)


def to_column(row, column, where):
    for k in range(row.shape[1] // 128):
        piece = jnp.broadcast_to(row[0:1, k * 128 : (k + 1) * 128], (8, 128))
        column[k * 128 : (k + 1) * 128, where : where + 1] = piece.T[:, 0:1]


def slope_of(index):
    value = jnp.float32(2.0 ** (-8.0 / HEADS))
    for head in range(1, HEADS):
        value = jnp.where(index == head, jnp.float32(2.0 ** (-8.0 * (head + 1) / HEADS)), value)
    return value


def key_distance():
    keys = lax.broadcasted_iota(jnp.int32, (BLOCK, BLOCK), 0)
    asks = lax.broadcasted_iota(jnp.int32, (BLOCK, BLOCK), 1)
    return jnp.abs(keys - asks).astype(F32)


def scores_by_key(keys, queries, slope, distance, same):
    raw = dot(keys, queries, ((1,), (1,))) * (HEAD_DIM**-0.5) - slope * distance
    return jnp.where(same, raw, -1e30)


class HeadGather:
    def __init__(self, wide, sems):
        self.wide, self.sems = wide, sems
        self.me, self.sibling, self.across, _ = place_of()

    def copy(self, b, kind, whose, peer):
        return send(self.wide.at[whose, b], self.wide.at[whose, b], self.sems.at[2 * kind, b],
                    self.sems.at[2 * kind + 1, b], tensor=peer)

    def start(self, b, values):
        fold_into(self.wide, (self.me, b), values, True)
        self.copy(b, 0, self.me, self.across).start()
        self.copy(b, 1, self.me, self.sibling).start()

    def relay(self, b):
        self.copy(b, 0, self.me, self.across).wait_recv()
        self.copy(b, 2, self.across, self.sibling).start()

    def land(self, b, out, width):
        self.copy(b, 1, self.me, self.sibling).wait_recv()
        self.copy(b, 2, self.across, self.sibling).wait_recv()
        for s in range(4):
            out[b * BLOCK : (b + 1) * BLOCK, s * width : (s + 1) * width] = unfold(self.wide[s, b], width, True)

    def end(self, b):
        self.copy(b, 0, self.me, self.across).wait_send()
        self.copy(b, 1, self.me, self.sibling).wait_send()
        self.copy(b, 2, self.across, self.sibling).wait_send()


def front_kernel(groups, blocks, tokens, cot, place_row, seq_row, qkv_w, qv_bias, out_w,
                 packed_out, cot_out, full_out, qkv, lse, context, wide_context, taking,
                 tokens_turned, cot_turned, tokens_here, cot_here, weight_here, start_col, chosen, taken, sent, recv, arrived,
                 wide, wide_heads, local_sems, group_sems, gather_sems, head_sems, out_sems):
    me, sibling, across, diagonal = place_of()
    mine = lax.axis_index("dp")
    rows, width = tokens_here.shape
    heads = width // HEAD_DIM
    piece = rows // groups
    halves = (piece // 2) % 8 == 0
    quarter = BLOCK // 4
    loads = [
        pltpu.make_async_copy(source, target, local_sems.at[k])
        for k, (source, target) in enumerate(((tokens, tokens_turned), (cot, cot_turned), (qkv_w, weight_here)))
    ]
    for load in loads:
        load.start()
    enter([sibling, across, diagonal], groups)

    def moved(kind, step):
        peer = (mine + step) % groups
        return send(sent.at[kind, peer], recv.at[kind, mine], group_sems.at[0, kind, step],
                    group_sems.at[1, kind, step], dp=peer)

    def give(kind, source):
        @pl.loop(1, groups)
        def _(step):
            peer = (mine + step) % groups
            values = source[pl.ds(pl.multiple_of(peer * piece, 8), piece), :]
            fold_into(sent, (kind, peer), values, halves)
            moved(kind, step).start()

        values = source[pl.ds(pl.multiple_of(mine * piece, 8), piece), :]
        fold_into(recv, (kind, mine), values, halves)

    loads[0].wait()
    tokens_here[...] = tokens_turned[...].T
    give(0, tokens_here)
    out_far = send(out_w, full_out.at[me], out_sems.at[0], out_sems.at[1], tensor=across)
    out_near = send(out_w, full_out.at[me], out_sems.at[2], out_sems.at[3], tensor=sibling)
    out_pass = send(full_out.at[across], full_out.at[across], out_sems.at[4], out_sems.at[5], tensor=sibling)
    out_far.start()
    out_near.start()
    loads[1].wait()
    cot_here[...] = cot_turned[...].T
    full_out[me] = out_w[...]
    to_column(seq_row, start_col, 0)
    for b in range(blocks):
        ids = lax.broadcasted_iota(jnp.int32, (BLOCK, rows), 0) + b * BLOCK
        chosen[b * BLOCK : (b + 1) * BLOCK, :] = jnp.where(ids == place_row[...], 1.0, 0.0).astype(BF)

    to_column(place_row, start_col, 1)
    for b in range(blocks):
        ids = lax.broadcasted_iota(jnp.int32, (BLOCK, rows), 1)
        here = slice(b * BLOCK, (b + 1) * BLOCK)
        taken[here, :] = jnp.where(ids == start_col[here, 1:2], 1.0, 0.0).astype(BF)
    store = pltpu.make_async_copy(taken, taking, local_sems.at[3])
    store.start()

    def placed(b):
        return dot(chosen[b * BLOCK : (b + 1) * BLOCK, :], arrived[...], ((1,), (0,))).astype(BF)

    out_far.wait_recv()
    out_pass.start()

    def land(kind):
        @pl.loop(1, groups)
        def _(step):
            moved(kind, step).wait_recv()

        @pl.loop(0, groups)
        def _(peer):
            arrived[pl.ds(pl.multiple_of(peer * piece, 8), piece), :] = unfold(recv[kind, peer], width, halves)

    token_gather = HeadGather(wide, gather_sems)
    head_gather = HeadGather(wide_heads, head_sems)
    land(0)
    for b in range(blocks):
        token_gather.start(b, placed(b))
        if b >= 1:
            token_gather.relay(b - 1)
    give(1, cot_here)
    loads[2].wait()

    def attend(b):
        here = slice(b * BLOCK, (b + 1) * BLOCK)
        token_gather.land(b, packed_out, width)
        for k in range(3):
            part = dot(packed_out[here, :], weight_here[k], ((1,), (1,)))
            if k != 1:
                part += qv_bias[k // 2 : k // 2 + 1, :].astype(F32)
            qkv[k, here, :] = part.astype(BF)
        same = start_col[here, 0:1] == seq_row[0:1, here]
        distance = key_distance()
        for h in range(heads):
            lanes = slice(h * HEAD_DIM, (h + 1) * HEAD_DIM)
            scored = scores_by_key(qkv[1, here, lanes], qkv[0, here, lanes], slope_of(me * heads + h), distance, same)
            top = jnp.max(scored, axis=0, keepdims=True)
            raised = jnp.exp(scored - top)
            total = jnp.sum(raised, axis=0, keepdims=True)
            lse[b, h : h + 1, :] = top + jnp.log(total)
            probs = (raised * (1.0 / total)).astype(BF)
            turned = dot(qkv[2, here, lanes].T, probs, ((1,), (0,)))
            context[here, lanes] = turned.T.astype(BF)
        head_gather.start(b, context[here, :])

    for b in range(blocks):
        if b == blocks - 1:
            token_gather.relay(b)
        attend(b)
        if b >= 1:
            head_gather.relay(b - 1)
    for b in range(blocks - 1):
        head_gather.land(b, wide_context, width)
    land(1)
    for b in range(blocks):
        cot_block = placed(b)
        for u in range(4):
            fold_into(cot_out, (u, b), cot_block[u * quarter : (u + 1) * quarter], True)
    head_gather.relay(blocks - 1)
    head_gather.land(blocks - 1, wide_context, width)
    for b in range(blocks):
        token_gather.end(b)
        head_gather.end(b)
    store.wait()
    out_near.wait()
    out_pass.wait()
    out_far.wait_send()
    for kind in range(2):
        @pl.loop(1, groups)
        def _(step):
            moved(kind, step).wait_send()


def front(groups, args, number):
    tokens, qkv_w, out_w = args[0], args[4], args[6]
    width, rows = tokens.shape
    piece = rows // groups
    blocks = rows // BLOCK
    heads = width // HEAD_DIM
    halves = (piece // 2) % 8 == 0
    slab = (2, groups, piece // 2, 2 * width) if halves else (2, groups, piece, width)
    here = pltpu.VMEM((rows, width), BF)
    wide = pltpu.VMEM((4, blocks, BLOCK // 2, 2 * width), BF)
    turned = pltpu.VMEM((width, rows), BF)
    dma = pltpu.SemaphoreType.DMA
    return call(
        functools.partial(front_kernel, groups, blocks),
        number,
        (
            shape((rows, 4 * width), BF),
            shape((4, blocks, BLOCK // 8, 2 * width), BF),
            shape((4,) + out_w.shape, BF),
            shape((3, rows, width), BF),
            shape((blocks, heads, BLOCK), F32),
            shape((rows, width), BF),
            shape((rows, 4 * width), BF),
            shape((rows, rows), BF),
        ),
        [
            turned,
            turned,
            here,
            here,
            pltpu.VMEM(qkv_w.shape, BF),
            pltpu.VMEM((rows, 8), jnp.int32),
            pltpu.VMEM((rows, rows), BF),
            pltpu.VMEM((rows, rows), BF),
            pltpu.VMEM(slab, BF),
            pltpu.VMEM(slab, BF),
            here,
            wide,
            wide,
            dma((4,)),
            dma((2, 2, groups)),
            dma((6, blocks)),
            dma((6, blocks)),
            dma((6,)),
        ],
        args,
        apart=(0, 1, 4),
        apart_outs=(7,),
    )


def norm_unit(values):
    center = values - jnp.mean(values, axis=-1, keepdims=True)
    rs = lax.rsqrt(jnp.mean(center * center, axis=-1, keepdims=True) + 1e-05)
    return center * rs, rs


def norm_back(weighted, unit, rs):
    inner = jnp.mean(weighted * unit, axis=-1, keepdims=True)
    return rs * (weighted - jnp.mean(weighted, axis=-1, keepdims=True) - unit * inner)


class GroupSum:
    def __init__(self, groups, grads, scratch, turned):
        self.groups, self.grads, self.turned = groups, grads, turned
        self.stages = groups.bit_length() - 1
        self.recv = scratch[: self.stages]
        self.held = (None,) + tuple(scratch[self.stages : 2 * self.stages - 1])
        self.sems = scratch[-1]
        mine = lax.axis_index("dp")
        self.mine = mine // 2 + mine % 2 * (groups // 2) if turned else mine

    def real(self, device):
        half = self.groups // 2
        return device % half * 2 + device // half if self.turned else device

    def count(self, stage):
        return self.groups >> (stage + 1)

    def index(self, stage, step):
        return (self.mine // (2 << stage) + step) % self.count(stage)

    def given(self, stage, step):
        bit = (self.mine // (1 << stage)) % 2
        low = self.mine % (1 << stage)
        return self.index(stage, step) * (2 << stage) + (1 - bit) * (1 << stage) + low

    def copy(self, stage, step):
        bit = (self.mine // (1 << stage)) % 2
        partner = self.mine + (1 - 2 * bit) * (1 << stage)
        at = self.index(stage, step)
        source = self.held[stage].at[at] if stage else self.grads.at[self.real(self.given(0, step))]
        return send(source, self.recv[stage].at[at], self.sems.at[0, stage, step], self.sems.at[1, stage, step],
                    dp=self.real(partner))

    def start(self):
        @pl.loop(1, self.count(0) + 1)
        def _(step):
            self.copy(0, step).start()

    def total(self, stages, piece):
        total = self.grads[self.real(piece)].astype(F32)
        for stage in range(stages):
            count = self.count(stage)
            at = piece // (2 << stage)
            step = (at + 2 * count - 1 - self.mine // (2 << stage)) % count + 1
            self.copy(stage, step).wait_recv()
            total += self.recv[stage][at].astype(F32)
        return total

    def stage(self, stage):
        @pl.loop(1, self.count(stage) + 1)
        def _(step):
            at = self.index(stage, step)
            self.held[stage][at] = self.total(stage, self.given(stage, step)).astype(BF)
            self.copy(stage, step).start()

    def rest(self, first):
        for stage in range(first, self.stages):
            self.stage(stage)

    def collect(self):
        return self.total(self.stages, self.mine)

    def end(self):
        for stage in range(self.stages):
            @pl.loop(1, self.count(stage) + 1)
            def _(step):
                self.copy(stage, step).wait_send()

    @staticmethod
    def scratch(groups, held, span):
        stages = groups.bit_length() - 1
        buffers = [pltpu.VMEM((groups >> (k + 1), held, span), BF) for k in range(stages)]
        return buffers + buffers[1:] + [pltpu.SemaphoreType.DMA((2, stages, groups // 2 + 1))]


def both_ways(groups, pair, scratch, turned=True):
    half = len(scratch) // 2
    return [
        GroupSum(groups, grads, scratch[k * half : (k + 1) * half], turned and k == 1) for k, grads in enumerate(pair)
    ]


class GiveBack:
    def __init__(self, groups, rows, width, chosen, sent, recv, sems):
        self.groups, self.piece, self.width = groups, rows // groups, width
        self.halves = (self.piece // 2) % 8 == 0
        self.chosen, self.sent, self.recv, self.sems = chosen, sent, recv, sems
        self.mine = lax.axis_index("dp")

    def moved(self, step):
        peer = (self.mine + step) % self.groups
        return send(self.sent.at[peer], self.recv.at[self.mine], self.sems.at[0, step], self.sems.at[1, step], dp=peer)

    def start(self, packed):
        @pl.loop(0, self.groups)
        def _(step):
            peer = (self.mine + step) % self.groups
            rows = self.chosen[pl.ds(pl.multiple_of(peer * self.piece, 8), self.piece), :]
            values = dot(rows, packed[...], ((1,), (0,))).astype(BF)

            @pl.when(step > 0)
            def _():
                fold_into(self.sent, (peer,), values, self.halves)
                self.moved(step).start()

            @pl.when(step == 0)
            def _():
                fold_into(self.recv, (self.mine,), values, self.halves)

    def land(self, target):
        @pl.loop(1, self.groups)
        def _(step):
            self.moved(step).wait_recv()

        @pl.loop(0, self.groups)
        def _(peer):
            here = pl.ds(pl.multiple_of(peer * self.piece, 8), self.piece)
            target[here, :] = unfold(self.recv[peer], self.width, self.halves)

        @pl.loop(1, self.groups)
        def _(step):
            self.moved(step).wait_send()

    @staticmethod
    def scratch(groups, rows, width):
        piece = rows // groups
        halves = (piece // 2) % 8 == 0
        slab = (groups, piece // 2, 2 * width) if halves else (groups, piece, width)
        return [pltpu.VMEM(slab, BF)] * 2 + [pltpu.SemaphoreType.DMA((2, groups))]


class RowSum:
    def __init__(self, part, first, second, third, sems):
        self.part, self.first, self.second, self.third, self.sems = part, first, second, third, sems
        self.me, self.sibling, self.across, self.diagonal = place_of()

    def cross(self, b):
        return send(self.part.at[b, self.diagonal], self.first.at[b], self.sems.at[0, b], self.sems.at[1, b],
                    tensor=self.sibling)

    def near(self, b):
        return send(self.part.at[b, self.sibling], self.second.at[b], self.sems.at[2, b], self.sems.at[3, b],
                    tensor=self.sibling)

    def far(self, b):
        return send(self.first.at[b], self.third.at[b], self.sems.at[4, b], self.sems.at[5, b], tensor=self.across)

    def start(self, b):
        self.cross(b).start()
        self.near(b).start()

    def relay(self, b):
        self.cross(b).wait()
        self.first[b] = (self.part[b, self.across].astype(F32) + self.first[b].astype(F32)).astype(BF)
        self.far(b).start()

    def total(self, b):
        self.near(b).wait()
        self.far(b).wait()
        return self.part[b, self.me].astype(F32) + self.second[b].astype(F32) + self.third[b].astype(F32)

    @staticmethod
    def scratch(blocks, rows, columns):
        buffer = pltpu.VMEM((blocks, rows, columns), BF)
        return [pltpu.VMEM((blocks, 4, rows, columns), BF)] + [buffer] * 3 + [pltpu.SemaphoreType.DMA((6, blocks))]


class RowGather:
    def __init__(self, out, sems):
        self.out, self.sems = out, sems
        self.me, self.sibling, self.across, _ = place_of()

    def copy(self, b, kind, whose, peer):
        return send(self.out.at[b, whose], self.out.at[b, whose], self.sems.at[2 * kind, b],
                    self.sems.at[2 * kind + 1, b], tensor=peer)

    def start(self, b):
        self.copy(b, 0, self.me, self.across).start()
        self.copy(b, 1, self.me, self.sibling).start()

    def relay(self, b):
        self.copy(b, 0, self.me, self.across).wait_recv()
        self.copy(b, 2, self.across, self.sibling).start()

    def land(self, b):
        self.copy(b, 1, self.me, self.sibling).wait_recv()
        self.copy(b, 2, self.across, self.sibling).wait_recv()

    def end(self, b):
        self.copy(b, 0, self.me, self.across).wait_send()
        self.copy(b, 1, self.me, self.sibling).wait_send()
        self.copy(b, 2, self.across, self.sibling).wait_send()


CHUNK = 256


def mid_kernel(groups, blocks, grad_scale, context, packed, full_out, up_w, up_bias, down_w, cot_folded, v0, v1, v2, v3, v4, v5,
               d_low, d_own, small, gate_grad, value_grad, down_grad, folded,
               normed_low, slope_term, gelu_term, gated, d_gate, d_value, unit_full, rs_full, unit_own, rs_own, d_mixed,
               mixed, whole_grad, down_left, down_right, cot_recv,
               part1, first1, second1, third1, sems1, part2, first2, second2, third2, sems2, sems3, sems4, c_sems,
               vector_rows, *sum_scratch):
    me, sibling, across, diagonal = place_of()
    columns = packed.shape[1]
    width = columns // 4
    quarter = BLOCK // 4
    held = down_left.shape[1]
    enter([sibling, across, diagonal], groups)
    swaps = [
        send(cot_folded.at[peer], cot_recv.at[me], c_sems.at[0, k], c_sems.at[1, k], tensor=peer)
        for k, peer in enumerate((across, diagonal, sibling))
    ]
    for swap in swaps:
        swap.start()
    cot_recv[me] = cot_folded[me]
    ffn = RowSum(part1, first1, second1, third1, sems1)
    back_sum = RowSum(part2, first2, second2, third2, sems2)
    mixed_gather = RowGather(mixed, sems3)
    hidden_gather = RowGather(d_low, sems4)
    sums = both_ways(groups, (down_left, down_right), sum_scratch)
    small[...] = jnp.zeros_like(small)
    for k, vector in enumerate((v0, v1, v2, v3, v4, v5)):
        vector_rows[k : k + 1, :] = vector[...].astype(F32).reshape(1, columns)
    out_bias, first_gain, first_shift, down_bias, second_gain, second_shift = (
        vector_rows.at[k : k + 1] for k in range(6)
    )

    def add_small(row, values):
        small[row : row + 1, :] += jnp.sum(values, axis=0, keepdims=True) * grad_scale

    def ahead(b, c):
        here = slice(b * BLOCK + c * CHUNK, b * BLOCK + (c + 1) * CHUNK)
        inner = slice(c * CHUNK, (c + 1) * CHUNK)
        hidden = packed[here, :].astype(F32) + (dot(context[here, :], full_out[...], ((1,), (0,))) + out_bias[...])
        unit, rs = norm_unit(hidden)
        unit_full[inner, :] = unit
        rs_full[inner, :] = rs
        low = (unit * first_gain[...] + first_shift[...]).astype(BF)
        normed_low[here, :] = low
        gate = dot(low, up_w[0], ((1,), (0,))) + up_bias[0:1, :].astype(F32)
        value = dot(low, up_w[1], ((1,), (0,))) + up_bias[1:2, :].astype(F32)
        half_erf = 0.5 * (1.0 + lax.erf(gate * (0.5**0.5)))
        gelu = gate * half_erf
        slope = half_erf + gate * jnp.exp(-0.5 * gate * gate) * ((2.0 * jnp.pi) ** (-0.5))
        slope_term[here, :] = value * slope
        gelu_term[here, :] = gelu
        low_gated = (gelu * value).astype(BF)
        gated[here, :] = low_gated
        out = dot(low_gated, down_w[...], ((1,), (0,))).astype(BF)
        for k in range(CHUNK // quarter):
            part1[b, c * (CHUNK // quarter) + k] = out[k * quarter : (k + 1) * quarter]

    def keep_own(b):
        mine = pl.ds(pl.multiple_of(me * quarter, quarter), quarter)
        unit_own[b] = unit_full[mine, :]
        rs_own[b] = rs_full[mine, :]
        ffn.start(b)

    def turn(b):
        if b == 0:
            for swap in swaps:
                swap.wait_recv()
        values = unit_own[b] * first_gain[...] + first_shift[...] + (ffn.total(b) + down_bias[...])
        unit, rs = norm_unit(values)
        out = (unit * second_gain[...] + second_shift[...]).astype(BF)
        for u in range(4):
            fold_into(folded, (u, b), out[:, u * width : (u + 1) * width], True)
        cot_rows = jnp.concatenate([unfold(cot_recv[s, b], width, True) for s in range(4)], axis=1).astype(F32)
        d_rows = norm_back(cot_rows * second_gain[...], unit, rs)
        d_mixed[b] = d_rows
        mixed[b, me] = d_rows.astype(BF)
        mixed_gather.start(b)
        add_small(3, d_rows)
        add_small(4, cot_rows * unit)
        add_small(5, cot_rows)

    def astern(b):
        mixed_gather.land(b)
        for c in range(BLOCK // CHUNK):
            here = slice(b * BLOCK + c * CHUNK, b * BLOCK + (c + 1) * CHUNK)
            count = CHUNK // quarter
            d_rows = jnp.concatenate([mixed[b, c * count + k] for k in range(count)], axis=0)
            d_gated = dot(d_rows, down_w[...], ((1,), (1,)))
            gate_rows = (d_gated * slope_term[here, :]).astype(BF)
            value_rows = (d_gated * gelu_term[here, :]).astype(BF)
            d_gate[here, :] = gate_rows
            d_value[here, :] = value_rows
            add_small(8, gate_rows.astype(F32))
            add_small(9, value_rows.astype(F32))
            out = dot(gate_rows, up_w[0], ((1,), (1,))) + dot(value_rows, up_w[1], ((1,), (1,)))
            out = out.astype(BF)
            for k in range(count):
                part2[b, c * count + k] = out[k * quarter : (k + 1) * quarter]
        back_sum.start(b)

    def finish(b):
        d_normed = d_mixed[b] + back_sum.total(b)
        d_hidden = norm_back(d_normed * first_gain[...], unit_own[b], rs_own[b])
        d_own[b] = d_hidden
        d_low[b, me] = d_hidden.astype(BF)
        hidden_gather.start(b)
        add_small(0, d_hidden)
        add_small(1, d_normed * unit_own[b])
        add_small(2, d_normed)

    def weight_grad(left, right, pieces):
        whole_grad[...] = dot(left, right[...], ((0,), (0,)))
        for g in range(groups):
            rows_here = (whole_grad[g * held : (g + 1) * held, :] * grad_scale).astype(BF)
            for k, target in enumerate(pieces):
                target[g] = rows_here[:, k * target.shape[2] : (k + 1) * target.shape[2]]

    last = blocks - 1
    for b in range(blocks):
        ahead(b, 0)
        if b >= 1:
            ffn.relay(b - 1)
        if b >= 2:
            turn(b - 2)
        ahead(b, 1)
        keep_own(b)
        if b >= 2:
            mixed_gather.relay(b - 2)
    ffn.relay(last)
    if blocks > 1:
        turn(last - 1)
    turn(last)
    if blocks > 1:
        mixed_gather.relay(last - 1)
    for b in range(blocks):
        if b == last:
            mixed_gather.relay(last)
        astern(b)
        if b >= 1:
            back_sum.relay(b - 1)
    back_sum.relay(last)
    d_mixed_rows = jnp.concatenate([mixed[b, k] for b in range(blocks) for k in range(4)], axis=0)
    weight_grad(d_mixed_rows, gated, (down_left, down_right))
    for half in sums:
        half.start()
    finish(0)
    weight_grad(normed_low[...], d_gate, (gate_grad,))
    if blocks > 1:
        finish(1)
    weight_grad(normed_low[...], d_value, (value_grad,))
    for b in range(2, blocks):
        finish(b)
    for half in sums:
        half.stage(1)
    for b in range(blocks):
        hidden_gather.relay(b)
    for half in sums:
        half.rest(2)
    for b in range(blocks):
        hidden_gather.land(b)
    for k, half in enumerate(sums):
        span = half.grads.shape[2]
        down_grad[:, k * span : (k + 1) * span] = half.collect()
    for b in range(blocks):
        mixed_gather.end(b)
        hidden_gather.end(b)
    for swap in swaps:
        swap.wait_send()
    for half in sums:
        half.end()


def mid(groups, grad_scale, args, number):
    context, up_w, cot_folded = args[0], args[3], args[6]
    rows, columns = context.shape
    units = up_w.shape[2]
    held = columns // groups
    blocks = rows // BLOCK
    quarter = BLOCK // 4
    own = (blocks, quarter, columns)
    dma = pltpu.SemaphoreType.DMA
    outs = (
        shape((blocks, 4, quarter, columns), BF),
        shape(own, F32),
        shape((16, columns), F32),
        shape((groups, held, units), BF),
        shape((groups, held, units), BF),
        shape((held, units), F32),
        shape(cot_folded.shape, BF),
    )
    return call(
        functools.partial(mid_kernel, groups, blocks, grad_scale),
        number,
        outs,
        [
            pltpu.VMEM((rows, columns), BF),
            pltpu.VMEM((rows, units), F32),
            pltpu.VMEM((rows, units), F32),
            pltpu.VMEM((rows, units), BF),
            pltpu.VMEM((rows, units), BF),
            pltpu.VMEM((rows, units), BF),
            pltpu.VMEM((BLOCK, columns), F32),
            pltpu.VMEM((BLOCK, 1), F32),
            pltpu.VMEM(own, F32),
            pltpu.VMEM((blocks, quarter, 1), F32),
            pltpu.VMEM(own, F32),
            pltpu.VMEM((blocks, 4, quarter, columns), BF),
            pltpu.VMEM((columns, units), F32),
            pltpu.VMEM((groups, held, units // 2), BF),
            pltpu.VMEM((groups, held, units // 2), BF),
            pltpu.VMEM(cot_folded.shape, BF),
        ]
        + RowSum.scratch(blocks, quarter, columns)
        + RowSum.scratch(blocks, quarter, columns)
        + [dma((6, blocks)), dma((6, blocks)), dma((2, 3)), pltpu.VMEM((6, columns), F32)]
        + GroupSum.scratch(groups, held, units // 2)
        + GroupSum.scratch(groups, held, units // 2),
        args,
    )


def back_kernel(groups, blocks, grad_scale, dh_low, dh_own, qkv, lse, seq_row, context, packed_in, qkv_w,
                out_w, gate_grad, value_grad, folded, small, taking,
                layer_out, input_grad, up_grad, qkv_grad, out_grad, small_out, qv_out, up_out,
                d_rows, d_part, late_sum, late_left, late_right, cols, one, two, three, packed, ssent, srecv, swide, x_sems, s_sems, w_sems,
                start_col, chosen, weight_here, returned, landed, load_sem, r_sems,
                sent, recv, a_sems, sent2, recv5, a_sems2, *sum_scratch):
    me, sibling, across, diagonal = place_of()
    mine = lax.axis_index("dp")
    width, rows = input_grad.shape
    heads = width // HEAD_DIM
    held = late_left.shape[1]
    quarter = BLOCK // 4
    load = pltpu.make_async_copy(qkv_w, weight_here, load_sem.at[0])
    load.start()
    load_rows = pltpu.make_async_copy(taking, chosen, load_sem.at[1])
    load_rows.start()
    enter([sibling, across, diagonal], groups)
    half_scratch = len(sum_scratch) // 2
    sums = both_ways(groups, (gate_grad, value_grad), sum_scratch[:half_scratch], False)
    late_sums = both_ways(groups, (late_left, late_right), sum_scratch[half_scratch:])
    giving = GiveBack(groups, rows, width, chosen, sent, recv, a_sems)
    giving_result = GiveBack(groups, rows, width, chosen, sent2, recv5, a_sems2)
    for each in sums:
        each.start()
    returns = [
        send(folded.at[peer], returned.at[me], r_sems.at[0, k], r_sems.at[1, k], tensor=peer)
        for k, peer in enumerate((across, diagonal, sibling))
    ]
    for swap in returns:
        swap.start()
    returned[me] = folded[me]
    def cross(b):
        return send(cols.at[diagonal, b], one.at[b], x_sems.at[0, b], x_sems.at[1, b], tensor=sibling)

    def near(b):
        return send(cols.at[sibling, b], two.at[b], x_sems.at[2, b], x_sems.at[3, b], tensor=sibling)

    def far(b):
        return send(one.at[b], three.at[b], x_sems.at[4, b], x_sems.at[5, b], tensor=across)

    def relay(b):
        cross(b).wait()
        one[b] = (cols[across, b].astype(F32) + one[b].astype(F32)).astype(BF)
        far(b).start()

    to_column(seq_row, start_col, 0)
    late_sum[:, 3 * width :] = dot(dh_low[...], context[...], ((0,), (0,)))
    load.wait()
    ssent[...] = small[...]

    @pl.loop(0, blocks)
    def _(b):
        here = pl.ds(pl.multiple_of(b * BLOCK, BLOCK), BLOCK)
        dh = dh_low[here, :]
        d_context = dot(dh, out_w[...], ((1,), (1,))).astype(BF)
        same = start_col[here, 0:1] == seq_row[0:1, here]
        distance = key_distance()
        for h in range(heads):
            lanes = slice(h * HEAD_DIM, (h + 1) * HEAD_DIM)
            queries = qkv[0, here, lanes]
            keys = qkv[1, here, lanes]
            values = qkv[2, here, lanes]
            d_rows_out = d_context[:, lanes]
            scored = scores_by_key(keys, queries, slope_of(me * heads + h), distance, same)
            probs = jnp.exp(scored - lse[b, h : h + 1, :])
            d_probs = dot(values, d_rows_out, ((1,), (1,)))
            d_rows[here, 2 * width + h * HEAD_DIM : 2 * width + (h + 1) * HEAD_DIM] = dot(probs.astype(BF), d_rows_out, ((1,), (0,))).astype(BF)
            center = jnp.sum(probs * d_probs, axis=0, keepdims=True)
            d_scores = (probs * (d_probs - center)).astype(BF)
            d_rows[here, 1 * width + h * HEAD_DIM : 1 * width + (h + 1) * HEAD_DIM] = (dot(d_scores, queries, ((1,), (0,))) * (HEAD_DIM**-0.5)).astype(BF)
            turned = dot(keys.T, d_scores, ((1,), (0,))) * (HEAD_DIM**-0.5)
            d_rows[here, 0 * width + h * HEAD_DIM : 0 * width + (h + 1) * HEAD_DIM] = turned.T.astype(BF)
        last = small.shape[0] - 6
        for k, c in enumerate((0, 2)):
            bias = jnp.sum(d_rows[here, c * width : (c + 1) * width].astype(F32), axis=0, keepdims=True) * grad_scale
            ssent[last : last + 1, k * 2 * 128 : k * 2 * 128 + width] += bias
        @pl.when(b == 1)
        def _():
            load_rows.wait()
            for swap in returns:
                swap.wait_recv()
            for q in range(blocks):
                for s in range(4):
                    start = q * BLOCK + s * quarter
                    packed[start : start + quarter, :] = unfold(returned[s, q], width, True)
            giving_result.start(packed)
            sums[0].stage(1)

    late_sum[:, : 3 * width] = dot(packed_in[...], d_rows[...], ((0,), (0,)))
    for g in range(groups):
        rows_here = (late_sum[g * held : (g + 1) * held, :] * grad_scale).astype(BF)
        late_left[g] = rows_here[:, : 2 * width]
        late_right[g] = rows_here[:, 2 * width :]

    for each in late_sums:
        each.start()
    sums[0].rest(2)

    @pl.loop(0, blocks)
    def _(b):
        here = pl.ds(pl.multiple_of(b * BLOCK, BLOCK), BLOCK)
        d_part[...] = dot(d_rows[here, :], weight_here[...], ((1,), (0,)))
        d_part[pl.ds(pl.multiple_of(me * quarter, quarter), quarter), :] += dh_own[b]
        for u in range(4):
            fold_into(cols, (u, b), d_part[:, u * width : (u + 1) * width].astype(BF), True)
        cross(b).start()
        near(b).start()
        relay(b)

    sums[1].stage(1)
    swaps = [
        send(ssent, srecv.at[me], s_sems.at[0, k], s_sems.at[1, k], tensor=peer)
        for k, peer in enumerate((sibling, across, diagonal))
    ]
    for swap in swaps:
        swap.start()
    srecv[me] = ssent[...]

    sums[1].rest(2)
    for each in late_sums:
        each.stage(1)
    for b in range(blocks):
        near(b).wait()
        far(b).wait_recv()
        total = cols[me, b].astype(F32) + two[b].astype(F32) + three[b].astype(F32)
        packed[b * BLOCK : (b + 1) * BLOCK, :] = unfold(total.astype(BF), width, True)
    giving.start(packed)
    for each in late_sums:
        each.rest(2)

    for swap in swaps:
        swap.wait_recv()
    shared = small.shape[0] // 2
    swide[mine, 0:shared] = srecv[0, 0:shared] + srecv[1, 0:shared] + srecv[2, 0:shared] + srecv[3, 0:shared]
    swide[mine, shared:] = ssent[shared:, :]

    def spread(step):
        peer = (mine + step) % groups
        return send(swide.at[mine], swide.at[mine], w_sems.at[0, step], w_sems.at[1, step], dp=peer)

    @pl.loop(1, groups)
    def _(step):
        spread(step).start()

    for k, each in enumerate(sums):
        up_grad[k] = each.collect()
    giving_result.land(landed)
    layer_out[...] = landed[...].T

    @pl.loop(1, groups)
    def _(step):
        spread(step).wait_recv()

    for swap in swaps:
        swap.wait_send()
    ssent[...] = swide[0]

    @pl.loop(1, groups)
    def _(peer):
        ssent[...] += swide[peer]

    small_out[...] = ssent[0:8, :]
    up_out[...] = ssent[8:10, :]
    for k in range(2):
        qv_out[k : k + 1, :] = ssent[10:11, k * 256 : k * 256 + width]
    for k, each in enumerate(late_sums):
        total = each.collect()
        qkv_grad[2 * k] = total[:, :width]
        if k == 0:
            qkv_grad[1] = total[:, width:]
        else:
            out_grad[...] = total[:, width:].T
    giving.land(landed)
    input_grad[...] = landed[...].T
    for b in range(blocks):
        far(b).wait_send()
    for copy in returns:
        copy.wait_send()
    for each in sums + late_sums:
        each.end()

    @pl.loop(1, groups)
    def _(step):
        spread(step).wait_send()


def back(groups, grad_scale, args, small, number):
    dh_low, qkv, qkv_w, grad, folded = args[0], args[2], args[7], args[9], args[11]
    rows, columns = dh_low.shape
    width = qkv.shape[2]
    held, units = grad.shape[1:]
    blocks = rows // BLOCK
    half = (blocks, BLOCK // 2, 2 * width)
    dma = pltpu.SemaphoreType.DMA
    outs = (
        shape((width, rows), BF),
        shape((width, rows), BF),
        shape((2, held, units), F32),
        shape((3, held, width), F32),
        shape((width, held), F32),
        shape((8, columns), F32),
        shape((2, width), F32),
        shape((2, units), F32),
    )
    return call(
        functools.partial(back_kernel, groups, blocks, grad_scale),
        number,
        outs,
        [
            pltpu.VMEM((rows, 3 * width), BF),
            pltpu.VMEM((BLOCK, columns), F32),
            pltpu.VMEM((columns, 4 * width), F32),
            pltpu.VMEM((groups, held, 2 * width), BF),
            pltpu.VMEM((groups, held, 2 * width), BF),
            pltpu.VMEM((4,) + half, BF),
            pltpu.VMEM(half, BF),
            pltpu.VMEM(half, BF),
            pltpu.VMEM(half, BF),
            pltpu.VMEM((rows, width), BF),
            pltpu.VMEM(small.shape, F32),
            pltpu.VMEM((4,) + small.shape, F32),
            pltpu.VMEM((groups,) + small.shape, F32),
            dma((6, blocks)),
            dma((2, 3)),
            dma((2, groups)),
            pltpu.VMEM((rows, 8), jnp.int32),
            pltpu.VMEM((rows, rows), BF),
            pltpu.VMEM(qkv_w.shape, BF),
            pltpu.VMEM(folded.shape, BF),
            pltpu.VMEM((rows, width), BF),
            dma((2,)),
            dma((2, 3)),
        ]
        + GiveBack.scratch(groups, rows, width)
        + GiveBack.scratch(groups, rows, width)
        + GroupSum.scratch(groups, held, units) * 2
        + GroupSum.scratch(groups, held, 2 * width) * 2,
        args,
        apart=(7, 13),
    )


def on_device(
    tokens,
    cotangent,
    seq_start,
    row_place,
    qkv_weight,
    qv_bias,
    out_weight,
    out_bias,
    first_gain,
    first_shift,
    up_weight,
    up_bias,
    down_weight,
    down_bias,
    second_gain,
    second_shift,
):
    row_count, width = tokens.shape
    columns = qkv_weight.shape[1]
    groups = lax.axis_size("dp")
    grad_scale = (row_count * groups) ** (-0.5)
    seq_row = seq_start.reshape(1, row_count)
    weight_turned = qkv_weight.transpose(0, 2, 1)
    packed_in, cot_folded, full_out, qkv_rows, log_total, context, wide_context, taking = front(
        groups, (tokens.T, cotangent.T, row_place, seq_row, weight_turned, qv_bias, out_weight), 0
    )
    d_low, d_own, small, gate_grad, value_grad, down_grad, folded = mid(
        groups,
        grad_scale,
        (
            wide_context,
            packed_in,
            full_out.reshape(columns, columns),
            up_weight,
            up_bias,
            down_weight,
            cot_folded,
            out_bias,
            first_gain,
            first_shift,
            down_bias,
            second_gain,
            second_shift,
        ),
        1,
    )
    layer_out, input_grad, up_grad, qkv_grad, out_grad, sums, qv_bias_grad, up_bias_grad = back(
        groups,
        grad_scale,
        (
            d_low.reshape(row_count, columns),
            d_own,
            qkv_rows,
            log_total,
            seq_row,
            context,
            packed_in,
            weight_turned.reshape(3 * width, columns),
            out_weight,
            gate_grad,
            value_grad,
            folded,
            small,
            taking,
        ),
        small,
        2,
    )
    rows_here = columns // groups
    sums_here = lax.dynamic_slice_in_dim(sums[:6], lax.axis_index("dp") * rows_here, rows_here, 1)
    return (
        layer_out.T,
        input_grad.T,
        qkv_grad,
        qv_bias_grad,
        out_grad,
        sums_here[0],
        sums_here[1],
        sums_here[2],
        up_grad,
        up_bias_grad,
        down_grad.T,
        sums_here[3],
        sums_here[4],
        sums_here[5],
    )


def solution(mesh):
    return jax.shard_map(
        on_device,
        mesh=mesh,
        in_specs=(
            P("dp", "tensor"),
            P("dp", "tensor"),
            P("dp"),
            P("dp", None),
            P(None, None, "tensor"),
            P(None, "tensor"),
            P("tensor", None),
            P(),
            P(),
            P(),
            P(None, None, "tensor"),
            P(None, "tensor"),
            P("tensor", None),
            P(),
            P(),
            P(),
        ),
        out_specs=(
            P("dp", "tensor"),
            P("dp", "tensor"),
            P(None, "dp", "tensor"),
            P(None, "tensor"),
            P("tensor", "dp"),
            P("dp"),
            P("dp"),
            P("dp"),
            P(None, "dp", "tensor"),
            P(None, "tensor"),
            P("tensor", "dp"),
            P("dp"),
            P("dp"),
            P("dp"),
        ),
        check_vma=False,
    )
```

```python
import functools

import jax
import jax.numpy as jnp
from jax import lax
from jax.experimental import pallas as pl
from jax.experimental.pallas import tpu as pltpu
from jax.sharding import PartitionSpec as P

HEADS = 12
HEAD_DIM = 64
BLOCK = 512
BF = jnp.bfloat16
F32 = jnp.float32
MESH = pl.DeviceIdType.MESH
VMEM_LIMIT = 67043328


def dot(a, b, dims):
    return lax.dot_general(a, b, (dims, ((), ())), preferred_element_type=F32)


def place_of():
    me = lax.axis_index("tensor")
    core = me % 2
    side = me // 2
    sibling = side * 2 + (1 - core)
    across = (1 - side) * 2 + core
    diagonal = (1 - side) * 2 + (1 - core)
    return me, sibling, across, diagonal


def enter(devices, groups):
    barrier = pltpu.get_barrier_semaphore()
    count = len(devices)
    for device in devices:
        pl.semaphore_signal(barrier, inc=1, device_id={"tensor": device}, device_id_type=MESH)
    if groups:
        mine = lax.axis_index("dp")

        @pl.loop(1, groups)
        def _(step):
            pl.semaphore_signal(barrier, inc=1, device_id={"dp": (mine + step) % groups}, device_id_type=MESH)

        count += groups - 1
    pl.semaphore_wait(barrier, count)


def send(source, target, send_sem, recv_sem, **where):
    return pltpu.make_async_remote_copy(
        src_ref=source, dst_ref=target, send_sem=send_sem, recv_sem=recv_sem, device_id=where, device_id_type=MESH
    )


def fold_into(buffer, index, values, halves):
    width = values.shape[1]
    if not halves:
        buffer[index] = values
        return
    half = values.shape[0] // 2
    buffer[index + (slice(None), slice(0, width))] = values[:half]
    buffer[index + (slice(None), slice(width, 2 * width))] = values[half:]


def unfold(values, width, halves):
    if not halves:
        return values
    return jnp.concatenate([values[:, :width], values[:, width:]], axis=0)


def call(kernel, number, outs, scratch, args, apart=(), apart_outs=()):
    specs = [pl.BlockSpec(memory_space=pl.ANY if k in apart else pltpu.VMEM) for k in range(len(args))]
    return pl.pallas_call(
        kernel,
        out_shape=outs,
        in_specs=specs,
        out_specs=tuple(
            pl.BlockSpec(memory_space=pl.ANY if k in apart_outs else pltpu.VMEM) for k in range(len(outs))
        ),
        scratch_shapes=scratch,
        compiler_params=pltpu.CompilerParams(
            collective_id=number, has_side_effects=True, vmem_limit_bytes=VMEM_LIMIT
        ),
    )(*args)


def shape(dims, kind):
    return jax.ShapeDtypeStruct(dims, kind)


def to_column(row, column, where):
    for k in range(row.shape[1] // 128):
        piece = jnp.broadcast_to(row[0:1, k * 128 : (k + 1) * 128], (8, 128))
        column[k * 128 : (k + 1) * 128, where : where + 1] = piece.T[:, 0:1]


def slope_of(index):
    value = jnp.float32(2.0 ** (-8.0 / HEADS))
    for head in range(1, HEADS):
        value = jnp.where(index == head, jnp.float32(2.0 ** (-8.0 * (head + 1) / HEADS)), value)
    return value


def key_distance():
    keys = lax.broadcasted_iota(jnp.int32, (BLOCK, BLOCK), 0)
    asks = lax.broadcasted_iota(jnp.int32, (BLOCK, BLOCK), 1)
    return jnp.abs(keys - asks).astype(F32)


def scores_by_key(keys, queries, slope, distance, same):
    raw = dot(keys, queries, ((1,), (1,))) * (HEAD_DIM**-0.5) - slope * distance
    return jnp.where(same, raw, -1e30)


class HeadGather:
    def __init__(self, wide, sems):
        self.wide, self.sems = wide, sems
        self.me, self.sibling, self.across, _ = place_of()

    def copy(self, b, kind, whose, peer):
        return send(self.wide.at[whose, b], self.wide.at[whose, b], self.sems.at[2 * kind, b],
                    self.sems.at[2 * kind + 1, b], tensor=peer)

    def start(self, b, values):
        fold_into(self.wide, (self.me, b), values, True)
        self.copy(b, 0, self.me, self.across).start()
        self.copy(b, 1, self.me, self.sibling).start()

    def relay(self, b):
        self.copy(b, 0, self.me, self.across).wait_recv()
        self.copy(b, 2, self.across, self.sibling).start()

    def land(self, b, out, width):
        self.copy(b, 1, self.me, self.sibling).wait_recv()
        self.copy(b, 2, self.across, self.sibling).wait_recv()
        for s in range(4):
            out[b * BLOCK : (b + 1) * BLOCK, s * width : (s + 1) * width] = unfold(self.wide[s, b], width, True)

    def end(self, b):
        self.copy(b, 0, self.me, self.across).wait_send()
        self.copy(b, 1, self.me, self.sibling).wait_send()
        self.copy(b, 2, self.across, self.sibling).wait_send()


def front_kernel(groups, blocks, tokens, cot, place_row, seq_row, qkv_w, qv_bias, out_w,
                 packed_out, cot_out, full_out, qkv, lse, context, wide_context, taking,
                 tokens_turned, cot_turned, tokens_here, cot_here, weight_here, start_col, chosen, taken, sent, recv, arrived,
                 wide, wide_heads, local_sems, group_sems, gather_sems, head_sems, out_sems):
    me, sibling, across, diagonal = place_of()
    mine = lax.axis_index("dp")
    rows, width = tokens_here.shape
    heads = width // HEAD_DIM
    piece = rows // groups
    halves = (piece // 2) % 8 == 0
    quarter = BLOCK // 4
    loads = [
        pltpu.make_async_copy(source, target, local_sems.at[k])
        for k, (source, target) in enumerate(((tokens, tokens_turned), (cot, cot_turned), (qkv_w, weight_here)))
    ]
    for load in loads:
        load.start()
    enter([sibling, across, diagonal], groups)

    def moved(kind, step):
        peer = (mine + step) % groups
        return send(sent.at[kind, peer], recv.at[kind, mine], group_sems.at[0, kind, step],
                    group_sems.at[1, kind, step], dp=peer)

    def give(kind, source):
        @pl.loop(1, groups)
        def _(step):
            peer = (mine + step) % groups
            values = source[pl.ds(pl.multiple_of(peer * piece, 8), piece), :]
            fold_into(sent, (kind, peer), values, halves)
            moved(kind, step).start()

        values = source[pl.ds(pl.multiple_of(mine * piece, 8), piece), :]
        fold_into(recv, (kind, mine), values, halves)

    loads[0].wait()
    tokens_here[...] = tokens_turned[...].T
    give(0, tokens_here)
    out_far = send(out_w, full_out.at[me], out_sems.at[0], out_sems.at[1], tensor=across)
    out_near = send(out_w, full_out.at[me], out_sems.at[2], out_sems.at[3], tensor=sibling)
    out_pass = send(full_out.at[across], full_out.at[across], out_sems.at[4], out_sems.at[5], tensor=sibling)
    out_far.start()
    out_near.start()
    loads[1].wait()
    cot_here[...] = cot_turned[...].T
    full_out[me] = out_w[...]
    to_column(seq_row, start_col, 0)
    for b in range(blocks):
        ids = lax.broadcasted_iota(jnp.int32, (BLOCK, rows), 0) + b * BLOCK
        chosen[b * BLOCK : (b + 1) * BLOCK, :] = jnp.where(ids == place_row[...], 1.0, 0.0).astype(BF)

    to_column(place_row, start_col, 1)
    for b in range(blocks):
        ids = lax.broadcasted_iota(jnp.int32, (BLOCK, rows), 1)
        here = slice(b * BLOCK, (b + 1) * BLOCK)
        taken[here, :] = jnp.where(ids == start_col[here, 1:2], 1.0, 0.0).astype(BF)
    store = pltpu.make_async_copy(taken, taking, local_sems.at[3])
    store.start()

    def placed(b):
        return dot(chosen[b * BLOCK : (b + 1) * BLOCK, :], arrived[...], ((1,), (0,))).astype(BF)

    out_far.wait_recv()
    out_pass.start()

    def land(kind):
        @pl.loop(1, groups)
        def _(step):
            moved(kind, step).wait_recv()

        @pl.loop(0, groups)
        def _(peer):
            arrived[pl.ds(pl.multiple_of(peer * piece, 8), piece), :] = unfold(recv[kind, peer], width, halves)

    token_gather = HeadGather(wide, gather_sems)
    head_gather = HeadGather(wide_heads, head_sems)
    land(0)
    for b in range(blocks):
        token_gather.start(b, placed(b))
        if b >= 1:
            token_gather.relay(b - 1)
    give(1, cot_here)
    loads[2].wait()

    def attend(b):
        here = slice(b * BLOCK, (b + 1) * BLOCK)
        token_gather.land(b, packed_out, width)
        for k in range(3):
            part = dot(packed_out[here, :], weight_here[k], ((1,), (1,)))
            if k != 1:
                part += qv_bias[k // 2 : k // 2 + 1, :].astype(F32)
            qkv[k, here, :] = part.astype(BF)
        same = start_col[here, 0:1] == seq_row[0:1, here]
        distance = key_distance()
        for h in range(heads):
            lanes = slice(h * HEAD_DIM, (h + 1) * HEAD_DIM)
            scored = scores_by_key(qkv[1, here, lanes], qkv[0, here, lanes], slope_of(me * heads + h), distance, same)
            top = jnp.max(scored, axis=0, keepdims=True)
            raised = jnp.exp(scored - top)
            total = jnp.sum(raised, axis=0, keepdims=True)
            lse[b, h : h + 1, :] = top + jnp.log(total)
            probs = (raised * (1.0 / total)).astype(BF)
            turned = dot(qkv[2, here, lanes].T, probs, ((1,), (0,)))
            context[here, lanes] = turned.T.astype(BF)
        head_gather.start(b, context[here, :])

    for b in range(blocks):
        if b == blocks - 1:
            token_gather.relay(b)
        attend(b)
        if b >= 1:
            head_gather.relay(b - 1)
    for b in range(blocks - 1):
        head_gather.land(b, wide_context, width)
    land(1)
    for b in range(blocks):
        cot_block = placed(b)
        for u in range(4):
            fold_into(cot_out, (u, b), cot_block[u * quarter : (u + 1) * quarter], True)
    head_gather.relay(blocks - 1)
    head_gather.land(blocks - 1, wide_context, width)
    for b in range(blocks):
        token_gather.end(b)
        head_gather.end(b)
    store.wait()
    out_near.wait()
    out_pass.wait()
    out_far.wait_send()
    for kind in range(2):
        @pl.loop(1, groups)
        def _(step):
            moved(kind, step).wait_send()


def front(groups, args, number):
    tokens, qkv_w, out_w = args[0], args[4], args[6]
    width, rows = tokens.shape
    piece = rows // groups
    blocks = rows // BLOCK
    heads = width // HEAD_DIM
    halves = (piece // 2) % 8 == 0
    slab = (2, groups, piece // 2, 2 * width) if halves else (2, groups, piece, width)
    here = pltpu.VMEM((rows, width), BF)
    wide = pltpu.VMEM((4, blocks, BLOCK // 2, 2 * width), BF)
    turned = pltpu.VMEM((width, rows), BF)
    dma = pltpu.SemaphoreType.DMA
    return call(
        functools.partial(front_kernel, groups, blocks),
        number,
        (
            shape((rows, 4 * width), BF),
            shape((4, blocks, BLOCK // 8, 2 * width), BF),
            shape((4,) + out_w.shape, BF),
            shape((3, rows, width), BF),
            shape((blocks, heads, BLOCK), F32),
            shape((rows, width), BF),
            shape((rows, 4 * width), BF),
            shape((rows, rows), BF),
        ),
        [
            turned,
            turned,
            here,
            here,
            pltpu.VMEM(qkv_w.shape, BF),
            pltpu.VMEM((rows, 8), jnp.int32),
            pltpu.VMEM((rows, rows), BF),
            pltpu.VMEM((rows, rows), BF),
            pltpu.VMEM(slab, BF),
            pltpu.VMEM(slab, BF),
            here,
            wide,
            wide,
            dma((4,)),
            dma((2, 2, groups)),
            dma((6, blocks)),
            dma((6, blocks)),
            dma((6,)),
        ],
        args,
        apart=(0, 1, 4),
        apart_outs=(7,),
    )


def norm_unit(values):
    center = values - jnp.mean(values, axis=-1, keepdims=True)
    rs = lax.rsqrt(jnp.mean(center * center, axis=-1, keepdims=True) + 1e-05)
    return center * rs, rs


def norm_back(weighted, unit, rs):
    inner = jnp.mean(weighted * unit, axis=-1, keepdims=True)
    return rs * (weighted - jnp.mean(weighted, axis=-1, keepdims=True) - unit * inner)


class GroupSum:
    def __init__(self, groups, grads, scratch, turned):
        self.groups, self.grads, self.turned = groups, grads, turned
        self.stages = groups.bit_length() - 1
        self.recv = scratch[: self.stages]
        self.held = (None,) + tuple(scratch[self.stages : 2 * self.stages - 1])
        self.sems = scratch[-1]
        mine = lax.axis_index("dp")
        self.mine = mine // 2 + mine % 2 * (groups // 2) if turned else mine

    def real(self, device):
        half = self.groups // 2
        return device % half * 2 + device // half if self.turned else device

    def count(self, stage):
        return self.groups >> (stage + 1)

    def index(self, stage, step):
        return (self.mine // (2 << stage) + step) % self.count(stage)

    def given(self, stage, step):
        bit = (self.mine // (1 << stage)) % 2
        low = self.mine % (1 << stage)
        return self.index(stage, step) * (2 << stage) + (1 - bit) * (1 << stage) + low

    def copy(self, stage, step):
        bit = (self.mine // (1 << stage)) % 2
        partner = self.mine + (1 - 2 * bit) * (1 << stage)
        at = self.index(stage, step)
        source = self.held[stage].at[at] if stage else self.grads.at[self.real(self.given(0, step))]
        return send(source, self.recv[stage].at[at], self.sems.at[0, stage, step], self.sems.at[1, stage, step],
                    dp=self.real(partner))

    def start(self):
        @pl.loop(1, self.count(0) + 1)
        def _(step):
            self.copy(0, step).start()

    def total(self, stages, piece):
        total = self.grads[self.real(piece)].astype(F32)
        for stage in range(stages):
            count = self.count(stage)
            at = piece // (2 << stage)
            step = (at + 2 * count - 1 - self.mine // (2 << stage)) % count + 1
            self.copy(stage, step).wait_recv()
            total += self.recv[stage][at].astype(F32)
        return total

    def stage(self, stage):
        @pl.loop(1, self.count(stage) + 1)
        def _(step):
            at = self.index(stage, step)
            self.held[stage][at] = self.total(stage, self.given(stage, step)).astype(BF)
            self.copy(stage, step).start()

    def rest(self, first):
        for stage in range(first, self.stages):
            self.stage(stage)

    def collect(self):
        return self.total(self.stages, self.mine)

    def end(self):
        for stage in range(self.stages):
            @pl.loop(1, self.count(stage) + 1)
            def _(step):
                self.copy(stage, step).wait_send()

    @staticmethod
    def scratch(groups, held, span):
        stages = groups.bit_length() - 1
        buffers = [pltpu.VMEM((groups >> (k + 1), held, span), BF) for k in range(stages)]
        return buffers + buffers[1:] + [pltpu.SemaphoreType.DMA((2, stages, groups // 2 + 1))]


def both_ways(groups, pair, scratch, turned=True):
    half = len(scratch) // 2
    return [
        GroupSum(groups, grads, scratch[k * half : (k + 1) * half], turned and k == 1) for k, grads in enumerate(pair)
    ]


class GiveBack:
    def __init__(self, groups, rows, width, chosen, sent, recv, sems):
        self.groups, self.piece, self.width = groups, rows // groups, width
        self.halves = (self.piece // 2) % 8 == 0
        self.chosen, self.sent, self.recv, self.sems = chosen, sent, recv, sems
        self.mine = lax.axis_index("dp")

    def moved(self, step):
        peer = (self.mine + step) % self.groups
        return send(self.sent.at[peer], self.recv.at[self.mine], self.sems.at[0, step], self.sems.at[1, step], dp=peer)

    def start(self, packed):
        @pl.loop(0, self.groups)
        def _(step):
            peer = (self.mine + step) % self.groups
            rows = self.chosen[pl.ds(pl.multiple_of(peer * self.piece, 8), self.piece), :]
            values = dot(rows, packed[...], ((1,), (0,))).astype(BF)

            @pl.when(step > 0)
            def _():
                fold_into(self.sent, (peer,), values, self.halves)
                self.moved(step).start()

            @pl.when(step == 0)
            def _():
                fold_into(self.recv, (self.mine,), values, self.halves)

    def land(self, target):
        @pl.loop(1, self.groups)
        def _(step):
            self.moved(step).wait_recv()

        @pl.loop(0, self.groups)
        def _(peer):
            here = pl.ds(pl.multiple_of(peer * self.piece, 8), self.piece)
            target[here, :] = unfold(self.recv[peer], self.width, self.halves)

        @pl.loop(1, self.groups)
        def _(step):
            self.moved(step).wait_send()

    @staticmethod
    def scratch(groups, rows, width):
        piece = rows // groups
        halves = (piece // 2) % 8 == 0
        slab = (groups, piece // 2, 2 * width) if halves else (groups, piece, width)
        return [pltpu.VMEM(slab, BF)] * 2 + [pltpu.SemaphoreType.DMA((2, groups))]


class RowSum:
    def __init__(self, part, first, second, third, sems):
        self.part, self.first, self.second, self.third, self.sems = part, first, second, third, sems
        self.me, self.sibling, self.across, self.diagonal = place_of()

    def cross(self, b):
        return send(self.part.at[b, self.diagonal], self.first.at[b], self.sems.at[0, b], self.sems.at[1, b],
                    tensor=self.sibling)

    def near(self, b):
        return send(self.part.at[b, self.sibling], self.second.at[b], self.sems.at[2, b], self.sems.at[3, b],
                    tensor=self.sibling)

    def far(self, b):
        return send(self.first.at[b], self.third.at[b], self.sems.at[4, b], self.sems.at[5, b], tensor=self.across)

    def start(self, b):
        self.cross(b).start()
        self.near(b).start()

    def relay(self, b):
        self.cross(b).wait()
        self.first[b] = (self.part[b, self.across].astype(F32) + self.first[b].astype(F32)).astype(BF)
        self.far(b).start()

    def total(self, b):
        self.near(b).wait()
        self.far(b).wait()
        return self.part[b, self.me].astype(F32) + self.second[b].astype(F32) + self.third[b].astype(F32)

    @staticmethod
    def scratch(blocks, rows, columns):
        buffer = pltpu.VMEM((blocks, rows, columns), BF)
        return [pltpu.VMEM((blocks, 4, rows, columns), BF)] + [buffer] * 3 + [pltpu.SemaphoreType.DMA((6, blocks))]


class RowGather:
    def __init__(self, out, sems):
        self.out, self.sems = out, sems
        self.me, self.sibling, self.across, _ = place_of()

    def copy(self, b, kind, whose, peer):
        return send(self.out.at[b, whose], self.out.at[b, whose], self.sems.at[2 * kind, b],
                    self.sems.at[2 * kind + 1, b], tensor=peer)

    def start(self, b):
        self.copy(b, 0, self.me, self.across).start()
        self.copy(b, 1, self.me, self.sibling).start()

    def relay(self, b):
        self.copy(b, 0, self.me, self.across).wait_recv()
        self.copy(b, 2, self.across, self.sibling).start()

    def land(self, b):
        self.copy(b, 1, self.me, self.sibling).wait_recv()
        self.copy(b, 2, self.across, self.sibling).wait_recv()

    def end(self, b):
        self.copy(b, 0, self.me, self.across).wait_send()
        self.copy(b, 1, self.me, self.sibling).wait_send()
        self.copy(b, 2, self.across, self.sibling).wait_send()


CHUNK = 256


def mid_kernel(groups, blocks, grad_scale, context, packed, full_out, up_w, up_bias, down_w, cot_folded, v0, v1, v2, v3, v4, v5,
               d_low, d_own, small, gate_sum, value_grad, down_grad, folded,
               normed_low, slope_term, gelu_term, gated, d_gate, d_value, unit_full, rs_full, unit_own, rs_own, d_mixed,
               mixed, whole_grad, down_left, down_right, gate_left, gate_right, cot_recv,
               part1, first1, second1, third1, sems1, part2, first2, second2, third2, sems2, sems3, sems4, c_sems,
               vector_rows, *sum_scratch):
    me, sibling, across, diagonal = place_of()
    columns = packed.shape[1]
    width = columns // 4
    quarter = BLOCK // 4
    held = down_left.shape[1]
    enter([sibling, across, diagonal], groups)
    swaps = [
        send(cot_folded.at[peer], cot_recv.at[me], c_sems.at[0, k], c_sems.at[1, k], tensor=peer)
        for k, peer in enumerate((across, diagonal, sibling))
    ]
    for swap in swaps:
        swap.start()
    cot_recv[me] = cot_folded[me]
    ffn = RowSum(part1, first1, second1, third1, sems1)
    back_sum = RowSum(part2, first2, second2, third2, sems2)
    mixed_gather = RowGather(mixed, sems3)
    hidden_gather = RowGather(d_low, sems4)
    half_scratch = len(sum_scratch) // 2
    sums = both_ways(groups, (down_left, down_right), sum_scratch[:half_scratch])
    gate_sums = both_ways(groups, (gate_left, gate_right), sum_scratch[half_scratch:])
    small[...] = jnp.zeros_like(small)
    for k, vector in enumerate((v0, v1, v2, v3, v4, v5)):
        vector_rows[k : k + 1, :] = vector[...].astype(F32).reshape(1, columns)
    out_bias, first_gain, first_shift, down_bias, second_gain, second_shift = (
        vector_rows.at[k : k + 1] for k in range(6)
    )

    def add_small(row, values):
        small[row : row + 1, :] += jnp.sum(values, axis=0, keepdims=True) * grad_scale

    def ahead(b, c):
        here = slice(b * BLOCK + c * CHUNK, b * BLOCK + (c + 1) * CHUNK)
        inner = slice(c * CHUNK, (c + 1) * CHUNK)
        hidden = packed[here, :].astype(F32) + (dot(context[here, :], full_out[...], ((1,), (0,))) + out_bias[...])
        unit, rs = norm_unit(hidden)
        unit_full[inner, :] = unit
        rs_full[inner, :] = rs
        low = (unit * first_gain[...] + first_shift[...]).astype(BF)
        normed_low[here, :] = low
        gate = dot(low, up_w[0], ((1,), (0,))) + up_bias[0:1, :].astype(F32)
        value = dot(low, up_w[1], ((1,), (0,))) + up_bias[1:2, :].astype(F32)
        half_erf = 0.5 * (1.0 + lax.erf(gate * (0.5**0.5)))
        gelu = gate * half_erf
        slope = half_erf + gate * jnp.exp(-0.5 * gate * gate) * ((2.0 * jnp.pi) ** (-0.5))
        slope_term[here, :] = value * slope
        gelu_term[here, :] = gelu
        low_gated = (gelu * value).astype(BF)
        gated[here, :] = low_gated
        out = dot(low_gated, down_w[...], ((1,), (0,))).astype(BF)
        for k in range(CHUNK // quarter):
            part1[b, c * (CHUNK // quarter) + k] = out[k * quarter : (k + 1) * quarter]

    def keep_own(b):
        mine = pl.ds(pl.multiple_of(me * quarter, quarter), quarter)
        unit_own[b] = unit_full[mine, :]
        rs_own[b] = rs_full[mine, :]
        ffn.start(b)

    def turn(b):
        if b == 0:
            for swap in swaps:
                swap.wait_recv()
        values = unit_own[b] * first_gain[...] + first_shift[...] + (ffn.total(b) + down_bias[...])
        unit, rs = norm_unit(values)
        out = (unit * second_gain[...] + second_shift[...]).astype(BF)
        for u in range(4):
            fold_into(folded, (u, b), out[:, u * width : (u + 1) * width], True)
        cot_rows = jnp.concatenate([unfold(cot_recv[s, b], width, True) for s in range(4)], axis=1).astype(F32)
        d_rows = norm_back(cot_rows * second_gain[...], unit, rs)
        d_mixed[b] = d_rows
        mixed[b, me] = d_rows.astype(BF)
        mixed_gather.start(b)
        add_small(3, d_rows)
        add_small(4, cot_rows * unit)
        add_small(5, cot_rows)

    def astern(b):
        mixed_gather.land(b)
        for c in range(BLOCK // CHUNK):
            here = slice(b * BLOCK + c * CHUNK, b * BLOCK + (c + 1) * CHUNK)
            count = CHUNK // quarter
            d_rows = jnp.concatenate([mixed[b, c * count + k] for k in range(count)], axis=0)
            d_gated = dot(d_rows, down_w[...], ((1,), (1,)))
            gate_rows = (d_gated * slope_term[here, :]).astype(BF)
            value_rows = (d_gated * gelu_term[here, :]).astype(BF)
            d_gate[here, :] = gate_rows
            d_value[here, :] = value_rows
            add_small(8, gate_rows.astype(F32))
            add_small(9, value_rows.astype(F32))
            out = dot(gate_rows, up_w[0], ((1,), (1,))) + dot(value_rows, up_w[1], ((1,), (1,)))
            out = out.astype(BF)
            for k in range(count):
                part2[b, c * count + k] = out[k * quarter : (k + 1) * quarter]
        back_sum.start(b)

    def finish(b):
        d_normed = d_mixed[b] + back_sum.total(b)
        d_hidden = norm_back(d_normed * first_gain[...], unit_own[b], rs_own[b])
        d_own[b] = d_hidden
        d_low[b, me] = d_hidden.astype(BF)
        hidden_gather.start(b)
        add_small(0, d_hidden)
        add_small(1, d_normed * unit_own[b])
        add_small(2, d_normed)

    def weight_grad(left, right, pieces):
        whole_grad[...] = dot(left, right[...], ((0,), (0,)))
        for g in range(groups):
            rows_here = (whole_grad[g * held : (g + 1) * held, :] * grad_scale).astype(BF)
            for k, target in enumerate(pieces):
                target[g] = rows_here[:, k * target.shape[2] : (k + 1) * target.shape[2]]

    last = blocks - 1
    for b in range(blocks):
        ahead(b, 0)
        if b >= 1:
            ffn.relay(b - 1)
        if b >= 2:
            turn(b - 2)
        ahead(b, 1)
        keep_own(b)
        if b >= 2:
            mixed_gather.relay(b - 2)
    ffn.relay(last)
    if blocks > 1:
        turn(last - 1)
    turn(last)
    if blocks > 1:
        mixed_gather.relay(last - 1)
    for b in range(blocks):
        if b == last:
            mixed_gather.relay(last)
        astern(b)
        if b >= 1:
            back_sum.relay(b - 1)
    back_sum.relay(last)
    d_mixed_rows = jnp.concatenate([mixed[b, k] for b in range(blocks) for k in range(4)], axis=0)
    weight_grad(d_mixed_rows, gated, (down_left, down_right))
    for half in sums:
        half.start()
    finish(0)
    weight_grad(normed_low[...], d_gate, (gate_left, gate_right))
    for half in gate_sums:
        half.start()
    if blocks > 1:
        finish(1)
    weight_grad(normed_low[...], d_value, (value_grad,))
    for b in range(2, blocks):
        finish(b)
    for half in sums:
        half.stage(1)
    for b in range(blocks):
        hidden_gather.relay(b)
    for half in sums:
        half.rest(2)
    for half in gate_sums:
        half.stage(1)
    for b in range(blocks):
        hidden_gather.land(b)
    for k, half in enumerate(sums):
        span = half.grads.shape[2]
        down_grad[:, k * span : (k + 1) * span] = half.collect()
    for half in gate_sums:
        half.rest(2)
    for k, half in enumerate(gate_sums):
        span = half.grads.shape[2]
        gate_sum[:, k * span : (k + 1) * span] = half.collect()
    for b in range(blocks):
        mixed_gather.end(b)
        hidden_gather.end(b)
    for swap in swaps:
        swap.wait_send()
    for half in sums + gate_sums:
        half.end()


def mid(groups, grad_scale, args, number):
    context, up_w, cot_folded = args[0], args[3], args[6]
    rows, columns = context.shape
    units = up_w.shape[2]
    held = columns // groups
    blocks = rows // BLOCK
    quarter = BLOCK // 4
    own = (blocks, quarter, columns)
    dma = pltpu.SemaphoreType.DMA
    outs = (
        shape((blocks, 4, quarter, columns), BF),
        shape(own, F32),
        shape((16, columns), F32),
        shape((held, units), F32),
        shape((groups, held, units), BF),
        shape((held, units), F32),
        shape(cot_folded.shape, BF),
    )
    return call(
        functools.partial(mid_kernel, groups, blocks, grad_scale),
        number,
        outs,
        [
            pltpu.VMEM((rows, columns), BF),
            pltpu.VMEM((rows, units), F32),
            pltpu.VMEM((rows, units), F32),
            pltpu.VMEM((rows, units), BF),
            pltpu.VMEM((rows, units), BF),
            pltpu.VMEM((rows, units), BF),
            pltpu.VMEM((BLOCK, columns), F32),
            pltpu.VMEM((BLOCK, 1), F32),
            pltpu.VMEM(own, F32),
            pltpu.VMEM((blocks, quarter, 1), F32),
            pltpu.VMEM(own, F32),
            pltpu.VMEM((blocks, 4, quarter, columns), BF),
            pltpu.VMEM((columns, units), F32),
            pltpu.VMEM((groups, held, units // 2), BF),
            pltpu.VMEM((groups, held, units // 2), BF),
            pltpu.VMEM((groups, held, units // 2), BF),
            pltpu.VMEM((groups, held, units // 2), BF),
            pltpu.VMEM(cot_folded.shape, BF),
        ]
        + RowSum.scratch(blocks, quarter, columns)
        + RowSum.scratch(blocks, quarter, columns)
        + [dma((6, blocks)), dma((6, blocks)), dma((2, 3)), pltpu.VMEM((6, columns), F32)]
        + GroupSum.scratch(groups, held, units // 2) * 4,
        args,
    )


def back_kernel(groups, blocks, grad_scale, dh_low, dh_own, qkv, lse, seq_row, context, packed_in, qkv_w,
                out_w, gate_sum, value_grad, folded, small, taking,
                layer_out, input_grad, up_grad, qkv_grad, out_grad, small_out, qv_out, up_out,
                d_rows, d_part, late_sum, late_left, late_right, cols, one, two, three, packed, ssent, srecv, swide, x_sems, s_sems, w_sems,
                start_col, chosen, weight_here, returned, landed, load_sem, r_sems,
                sent, recv, a_sems, sent2, recv5, a_sems2, *sum_scratch):
    me, sibling, across, diagonal = place_of()
    mine = lax.axis_index("dp")
    width, rows = input_grad.shape
    heads = width // HEAD_DIM
    held = late_left.shape[1]
    quarter = BLOCK // 4
    load = pltpu.make_async_copy(qkv_w, weight_here, load_sem.at[0])
    load.start()
    load_rows = pltpu.make_async_copy(taking, chosen, load_sem.at[1])
    load_rows.start()
    enter([sibling, across, diagonal], groups)
    part_scratch = len(sum_scratch) // 3
    value_sum = GroupSum(groups, value_grad, sum_scratch[:part_scratch], False)
    late_sums = both_ways(groups, (late_left, late_right), sum_scratch[part_scratch:])
    giving = GiveBack(groups, rows, width, chosen, sent, recv, a_sems)
    giving_result = GiveBack(groups, rows, width, chosen, sent2, recv5, a_sems2)
    value_sum.start()
    up_grad[0] = gate_sum[...]
    returns = [
        send(folded.at[peer], returned.at[me], r_sems.at[0, k], r_sems.at[1, k], tensor=peer)
        for k, peer in enumerate((across, diagonal, sibling))
    ]
    for swap in returns:
        swap.start()
    returned[me] = folded[me]
    def cross(b):
        return send(cols.at[diagonal, b], one.at[b], x_sems.at[0, b], x_sems.at[1, b], tensor=sibling)

    def near(b):
        return send(cols.at[sibling, b], two.at[b], x_sems.at[2, b], x_sems.at[3, b], tensor=sibling)

    def far(b):
        return send(one.at[b], three.at[b], x_sems.at[4, b], x_sems.at[5, b], tensor=across)

    def relay(b):
        cross(b).wait()
        one[b] = (cols[across, b].astype(F32) + one[b].astype(F32)).astype(BF)
        far(b).start()

    to_column(seq_row, start_col, 0)
    late_sum[:, 3 * width :] = dot(dh_low[...], context[...], ((0,), (0,)))
    load.wait()
    ssent[...] = small[...]

    @pl.loop(0, blocks)
    def _(b):
        here = pl.ds(pl.multiple_of(b * BLOCK, BLOCK), BLOCK)
        dh = dh_low[here, :]
        d_context = dot(dh, out_w[...], ((1,), (1,))).astype(BF)
        same = start_col[here, 0:1] == seq_row[0:1, here]
        distance = key_distance()
        for h in range(heads):
            lanes = slice(h * HEAD_DIM, (h + 1) * HEAD_DIM)
            queries = qkv[0, here, lanes]
            keys = qkv[1, here, lanes]
            values = qkv[2, here, lanes]
            d_rows_out = d_context[:, lanes]
            scored = scores_by_key(keys, queries, slope_of(me * heads + h), distance, same)
            probs = jnp.exp(scored - lse[b, h : h + 1, :])
            d_probs = dot(values, d_rows_out, ((1,), (1,)))
            d_rows[here, 2 * width + h * HEAD_DIM : 2 * width + (h + 1) * HEAD_DIM] = dot(probs.astype(BF), d_rows_out, ((1,), (0,))).astype(BF)
            center = jnp.sum(probs * d_probs, axis=0, keepdims=True)
            d_scores = (probs * (d_probs - center)).astype(BF)
            d_rows[here, 1 * width + h * HEAD_DIM : 1 * width + (h + 1) * HEAD_DIM] = (dot(d_scores, queries, ((1,), (0,))) * (HEAD_DIM**-0.5)).astype(BF)
            turned = dot(keys.T, d_scores, ((1,), (0,))) * (HEAD_DIM**-0.5)
            d_rows[here, 0 * width + h * HEAD_DIM : 0 * width + (h + 1) * HEAD_DIM] = turned.T.astype(BF)
        last = small.shape[0] - 6
        for k, c in enumerate((0, 2)):
            bias = jnp.sum(d_rows[here, c * width : (c + 1) * width].astype(F32), axis=0, keepdims=True) * grad_scale
            ssent[last : last + 1, k * 2 * 128 : k * 2 * 128 + width] += bias
        @pl.when(b == 1)
        def _():
            load_rows.wait()
            for swap in returns:
                swap.wait_recv()
            for q in range(blocks):
                for s in range(4):
                    start = q * BLOCK + s * quarter
                    packed[start : start + quarter, :] = unfold(returned[s, q], width, True)
            giving_result.start(packed)
            value_sum.stage(1)

    late_sum[:, : 3 * width] = dot(packed_in[...], d_rows[...], ((0,), (0,)))
    for g in range(groups):
        rows_here = (late_sum[g * held : (g + 1) * held, :] * grad_scale).astype(BF)
        late_left[g] = rows_here[:, : 2 * width]
        late_right[g] = rows_here[:, 2 * width :]

    for each in late_sums:
        each.start()
    value_sum.rest(2)

    @pl.loop(0, blocks)
    def _(b):
        here = pl.ds(pl.multiple_of(b * BLOCK, BLOCK), BLOCK)
        d_part[...] = dot(d_rows[here, :], weight_here[...], ((1,), (0,)))
        d_part[pl.ds(pl.multiple_of(me * quarter, quarter), quarter), :] += dh_own[b]
        for u in range(4):
            fold_into(cols, (u, b), d_part[:, u * width : (u + 1) * width].astype(BF), True)
        cross(b).start()
        near(b).start()
        relay(b)

    swaps = [
        send(ssent, srecv.at[me], s_sems.at[0, k], s_sems.at[1, k], tensor=peer)
        for k, peer in enumerate((sibling, across, diagonal))
    ]
    for swap in swaps:
        swap.start()
    srecv[me] = ssent[...]

    for each in late_sums:
        each.stage(1)
    for b in range(blocks):
        near(b).wait()
        far(b).wait_recv()
        total = cols[me, b].astype(F32) + two[b].astype(F32) + three[b].astype(F32)
        packed[b * BLOCK : (b + 1) * BLOCK, :] = unfold(total.astype(BF), width, True)
    giving.start(packed)
    for each in late_sums:
        each.rest(2)

    for swap in swaps:
        swap.wait_recv()
    shared = small.shape[0] // 2
    swide[mine, 0:shared] = srecv[0, 0:shared] + srecv[1, 0:shared] + srecv[2, 0:shared] + srecv[3, 0:shared]
    swide[mine, shared:] = ssent[shared:, :]

    def spread(step):
        peer = (mine + step) % groups
        return send(swide.at[mine], swide.at[mine], w_sems.at[0, step], w_sems.at[1, step], dp=peer)

    @pl.loop(1, groups)
    def _(step):
        spread(step).start()

    up_grad[1] = value_sum.collect()
    giving_result.land(landed)
    layer_out[...] = landed[...].T

    @pl.loop(1, groups)
    def _(step):
        spread(step).wait_recv()

    for swap in swaps:
        swap.wait_send()
    ssent[...] = swide[0]

    @pl.loop(1, groups)
    def _(peer):
        ssent[...] += swide[peer]

    small_out[...] = ssent[0:8, :]
    up_out[...] = ssent[8:10, :]
    for k in range(2):
        qv_out[k : k + 1, :] = ssent[10:11, k * 256 : k * 256 + width]
    for k, each in enumerate(late_sums):
        total = each.collect()
        qkv_grad[2 * k] = total[:, :width]
        if k == 0:
            qkv_grad[1] = total[:, width:]
        else:
            out_grad[...] = total[:, width:].T
    giving.land(landed)
    input_grad[...] = landed[...].T
    for b in range(blocks):
        far(b).wait_send()
    for copy in returns:
        copy.wait_send()
    for each in [value_sum] + late_sums:
        each.end()

    @pl.loop(1, groups)
    def _(step):
        spread(step).wait_send()


def back(groups, grad_scale, args, small, number):
    dh_low, qkv, qkv_w, grad, folded = args[0], args[2], args[7], args[10], args[11]
    rows, columns = dh_low.shape
    width = qkv.shape[2]
    held, units = grad.shape[1:]
    blocks = rows // BLOCK
    half = (blocks, BLOCK // 2, 2 * width)
    dma = pltpu.SemaphoreType.DMA
    outs = (
        shape((width, rows), BF),
        shape((width, rows), BF),
        shape((2, held, units), F32),
        shape((3, held, width), F32),
        shape((width, held), F32),
        shape((8, columns), F32),
        shape((2, width), F32),
        shape((2, units), F32),
    )
    return call(
        functools.partial(back_kernel, groups, blocks, grad_scale),
        number,
        outs,
        [
            pltpu.VMEM((rows, 3 * width), BF),
            pltpu.VMEM((BLOCK, columns), F32),
            pltpu.VMEM((columns, 4 * width), F32),
            pltpu.VMEM((groups, held, 2 * width), BF),
            pltpu.VMEM((groups, held, 2 * width), BF),
            pltpu.VMEM((4,) + half, BF),
            pltpu.VMEM(half, BF),
            pltpu.VMEM(half, BF),
            pltpu.VMEM(half, BF),
            pltpu.VMEM((rows, width), BF),
            pltpu.VMEM(small.shape, F32),
            pltpu.VMEM((4,) + small.shape, F32),
            pltpu.VMEM((groups,) + small.shape, F32),
            dma((6, blocks)),
            dma((2, 3)),
            dma((2, groups)),
            pltpu.VMEM((rows, 8), jnp.int32),
            pltpu.VMEM((rows, rows), BF),
            pltpu.VMEM(qkv_w.shape, BF),
            pltpu.VMEM(folded.shape, BF),
            pltpu.VMEM((rows, width), BF),
            dma((2,)),
            dma((2, 3)),
        ]
        + GiveBack.scratch(groups, rows, width)
        + GiveBack.scratch(groups, rows, width)
        + GroupSum.scratch(groups, held, units)
        + GroupSum.scratch(groups, held, 2 * width) * 2,
        args,
        apart=(7, 13),
    )


def on_device(
    tokens,
    cotangent,
    seq_start,
    row_place,
    qkv_weight,
    qv_bias,
    out_weight,
    out_bias,
    first_gain,
    first_shift,
    up_weight,
    up_bias,
    down_weight,
    down_bias,
    second_gain,
    second_shift,
):
    row_count, width = tokens.shape
    columns = qkv_weight.shape[1]
    groups = lax.axis_size("dp")
    grad_scale = (row_count * groups) ** (-0.5)
    seq_row = seq_start.reshape(1, row_count)
    weight_turned = qkv_weight.transpose(0, 2, 1)
    packed_in, cot_folded, full_out, qkv_rows, log_total, context, wide_context, taking = front(
        groups, (tokens.T, cotangent.T, row_place, seq_row, weight_turned, qv_bias, out_weight), 0
    )
    d_low, d_own, small, gate_sum, value_grad, down_grad, folded = mid(
        groups,
        grad_scale,
        (
            wide_context,
            packed_in,
            full_out.reshape(columns, columns),
            up_weight,
            up_bias,
            down_weight,
            cot_folded,
            out_bias,
            first_gain,
            first_shift,
            down_bias,
            second_gain,
            second_shift,
        ),
        1,
    )
    layer_out, input_grad, up_grad, qkv_grad, out_grad, sums, qv_bias_grad, up_bias_grad = back(
        groups,
        grad_scale,
        (
            d_low.reshape(row_count, columns),
            d_own,
            qkv_rows,
            log_total,
            seq_row,
            context,
            packed_in,
            weight_turned.reshape(3 * width, columns),
            out_weight,
            gate_sum,
            value_grad,
            folded,
            small,
            taking,
        ),
        small,
        2,
    )
    rows_here = columns // groups
    sums_here = lax.dynamic_slice_in_dim(sums[:6], lax.axis_index("dp") * rows_here, rows_here, 1)
    return (
        layer_out.T,
        input_grad.T,
        qkv_grad,
        qv_bias_grad,
        out_grad,
        sums_here[0],
        sums_here[1],
        sums_here[2],
        up_grad,
        up_bias_grad,
        down_grad.T,
        sums_here[3],
        sums_here[4],
        sums_here[5],
    )


def solution(mesh):
    return jax.shard_map(
        on_device,
        mesh=mesh,
        in_specs=(
            P("dp", "tensor"),
            P("dp", "tensor"),
            P("dp"),
            P("dp", None),
            P(None, None, "tensor"),
            P(None, "tensor"),
            P("tensor", None),
            P(),
            P(),
            P(),
            P(None, None, "tensor"),
            P(None, "tensor"),
            P("tensor", None),
            P(),
            P(),
            P(),
        ),
        out_specs=(
            P("dp", "tensor"),
            P("dp", "tensor"),
            P(None, "dp", "tensor"),
            P(None, "tensor"),
            P("tensor", "dp"),
            P("dp"),
            P("dp"),
            P("dp"),
            P(None, "dp", "tensor"),
            P(None, "tensor"),
            P("tensor", "dp"),
            P("dp"),
            P("dp"),
            P("dp"),
        ),
        check_vma=False,
    )
```
